32 devices in a mesh: dp: 8 (over z, y), mp: 4 (over x, core).
Axes of the slice: x: 2, y: 2, z: 4, core: 2. Of those that a mesh axis runs over, the one named last changes fastest.
Arguments:
- frames: bfloat16 [16384, 1536], P(('dp', 'mp')), may hold values from -6 to 6
- cond_table: bfloat16 [8, 1536], replicated, may hold values from -6 to 6
- bucket_ids: int32 [8], P('dp'), may hold values from 0 to 7
- prompt: bfloat16 [8, 128, 768], P('dp'), may hold values from -6 to 6
- prompt_len: int32 [8], P('dp'), may hold values from 4 to 128, as said below
- attn_query: bfloat16 [1536, 1536], P('dp', 'mp'), may hold values from -0.15625 to 0.15625
- attn_key: bfloat16 [1536, 1536], P('dp', 'mp'), may hold values from -0.15625 to 0.15625
- attn_value: bfloat16 [1536, 1536], P('dp', 'mp'), may hold values from -0.15625 to 0.15625
- attn_out: bfloat16 [1536, 1536], P('dp', 'mp'), may hold values from -2.5 to 2.5
- cross_query: bfloat16 [1536, 1536], P('dp', 'mp'), may hold values from -0.15625 to 0.15625
- cross_key: bfloat16 [768, 1536], P('dp', 'mp'), may hold values from -0.21875 to 0.21875
- cross_value: bfloat16 [768, 1536], P('dp', 'mp'), may hold values from -0.21875 to 0.21875
- cross_out: bfloat16 [1536, 1536], P('dp', 'mp'), may hold values from -0.875 to 0.875
- glu_gate: bfloat16 [1536, 6144], P('dp', 'mp'), may hold values from -0.15625 to 0.15625
- glu_up: bfloat16 [1536, 6144], P('dp', 'mp'), may hold values from -0.15625 to 0.15625
- glu_down: bfloat16 [1536, 6144], P('dp', 'mp'), may hold values from -0.078125 to 0.078125
- first_gain: bfloat16 [1536], P('dp'), may hold values from 0.5 to 1.5
- second_gain: bfloat16 [1536], P('dp'), may hold values from 0.5 to 1.5
- third_gain: bfloat16 [1536], P('dp'), may hold values from 0.5 to 1.5
- grad_out: bfloat16 [16384, 1536], P(('dp', 'mp')), may hold values from -6 to 6
Outputs:
- block_out: bfloat16 [16384, 1536], P(('dp', 'mp'))
- frames_grad: float32 [16384, 1536], P(('dp', 'mp'))
- cond_grad: float32 [8, 1536], replicated
- attn_query_grad: float32 [1536, 1536], P('dp', 'mp')
- attn_key_grad: float32 [1536, 1536], P('dp', 'mp')
- attn_value_grad: float32 [1536, 1536], P('dp', 'mp')
- attn_out_grad: float32 [1536, 1536], P('dp', 'mp')
- cross_query_grad: float32 [1536, 1536], P('dp', 'mp')
- cross_key_grad: float32 [768, 1536], P('dp', 'mp')
- cross_value_grad: float32 [768, 1536], P('dp', 'mp')
- cross_out_grad: float32 [1536, 1536], P('dp', 'mp')
- glu_gate_grad: float32 [1536, 6144], P('dp', 'mp')
- glu_up_grad: float32 [1536, 6144], P('dp', 'mp')
- glu_down_grad: float32 [1536, 6144], P('dp', 'mp')
- first_gain_grad: float32 [1536], replicated
- second_gain_grad: float32 [1536], replicated
- third_gain_grad: float32 [1536], replicated
The draws below stay inside these ranges and needn't reach their ends.
Inputs may be any that keep to these rules, and one draw needn't show every extreme that they name: `prompt_len`: one sequence has exactly 128 prompt tokens and another exactly 4.
All inputs are finite; a program needn't handle non-finite values.
Results may differ from the reference program's by a relative error of at most 0.02.
Values may be sent and summed in bfloat16 or wider, within the bound.
A program may use at most 320 MiB of HBM per device.

```python
import math
import jax
import jax.numpy as jnp
import numpy as np
from jax import lax

D = 1536
HD = 64
ROT = 32
FF = 6144
CTX = 768
PROMPT = 128
FRAMES = 2048
BUCKETS = 8
SEQS = 8
ROWS = 16384


def draw_prompt_len(key, part):
    first_draw = jax.random.randint(jax.random.fold_in(key, 11), (SEQS,), 0, PROMPT - 3)
    second_draw = jax.random.randint(jax.random.fold_in(key, 12), (SEQS,), 0, PROMPT - 3)
    third_draw = jax.random.randint(jax.random.fold_in(key, 13), (SEQS,), 0, PROMPT - 3)
    lengths = 4 + jnp.minimum(jnp.minimum(first_draw, second_draw), third_draw)
    chosen = jax.random.randint(jax.random.fold_in(key, 14), (), 0, SEQS)
    positions = jnp.arange(SEQS)
    lengths = jnp.where(positions == chosen, PROMPT, lengths)
    lengths = jnp.where(positions == (chosen + 1) % SEQS, 4, lengths)
    return lengths.astype(jnp.int32)


def place_ends(values, own_key, low, largest):
    shape = values.shape
    index_at = [jax.random.randint(jax.random.fold_in(own_key, axis), (), 0, shape[axis]) for axis in range(len(shape))]
    values = values.at[tuple(index_at)].set(low)
    longest = shape.index(max(shape))
    index_at[longest] = (index_at[longest] + 1) % shape[longest]
    return values.at[tuple(index_at)].set(largest)


def steps_of(rng, dims, cuts, low, largest):
    gain, own = 1.0, jax.random.fold_in(rng, 6)
    for axis_at, shards_of in cuts:
        steps = jnp.exp(jax.random.uniform(jax.random.fold_in(own, axis_at), (shards_of,), jnp.float32, low / len(cuts), largest / len(cuts)))
        gain = gain * jnp.repeat(steps, dims[axis_at] // shards_of).reshape([-1 if axis == axis_at else 1 for axis in range(len(dims))])
    return gain


def rank_table(count, lean):
    weights = [(1 << 20) // math.isqrt(rank ** lean) + 1 for rank in range(1, count + 1)]
    deviation = 1 + sum(weights) // (1 << 30)
    return np.cumsum(np.array([max(1, weight // deviation) for weight in weights]))


def ranked(stream_key, extent, number_of, lean):
    table = rank_table(number_of, lean)
    pick = jax.random.randint(jax.random.fold_in(stream_key, 1), extent, 0, int(table[number_of - 1]))
    rank = jnp.searchsorted(jnp.asarray(table, jnp.int32), pick, side="right")
    return jax.random.permutation(jax.random.fold_in(stream_key, 2), number_of)[rank].astype(jnp.int32)


def normal_values(rng, shape, width, limit, cuts=(), dtype=jnp.bfloat16):
    drawn = width * jax.random.normal(rng, shape, jnp.float32)
    if cuts:
        drawn = drawn * steps_of(rng, shape, cuts, -0.22, 0.18)
    return jnp.clip(drawn, -limit, limit).astype(dtype)


def setup_inputs(seed: int = 0) -> dict:
    streams_of = jax.random.split(jax.random.key(seed), 21)
    frames = normal_values(streams_of[0], (ROWS, D), 1.0, 6.0, ((0, 32),))
    cond_table = normal_values(streams_of[1], (BUCKETS, D), 1.0, 6.0)
    bucket_ids = place_ends(ranked(streams_of[2], (SEQS,), BUCKETS, 2), jax.random.fold_in(streams_of[2], 3), 0, BUCKETS - 1).astype(jnp.int32)
    prompt = normal_values(streams_of[3], (SEQS, PROMPT, CTX), 1.0, 6.0, ((0, 8),))
    prompt_len = draw_prompt_len(jax.random.fold_in(streams_of[20], 71), 0)
    attn_query = normal_values(streams_of[5], (D, D), D ** -0.5, 0.15625, ((0, 8), (1, 4)))
    attn_key = normal_values(streams_of[6], (D, D), D ** -0.5, 0.15625, ((0, 8), (1, 4)))
    attn_value = normal_values(streams_of[7], (D, D), D ** -0.5, 0.15625, ((0, 8), (1, 4)))
    attn_out = normal_values(streams_of[8], (D, D), (max(D // 256, 1)) ** -0.5, 2.5, ((0, 8), (1, 4)))
    cross_query = normal_values(streams_of[9], (D, D), D ** -0.5, 0.15625, ((0, 8), (1, 4)))
    cross_key = normal_values(streams_of[10], (CTX, D), CTX ** -0.5, 0.21875, ((0, 8), (1, 4)))
    cross_value = normal_values(streams_of[11], (CTX, D), CTX ** -0.5, 0.21875, ((0, 8), (1, 4)))
    cross_out = normal_values(streams_of[12], (D, D), (max(D // 32, 1)) ** -0.5, 0.875, ((0, 8), (1, 4)))
    glu_gate = normal_values(streams_of[13], (D, FF), D ** -0.5, 0.15625, ((0, 8), (1, 4)))
    glu_up = normal_values(streams_of[14], (D, FF), D ** -0.5, 0.15625, ((0, 8), (1, 4)))
    glu_down = normal_values(streams_of[15], (D, FF), FF ** -0.5, 0.078125, ((0, 8), (1, 4)))
    first_gain = jnp.clip(1.0 + 0.1 * jax.random.normal(streams_of[16], (D,), jnp.float32), 0.5, 1.5).astype(jnp.bfloat16)
    second_gain = jnp.clip(1.0 + 0.1 * jax.random.normal(streams_of[17], (D,), jnp.float32), 0.5, 1.5).astype(jnp.bfloat16)
    third_gain = jnp.clip(1.0 + 0.1 * jax.random.normal(streams_of[18], (D,), jnp.float32), 0.5, 1.5).astype(jnp.bfloat16)
    grad_out = normal_values(streams_of[19], (ROWS, D), 1.0, 6.0, ((0, 32),))
    return {"frames": frames, "cond_table": cond_table, "bucket_ids": bucket_ids, "prompt": prompt, "prompt_len": prompt_len, "attn_query": attn_query, "attn_key": attn_key, "attn_value": attn_value, "attn_out": attn_out, "cross_query": cross_query, "cross_key": cross_key, "cross_value": cross_value, "cross_out": cross_out, "glu_gate": glu_gate, "glu_up": glu_up, "glu_down": glu_down, "first_gain": first_gain, "second_gain": second_gain, "third_gain": third_gain, "grad_out": grad_out}


@jax.custom_vjp
def low(v):
    return lax.optimization_barrier(v.astype(jnp.bfloat16)).astype(jnp.float32)

@jax.custom_vjp
def low_back(v):
    return v

def low_keep(v):
    return (low(v), None)

def low_pass(kept, grad):
    return (grad,)

def back_keep(v):
    return (v, None)

def back_low(kept, grad):
    return (low(grad),)
low.defvjp(low_keep, low_pass)
low_back.defvjp(back_keep, back_low)
highest = lax.Precision.HIGHEST

def matmul(first_op, second_op):
    return jnp.dot(first_op, second_op, precision=highest)

def layer_norm(values, gain_row):
    center = values - lax.optimization_barrier(jnp.mean(values, -1, keepdims=True))
    spread = lax.rsqrt(lax.optimization_barrier(jnp.mean(center * center, -1, keepdims=True)) + 1e-05)
    return center * spread * gain_row

def rotate(tensor, offset, direction):
    count_rows = tensor.shape[-3]
    half_dim = ROT // 2
    position = offset + jnp.arange(count_rows).astype(jnp.float32)
    frequency = jnp.power(10000.0, -2.0 * jnp.arange(half_dim).astype(jnp.float32) / ROT)
    angles = position[:, None] * frequency[None, :]
    cosine = jnp.cos(angles)[:, None, :]
    sine_part = jnp.sin(angles)[:, None, :]
    first_half = tensor[..., :half_dim]
    second_half = tensor[..., half_dim:ROT]
    remainder = tensor[..., ROT:]
    return jnp.concatenate([first_half * cosine - direction * second_half * sine_part, second_half * cosine + direction * first_half * sine_part, remainder], -1)

def attention(queries, key_rows, value_rows, key_mask):
    scores = low_back(jnp.einsum('qhd,khd->hqk', queries, key_rows, precision=highest) * HD ** (-0.5))
    masked = jnp.where(key_mask[None, None, :], scores, -1000000000.0)
    peak = lax.optimization_barrier(jnp.max(masked, -1, keepdims=True))
    exponent = jnp.exp(masked - peak)
    probabilities = exponent / lax.optimization_barrier(jnp.sum(exponent, -1, keepdims=True))
    return jnp.einsum('hqk,khd->qhd', low(probabilities), value_rows, precision=highest)

def block(frames_in, cond_row, prompt_in, key_mask, weights, gains):
    w_query, w_key, w_value, w_out, wc_query, wc_key, wc_value, wc_out, w_gate, w_up, w_down = weights
    gain_one, gain_two, gain_three = gains
    length = frames_in.shape[0]
    head_count = w_query.shape[1] // HD
    prompt_rows = prompt_in.shape[0]
    joined = jnp.concatenate([cond_row[None, :], frames_in], 0)
    normed_one = low(layer_norm(joined, gain_one))
    queries = low(rotate(low_back(matmul(normed_one[1:], w_query)).reshape(length, head_count, HD), 1.0, 1.0))
    key_rows = low(rotate(low_back(matmul(normed_one, w_key)).reshape(length + 1, head_count, HD), 0.0, 1.0))
    value_rows = low(low_back(matmul(normed_one, w_value))).reshape(length + 1, head_count, HD)
    self_mask = jnp.arange(length + 1) >= 0
    mixed = low(low_back(attention(queries, key_rows, value_rows, self_mask).reshape(length, -1)))
    after_self = frames_in + low_back(matmul(mixed, w_out.T))
    normed_two = low(layer_norm(after_self, gain_two))
    cross_queries = low(low_back(matmul(normed_two, wc_query))).reshape(length, head_count, HD)
    cross_keys = low(low_back(matmul(prompt_in, wc_key))).reshape(prompt_rows, head_count, HD)
    cross_values = low(low_back(matmul(prompt_in, wc_value))).reshape(prompt_rows, head_count, HD)
    cross_mixed = low(low_back(attention(cross_queries, cross_keys, cross_values, key_mask).reshape(length, -1)))
    after_cross = after_self + low_back(matmul(cross_mixed, wc_out.T))
    normed_three = low(layer_norm(after_cross, gain_three))
    gate_value = low_back(matmul(normed_three, w_gate))
    up_value = low_back(matmul(normed_three, w_up))
    hidden = low(jax.nn.silu(gate_value) * up_value)
    return after_cross + low_back(matmul(hidden, w_down.T))

def reference(frames, cond_table, bucket_ids, prompt, prompt_len, attn_query, attn_key, attn_value, attn_out, cross_query, cross_key, cross_value, cross_out, glu_gate, glu_up, glu_down, first_gain, second_gain, third_gain, grad_out):
    weights = tuple((matrix.astype(jnp.float32) for matrix in (attn_query, attn_key, attn_value, attn_out, cross_query, cross_key, cross_value, cross_out, glu_gate, glu_up, glu_down)))
    gains = tuple((matrix.astype(jnp.float32) for matrix in (first_gain, second_gain, third_gain)))
    onehot_rows = (bucket_ids[:, None] == jnp.arange(BUCKETS)[None, :]).astype(jnp.float32)
    counts = lax.optimization_barrier(jnp.sum(onehot_rows, 0))
    seq_weight = SEQS / (BUCKETS * lax.optimization_barrier(jnp.sum(onehot_rows * counts[None, :], 1)))
    cond_rows = matmul(onehot_rows, cond_table.astype(jnp.float32))
    frame_seqs = frames.astype(jnp.float32).reshape(SEQS, FRAMES, D)
    cotangent = grad_out.astype(jnp.float32).reshape(SEQS, FRAMES, D) * seq_weight[:, None, None]
    prompt_masks = jnp.arange(PROMPT)[None, :] < prompt_len[:, None]
    prompt_seqs = prompt.astype(jnp.float32)

    def one_sequence(totals, pieces):
        frame_piece, cot_piece, cond_piece, prompt_piece, mask_piece = pieces

        def local(frames_in, cond_in, weights_in, gains_in):
            return block(frames_in, cond_in, prompt_piece, mask_piece, weights_in, gains_in)
        result, pullback = jax.vjp(local, frame_piece, cond_piece, weights, gains)
        grad_frames, grad_cond, grad_weights, grad_gains = pullback(cot_piece)
        totals = jax.tree.map(lambda running, addend: running + addend, totals, (grad_weights, grad_gains))
        return (totals, (result, grad_frames, grad_cond))
    start = jax.tree.map(jnp.zeros_like, (weights, gains))
    (grad_weights, grad_gains), (outputs, grad_frames, grad_conds) = lax.scan(one_sequence, start, (frame_seqs, cotangent, cond_rows, prompt_seqs, prompt_masks))
    cond_grad = matmul(onehot_rows.T, grad_conds)
    return (outputs.reshape(ROWS, D).astype(jnp.bfloat16), grad_frames.reshape(ROWS, D), cond_grad, grad_weights[0], grad_weights[1], grad_weights[2], grad_weights[3], grad_weights[4], grad_weights[5], grad_weights[6], grad_weights[7], grad_weights[8], grad_weights[9], grad_weights[10], grad_gains[0], grad_gains[1], grad_gains[2])
```

```python
import functools

import jax
import jax.numpy as jnp
from jax import lax
from jax.experimental import pallas as pl
from jax.experimental.pallas import tpu as pltpu
from jax.sharding import PartitionSpec as P

HD = 64
ROT = 32
LOG2E = 1.4426950408889634
EPS = 1e-05
MESH = pl.DeviceIdType.MESH
NT = (((1,), (1,)), ((), ()))
TN = (((0,), (0,)), ((), ()))
NN = (((1,), (0,)), ((), ()))
BF = jnp.bfloat16
F32 = jnp.float32
ANY = pl.BlockSpec(memory_space=pl.ANY)
VM = 58 << 20


def shape_of(dims, dtype):
    return jax.ShapeDtypeStruct(dims, dtype)


def dot(left, right, dims):
    return lax.dot_general(left, right, dims, preferred_element_type=F32)


def local_params(**extra):
    return pltpu.CompilerParams(vmem_limit_bytes=VM, **extra)


def cost(flops, nbytes, trans=0):
    return pl.CostEstimate(flops=int(flops), bytes_accessed=int(nbytes), transcendentals=int(trans))


def norm_rows(values):
    center = values - jnp.mean(values, -1, keepdims=True)
    spread = lax.rsqrt(jnp.mean(center * center, -1, keepdims=True) + EPS)
    return center * spread, spread


def norm_back(grad_rows, unit_rows, spread, gain_row):
    scaled = grad_rows * gain_row
    result = spread * (
        scaled
        - jnp.mean(scaled, -1, keepdims=True)
        - unit_rows * jnp.mean(scaled * unit_rows, -1, keepdims=True)
    )
    return result, jnp.sum(grad_rows * unit_rows, 0, keepdims=True)


def rope_tables(length, offset):
    lane = jnp.arange(2 * HD) % HD
    half = ROT // 2
    frequency = jnp.power(10000.0, -2.0 * (lane % half).astype(F32) / ROT)
    angles = (offset + jnp.arange(length).astype(F32))[:, None] * frequency[None, :]
    cosine = jnp.where(lane[None] < ROT, jnp.cos(angles), 1.0)
    sine = jnp.sin(angles)
    upper = jnp.where((lane[None] >= half) & (lane[None] < ROT), sine, 0.0)
    lower = jnp.where(lane[None] < half, -sine, 0.0)
    return cosine, upper, lower


def rope(values, cosine, upper, lower):
    half = ROT // 2
    return (
        values * cosine
        + pltpu.roll(values, half, 1) * upper
        + pltpu.roll(values, 2 * HD - half, 1) * lower
    )


def lanes(dims):
    return lax.broadcasted_iota(jnp.int32, dims, 1)


def half_mask(values, head):
    lane = lanes(values.shape)
    keep = (lane < HD) if head == 0 else (lane >= HD)
    return jnp.where(keep, values, jnp.zeros_like(values))


def pieces(column, dims, base):
    high = column.astype(BF).astype(F32)
    rest = column - high
    middle = rest.astype(BF).astype(F32)
    low = rest - middle
    lane = lanes(dims)
    return jnp.where(
        lane == base,
        high,
        jnp.where(lane == base + 1, middle, jnp.where(lane == base + 2, low, 0.0)),
    )


def mp_peers():
    me = lax.axis_index("mp")
    chip, core = me // 2, me % 2
    return me, chip * 2 + (1 - core), (1 - chip) * 2 + core, (1 - chip) * 2 + (1 - core)


def greet(devices):
    barrier = pltpu.get_barrier_semaphore()
    for device in devices:
        pl.semaphore_signal(barrier, inc=1, device_id=device, device_id_type=MESH)
    pl.semaphore_wait(barrier, len(devices))


def remote(source, target, send, recv, device):
    return pltpu.make_async_remote_copy(
        source, target, send, recv, device_id=device, device_id_type=MESH
    )


CHUNKS = 4


class Gather:
    def __init__(self, x_ref, o_ref, lsem, ssem, rsem):
        self.me, self.sib, self.far, self.diag = mp_peers()
        dp = lax.axis_index("dp")
        self.to_sib = {"dp": dp, "mp": self.sib}
        self.to_far = {"dp": dp, "mp": self.far}
        rows = x_ref.shape[0]
        part = rows // CHUNKS

        def slot(i, k):
            return o_ref.at[pl.ds(pl.multiple_of(i * rows + k * part, part), part)]

        self.own = pltpu.make_async_copy(
            x_ref, o_ref.at[pl.ds(pl.multiple_of(self.me * rows, rows), rows)], lsem
        )
        self.across = []
        self.beside = []
        self.onward = []
        for k in range(CHUNKS):
            mine = x_ref.at[pl.ds(k * part, part)]
            self.across.append(
                remote(mine, slot(self.me, k), ssem.at[0, k], rsem.at[0, k], self.to_far)
            )
            self.beside.append(
                remote(mine, slot(self.me, k), ssem.at[1, k], rsem.at[1, k], self.to_sib)
            )
            self.onward.append(
                remote(
                    slot(self.far, k), slot(self.far, k), ssem.at[2, k], rsem.at[2, k], self.to_sib
                )
            )

    def start(self):
        for copy in self.across:
            copy.start()
        self.own.start()
        for copy in self.beside:
            copy.start()

    def forward(self, k):
        self.across[k].wait_recv()
        self.onward[k].start()

    def finish(self):
        for k in range(CHUNKS):
            self.beside[k].wait_recv()
            self.onward[k].wait_recv()
        for k in range(CHUNKS):
            self.across[k].wait_send()
            self.beside[k].wait_send()
            self.onward[k].wait_send()
        self.own.wait()


GATHER_SEMS = [
    pltpu.SemaphoreType.DMA(()),
    pltpu.SemaphoreType.DMA((3, CHUNKS)),
    pltpu.SemaphoreType.DMA((3, CHUNKS)),
]


def gather_kernel(x_ref, o_ref, lsem, ssem, rsem):
    job = Gather(x_ref, o_ref, lsem, ssem, rsem)
    greet([job.to_sib, job.to_far])
    job.start()
    for k in range(CHUNKS):
        job.forward(k)
    job.finish()


def gather_rows(share, ident):
    rows, width = share.shape
    return pl.pallas_call(
        gather_kernel,
        out_shape=shape_of((4 * rows, width), share.dtype),
        in_specs=[ANY],
        out_specs=ANY,
        scratch_shapes=GATHER_SEMS,
        compiler_params=local_params(collective_id=ident, has_side_effects=True),
        name="gather_rows_%d" % ident,
    )(share)


def head_kernel(count, f_ref, w_ref, fo_ref, wo_ref, lsem, ssem, rsem, wl, fs, fr, bs, br):
    job = Gather(f_ref, fo_ref, lsem, ssem, rsem)
    me = lax.axis_index("dp")
    mp = lax.axis_index("mp")
    rows = w_ref.shape[0]

    def ring_at(spot):
        spot = (spot + count) % count
        late = spot // (count // 2)
        return (1 - late) * 2 * spot + late * (2 * (count - 1 - spot) + 1)

    odd = me % 2
    spot = (1 - odd) * (me // 2) + odd * (count - 1 - me // 2)
    ahead = {"dp": ring_at(spot + 1), "mp": mp}
    behind = {"dp": ring_at(spot - 1), "mp": mp}
    greet([job.to_sib, job.to_far, ahead, behind])

    def slot(i):
        return wo_ref.at[pl.ds(pl.multiple_of(i * rows, rows), rows)]

    half = count // 2
    forward = []
    backward = []
    for hop in range(half):
        block = ring_at(spot - hop)
        forward.append(
            remote(w_ref if hop == 0 else slot(block), slot(block), fs.at[hop], fr.at[hop], ahead)
        )
        block = ring_at(spot + hop)
        backward.append(
            remote(w_ref if hop == 0 else slot(block), slot(block), bs.at[hop], br.at[hop], behind)
        )
    forward[0].start()
    backward[0].start()
    job.start()
    own = pltpu.make_async_copy(w_ref, slot(me), wl)
    own.start()
    for hop in range(1, half):
        forward[hop - 1].wait_recv()
        forward[hop].start()
        backward[hop - 1].wait_recv()
        if hop < half - 1:
            backward[hop].start()
        if hop - 1 < CHUNKS:
            job.forward(hop - 1)
    for k in range(min(half - 1, CHUNKS), CHUNKS):
        job.forward(k)
    forward[half - 1].wait_recv()
    job.finish()
    own.wait()
    for hop in range(half):
        forward[hop].wait_send()
        if hop < half - 1:
            backward[hop].wait_send()


def head_gather(frames, packed, count):
    rows, width = frames.shape
    half = count // 2
    sems = [pltpu.SemaphoreType.DMA((half,))] * 4
    return pl.pallas_call(
        functools.partial(head_kernel, count),
        out_shape=(
            shape_of((4 * rows, width), BF),
            shape_of((count * packed.shape[0], packed.shape[1]), BF),
        ),
        in_specs=[ANY, ANY],
        out_specs=(ANY, ANY),
        scratch_shapes=GATHER_SEMS + [pltpu.SemaphoreType.DMA(())] + sems,
        compiler_params=local_params(collective_id=0, has_side_effects=True),
        name="head_gather",
    )(frames, packed)


def scatter_kernel(x_ref, o_ref, mine, ra, rb, rc, sb, lsem, ssem, rsem):
    me, sib, far, diag = mp_peers()
    dp = lax.axis_index("dp")
    to_sib = {"dp": dp, "mp": sib}
    to_far = {"dp": dp, "mp": far}
    rows = o_ref.shape[0]
    part = rows // CHUNKS
    greet([to_sib, to_far])

    def slot(i, k):
        return x_ref.at[pl.ds(pl.multiple_of(i * rows + k * part, part), part)]

    def piece(ref, k):
        return ref.at[pl.ds(k * part, part)]

    def whole(i):
        return x_ref.at[pl.ds(pl.multiple_of(i * rows, rows), rows)]

    first = [
        remote(slot(diag, k), piece(ra, k), ssem.at[0, k], rsem.at[0, k], to_sib)
        for k in range(CHUNKS)
    ]
    second = [
        remote(slot(sib, k), piece(rb, k), ssem.at[1, k], rsem.at[1, k], to_sib)
        for k in range(CHUNKS)
    ]
    third = [
        remote(piece(sb, k), piece(rc, k), ssem.at[2, k], rsem.at[2, k], to_far)
        for k in range(CHUNKS)
    ]
    load0 = pltpu.make_async_copy(whole(far), mine.at[0], lsem.at[0])
    load1 = pltpu.make_async_copy(whole(me), mine.at[1], lsem.at[1])
    load0.start()
    for copy in first:
        copy.start()
    load1.start()
    for copy in second:
        copy.start()
    load0.wait()
    for k in range(CHUNKS):
        first[k].wait_recv()
        span = pl.ds(k * part, part)
        sb[span, :] = (mine[0, span, :].astype(F32) + ra[span, :].astype(F32)).astype(BF)
        third[k].start()
    load1.wait()
    for k in range(CHUNKS):
        second[k].wait_recv()
        span = pl.ds(k * part, part)
        o_ref[span, :] = mine[1, span, :].astype(F32) + rb[span, :].astype(F32)
    for k in range(CHUNKS):
        third[k].wait_recv()
        span = pl.ds(k * part, part)
        o_ref[span, :] += rc[span, :].astype(F32)
    for k in range(CHUNKS):
        first[k].wait_send()
        second[k].wait_send()
        third[k].wait_send()


def scatter_rows(term, ident):
    rows, width = term.shape[0] // 4, term.shape[1]
    return pl.pallas_call(
        scatter_kernel,
        out_shape=shape_of((rows, width), F32),
        in_specs=[ANY],
        out_specs=pl.BlockSpec(memory_space=pltpu.VMEM),
        scratch_shapes=[pltpu.VMEM((2, rows, width), BF)]
        + [pltpu.VMEM((rows, width), BF)] * 4
        + [
            pltpu.SemaphoreType.DMA((2,)),
            pltpu.SemaphoreType.DMA((3, CHUNKS)),
            pltpu.SemaphoreType.DMA((3, CHUNKS)),
        ],
        compiler_params=local_params(collective_id=ident, has_side_effects=True),
        name="scatter_rows_%d" % ident,
    )(term)


def qkv_kernel(x_ref, g_ref, w_ref, c_ref, u_ref, l_ref, n_ref, q_ref, k_ref, v_ref):
    unit, _ = norm_rows(x_ref[...].astype(F32))
    normed = (unit * g_ref[...]).astype(BF)
    n_ref[...] = normed
    width = q_ref.shape[1]
    out = dot(normed, w_ref[...], NN)
    cosine, upper, lower = c_ref[...], u_ref[...], l_ref[...]
    for pair in range(width // 128):
        span = slice(128 * pair, 128 * pair + 128)
        q_ref[:, span] = (rope(out[:, span], cosine, upper, lower) * (LOG2E / 8.0)).astype(BF)
        keys = out[:, width + 128 * pair : width + 128 * pair + 128]
        k_ref[:, span] = rope(keys, cosine, upper, lower).astype(BF)
    v_ref[...] = out[:, 2 * width : 3 * width].astype(BF)


def qkv_project(frames, gain, weights, tables, width):
    length, model = frames.shape
    rows = 256
    block = pl.BlockSpec((rows, model), lambda i: (i, 0))
    table = pl.BlockSpec((rows, 128), lambda i: (i, 0))
    head = pl.BlockSpec((rows, width), lambda i: (i, 0))
    return pl.pallas_call(
        qkv_kernel,
        grid=(length // rows,),
        in_specs=[
            block,
            pl.BlockSpec((1, model), lambda i: (0, 0)),
            pl.BlockSpec((model, 3 * width), lambda i: (0, 0)),
            table,
            table,
            table,
        ],
        out_specs=[block, head, head, head],
        out_shape=[shape_of((length, model), BF)] + [shape_of((length, width), BF)] * 3,
        compiler_params=local_params(),
        cost_estimate=cost(6 * length * model * width, 8 * length * model),
        name="qkv_project",
    )(frames, gain, weights, *tables)


def attend_kernel(bk, q_ref, k_ref, v_ref, k0_ref, v0_ref, o_ref, aug_ref, vaug):
    length = k_ref.shape[0]
    bq = q_ref.shape[0]

    @pl.when(pl.program_id(1) == 0)
    def _():
        vaug[:, :128] = v_ref[...]
        vaug[:, 128:] = jnp.ones((length, 128), BF)

    queries = q_ref[...]
    key0 = k0_ref[0:1, :].astype(F32)
    value0 = v0_ref[0:1, :].astype(F32)
    outs = []
    logs = []
    for head in range(2):
        masked = half_mask(queries, head)
        peak = jnp.sum(masked.astype(F32) * key0, axis=1, keepdims=True)
        total = jnp.concatenate(
            [jnp.broadcast_to(value0, (bq, 128)), jnp.ones((bq, 128), F32)], 1
        )
        for block in range(length // bk):
            span = slice(block * bk, (block + 1) * bk)
            scores = dot(masked, k_ref[span, :], NT)
            higher = jnp.maximum(peak, jnp.max(scores, axis=1, keepdims=True))
            exponent = jnp.exp2(scores - higher).astype(BF)
            total = total * jnp.exp2(peak - higher) + dot(exponent, vaug[span, :], NN)
            peak = higher
        weight = total[:, 128:129]
        outs.append(total[:, :128] * (1.0 / weight))
        logs.append(-(peak + jnp.log2(weight)))
    lane = lanes((bq, 128))
    o_ref[...] = jnp.where(lane < HD, outs[0], outs[1]).astype(BF)
    aug_ref[...] = (pieces(logs[0], (bq, 128), 0) + pieces(logs[1], (bq, 128), HD)).astype(BF)


def attend(queries, keys, values, key0, value0, bq=512, bk=1024):
    length, width = queries.shape
    row = pl.BlockSpec((bq, 128), lambda p, i: (i, p))
    full = pl.BlockSpec((length, 128), lambda p, i: (0, p))
    zero = pl.BlockSpec((16, 128), lambda p, i: (0, p))
    return pl.pallas_call(
        functools.partial(attend_kernel, bk),
        grid=(width // 128, length // bq),
        in_specs=[row, full, full, zero, zero],
        out_specs=[row, row],
        out_shape=[shape_of((length, width), BF)] * 2,
        scratch_shapes=[pltpu.VMEM((length, 256), BF)],
        compiler_params=local_params(),
        cost_estimate=cost(16 * length * length * width, 10 * length * width),
        name="attend",
    )(queries, keys, values, key0, value0)


def attend_back_kernel(
    bk, q_ref, aug_ref, o_ref, do_ref, k_ref, v_ref, k0_ref, v0_ref,
    cq_ref, uq_ref, lq_ref, ck_ref, uk_ref, lk_ref,
    dq_ref, dk_ref, dv_ref, dk0_ref, dv0_ref, kaug, vaug, kt, dka, dva,
):
    length = k_ref.shape[0]
    bq = q_ref.shape[0]
    step = pl.program_id(1)

    @pl.when(step == 0)
    def _():
        lane = lanes((length, 128))
        ones = jnp.where((lane % HD) < 3, 1.0, 0.0).astype(BF)
        kaug[:, :128] = k_ref[...]
        kaug[:, 128:] = ones
        vaug[:, :128] = v_ref[...]
        vaug[:, 128:] = ones
        kt[...] = k_ref[...].astype(F32).T.astype(BF)
        dka[...] = jnp.zeros_like(dka)
        dva[...] = jnp.zeros_like(dva)
        dk0_ref[...] = jnp.zeros_like(dk0_ref)
        dv0_ref[...] = jnp.zeros_like(dv0_ref)

    queries = q_ref[...]
    grads = do_ref[...]
    aug = aug_ref[...]
    product = grads.astype(F32) * o_ref[...].astype(F32)
    lane = lanes((bq, 128))
    ones0 = jnp.where((lanes((16, 128)) % HD) < 3, 1.0, 0.0).astype(BF)
    key0 = jnp.concatenate([k0_ref[...], ones0], 1)
    value0 = jnp.concatenate([v0_ref[...], ones0], 1)
    row0 = lax.broadcasted_iota(jnp.int32, (16, bq), 0) == 0
    qa, da, qm, dm, dq = [], [], [], [], []
    for head in range(2):
        qm.append(half_mask(queries, head))
        dm.append(half_mask(grads, head))
        mine = (lane < HD) if head == 0 else (lane >= HD)
        inner = jnp.sum(jnp.where(mine, product, 0.0), axis=1, keepdims=True)
        qa.append(jnp.concatenate([qm[head], half_mask(aug, head)], 1))
        da.append(
            jnp.concatenate([dm[head], pieces(-inner, (bq, 128), HD * head).astype(BF)], 1)
        )
        prob0 = jnp.where(row0, jnp.exp2(dot(key0, qa[head], NT)), 0.0)
        ds0 = (prob0 * dot(value0, da[head], NT)).astype(BF)
        dv0_ref[...] += dot(prob0.astype(BF), dm[head], NN)
        dk0_ref[...] += dot(ds0, qm[head], NN)
        dq.append(dot(k0_ref[:, HD * head : HD * head + HD], ds0, TN))
    for block in range(length // bk):
        span = slice(block * bk, (block + 1) * bk)
        for head in range(2):
            probs = jnp.exp2(dot(kaug[span, :], qa[head], NT))
            ds = (probs * dot(vaug[span, :], da[head], NT)).astype(BF)
            dva[span, :] += dot(probs.astype(BF), dm[head], NN)
            dka[span, :] += dot(ds, qm[head], NN)
            dq[head] = dq[head] + dot(kt[HD * head : HD * head + HD, span], ds, NN)
    grad_q = jnp.concatenate(dq, 0).T * 0.125
    dq_ref[...] = rope(grad_q, cq_ref[...], -uq_ref[...], -lq_ref[...]).astype(BF)

    @pl.when(step == pl.num_programs(1) - 1)
    def _():
        grad_k = dka[...] * (1.0 / LOG2E)
        dk_ref[...] = rope(grad_k, ck_ref[...], -uk_ref[...], -lk_ref[...]).astype(BF)
        dv_ref[...] = dva[...].astype(BF)
        dk0_ref[...] = dk0_ref[...] * (1.0 / LOG2E)


def attend_back(queries, aug, mixed, grads, keys, values, key0, value0, tables, bq=512, bk=512):
    length, width = queries.shape
    row = pl.BlockSpec((bq, 128), lambda p, i: (i, p))
    full = pl.BlockSpec((length, 128), lambda p, i: (0, p))
    zero = pl.BlockSpec((16, 128), lambda p, i: (0, p))
    tq = pl.BlockSpec((bq, 128), lambda p, i: (i, 0))
    tk = pl.BlockSpec((length, 128), lambda p, i: (0, 0))
    big = shape_of((length, width), BF)
    small = shape_of((16, width), F32)
    return pl.pallas_call(
        functools.partial(attend_back_kernel, bk),
        grid=(width // 128, length // bq),
        in_specs=[row, row, row, row, full, full, zero, zero, tq, tq, tq, tk, tk, tk],
        out_specs=[row, full, full, zero, zero],
        out_shape=[big, big, big, small, small],
        scratch_shapes=[pltpu.VMEM((length, 256), BF)] * 2
        + [pltpu.VMEM((128, length), BF)]
        + [pltpu.VMEM((length, 128), F32)] * 2,
        compiler_params=local_params(),
        cost_estimate=cost(40 * length * length * width, 20 * length * width),
        name="attend_back",
    )(queries, aug, mixed, grads, keys, values, key0, value0, *tables, *tables)


def softmax_keys(scores, length):
    lane = lanes(scores.shape)
    masked = jnp.where(lane < length, scores, -1e9)
    exponent = jnp.exp2(masked - jnp.max(masked, axis=1, keepdims=True))
    return exponent * (1.0 / jnp.sum(exponent, axis=1, keepdims=True))


def cross_kernel(
    len_ref, f_ref, s_ref, g2_ref, g3_ref, wq_ref, wo_ref, kv_ref,
    as_ref, n2_ref, q_ref, m_ref, ac_ref, n3_ref,
):
    groups, model, width = wq_ref.shape
    after_self = f_ref[...].astype(F32) + s_ref[...]
    as_ref[...] = after_self
    unit, _ = norm_rows(after_self)
    normed = (unit * g2_ref[...]).astype(BF)
    n2_ref[...] = normed
    rows = normed.shape[0]
    lane = lanes((rows, 128))
    total = after_self
    for group in range(groups):
        queries = (dot(normed, wq_ref[group], NN) * (LOG2E / 8.0)).astype(BF)
        base = group * width
        q_ref[:, base : base + width] = queries
        for pair in range(width // 128):
            span = slice(128 * pair, 128 * pair + 128)
            values = kv_ref[group, :, width + 128 * pair : width + 128 * pair + 128]
            outs = []
            for head in range(2):
                scores = dot(half_mask(queries[:, span], head), kv_ref[group, :, span], NT)
                probs = softmax_keys(scores, len_ref[0])
                outs.append(dot(probs.astype(BF), values, NN))
            m_ref[:, base + 128 * pair : base + 128 * pair + 128] = jnp.where(
                lane < HD, outs[0], outs[1]
            ).astype(BF)
        total = total + dot(m_ref[:, base : base + width], wo_ref[group], NT)
    ac_ref[...] = total
    unit, _ = norm_rows(total)
    n3_ref[...] = (unit * g3_ref[...]).astype(BF)


def cross_forward(plen, frames, summed, gain2, gain3, weights, prompt_kv):
    share, model = frames.shape
    groups, _, both = weights.shape
    width = both // 2
    rows = 256
    block = pl.BlockSpec((rows, model), lambda i: (i, 0))
    gain = pl.BlockSpec((1, model), lambda i: (0, 0))
    once = pl.Buffered(1)
    return pl.pallas_call(
        cross_kernel,
        grid=(share // rows,),
        in_specs=[
            pl.BlockSpec(memory_space=pltpu.SMEM),
            block,
            block,
            gain,
            gain,
            pl.BlockSpec((groups, model, width), lambda i: (0, 0, 0), pipeline_mode=once),
            pl.BlockSpec((groups, model, width), lambda i: (0, 0, 1), pipeline_mode=once),
            pl.BlockSpec(prompt_kv.shape, lambda i: (0, 0, 0)),
        ],
        out_specs=[block] * 6,
        out_shape=[
            shape_of((share, model), F32),
            shape_of((share, model), BF),
            shape_of((share, model), BF),
            shape_of((share, model), BF),
            shape_of((share, model), F32),
            shape_of((share, model), BF),
        ],
        compiler_params=local_params(),
        cost_estimate=cost(4 * share * model * model, 4 * model * model + 20 * share * model),
        name="cross_forward",
    )(plen, frames, summed, gain2, gain3, weights, weights, prompt_kv)


def cross_back_kernel(
    len_ref, w_ref, go_ref, e_ref, ac_ref, as_ref, g2_ref, g3_ref, q_ref, wq_ref, wo_ref, kv_ref,
    cb_ref, dq_ref, c3_ref, c3b_ref, dkv_ref, dg2_ref, dg3_ref,
):
    groups, model, width = wq_ref.shape

    @pl.when(pl.program_id(0) == 0)
    def _():
        dkv_ref[...] = jnp.zeros_like(dkv_ref)
        dg2_ref[...] = jnp.zeros_like(dg2_ref)
        dg3_ref[...] = jnp.zeros_like(dg3_ref)

    unit, spread = norm_rows(ac_ref[...])
    back, part = norm_back(e_ref[...], unit, spread, g3_ref[...])
    dg3_ref[...] += part
    carried = go_ref[...].astype(F32) * w_ref[0] + back
    cross_back = carried.astype(BF)
    cb_ref[...] = cross_back
    rows = cross_back.shape[0]
    lane = lanes((rows, 128))
    total = jnp.zeros((rows, model), F32)
    for group in range(groups):
        grads = dot(cross_back, wo_ref[group], NN).astype(BF)
        base = group * width
        for pair in range(width // 128):
            span = slice(128 * pair, 128 * pair + 128)
            vspan = slice(width + 128 * pair, width + 128 * pair + 128)
            wide = slice(base + 128 * pair, base + 128 * pair + 128)
            outs = []
            for head in range(2):
                queries = half_mask(q_ref[:, wide], head)
                masked = half_mask(grads[:, span], head)
                probs = softmax_keys(dot(queries, kv_ref[group, :, span], NT), len_ref[0])
                dprobs = dot(masked, kv_ref[group, :, vspan], NT)
                inner = jnp.sum(dprobs * probs, axis=1, keepdims=True)
                ds = (probs * (dprobs - inner)).astype(BF)
                outs.append(dot(ds, kv_ref[group, :, span], NN))
                dkv_ref[group, :, span] += dot(ds, queries, TN) * (1.0 / LOG2E)
                dkv_ref[group, :, vspan] += dot(probs.astype(BF), masked, TN)
            dq_ref[:, wide] = (jnp.where(lane < HD, outs[0], outs[1]) * 0.125).astype(BF)
        total = total + dot(dq_ref[:, base : base + width], wq_ref[group], NT)
    unit, spread = norm_rows(as_ref[...])
    back, part = norm_back(total, unit, spread, g2_ref[...])
    dg2_ref[...] += part
    carried = carried + back
    c3_ref[...] = carried
    c3b_ref[...] = carried.astype(BF)


def cross_backward(plen, weight, grad_out, summed, after_cross, after_self, gain2, gain3,
                   queries, weights, prompt_kv):
    share, model = grad_out.shape
    groups, _, both = weights.shape
    width = both // 2
    rows = 256
    block = pl.BlockSpec((rows, model), lambda i: (i, 0))
    gain = pl.BlockSpec((1, model), lambda i: (0, 0))
    smem = pl.BlockSpec(memory_space=pltpu.SMEM)
    once = pl.Buffered(1)
    return pl.pallas_call(
        cross_back_kernel,
        grid=(share // rows,),
        in_specs=[
            smem,
            smem,
            block,
            block,
            block,
            block,
            gain,
            gain,
            block,
            pl.BlockSpec((groups, model, width), lambda i: (0, 0, 0), pipeline_mode=once),
            pl.BlockSpec((groups, model, width), lambda i: (0, 0, 1), pipeline_mode=once),
            pl.BlockSpec(prompt_kv.shape, lambda i: (0, 0, 0)),
        ],
        out_specs=[block, block, block, block, pl.BlockSpec(prompt_kv.shape, lambda i: (0, 0, 0)),
                   gain, gain],
        out_shape=[
            shape_of((share, model), BF),
            shape_of((share, model), BF),
            shape_of((share, model), F32),
            shape_of((share, model), BF),
            shape_of(prompt_kv.shape, F32),
            shape_of((1, model), F32),
            shape_of((1, model), F32),
        ],
        compiler_params=local_params(),
        cost_estimate=cost(4 * share * model * model, 4 * model * model + 24 * share * model),
        name="cross_backward",
    )(plen, weight, grad_out, summed, after_cross, after_self, gain2, gain3, queries,
      weights, weights, prompt_kv)


def glu_kernel(n_ref, c_ref, w_ref, h_ref, d_ref):
    width = h_ref.shape[1]
    normed = n_ref[...]
    gate = dot(normed, w_ref[:, :width], NN)
    up = dot(normed, w_ref[:, width : 2 * width], NN)
    grads = dot(c_ref[...], w_ref[:, 2 * width :], NN)
    sig = 1.0 / (1.0 + jnp.exp(-gate))
    silu = gate * sig
    h_ref[...] = (silu * up).astype(BF)
    d_ref[:, :width] = (grads * up * sig * (1.0 + gate * (1.0 - sig))).astype(BF)
    d_ref[:, width:] = (grads * silu).astype(BF)


def glu_block(normed, cot, weights):
    length, model = normed.shape
    width = weights.shape[1] // 3
    rows = 512
    block = pl.BlockSpec((rows, model), lambda i: (i, 0))
    return pl.pallas_call(
        glu_kernel,
        grid=(length // rows,),
        in_specs=[block, block, pl.BlockSpec(weights.shape, lambda i: (0, 0))],
        out_specs=[
            pl.BlockSpec((rows, width), lambda i: (i, 0)),
            pl.BlockSpec((rows, 2 * width), lambda i: (i, 0)),
        ],
        out_shape=[shape_of((length, width), BF), shape_of((length, 2 * width), BF)],
        compiler_params=local_params(),
        cost_estimate=cost(6 * length * model * width, 6 * length * model),
        name="glu_block",
    )(normed, cot, weights)


def sum_kernel(count, *refs):
    total = dot(refs[0][...], refs[count][...], NT)
    for i in range(1, count):
        total = total + dot(refs[i][...], refs[count + i][...], NT)
    refs[2 * count][...] = total.astype(BF)


def sum_products(lefts, rights, column):
    length = lefts[0].shape[0]
    model = rights[0].shape[0]
    rows = 256
    count = len(lefts)
    once = pl.Buffered(1)
    in_specs = [pl.BlockSpec((rows, left.shape[1]), lambda i: (i, 0)) for left in lefts]
    for left, index in zip(lefts, column):
        in_specs.append(
            pl.BlockSpec(
                (model, left.shape[1]), functools.partial(lambda at, i: (0, at), index),
                pipeline_mode=once,
            )
        )
    depth = sum(left.shape[1] for left in lefts)
    return pl.pallas_call(
        functools.partial(sum_kernel, count),
        grid=(length // rows,),
        in_specs=in_specs,
        out_specs=pl.BlockSpec((rows, model), lambda i: (i, 0)),
        out_shape=shape_of((length, model), BF),
        compiler_params=local_params(),
        cost_estimate=cost(2 * length * model * depth, 2 * (length + model) * (depth + model)),
        name="sum_products_%d" % count,
    )(*lefts, *rights)


def weight_grad(left, right):
    return dot(left, right, TN)


def spread_dp(share):
    return lax.all_gather(share, "dp", axis=0, tiled=True)


def owner_sum(term):
    return lax.psum_scatter(term, "dp", scatter_dimension=0, tiled=True)


GLU_PARTS = 3


def per_device(
    frames, cond_table, bucket_ids, prompt, prompt_len,
    attn_query, attn_key, attn_value, attn_out,
    cross_query, cross_key, cross_value, cross_out,
    glu_gate, glu_up, glu_down, first_gain, second_gain, third_gain, grad_out,
):
    groups = lax.axis_size("mp")
    count = lax.axis_size("dp")
    sequences = bucket_ids.shape[0]
    assert sequences == 1 and groups == 4
    share, model = frames.shape
    length = share * groups
    buckets = cond_table.shape[0]
    own_rows, width = attn_query.shape
    hidden = glu_gate.shape[1] // GLU_PARTS

    onehot = (bucket_ids[:, None] == jnp.arange(buckets)[None, :]).astype(F32)
    extra = jnp.concatenate(
        [
            first_gain[:, None],
            second_gain[:, None],
            third_gain[:, None],
            jnp.broadcast_to(onehot.astype(BF), (own_rows, buckets)),
            jnp.zeros((own_rows, 128 - 3 - buckets), BF),
        ],
        1,
    )
    packed = jnp.concatenate([attn_query, attn_key, attn_value, extra], 1)
    frames_all, first = head_gather(frames, packed, count)
    gains = first[:, 3 * width : 3 * width + 3].astype(F32).T
    gain1, gain2, gain3 = gains[0:1], gains[1:2], gains[2:3]
    marks = first[:, 3 * width + 3 : 3 * width + 3 + buckets].reshape(count, own_rows, buckets)
    counts = jnp.sum(marks[:, 0].astype(F32), 0)
    seq_weight = sequences * count / (buckets * jnp.sum(onehot * counts[None, :], 1))

    prompt_pack = jnp.concatenate([cross_key, cross_value], 1).reshape(own_rows, width)
    second = spread_dp(jnp.concatenate([attn_out, cross_query, cross_out, prompt_pack], 1))
    out_full = second[:, :width]
    prompt_full = second[:, 3 * width :].reshape(model // 2, 2 * width)
    cross_full = lax.all_gather(second[:, width : 3 * width], "mp", axis=0, tiled=False)
    kv_local = dot(prompt[0], prompt_full, NN).astype(BF)
    prompt_kv = lax.all_gather(kv_local, "mp", axis=0, tiled=False)
    grad_all = lax.all_gather(grad_out, "mp", axis=0, tiled=True)
    glu_full = []
    for j in range(GLU_PARTS):
        span = slice(j * hidden, (j + 1) * hidden)
        glu_full.append(
            spread_dp(jnp.concatenate([glu_gate[:, span], glu_up[:, span], glu_down[:, span]], 1))
        )
    cot_all = (grad_all.astype(F32) * seq_weight[0]).astype(BF)

    tables = rope_tables(length, 1.0)
    cond_row = dot(onehot.astype(BF), cond_table, NN)
    unit_cond, spread_cond = norm_rows(cond_row)
    normed_cond = (unit_cond * gain1).astype(BF)
    kv0 = dot(normed_cond, first[:, width : 3 * width], NN).astype(BF)
    kv0 = jnp.pad(kv0, ((0, 15), (0, 0)))
    key0, value0 = kv0[:, :width], kv0[:, width:]
    normed_one, queries, keys, values = qkv_project(frames_all, gain1, first, tables, width)
    mixed, aug = attend(queries, keys, values, key0, value0)
    self_out = scatter_rows(sum_products([mixed], [second], [0]), 1)

    after_self, normed_two, cross_q, cross_mixed, after_cross, normed_three = cross_forward(
        prompt_len, frames, self_out, gain2, gain3, cross_full, prompt_kv
    )
    normed_three = gather_rows(normed_three, 2)

    hiddens, dgus, glu_grads = [], [], []
    for j in range(GLU_PARTS):
        h, d = glu_block(normed_three, cot_all, glu_full[j])
        hiddens.append(h)
        dgus.append(d)
        grad = jnp.concatenate([weight_grad(normed_three, d), weight_grad(cot_all, h)], 1)
        glu_grads.append(owner_sum(grad.astype(BF)))
    back_term = scatter_rows(sum_products(dgus, glu_full, [0] * GLU_PARTS), 3)
    out_term = lax.psum_scatter(
        sum_products(hiddens, glu_full, [2] * GLU_PARTS), "mp", scatter_dimension=0, tiled=True
    )
    block_out = (after_cross + out_term.astype(F32)).astype(BF)

    cross_back, grad_cq, carried, carried_low, grad_kv, dg2, dg3 = cross_backward(
        prompt_len, seq_weight, grad_out, back_term, after_cross, after_self, gain2, gain3,
        cross_q, cross_full, prompt_kv,
    )
    carried_all = gather_rows(carried_low, 4)
    cross_term = jnp.concatenate(
        [
            jnp.einsum("rd,rjc->jdc", normed_two, grad_cq.reshape(share, groups, width),
                       preferred_element_type=F32),
            jnp.einsum("rd,rjc->jdc", cross_back, cross_mixed.reshape(share, groups, width),
                       preferred_element_type=F32),
        ],
        2,
    ).astype(BF)
    cross_sum = lax.psum_scatter(cross_term, "mp", scatter_dimension=0, tiled=False)
    grad_kv = lax.psum_scatter(grad_kv, "mp", scatter_dimension=0, tiled=False).astype(BF)
    grad_prompt = dot(prompt[0], grad_kv, TN).astype(BF).reshape(model, width)
    grad_out_weight = weight_grad(carried_all, mixed).astype(BF)
    second_grad = owner_sum(jnp.concatenate([grad_out_weight, cross_sum, grad_prompt], 1))

    grad_mixed = dot(carried_all, out_full, NN).astype(BF)
    dq, dk, dv, dk0, dv0 = attend_back(
        queries, aug, mixed, grad_mixed, keys, values, key0, value0, tables
    )
    dk0 = dk0[:1].astype(BF)
    dv0 = dv0[:1].astype(BF)
    last_term = scatter_rows(sum_products([dq, dk, dv], [first] * 3, [0, 1, 2]), 5)
    edge = normed_cond.astype(F32)
    first_grad = owner_sum(
        jnp.concatenate(
            [
                weight_grad(normed_one, dq),
                weight_grad(normed_one, dk) + edge.T * dk0.astype(F32),
                weight_grad(normed_one, dv) + edge.T * dv0.astype(F32),
            ],
            1,
        ).astype(BF)
    )
    unit_one, spread_one = norm_rows(frames.astype(F32))
    back_one, dg1 = norm_back(last_term, unit_one, spread_one, gain1)
    frames_grad = carried + back_one
    cond_term = dot(dk0, first[:, width : 2 * width], NT) + dot(
        dv0, first[:, 2 * width : 3 * width], NT
    )
    cond_back, dg1_cond = norm_back(cond_term, unit_cond, spread_cond, gain1)
    sums = lax.psum(
        jnp.concatenate([onehot.T * cond_back, dg1 + dg1_cond, dg2, dg3], 0), ("dp", "mp")
    )

    first_grad = first_grad.astype(F32)
    second_grad = second_grad.astype(F32)
    prompt_grad = second_grad[:, 3 * width :].reshape(own_rows // 2, 2 * width)
    glu_grads = [grad.astype(F32) for grad in glu_grads]
    glu_out = [
        jnp.concatenate([grad[:, i * hidden : (i + 1) * hidden] for grad in glu_grads], 1)
        for i in range(3)
    ]
    return (
        block_out,
        frames_grad,
        sums[:buckets],
        first_grad[:, :width],
        first_grad[:, width : 2 * width],
        first_grad[:, 2 * width :],
        second_grad[:, :width],
        second_grad[:, width : 2 * width],
        prompt_grad[:, :width],
        prompt_grad[:, width:],
        second_grad[:, 2 * width : 3 * width],
        glu_out[0],
        glu_out[1],
        glu_out[2],
        sums[buckets],
        sums[buckets + 1],
        sums[buckets + 2],
    )


def solution(mesh):
    both = P(("dp", "mp"), None)
    weight = P("dp", "mp")
    return jax.shard_map(
        per_device,
        mesh=mesh,
        in_specs=(both, P(), P("dp"), P("dp", None, None), P("dp"))
        + (weight,) * 11
        + (P("dp"),) * 3
        + (both,),
        out_specs=(both, both, P()) + (weight,) * 11 + (P(),) * 3,
        check_vma=False,
    )
```

```python
import functools

import jax
import jax.numpy as jnp
import numpy as np
from jax import lax
from jax.experimental import pallas as pl
from jax.experimental.pallas import tpu as pltpu
from jax.sharding import PartitionSpec as P

HD = 64
ROT = 32
LOG2E = 1.4426950408889634
EPS = 1e-05
MESH = pl.DeviceIdType.MESH
NT = (((1,), (1,)), ((), ()))
TN = (((0,), (0,)), ((), ()))
NN = (((1,), (0,)), ((), ()))
BF = jnp.bfloat16
F32 = jnp.float32
ANY = pl.BlockSpec(memory_space=pl.ANY)
VM = 58 << 20


def shape_of(dims, dtype):
    return jax.ShapeDtypeStruct(dims, dtype)


def dot(left, right, dims):
    return lax.dot_general(left, right, dims, preferred_element_type=F32)


def local_params(**extra):
    return pltpu.CompilerParams(vmem_limit_bytes=VM, **extra)


def cost(flops, nbytes, trans=0):
    return pl.CostEstimate(flops=int(flops), bytes_accessed=int(nbytes), transcendentals=int(trans))


def norm_rows(values):
    center = values - jnp.mean(values, -1, keepdims=True)
    spread = lax.rsqrt(jnp.mean(center * center, -1, keepdims=True) + EPS)
    return center * spread, spread


def norm_back(grad_rows, unit_rows, spread, gain_row):
    scaled = grad_rows * gain_row
    result = spread * (
        scaled
        - jnp.mean(scaled, -1, keepdims=True)
        - unit_rows * jnp.mean(scaled * unit_rows, -1, keepdims=True)
    )
    return result, jnp.sum(grad_rows * unit_rows, 0, keepdims=True)


def rope_tables(length, offset):
    lane = np.arange(2 * HD) % HD
    half = ROT // 2
    frequency = np.power(10000.0, -2.0 * (lane % half) / ROT)
    angles = (offset + np.arange(length))[:, None] * frequency[None, :]
    cosine = np.where(lane[None] < ROT, np.cos(angles), 1.0)
    sine = np.sin(angles)
    upper = np.where((lane[None] >= half) & (lane[None] < ROT), sine, 0.0)
    lower = np.where(lane[None] < half, -sine, 0.0)
    return [jnp.asarray(table.astype(np.float32)) for table in (cosine, upper, lower)]


def rope(values, cosine, upper, lower):
    half = ROT // 2
    return (
        values * cosine
        + pltpu.roll(values, half, 1) * upper
        + pltpu.roll(values, 2 * HD - half, 1) * lower
    )


def lanes(dims):
    return lax.broadcasted_iota(jnp.int32, dims, 1)


def half_mask(values, head):
    lane = lanes(values.shape)
    keep = (lane < HD) if head == 0 else (lane >= HD)
    return jnp.where(keep, values, jnp.zeros_like(values))


def pieces(column, dims, base):
    high = column.astype(BF).astype(F32)
    rest = column - high
    middle = rest.astype(BF).astype(F32)
    low = rest - middle
    lane = lanes(dims)
    return jnp.where(
        lane == base,
        high,
        jnp.where(lane == base + 1, middle, jnp.where(lane == base + 2, low, 0.0)),
    )


def mp_peers():
    me = lax.axis_index("mp")
    chip, core = me // 2, me % 2
    return me, chip * 2 + (1 - core), (1 - chip) * 2 + core, (1 - chip) * 2 + (1 - core)


def greet(devices):
    barrier = pltpu.get_barrier_semaphore()
    for device in devices:
        pl.semaphore_signal(barrier, inc=1, device_id=device, device_id_type=MESH)
    pl.semaphore_wait(barrier, len(devices))


def remote(source, target, send, recv, device):
    return pltpu.make_async_remote_copy(
        source, target, send, recv, device_id=device, device_id_type=MESH
    )


CHUNKS = 4
BUSY = cost(1, 140 << 20)


def gather_scratch(rows, width):
    return [
        pltpu.VMEM((rows, width), BF),
        pltpu.SemaphoreType.DMA((2,)),
        pltpu.SemaphoreType.DMA((3, CHUNKS)),
        pltpu.SemaphoreType.DMA((3, CHUNKS)),
    ]


class Gather:
    def __init__(self, x_ref, o_ref, sems, columns=None):
        bounce, lsem, ssem, rsem = sems
        self.me, self.sib, self.far, _ = mp_peers()
        dp = lax.axis_index("dp")
        self.to_sib = {"dp": dp, "mp": self.sib}
        self.to_far = {"dp": dp, "mp": self.far}
        rows = x_ref.shape[0]
        part = rows // CHUNKS

        def slot(i, k):
            return o_ref.at[pl.ds(pl.multiple_of(i * rows + k * part, part), part)]

        def source(first, size):
            if columns is None:
                return x_ref.at[pl.ds(first, size)]
            return x_ref.at[pl.ds(first, size), columns]

        self.load = pltpu.make_async_copy(source(0, rows), bounce, lsem.at[0])
        self.store = pltpu.make_async_copy(
            bounce, o_ref.at[pl.ds(pl.multiple_of(self.me * rows, rows), rows)], lsem.at[1]
        )
        self.across = []
        self.beside = []
        self.onward = []
        for k in range(CHUNKS):
            mine = source(k * part, part)
            self.across.append(
                remote(mine, slot(self.me, k), ssem.at[0, k], rsem.at[0, k], self.to_far)
            )
            self.beside.append(
                remote(mine, slot(self.me, k), ssem.at[1, k], rsem.at[1, k], self.to_sib)
            )
            self.onward.append(
                remote(
                    slot(self.far, k), slot(self.far, k), ssem.at[2, k], rsem.at[2, k], self.to_sib
                )
            )

    def start(self):
        for copy in self.across:
            copy.start()
        self.load.start()
        for copy in self.beside:
            copy.start()
        self.load.wait()
        self.store.start()

    def forward(self, k):
        self.across[k].wait_recv()
        self.onward[k].start()

    def finish(self):
        for k in range(CHUNKS):
            self.beside[k].wait_recv()
            self.onward[k].wait_recv()
        for k in range(CHUNKS):
            self.across[k].wait_send()
            self.beside[k].wait_send()
            self.onward[k].wait_send()
        self.store.wait()


def scatter_scratch(rows, width):
    return [pltpu.VMEM((2, rows, width), BF)] + [pltpu.VMEM((rows, width), BF)] * 4 + [
        pltpu.SemaphoreType.DMA((2,)),
        pltpu.SemaphoreType.DMA((3, CHUNKS)),
        pltpu.SemaphoreType.DMA((3, CHUNKS)),
    ]


class Scatter:
    def __init__(self, x_ref, o_ref, scratch):
        mine, ra, rb, rc, sb, lsem, ssem, rsem = scratch
        me, sib, far, diag = mp_peers()
        dp = lax.axis_index("dp")
        self.to_sib = {"dp": dp, "mp": sib}
        self.to_far = {"dp": dp, "mp": far}
        self.o_ref, self.mine, self.ra, self.rb, self.rc, self.sb = o_ref, mine, ra, rb, rc, sb
        rows = ra.shape[0]
        part = rows // CHUNKS
        self.spans = [pl.ds(k * part, part) for k in range(CHUNKS)]

        def slot(i, k):
            return x_ref.at[pl.ds(pl.multiple_of(i * rows + k * part, part), part)]

        def whole(i):
            return x_ref.at[pl.ds(pl.multiple_of(i * rows, rows), rows)]

        self.first, self.second, self.third = [], [], []
        for k, span in enumerate(self.spans):
            self.first.append(
                remote(slot(diag, k), ra.at[span], ssem.at[0, k], rsem.at[0, k], self.to_sib)
            )
            self.second.append(
                remote(slot(sib, k), rb.at[span], ssem.at[1, k], rsem.at[1, k], self.to_sib)
            )
            self.third.append(
                remote(sb.at[span], rc.at[span], ssem.at[2, k], rsem.at[2, k], self.to_far)
            )
        self.load0 = pltpu.make_async_copy(whole(far), mine.at[0], lsem.at[0])
        self.load1 = pltpu.make_async_copy(whole(me), mine.at[1], lsem.at[1])

    def start(self):
        self.load0.start()
        for copy in self.first:
            copy.start()
        self.load1.start()
        for copy in self.second:
            copy.start()

    def fold(self):
        self.load0.wait()
        for k, span in enumerate(self.spans):
            self.first[k].wait_recv()
            total = self.mine[0, span, :].astype(F32) + self.ra[span, :].astype(F32)
            self.sb[span, :] = total.astype(BF)
            self.third[k].start()

    def local(self):
        self.load1.wait()
        for k in range(CHUNKS):
            self.second[k].wait_recv()

    def land(self):
        for k, span in enumerate(self.spans):
            self.third[k].wait_recv()
            total = self.mine[1, span, :].astype(F32) + self.rb[span, :].astype(F32)
            self.o_ref[span, :] = (total + self.rc[span, :].astype(F32)).astype(self.o_ref.dtype)

    def finish(self):
        for k in range(CHUNKS):
            self.first[k].wait_send()
            self.second[k].wait_send()
            self.third[k].wait_send()


def sum_scratch(rows, width):
    return [pltpu.VMEM((4, rows, width), BF)] + [pltpu.VMEM((rows, width), BF)] * 4 + [
        pltpu.SemaphoreType.DMA((3, CHUNKS)),
        pltpu.SemaphoreType.DMA((3, CHUNKS)),
    ]


class LocalSum:
    def __init__(self, o_ref, scratch):
        terms, ra, rb, rc, sb, ssem, rsem = scratch
        _, sib, far, _ = mp_peers()
        dp = lax.axis_index("dp")
        self.to_sib = {"dp": dp, "mp": sib}
        self.to_far = {"dp": dp, "mp": far}
        self.o_ref, self.terms, self.ra, self.rb, self.rc, self.sb = o_ref, terms, ra, rb, rc, sb
        rows = ra.shape[0]
        part = rows // CHUNKS
        self.spans = [pl.ds(k * part, part) for k in range(CHUNKS)]
        self.first, self.second, self.third = [], [], []
        for k, span in enumerate(self.spans):
            self.first.append(
                remote(terms.at[0, span], ra.at[span], ssem.at[0, k], rsem.at[0, k], self.to_sib)
            )
            self.second.append(
                remote(terms.at[2, span], rb.at[span], ssem.at[1, k], rsem.at[1, k], self.to_sib)
            )
            self.third.append(
                remote(sb.at[span], rc.at[span], ssem.at[2, k], rsem.at[2, k], self.to_far)
            )

    def put(self, step, value):
        half = value.shape[0]
        self.terms[step // 2, pl.ds(pl.multiple_of((step % 2) * half, half), half), :] = value

    def after_step(self, step):
        @pl.when(step == 1)
        def _():
            for copy in self.first:
                copy.start()

        @pl.when(step == 3)
        def _():
            for k, span in enumerate(self.spans):
                self.first[k].wait_recv()
                total = self.terms[1, span, :].astype(F32) + self.ra[span, :].astype(F32)
                self.sb[span, :] = total.astype(BF)
                self.third[k].start()

        @pl.when(step == 5)
        def _():
            for copy in self.second:
                copy.start()

    def land(self):
        for k, span in enumerate(self.spans):
            self.second[k].wait_recv()
            self.third[k].wait_recv()
            total = self.terms[3, span, :].astype(F32) + self.rb[span, :].astype(F32)
            self.o_ref[span, :] = (total + self.rc[span, :].astype(F32)).astype(self.o_ref.dtype)

    def finish(self):
        for copy in self.first + self.second + self.third:
            copy.wait_send()


def order_block(step):
    me = lax.axis_index("mp")
    chip, core = me // 2, me % 2
    other = 1 - step // 4
    cross = 1 - (step // 2) % 2
    quarter = (chip + other - 2 * chip * other) * 2 + (core + cross - 2 * core * cross)
    return quarter * 2 + step % 2


def arrival_quarter(turn):
    me = lax.axis_index("mp")
    chip, core = me // 2, me % 2
    other = turn // 2
    cross = turn % 2
    return (chip + other - 2 * chip * other) * 2 + (core + cross - 2 * core * cross)


class Ring:
    def __init__(self, count):
        self.count = count
        self.half = count // 2
        me = lax.axis_index("dp")
        mp = lax.axis_index("mp")
        odd = me % 2
        self.me = me
        self.spot = (1 - odd) * (me // 2) + odd * (count - 1 - me // 2)
        self.ahead = {"dp": self.at(1), "mp": mp}
        self.behind = {"dp": self.at(-1), "mp": mp}

    def at(self, distance):
        spot = (self.spot + distance + self.count) % self.count
        late = spot // self.half
        return (1 - late) * 2 * spot + late * (2 * (self.count - 1 - spot) + 1)


def ring_scratch(rows, width, half):
    return [pltpu.VMEM((rows, width), BF), pltpu.SemaphoreType.DMA((2,))] + [
        pltpu.SemaphoreType.DMA((half,))
    ] * 4


class RingGather:
    def __init__(self, count, w_ref, o_ref, scratch):
        bounce, lsem, fs, fr, bs, br = scratch
        ring = Ring(count)
        self.ahead, self.behind, self.half = ring.ahead, ring.behind, ring.half
        rows = w_ref.shape[0]

        def slot(i):
            return o_ref.at[pl.ds(pl.multiple_of(i * rows, rows), rows)]

        self.forward = []
        self.backward = []
        for hop in range(self.half):
            block = ring.at(-hop)
            source = w_ref if hop == 0 else slot(block)
            self.forward.append(
                remote(source, slot(block), fs.at[hop], fr.at[hop], ring.ahead)
            )
            block = ring.at(hop)
            source = w_ref if hop == 0 else slot(block)
            if hop < self.half - 1:
                self.backward.append(
                    remote(source, slot(block), bs.at[hop], br.at[hop], ring.behind)
                )
        self.load = pltpu.make_async_copy(w_ref, bounce, lsem.at[0])
        self.store = pltpu.make_async_copy(bounce, slot(ring.me), lsem.at[1])

    def start(self):
        self.forward[0].start()
        self.backward[0].start()
        self.load.start()

    def place(self):
        self.load.wait()
        self.store.start()

    def hop(self, hop):
        self.forward[hop - 1].wait_recv()
        self.forward[hop].start()
        self.backward[hop - 1].wait_recv()
        if hop < self.half - 1:
            self.backward[hop].start()

    def finish(self):
        self.forward[self.half - 1].wait_recv()
        self.store.wait()
        for copy in self.forward + self.backward:
            copy.wait_send()


def plain_gather_kernel(x_ref, o_ref, *scratch):
    job = Gather(x_ref, o_ref, scratch)
    greet([job.to_sib, job.to_far])
    job.start()
    for k in range(CHUNKS):
        job.forward(k)
    job.finish()


def plain_gather(share, ident):
    rows, width = share.shape
    return pl.pallas_call(
        plain_gather_kernel,
        out_shape=shape_of((4 * rows, width), share.dtype),
        in_specs=[ANY],
        out_specs=ANY,
        scratch_shapes=gather_scratch(rows, width),
        compiler_params=local_params(collective_id=ident, has_side_effects=True),
        cost_estimate=BUSY,
        name="plain_gather_%d" % ident,
    )(share)


def head_kernel(count, f_ref, g_ref, w_ref, fo_ref, go_ref, wo_ref, *scratch):
    job = Gather(f_ref, fo_ref, scratch[0:4])
    late = Gather(g_ref, go_ref, scratch[4:8])
    ring = RingGather(count, w_ref, wo_ref, scratch[8:])
    greet([job.to_sib, job.to_far, ring.ahead, ring.behind])
    ring.start()
    job.start()
    ring.place()
    ring.hop(1)
    for k in range(CHUNKS):
        job.forward(k)
    late.start()
    for hop in range(2, ring.half):
        ring.hop(hop)
    for k in range(CHUNKS):
        late.forward(k)
    job.finish()
    late.finish()
    ring.finish()


def head_gather(frames, grads, packed, count):
    rows, width = frames.shape
    wide = shape_of((4 * rows, width), BF)
    return pl.pallas_call(
        functools.partial(head_kernel, count),
        out_shape=(wide, wide, shape_of((count * packed.shape[0], packed.shape[1]), BF)),
        in_specs=[ANY] * 3,
        out_specs=(ANY,) * 3,
        scratch_shapes=gather_scratch(rows, width) * 2 + ring_scratch(*packed.shape, count // 2),
        compiler_params=local_params(collective_id=0, has_side_effects=True),
        cost_estimate=BUSY,
        name="head_gather",
    )(frames, grads, packed)


SMALL = 16


def tail_kernel(
    count, buckets, q_ref, k_ref, v_ref, wq_ref, wk_ref, wv_ref,
    a_ref, b_ref, f_ref, c_ref, g1_ref, dg2_ref, dg3_ref, mark_ref, cb_ref,
    dg1_ref, o_ref, s_ref, *scratch,
):
    outs = scratch[:5]
    scratch = scratch[5:]
    total, held = scratch[0:2]
    job = LocalSum(total, scratch[2:9])
    lf, lb, rf, rb, lsem, fs, fr, bs, br, sent, got, ss, rs = scratch[9:]
    step = pl.program_id(0)
    ring = Ring(count)
    half = ring.half
    rows = outs[0].shape[0]
    split = a_ref.shape[1]
    mp = lax.axis_index("mp")
    partners = [job.to_sib, job.to_far]
    bit = 1
    while bit < count:
        partners.append({"dp": ring.me + bit * (1 - 2 * ((ring.me // bit) % 2)), "mp": mp})
        bit *= 2

    def loads(block, target, sem):
        span = pl.ds(pl.multiple_of(block * rows, rows), rows)
        return [
            pltpu.make_async_copy(a_ref.at[span], target.at[:, pl.ds(0, split)], sem.at[0]),
            pltpu.make_async_copy(
                b_ref.at[span], target.at[:, pl.ds(split, b_ref.shape[1])], sem.at[1]
            ),
        ]

    forward, backward, local_f, local_b = [], [], [], []
    for hop in range(half):
        local_f.append(loads(ring.at(half - hop), lf.at[hop], lsem.at[0, hop]))
        forward.append(remote(lf.at[hop], rf.at[hop], fs.at[hop], fr.at[hop], ring.ahead))
        if hop < half - 1:
            local_b.append(loads(ring.at(hop + 1 - half), lb.at[hop], lsem.at[1, hop]))
            backward.append(remote(lb.at[hop], rb.at[hop], bs.at[hop], br.at[hop], ring.behind))
    local_b.append(loads(ring.me, lb.at[half - 1], lsem.at[1, half - 1]))
    @pl.when(step == 0)
    def _():
        greet(partners + [ring.ahead, ring.behind])
        for hop in range(half):
            for copy in local_f[hop] + local_b[hop]:
                copy.start()
        for copy in local_f[0] + local_b[0]:
            copy.wait()
        forward[0].start()
        backward[0].start()

    @pl.when(step < 8)
    def _():
        term = (
            dot(q_ref[...], wq_ref[...], NT)
            + dot(k_ref[...], wk_ref[...], NT)
            + dot(v_ref[...], wv_ref[...], NT)
        )
        job.put(step, term.astype(BF))

    job.after_step(step)

    def ring_hop(hop):
        for copy in local_f[hop]:
            copy.wait()
        forward[hop - 1].wait_recv()
        lf[hop] = (lf[hop].astype(F32) + rf[hop - 1].astype(F32)).astype(BF)
        forward[hop].start()
        for copy in local_b[hop]:
            copy.wait()
        backward[hop - 1].wait_recv()
        if hop < half - 1:
            lb[hop] = (lb[hop].astype(F32) + rb[hop - 1].astype(F32)).astype(BF)
            backward[hop].start()

    @pl.when(step == 8)
    def _():
        for hop in range(1, half - 1):
            ring_hop(hop)
        job.land()
        unit, spread = norm_rows(f_ref[...].astype(F32))
        back, part = norm_back(total[...], unit, spread, g1_ref[...])
        o_ref[...] = c_ref[...] + back
        row = lax.broadcasted_iota(jnp.int32, held.shape, 0)
        held[...] = (
            mark_ref[...] * cb_ref[...]
            + jnp.where(row == buckets, part + dg1_ref[...], 0.0)
            + jnp.where(row == buckets + 1, dg2_ref[...], 0.0)
            + jnp.where(row == buckets + 2, dg3_ref[...], 0.0)
        )
        ring_hop(half - 1)
        for i, partner in enumerate(partners):
            sent[i] = held[...]
            copy = remote(sent.at[i], got.at[i], ss.at[i], rs.at[i], partner)
            copy.start()
            copy.wait_recv()
            held[...] += got[i]
            copy.wait_send()
        s_ref[...] = held[...]
        forward[half - 1].wait_recv()
        base = 0
        for out in outs:
            span = slice(base, base + out.shape[1])
            base += out.shape[1]
            out[...] = (
                lb[half - 1, :, span].astype(F32)
                + rf[half - 1, :, span].astype(F32)
                + rb[half - 2, :, span].astype(F32)
            )
        for copy in forward + backward:
            copy.wait_send()
        job.finish()


def tail_sums(
    count, buckets, grads_qkv, weights, grads, more, frames, carried, gain1, dg2, dg3, mark,
    cond_back, dg1,
):
    share, model = frames.shape
    width = grads_qkv[0].shape[1]
    block = 2 * share // 4
    rows = grads.shape[0] // count
    wide = grads.shape[1] + more.shape[1]
    half = count // 2
    steps = 2 + (count - 1).bit_length()
    once = pl.Buffered(1)

    def full(array):
        return pl.BlockSpec(array.shape, lambda i: (0,) * array.ndim, pipeline_mode=once)

    slots = pltpu.VMEM((half, rows, wide), BF)
    hops = pltpu.SemaphoreType.DMA((half,))
    small = pltpu.VMEM((steps, SMALL, model), F32)
    out_shape = (shape_of((share, model), F32), shape_of((SMALL, model), F32)) + (
        shape_of((rows, wide // 5), F32),
    ) * 5
    whole = [frames, carried, gain1, dg2, dg3, mark, cond_back, dg1]
    return pl.pallas_call(
        functools.partial(tail_kernel, count, buckets),
        grid=(9,),
        out_shape=out_shape,
        in_specs=[
            pl.BlockSpec((block, width), lambda i: (order_block(jnp.minimum(i, 7)), 0))
            for _ in range(3)
        ]
        + [
            pl.BlockSpec(
                (model, width), functools.partial(lambda at, i: (0, at), at), pipeline_mode=once
            )
            for at in range(3)
        ]
        + [ANY, ANY]
        + [full(array) for array in whole],
        out_specs=tuple(pl.BlockSpec(out.shape, lambda i: (0, 0)) for out in out_shape),
        scratch_shapes=[pltpu.VMEM((share, model), F32), pltpu.VMEM((SMALL, model), F32)]
        + sum_scratch(share, model)
        + [slots] * 4
        + [pltpu.SemaphoreType.DMA((2, half, 2))]
        + [hops] * 4
        + [small, small, pltpu.SemaphoreType.DMA((steps,)), pltpu.SemaphoreType.DMA((steps,))],
        compiler_params=local_params(collective_id=6, has_side_effects=True),
        cost_estimate=BUSY,
        name="tail_sums",
    )(*grads_qkv, weights, weights, weights, grads, more, *whole)


def out_kernel(m_ref, w_ref, kv_ref, o_ref, kvo_ref, *scratch):
    side = Gather(kv_ref, kvo_ref, scratch[:4])
    job = LocalSum(o_ref, scratch[4:])
    step = pl.program_id(0)

    @pl.when(step == 0)
    def _():
        greet([job.to_sib, job.to_far])
        side.start()

    job.put(step, dot(m_ref[...], w_ref[...], NT).astype(BF))
    job.after_step(step)

    @pl.when(step == 7)
    def _():
        for k in range(CHUNKS):
            side.forward(k)
        job.land()
        side.finish()
        job.finish()


def out_project(mixed, weights, side):
    length, width = mixed.shape
    model = weights.shape[0]
    rows = length // 8
    share = length // 4
    return pl.pallas_call(
        out_kernel,
        grid=(8,),
        out_shape=(shape_of((share, model), F32), shape_of((4 * side.shape[0], side.shape[1]), BF)),
        in_specs=[
            pl.BlockSpec((rows, width), lambda i: (order_block(i), 0)),
            pl.BlockSpec((model, width), lambda i: (0, 0), pipeline_mode=pl.Buffered(1)),
            ANY,
        ],
        out_specs=(pl.BlockSpec((share, model), lambda i: (0, 0)), ANY),
        scratch_shapes=gather_scratch(*side.shape) + sum_scratch(share, model),
        compiler_params=local_params(collective_id=1, has_side_effects=True),
        cost_estimate=BUSY,
        name="out_project",
    )(mixed, weights, side)


def glu_back_kernel(
    d0_ref, d1_ref, g0_ref, g1_ref, h0_ref, h1_ref, w0_ref, w1_ref, o_ref, t_ref, *scratch
):
    job = LocalSum(o_ref, scratch)
    step = pl.program_id(0)

    @pl.when(step == 0)
    def _():
        greet([job.to_sib, job.to_far])

    @pl.when(step < 8)
    def _():
        term = dot(d0_ref[...], g0_ref[...], NT) + dot(d1_ref[...], g1_ref[...], NT)
        job.put(step, term.astype(BF))

    job.after_step(step)

    @pl.when(step >= 8)
    def _():
        term = dot(h0_ref[...], w0_ref[...], NT) + dot(h1_ref[...], w1_ref[...], NT)
        t_ref[...] = term.astype(BF)

    @pl.when(step == 15)
    def _():
        job.land()
        job.finish()


def glu_back(dgus, hiddens, weights):
    length = dgus[0].shape[0]
    model = weights[0].shape[0]
    rows = length // 8
    share = length // 4
    once = pl.Buffered(1)
    in_specs = []
    for d in dgus:
        in_specs.append(
            pl.BlockSpec((rows, d.shape[1]), lambda i: (order_block(jnp.minimum(i, 7)), 0))
        )
    for d in dgus:
        in_specs.append(pl.BlockSpec((model, d.shape[1]), lambda i: (0, 0), pipeline_mode=once))
    for h in hiddens:
        in_specs.append(pl.BlockSpec((rows, h.shape[1]), lambda i: (jnp.maximum(i - 8, 0), 0)))
    for h in hiddens:
        in_specs.append(pl.BlockSpec((model, h.shape[1]), lambda i: (0, 2), pipeline_mode=once))
    return pl.pallas_call(
        glu_back_kernel,
        grid=(16,),
        out_shape=(shape_of((share, model), F32), shape_of((length, model), BF)),
        in_specs=in_specs,
        out_specs=(
            pl.BlockSpec((share, model), lambda i: (0, 0)),
            pl.BlockSpec((rows, model), lambda i: (jnp.maximum(i - 8, 0), 0)),
        ),
        scratch_shapes=sum_scratch(share, model),
        compiler_params=local_params(collective_id=3, has_side_effects=True),
        cost_estimate=BUSY,
        name="glu_back",
    )(*dgus, *weights, *hiddens, *weights)


def mid_kernel(
    c_ref, t_ref, n_ref, cb_ref, q_ref, cm_ref, w_ref, m_ref,
    x_ref, g_ref, dw_ref, s_ref, slots, total, ssem, rsem, *scratch,
):
    small = Scatter(t_ref, s_ref, scratch)
    me, sib, far, diag = mp_peers()
    dp = lax.axis_index("dp")
    to_sib = {"dp": dp, "mp": sib}
    to_far = {"dp": dp, "mp": far}
    step = pl.program_id(0)
    rows = c_ref.shape[0]
    part = rows // CHUNKS
    spans = [pl.ds(k * part, part) for k in range(CHUNKS)]
    beside = remote(c_ref, slots.at[0], ssem.at[0], rsem.at[0], to_sib)
    across = [
        remote(c_ref.at[span], slots.at[1, span], ssem.at[1 + k], rsem.at[1 + k], to_far)
        for k, span in enumerate(spans)
    ]
    onward = [
        remote(
            slots.at[1, span],
            slots.at[2, span],
            ssem.at[1 + CHUNKS + k],
            rsem.at[1 + CHUNKS + k],
            to_sib,
        )
        for k, span in enumerate(spans)
    ]

    @pl.when(step == 0)
    def _():
        greet([to_sib, to_far])
        for copy in across:
            copy.start()
        small.start()
        beside.start()

    @pl.when(step == 1)
    def _():
        small.fold()
        small.local()

    @pl.when(step < 8)
    def _():
        width = q_ref.shape[1]
        x_ref[:, :width] = dot(n_ref[...], q_ref[...], TN).astype(BF)
        x_ref[:, width:] = dot(cb_ref[...], cm_ref[...], TN).astype(BF)

    def use(grads):
        g_ref[...] = dot(grads, w_ref[...], NN).astype(BF)
        return dot(grads, m_ref[...], TN)

    @pl.when(step == 8)
    def _():
        total[...] = use(c_ref[...])

    @pl.when(step == 9)
    def _():
        beside.wait_recv()
        total[...] += use(slots[0])

    @pl.when(step == 10)
    def _():
        small.land()
        for k in range(CHUNKS):
            across[k].wait_recv()
            onward[k].start()
        total[...] += use(slots[1])

    @pl.when(step == 11)
    def _():
        for copy in onward:
            copy.wait_recv()
        dw_ref[...] = (total[...] + use(slots[2])).astype(BF)
        small.finish()
        beside.wait_send()
        for copy in across + onward:
            copy.wait_send()


def mid_gather(carried, term, normed, cross_back, grad_cq, cross_mixed, weights, mixed, groups):
    share, model = carried.shape
    length, width = mixed.shape
    short, narrow = term.shape[0] // 4, term.shape[1]
    tile = 2 * model // 4
    once = pl.Buffered(1)
    fixed = pl.BlockSpec((share, model), lambda i: (0, 0), pipeline_mode=once)
    left = pl.BlockSpec((share, tile), lambda i: (0, jnp.minimum(i, 7) % 2))
    right = pl.BlockSpec((share, width), lambda i: (0, jnp.minimum(i, 7) // 2))

    def turn(i):
        return (arrival_quarter(jnp.maximum(i - 8, 0)), 0)

    return pl.pallas_call(
        mid_kernel,
        grid=(12,),
        in_specs=[
            fixed,
            ANY,
            left,
            left,
            right,
            right,
            pl.BlockSpec((model, width), lambda i: (0, 0), pipeline_mode=once),
            pl.BlockSpec((share, width), turn),
        ],
        out_specs=(
            pl.BlockSpec((tile, 2 * width), lambda i: (jnp.minimum(i, 7), 0)),
            pl.BlockSpec((share, width), turn),
            pl.BlockSpec((model, width), lambda i: (0, 0)),
            pl.BlockSpec((short, narrow), lambda i: (0, 0)),
        ),
        out_shape=(
            shape_of((groups * model, 2 * width), BF),
            shape_of((length, width), BF),
            shape_of((model, width), BF),
            shape_of((short, narrow), F32),
        ),
        scratch_shapes=[
            pltpu.VMEM((3, share, model), BF),
            pltpu.VMEM((model, width), F32),
            pltpu.SemaphoreType.DMA((1 + 2 * CHUNKS,)),
            pltpu.SemaphoreType.DMA((1 + 2 * CHUNKS,)),
        ]
        + scatter_scratch(short, narrow),
        compiler_params=local_params(collective_id=4, has_side_effects=True),
        cost_estimate=BUSY,
        name="mid_gather",
    )(carried, term, normed, cross_back, grad_cq, cross_mixed, weights, mixed)


def qkv_kernel(x_ref, g_ref, w_ref, c_ref, u_ref, l_ref, n_ref, q_ref, k_ref, v_ref):
    unit, _ = norm_rows(x_ref[...].astype(F32))
    normed = (unit * g_ref[...]).astype(BF)
    n_ref[...] = normed
    width = q_ref.shape[1]
    out = dot(normed, w_ref[...], NN)
    cosine, upper, lower = c_ref[...], u_ref[...], l_ref[...]
    for pair in range(width // 128):
        span = slice(128 * pair, 128 * pair + 128)
        q_ref[:, span] = (rope(out[:, span], cosine, upper, lower) * (LOG2E / 8.0)).astype(BF)
        keys = out[:, width + 128 * pair : width + 128 * pair + 128]
        k_ref[:, span] = rope(keys, cosine, upper, lower).astype(BF)
    v_ref[...] = out[:, 2 * width : 3 * width].astype(BF)


def qkv_project(frames, gain, weights, tables, width):
    length, model = frames.shape
    rows = 256
    block = pl.BlockSpec((rows, model), lambda i: (i, 0))
    table = pl.BlockSpec((rows, 128), lambda i: (i, 0))
    head = pl.BlockSpec((rows, width), lambda i: (i, 0))
    return pl.pallas_call(
        qkv_kernel,
        grid=(length // rows,),
        in_specs=[
            block,
            pl.BlockSpec((1, model), lambda i: (0, 0)),
            pl.BlockSpec((model, 3 * width), lambda i: (0, 0)),
            table,
            table,
            table,
        ],
        out_specs=[block, head, head, head],
        out_shape=[shape_of((length, model), BF)] + [shape_of((length, width), BF)] * 3,
        compiler_params=local_params(),
        cost_estimate=cost(6 * length * model * width, 8 * length * model),
        name="qkv_project",
    )(frames, gain, weights, *tables)


def attend_kernel(
    bk, first, count, q_ref, k_ref, v_ref, k0_ref, v0_ref, x_ref, w_ref,
    o_ref, aug_ref, xo_ref, wo_ref, vaug, *scratch,
):
    length = k_ref.shape[0]
    bq = q_ref.shape[0]
    step = pl.program_id(0) * pl.num_programs(1) + pl.program_id(1)
    wide = xo_ref.shape[1]
    job = Gather(x_ref, xo_ref, scratch[:4], pl.ds(first, wide))
    ring = RingGather(count, w_ref, wo_ref, scratch[4:])
    last = pl.num_programs(0) * pl.num_programs(1) - 1

    @pl.when(step == 0)
    def _():
        greet([job.to_sib, job.to_far, ring.ahead, ring.behind])
        ring.start()
        job.start()
        ring.place()

    for hop in range(1, ring.half):

        @pl.when(step == min(4 * hop, 11))
        def _(hop=hop):
            ring.hop(hop)

    @pl.when(pl.program_id(1) == 0)
    def _():
        vaug[:, :128] = v_ref[...]
        vaug[:, 128:] = jnp.ones((length, 128), BF)

    queries = q_ref[...]
    key0 = k0_ref[0:1, :].astype(F32)
    value0 = v0_ref[0:1, :].astype(F32)
    outs = []
    logs = []
    for head in range(2):
        masked = half_mask(queries, head)
        peak = jnp.sum(masked.astype(F32) * key0, axis=1, keepdims=True)
        total = jnp.concatenate(
            [jnp.broadcast_to(value0, (bq, 128)), jnp.ones((bq, 128), F32)], 1
        )
        for block in range(length // bk):
            span = slice(block * bk, (block + 1) * bk)
            scores = dot(masked, k_ref[span, :], NT)
            higher = jnp.maximum(peak, jnp.max(scores, axis=1, keepdims=True))
            exponent = jnp.exp2(scores - higher).astype(BF)
            total = total * jnp.exp2(peak - higher) + dot(exponent, vaug[span, :], NN)
            peak = higher
        weight = total[:, 128:129]
        outs.append(total[:, :128] * (1.0 / weight))
        logs.append(-(peak + jnp.log2(weight)))
    lane = lanes((bq, 128))
    o_ref[...] = jnp.where(lane < HD, outs[0], outs[1]).astype(BF)
    aug_ref[...] = (pieces(logs[0], (bq, 128), 0) + pieces(logs[1], (bq, 128), HD)).astype(BF)

    @pl.when(step == last)
    def _():
        for k in range(CHUNKS):
            job.forward(k)
        job.finish()
        ring.finish()


def attend(queries, keys, values, key0, value0, packed, first, share, count, bq=512, bk=1024):
    length, width = queries.shape
    row = pl.BlockSpec((bq, 128), lambda p, i: (i, p))
    full = pl.BlockSpec((length, 128), lambda p, i: (0, p))
    zero = pl.BlockSpec((16, 128), lambda p, i: (0, p))
    return pl.pallas_call(
        functools.partial(attend_kernel, bk, first, count),
        grid=(width // 128, length // bq),
        in_specs=[row, full, full, zero, zero, ANY, ANY],
        out_specs=[row, row, ANY, ANY],
        out_shape=[shape_of((length, width), BF)] * 2
        + [
            shape_of((4 * packed.shape[0], packed.shape[1] - first), BF),
            shape_of((count * share.shape[0], share.shape[1]), BF),
        ],
        scratch_shapes=[pltpu.VMEM((length, 256), BF)]
        + gather_scratch(packed.shape[0], packed.shape[1] - first)
        + ring_scratch(*share.shape, count // 2),
        compiler_params=local_params(collective_id=7, has_side_effects=True),
        cost_estimate=cost(16 * length * length * width, 10 * length * width),
        name="attend",
    )(queries, keys, values, key0, value0, packed, share)


def attend_back_kernel(
    bk, q_ref, aug_ref, o_ref, do_ref, k_ref, v_ref, k0_ref, v0_ref,
    cq_ref, uq_ref, lq_ref, ck_ref, uk_ref, lk_ref,
    x_ref, dq_ref, dk_ref, dv_ref, dk0_ref, dv0_ref, xo_ref,
    kaug, vaug, kt, dka, dva, *scratch,
):
    length = k_ref.shape[0]
    bq = q_ref.shape[0]
    step = pl.program_id(1)
    turn = pl.program_id(0) * pl.num_programs(1) + step
    job = Scatter(x_ref, xo_ref, scratch)

    @pl.when(turn == 0)
    def _():
        greet([job.to_sib, job.to_far])
        job.start()

    @pl.when(turn == 1)
    def _():
        job.fold()
        job.local()

    @pl.when(turn == pl.num_programs(0) * pl.num_programs(1) - 1)
    def _():
        job.land()
        job.finish()

    @pl.when(step == 0)
    def _():
        lane = lanes((length, 128))
        ones = jnp.where((lane % HD) < 3, 1.0, 0.0).astype(BF)
        kaug[:, :128] = k_ref[...]
        kaug[:, 128:] = ones
        vaug[:, :128] = v_ref[...]
        vaug[:, 128:] = ones
        kt[...] = k_ref[...].astype(F32).T.astype(BF)
        dka[...] = jnp.zeros_like(dka)
        dva[...] = jnp.zeros_like(dva)
        dk0_ref[...] = jnp.zeros_like(dk0_ref)
        dv0_ref[...] = jnp.zeros_like(dv0_ref)

    queries = q_ref[...]
    grads = do_ref[...]
    aug = aug_ref[...]
    product = grads.astype(F32) * o_ref[...].astype(F32)
    lane = lanes((bq, 128))
    ones0 = jnp.where((lanes((16, 128)) % HD) < 3, 1.0, 0.0).astype(BF)
    key0 = jnp.concatenate([k0_ref[...], ones0], 1)
    value0 = jnp.concatenate([v0_ref[...], ones0], 1)
    row0 = lax.broadcasted_iota(jnp.int32, (16, bq), 0) == 0
    qa, da, qm, dm, dq = [], [], [], [], []
    for head in range(2):
        qm.append(half_mask(queries, head))
        dm.append(half_mask(grads, head))
        mine = (lane < HD) if head == 0 else (lane >= HD)
        inner = jnp.sum(jnp.where(mine, product, 0.0), axis=1, keepdims=True)
        qa.append(jnp.concatenate([qm[head], half_mask(aug, head)], 1))
        da.append(
            jnp.concatenate([dm[head], pieces(-inner, (bq, 128), HD * head).astype(BF)], 1)
        )
        prob0 = jnp.where(row0, jnp.exp2(dot(key0, qa[head], NT)), 0.0)
        ds0 = (prob0 * dot(value0, da[head], NT)).astype(BF)
        dv0_ref[...] += dot(prob0.astype(BF), dm[head], NN)
        dk0_ref[...] += dot(ds0, qm[head], NN)
        dq.append(dot(k0_ref[:, HD * head : HD * head + HD], ds0, TN))
    for block in range(length // bk):
        span = slice(block * bk, (block + 1) * bk)
        for head in range(2):
            probs = jnp.exp2(dot(kaug[span, :], qa[head], NT))
            ds = (probs * dot(vaug[span, :], da[head], NT)).astype(BF)
            dva[span, :] += dot(probs.astype(BF), dm[head], NN)
            dka[span, :] += dot(ds, qm[head], NN)
            dq[head] = dq[head] + dot(kt[HD * head : HD * head + HD, span], ds, NN)
    grad_q = jnp.concatenate(dq, 0).T * 0.125
    dq_ref[...] = rope(grad_q, cq_ref[...], -uq_ref[...], -lq_ref[...]).astype(BF)

    @pl.when(step == pl.num_programs(1) - 1)
    def _():
        grad_k = dka[...] * (1.0 / LOG2E)
        dk_ref[...] = rope(grad_k, ck_ref[...], -uk_ref[...], -lk_ref[...]).astype(BF)
        dv_ref[...] = dva[...].astype(BF)
        dk0_ref[...] = dk0_ref[...] * (1.0 / LOG2E)


def attend_back(
    queries, aug, mixed, grads, keys, values, key0, value0, tables, extra, bq=512, bk=512
):
    length, width = queries.shape
    row = pl.BlockSpec((bq, 128), lambda p, i: (i, p))
    full = pl.BlockSpec((length, 128), lambda p, i: (0, p))
    zero = pl.BlockSpec((16, 128), lambda p, i: (0, p))
    tq = pl.BlockSpec((bq, 128), lambda p, i: (i, 0))
    tk = pl.BlockSpec((length, 128), lambda p, i: (0, 0), pipeline_mode=pl.Buffered(1))
    sums = pl.BlockSpec((extra.shape[0] // 4, extra.shape[1]), lambda p, i: (0, 0))
    big = shape_of((length, width), BF)
    small = shape_of((16, width), F32)
    return pl.pallas_call(
        functools.partial(attend_back_kernel, bk),
        grid=(width // 128, length // bq),
        in_specs=[row, row, row, row, full, full, zero, zero, tq, tq, tq, tk, tk, tk, ANY],
        out_specs=[row, full, full, zero, zero, sums],
        out_shape=[big, big, big, small, small]
        + [shape_of((extra.shape[0] // 4, extra.shape[1]), BF)],
        scratch_shapes=[pltpu.VMEM((length, 256), BF)] * 2
        + [pltpu.VMEM((128, length), BF)]
        + [pltpu.VMEM((length, 128), F32)] * 2
        + scatter_scratch(extra.shape[0] // 4, extra.shape[1]),
        compiler_params=local_params(collective_id=8, has_side_effects=True),
        cost_estimate=cost(40 * length * length * width, 20 * length * width),
        name="attend_back",
    )(queries, aug, mixed, grads, keys, values, key0, value0, *tables, *tables, extra)


def softmax_keys(scores, length):
    key = lax.broadcasted_iota(jnp.int32, scores.shape, 0)
    masked = jnp.where(key < length, scores, -1e9)
    exponent = jnp.exp2(masked - jnp.max(masked, axis=0, keepdims=True))
    return exponent * (1.0 / jnp.sum(exponent, axis=0, keepdims=True))


def cross_kernel(
    len_ref, f_ref, s_ref, g2_ref, g3_ref, wq_ref, wo_ref, kv_ref,
    as_ref, n2_ref, q_ref, m_ref, ac_ref, n3_ref,
):
    groups, model, width = wq_ref.shape
    after_self = f_ref[...].astype(F32) + s_ref[...]
    as_ref[...] = after_self
    unit, _ = norm_rows(after_self)
    normed = (unit * g2_ref[...]).astype(BF)
    n2_ref[...] = normed
    rows = normed.shape[0]
    lane = lanes((rows, 128))
    total = after_self
    for group in range(groups):
        queries = (dot(normed, wq_ref[group], NN) * (LOG2E / 8.0)).astype(BF)
        base = group * width
        q_ref[:, base : base + width] = queries
        for pair in range(width // 128):
            span = slice(128 * pair, 128 * pair + 128)
            values = kv_ref[group, :, width + 128 * pair : width + 128 * pair + 128]
            outs = []
            for head in range(2):
                scores = dot(kv_ref[group, :, span], half_mask(queries[:, span], head), NT)
                probs = softmax_keys(scores, len_ref[0])
                outs.append(dot(probs.astype(BF), values, TN))
            m_ref[:, base + 128 * pair : base + 128 * pair + 128] = jnp.where(
                lane < HD, outs[0], outs[1]
            ).astype(BF)
        total = total + dot(m_ref[:, base : base + width], wo_ref[group], NT)
    ac_ref[...] = total
    unit, _ = norm_rows(total)
    n3_ref[...] = (unit * g3_ref[...]).astype(BF)


def cross_forward(plen, frames, summed, gain2, gain3, weights, prompt_kv):
    share, model = frames.shape
    groups, _, both = weights.shape
    width = both // 2
    rows = 256
    block = pl.BlockSpec((rows, model), lambda i: (i, 0))
    gain = pl.BlockSpec((1, model), lambda i: (0, 0))
    once = pl.Buffered(1)
    return pl.pallas_call(
        cross_kernel,
        grid=(share // rows,),
        in_specs=[
            pl.BlockSpec(memory_space=pltpu.SMEM),
            block,
            block,
            gain,
            gain,
            pl.BlockSpec((groups, model, width), lambda i: (0, 0, 0), pipeline_mode=once),
            pl.BlockSpec((groups, model, width), lambda i: (0, 0, 1), pipeline_mode=once),
            pl.BlockSpec(prompt_kv.shape, lambda i: (0, 0, 0)),
        ],
        out_specs=[block] * 6,
        out_shape=[
            shape_of((share, model), F32),
            shape_of((share, model), BF),
            shape_of((share, model), BF),
            shape_of((share, model), BF),
            shape_of((share, model), F32),
            shape_of((share, model), BF),
        ],
        compiler_params=local_params(),
        cost_estimate=cost(4 * share * model * model, 4 * model * model + 20 * share * model),
        name="cross_forward",
    )(plen, frames, summed, gain2, gain3, weights, weights, prompt_kv)


def cross_back_kernel(
    len_ref, w_ref, go_ref, e_ref, ac_ref, as_ref, g2_ref, g3_ref, q_ref, wq_ref, wo_ref, kv_ref,
    t_ref, cb_ref, dq_ref, c3_ref, c3b_ref, dkv_ref, dg2_ref, dg3_ref, bo_ref, total_ref, dkv, hold, *scratch,
):
    groups, model, width = wq_ref.shape
    job = Scatter(t_ref, total_ref, scratch)
    last = pl.num_programs(0) - 1

    @pl.when(pl.program_id(0) == 0)
    def _():
        greet([job.to_sib, job.to_far])
        job.start()
        job.fold()
        job.local()

    @pl.when(pl.program_id(0) == 0)
    def _():
        dkv[...] = jnp.zeros_like(dkv)
        dg2_ref[...] = jnp.zeros_like(dg2_ref)
        dg3_ref[...] = jnp.zeros_like(dg3_ref)

    unit, spread = norm_rows(ac_ref[...])
    back, part = norm_back(e_ref[...], unit, spread, g3_ref[...])
    dg3_ref[...] += part
    carried = go_ref[...].astype(F32) * w_ref[0] + back
    cross_back = carried.astype(BF)
    cb_ref[...] = cross_back
    rows = cross_back.shape[0]
    lane = lanes((rows, 128))
    total = jnp.zeros((rows, model), F32)
    for group in range(groups):
        grads = dot(cross_back, wo_ref[group], NN).astype(BF)
        base = group * width
        for pair in range(width // 128):
            span = slice(128 * pair, 128 * pair + 128)
            vspan = slice(width + 128 * pair, width + 128 * pair + 128)
            wide = slice(base + 128 * pair, base + 128 * pair + 128)
            outs = []
            for head in range(2):
                queries = half_mask(q_ref[:, wide], head)
                masked = half_mask(grads[:, span], head)
                probs = softmax_keys(dot(kv_ref[group, :, span], queries, NT), len_ref[0])
                dprobs = dot(kv_ref[group, :, vspan], masked, NT)
                inner = jnp.sum(dprobs * probs, axis=0, keepdims=True)
                ds = (probs * (dprobs - inner)).astype(BF)
                outs.append(dot(ds, kv_ref[group, :, span], TN))
                dkv[group, :, span] += dot(ds, queries, NN) * (1.0 / LOG2E)
                dkv[group, :, vspan] += dot(probs.astype(BF), masked, NN)
            dq_ref[:, wide] = (jnp.where(lane < HD, outs[0], outs[1]) * 0.125).astype(BF)
        total = total + dot(dq_ref[:, base : base + width], wq_ref[group], NT)
    unit, spread = norm_rows(as_ref[...])
    back, part = norm_back(total, unit, spread, g2_ref[...])
    dg2_ref[...] += part
    carried = carried + back
    c3_ref[...] = carried
    c3b_ref[...] = carried.astype(BF)
    hold[pl.ds(pl.multiple_of(pl.program_id(0) * rows, rows), rows), :] = ac_ref[...]

    @pl.when(pl.program_id(0) == last)
    def _():
        job.land()
        bo_ref[...] = (hold[...] + total_ref[...]).astype(BF)
        dkv_ref[...] = dkv[...].astype(BF)
        job.finish()


def cross_backward(plen, weight, grad_out, summed, after_cross, after_self, gain2, gain3,
                   queries, weights, prompt_kv, term):
    share, model = grad_out.shape
    groups, _, both = weights.shape
    width = both // 2
    rows = 256
    block = pl.BlockSpec((rows, model), lambda i: (i, 0))
    gain = pl.BlockSpec((1, model), lambda i: (0, 0))
    smem = pl.BlockSpec(memory_space=pltpu.SMEM)
    once = pl.Buffered(1)
    return pl.pallas_call(
        cross_back_kernel,
        grid=(share // rows,),
        in_specs=[
            smem,
            smem,
            block,
            block,
            block,
            block,
            gain,
            gain,
            block,
            pl.BlockSpec((groups, model, width), lambda i: (0, 0, 0), pipeline_mode=once),
            pl.BlockSpec((groups, model, width), lambda i: (0, 0, 1), pipeline_mode=once),
            pl.BlockSpec(prompt_kv.shape, lambda i: (0, 0, 0)),
            ANY,
        ],
        out_specs=[block, block, block, block, pl.BlockSpec(prompt_kv.shape, lambda i: (0, 0, 0)),
                   gain, gain, pl.BlockSpec((share, model), lambda i: (0, 0))],
        out_shape=[
            shape_of((share, model), BF),
            shape_of((share, model), BF),
            shape_of((share, model), F32),
            shape_of((share, model), BF),
            shape_of(prompt_kv.shape, BF),
            shape_of((1, model), F32),
            shape_of((1, model), F32),
            shape_of((share, model), BF),
        ],
        scratch_shapes=[
            pltpu.VMEM((share, model), F32),
            pltpu.VMEM(prompt_kv.shape, F32),
            pltpu.VMEM((share, model), F32),
        ]
        + scatter_scratch(share, model),
        compiler_params=local_params(collective_id=9, has_side_effects=True),
        cost_estimate=cost(4 * share * model * model, 4 * model * model + 24 * share * model),
        name="cross_backward",
    )(plen, weight, grad_out, summed, after_cross, after_self, gain2, gain3, queries,
      weights, weights, prompt_kv, term)


def glu_kernel(scaled, *refs):
    if scaled:
        n_ref, c_ref, w_ref, h_ref, d_ref = refs
        cot = c_ref[...]
    else:
        s_ref, n_ref, c_ref, w_ref, h_ref, d_ref, o_ref = refs
        cot = (c_ref[...].astype(F32) * s_ref[0]).astype(BF)
        o_ref[...] = cot
    width = h_ref.shape[1]
    normed = n_ref[...]
    piece = 256
    for base in range(0, width, piece):
        gate = dot(normed, w_ref[:, base : base + piece], NN)
        up = dot(normed, w_ref[:, width + base : width + base + piece], NN)
        grads = dot(cot, w_ref[:, 2 * width + base : 2 * width + base + piece], NN)
        sig = 1.0 / (1.0 + jnp.exp(-gate))
        silu = gate * sig
        h_ref[:, base : base + piece] = (silu * up).astype(BF)
        grad_gate = grads * up * sig * (1.0 + gate * (1.0 - sig))
        d_ref[:, base : base + piece] = grad_gate.astype(BF)
        d_ref[:, width + base : width + base + piece] = (grads * silu).astype(BF)


def glu_block(normed, cot, weights, scale=None):
    length, model = normed.shape
    width = weights.shape[1] // 3
    rows = 512
    block = pl.BlockSpec((rows, model), lambda i: (i, 0))
    first = scale is not None
    return pl.pallas_call(
        functools.partial(glu_kernel, not first),
        grid=(length // rows,),
        in_specs=[pl.BlockSpec(memory_space=pltpu.SMEM)] * first
        + [
            block,
            block,
            pl.BlockSpec(weights.shape, lambda i: (0, 0), pipeline_mode=pl.Buffered(1)),
        ],
        out_specs=[
            pl.BlockSpec((rows, width), lambda i: (i, 0)),
            pl.BlockSpec((rows, 2 * width), lambda i: (i, 0)),
        ]
        + [block] * first,
        out_shape=[shape_of((length, width), BF), shape_of((length, 2 * width), BF)]
        + [shape_of((length, model), BF)] * first,
        compiler_params=local_params(),
        cost_estimate=cost(6 * length * model * width, 6 * length * model),
        name="glu_block_%d" % width,
    )(*([scale] if first else []), normed, cot, weights)


def grads_kernel(picks, count, *refs):
    lefts, rest = refs[:count], refs[count:]
    out = rest[-1]
    base = 0
    for at, pick in enumerate(picks):
        right = rest[at][...]
        total = dot(lefts[pick][...], right, TN)
        if len(rest) > len(picks) + 1:
            edge, edges = rest[len(picks)], rest[len(picks) + 1 + at]
            total = total + dot(edge[...], edges[...], TN)
        out[:, base : base + right.shape[1]] = total.astype(BF)
        base += right.shape[1]


def weight_grads(lefts, rights, picks, edge=None, edges=(), tile=256):
    length, model = lefts[0].shape
    wide = sum(right.shape[1] for right in rights)
    once = pl.Buffered(1)
    fixed = lambda i: (0, 0)
    in_specs = [pl.BlockSpec((length, tile), lambda i: (0, i)) for _ in lefts]
    in_specs += [pl.BlockSpec(right.shape, fixed, pipeline_mode=once) for right in rights]
    extra = []
    if edge is not None:
        in_specs.append(pl.BlockSpec((edge.shape[0], tile), lambda i: (0, i)))
        in_specs += [pl.BlockSpec(array.shape, fixed) for array in edges]
        extra = [edge, *edges]
    return pl.pallas_call(
        functools.partial(grads_kernel, picks, len(lefts)),
        grid=(model // tile,),
        in_specs=in_specs,
        out_specs=pl.BlockSpec((tile, wide), lambda i: (i, 0)),
        out_shape=shape_of((model, wide), BF),
        compiler_params=local_params(),
        cost_estimate=cost(2 * length * model * wide, 2 * length * (2 * model + wide)),
        name="weight_grads_%d" % wide,
    )(*lefts, *rights, *extra)


def spread_dp(share):
    return lax.all_gather(share, "dp", axis=0, tiled=True)


def owner_sum(term):
    return lax.psum_scatter(term, "dp", scatter_dimension=0, tiled=True)


def after(value, *others):
    return lax.optimization_barrier((value,) + others)[0]


GLU_PARTS = ((0, 1), (1, 6))


def per_device(
    frames, cond_table, bucket_ids, prompt, prompt_len,
    attn_query, attn_key, attn_value, attn_out,
    cross_query, cross_key, cross_value, cross_out,
    glu_gate, glu_up, glu_down, first_gain, second_gain, third_gain, grad_out,
):
    groups = lax.axis_size("mp")
    count = lax.axis_size("dp")
    sequences = bucket_ids.shape[0]
    assert sequences == 1 and groups == 4
    share, model = frames.shape
    length = share * groups
    buckets = cond_table.shape[0]
    own_rows, width = attn_query.shape
    unit = glu_gate.shape[1] // GLU_PARTS[-1][1]
    context = prompt.shape[2]

    onehot = (bucket_ids[:, None] == jnp.arange(buckets)[None, :]).astype(F32)
    extra = jnp.concatenate(
        [
            first_gain[:, None],
            second_gain[:, None],
            third_gain[:, None],
            jnp.broadcast_to(onehot.astype(BF), (own_rows, buckets)),
            jnp.zeros((own_rows, 128 - 3 - buckets), BF),
        ],
        1,
    )
    prompt_pack = jnp.concatenate([cross_key, cross_value], 1).reshape(own_rows, width)
    packed = jnp.concatenate(
        [attn_query, attn_key, attn_value, extra, attn_out, prompt_pack, cross_query, cross_out], 1
    )
    frames_all, grad_all, first = head_gather(frames, grad_out, packed, count)
    glu_gate, glu_up, glu_down, first = lax.optimization_barrier(
        (glu_gate, glu_up, glu_down, first)
    )
    second = first[:, 3 * width + 128 : 5 * width + 128]
    glu_share = []
    for low, high in GLU_PARTS:
        span = slice(low * unit, high * unit)
        glu_share.append(
            jnp.concatenate([glu_gate[:, span], glu_up[:, span], glu_down[:, span]], 1)
        )
    glu_rest = spread_dp(glu_share[1])

    side = first[:, 3 * width : 3 * width + 128]
    gains = dot(jnp.eye(8, 128, dtype=BF), side, NT)
    gain1, gain2, gain3 = gains[0:1], gains[1:2], gains[2:3]
    marks = side.reshape(count, own_rows, 128)[:, 0, 3 : 3 + buckets]
    counts = jnp.sum(marks.astype(F32), 0)
    seq_weight = sequences * count / (buckets * jnp.sum(onehot * counts[None, :], 1))

    tables = rope_tables(length, 1.0)
    cond_row = dot(onehot.astype(BF), cond_table, NN)
    unit_cond, spread_cond = norm_rows(cond_row)
    normed_cond = jnp.pad((unit_cond * gain1).astype(BF), ((0, 15), (0, 0)))
    kv0 = dot(normed_cond, first[:, width : 3 * width], NN).astype(BF)
    key0, value0 = kv0[:, :width], kv0[:, width:]
    normed_one, queries, keys, values = qkv_project(frames_all, gain1, first, tables, width)
    mixed, aug, cross_full, glu_first = attend(
        queries, keys, values, key0, value0, first, 5 * width + 128, glu_share[0], count
    )
    glu_full = (glu_first, glu_rest)
    cross_full = cross_full.reshape(groups, model, 2 * width)
    out_full = second[:, :width]
    prompt_full = second[:, width:].reshape(context, 2 * width)
    prompt_local = dot(prompt[0], prompt_full, NN).astype(BF)
    self_out, prompt_kv = out_project(mixed, out_full, prompt_local)
    prompt_kv = prompt_kv.reshape(groups, prompt.shape[1], 2 * width)

    after_self, normed_two, cross_q, cross_mixed, after_cross, normed_three = cross_forward(
        prompt_len, frames, self_out, gain2, gain3, cross_full, prompt_kv
    )
    normed_three = plain_gather(normed_three, 2)

    h0, d0, cot_all = glu_block(normed_three, grad_all, glu_full[0], seq_weight)
    pack0 = weight_grads([normed_three, cot_all], [d0, h0], (0, 1))
    h1, d1 = glu_block(after(normed_three, pack0), cot_all, glu_full[1])
    pack1 = weight_grads([normed_three, cot_all], [d1, h1], (0, 1))
    glu_grads = [owner_sum(pack0)]
    glu_grads.append(owner_sum(pack1))
    back_term, out_term = glu_back([after(d0, pack1), d1], [h0, h1], glu_full)

    cross_back, grad_cq, carried, carried_low, grad_kv, dg2, dg3, block_out = cross_backward(
        prompt_len, seq_weight, grad_out, back_term, after_cross, after_self, gain2, gain3,
        cross_q, cross_full, prompt_kv, out_term,
    )
    cross_term, grad_mixed, grad_out_weight, grad_kv = mid_gather(
        carried_low, grad_kv.reshape(-1, 2 * width), normed_two, cross_back, grad_cq, cross_mixed,
        out_full, mixed, groups,
    )
    grad_prompt = dot(prompt[0], grad_kv.astype(BF), TN).astype(BF).reshape(model, width)
    second_pack = jnp.concatenate([grad_out_weight, grad_prompt], 1)
    dq, dk, dv, dk0, dv0, cross_sum = attend_back(
        queries, aug, mixed, grad_mixed, keys, values, key0, value0, tables, cross_term
    )
    second_grad = owner_sum(after(second_pack, glu_grads[1], dk0))
    dk0 = dk0.astype(BF)
    dv0 = dv0.astype(BF)
    first_pack = weight_grads(
        [normed_one], [dq, dk, dv], (0, 0, 0), normed_cond, [jnp.zeros_like(dk0), dk0, dv0]
    )
    cond_term = dot(dk0, first[:, width : 2 * width], NT) + dot(
        dv0, first[:, 2 * width : 3 * width], NT
    )
    cond_back, dg1_cond = norm_back(cond_term[:1], unit_cond, spread_cond, gain1)
    mark = jnp.pad(onehot.T, ((0, SMALL - buckets), (0, 0)))
    frames_grad, sums, *first_grads = tail_sums(
        count, buckets, [dq, dk, dv], first, first_pack, cross_sum, frames, carried, gain1, dg2,
        dg3, mark, cond_back, dg1_cond,
    )

    second_grad = second_grad.astype(F32)
    prompt_grad = second_grad[:, width:].reshape(context // count, 2 * width)
    glu_out = []
    for i in range(3):
        cuts = []
        for (low, high), grad in zip(GLU_PARTS, glu_grads):
            size = (high - low) * unit
            cuts.append(grad[:, i * size : (i + 1) * size].astype(F32))
        glu_out.append(jnp.concatenate(cuts, 1))
    return (
        block_out,
        frames_grad,
        sums[:buckets],
        *first_grads[:3],
        second_grad[:, :width],
        first_grads[3],
        prompt_grad[:, :width],
        prompt_grad[:, width:],
        first_grads[4],
        glu_out[0],
        glu_out[1],
        glu_out[2],
        sums[buckets],
        sums[buckets + 1],
        sums[buckets + 2],
    )


def solution(mesh):
    both = P(("dp", "mp"), None)
    weight = P("dp", "mp")
    return jax.shard_map(
        per_device,
        mesh=mesh,
        in_specs=(both, P(), P("dp"), P("dp", None, None), P("dp"))
        + (weight,) * 11
        + (P("dp"),) * 3
        + (both,),
        out_specs=(both, both, P()) + (weight,) * 11 + (P(),) * 3,
        check_vma=False,
    )
```

```python
import functools

import jax
import jax.numpy as jnp
import numpy as np
from jax import lax
from jax.experimental import pallas as pl
from jax.experimental.pallas import tpu as pltpu
from jax.sharding import PartitionSpec as P

HD = 64
ROT = 32
LOG2E = 1.4426950408889634
EPS = 1e-05
MESH = pl.DeviceIdType.MESH
NT = (((1,), (1,)), ((), ()))
TN = (((0,), (0,)), ((), ()))
NN = (((1,), (0,)), ((), ()))
BF = jnp.bfloat16
F32 = jnp.float32
ANY = pl.BlockSpec(memory_space=pl.ANY)
VM = 58 << 20


def shape_of(dims, dtype):
    return jax.ShapeDtypeStruct(dims, dtype)


def dot(left, right, dims):
    return lax.dot_general(left, right, dims, preferred_element_type=F32)


def local_params(**extra):
    return pltpu.CompilerParams(vmem_limit_bytes=VM, **extra)


def cost(flops, nbytes, trans=0):
    return pl.CostEstimate(flops=int(flops), bytes_accessed=int(nbytes), transcendentals=int(trans))


def norm_rows(values):
    center = values - jnp.mean(values, -1, keepdims=True)
    spread = lax.rsqrt(jnp.mean(center * center, -1, keepdims=True) + EPS)
    return center * spread, spread


def norm_back(grad_rows, unit_rows, spread, gain_row):
    scaled = grad_rows * gain_row
    result = spread * (
        scaled
        - jnp.mean(scaled, -1, keepdims=True)
        - unit_rows * jnp.mean(scaled * unit_rows, -1, keepdims=True)
    )
    return result, jnp.sum(grad_rows * unit_rows, 0, keepdims=True)


def rope_tables(length, offset):
    lane = np.arange(2 * HD) % HD
    half = ROT // 2
    frequency = np.power(10000.0, -2.0 * (lane % half) / ROT)
    angles = (offset + np.arange(length))[:, None] * frequency[None, :]
    cosine = np.where(lane[None] < ROT, np.cos(angles), 1.0)
    sine = np.sin(angles)
    upper = np.where((lane[None] >= half) & (lane[None] < ROT), sine, 0.0)
    lower = np.where(lane[None] < half, -sine, 0.0)
    return [jnp.asarray(table.astype(np.float32)) for table in (cosine, upper, lower)]


def rope(values, cosine, upper, lower):
    half = ROT // 2
    return (
        values * cosine
        + pltpu.roll(values, half, 1) * upper
        + pltpu.roll(values, 2 * HD - half, 1) * lower
    )


def lanes(dims):
    return lax.broadcasted_iota(jnp.int32, dims, 1)


def half_mask(values, head):
    lane = lanes(values.shape)
    keep = (lane < HD) if head == 0 else (lane >= HD)
    return jnp.where(keep, values, jnp.zeros_like(values))


def pieces(column, dims, base):
    high = column.astype(BF).astype(F32)
    rest = column - high
    middle = rest.astype(BF).astype(F32)
    low = rest - middle
    lane = lanes(dims)
    return jnp.where(
        lane == base,
        high,
        jnp.where(lane == base + 1, middle, jnp.where(lane == base + 2, low, 0.0)),
    )


def mp_peers():
    me = lax.axis_index("mp")
    chip, core = me // 2, me % 2
    return me, chip * 2 + (1 - core), (1 - chip) * 2 + core, (1 - chip) * 2 + (1 - core)


def greet(devices):
    barrier = pltpu.get_barrier_semaphore()
    for device in devices:
        pl.semaphore_signal(barrier, inc=1, device_id=device, device_id_type=MESH)
    pl.semaphore_wait(barrier, len(devices))


def remote(source, target, send, recv, device):
    return pltpu.make_async_remote_copy(
        source, target, send, recv, device_id=device, device_id_type=MESH
    )


CHUNKS = 4
CUTS = 2


def column_cuts(width):
    first = 128 * ((width // 128 + 1) // 2)
    return [pl.ds(0, first), pl.ds(first, width - first)]


BUSY = cost(1, 140 << 20)


def gather_scratch(rows, width):
    return [
        pltpu.VMEM((rows, width), BF),
        pltpu.SemaphoreType.DMA((2,)),
        pltpu.SemaphoreType.DMA((3, CHUNKS)),
        pltpu.SemaphoreType.DMA((3, CHUNKS)),
    ]


class Gather:
    def __init__(self, x_ref, o_ref, sems, columns=None, here=False):
        bounce, lsem, ssem, rsem = sems
        if here:
            bounce = x_ref
        self.me, self.sib, self.far, _ = mp_peers()
        dp = lax.axis_index("dp")
        self.to_sib = {"dp": dp, "mp": self.sib}
        self.to_far = {"dp": dp, "mp": self.far}
        rows = x_ref.shape[0]
        part = rows // CHUNKS

        def slot(i, k):
            return o_ref.at[pl.ds(pl.multiple_of(i * rows + k * part, part), part)]

        def source(first, size):
            if columns is None:
                return x_ref.at[pl.ds(first, size)]
            return x_ref.at[pl.ds(first, size), columns]

        self.load = None if here else pltpu.make_async_copy(source(0, rows), bounce, lsem.at[0])
        self.store = pltpu.make_async_copy(
            bounce, o_ref.at[pl.ds(pl.multiple_of(self.me * rows, rows), rows)], lsem.at[1]
        )
        self.across = []
        self.beside = []
        self.onward = []
        for k in range(CHUNKS):
            mine = source(k * part, part)
            self.across.append(
                remote(mine, slot(self.me, k), ssem.at[0, k], rsem.at[0, k], self.to_far)
            )
            self.beside.append(
                remote(mine, slot(self.me, k), ssem.at[1, k], rsem.at[1, k], self.to_sib)
            )
            self.onward.append(
                remote(
                    slot(self.far, k), slot(self.far, k), ssem.at[2, k], rsem.at[2, k], self.to_sib
                )
            )

    def start(self):
        for copy in self.across:
            copy.start()
        if self.load is not None:
            self.load.start()
        for copy in self.beside:
            copy.start()
        if self.load is not None:
            self.load.wait()
        self.store.start()

    def forward(self, k):
        self.across[k].wait_recv()
        self.onward[k].start()

    def finish(self):
        for k in range(CHUNKS):
            self.beside[k].wait_recv()
            self.onward[k].wait_recv()
        for k in range(CHUNKS):
            self.across[k].wait_send()
            self.beside[k].wait_send()
            self.onward[k].wait_send()
        self.store.wait()


def scatter_scratch(rows, width):
    return [pltpu.VMEM((2, rows, width), BF)] + [pltpu.VMEM((rows, width), BF)] * 4 + [
        pltpu.SemaphoreType.DMA((2,)),
        pltpu.SemaphoreType.DMA((3, CHUNKS)),
        pltpu.SemaphoreType.DMA((3, CHUNKS)),
    ]


class Scatter:
    def __init__(self, x_ref, o_ref, scratch):
        mine, ra, rb, rc, sb, lsem, ssem, rsem = scratch
        me, sib, far, diag = mp_peers()
        dp = lax.axis_index("dp")
        self.to_sib = {"dp": dp, "mp": sib}
        self.to_far = {"dp": dp, "mp": far}
        self.o_ref, self.mine, self.ra, self.rb, self.rc, self.sb = o_ref, mine, ra, rb, rc, sb
        rows = ra.shape[0]
        part = rows // CHUNKS
        self.spans = [pl.ds(k * part, part) for k in range(CHUNKS)]

        def slot(i, k):
            return x_ref.at[pl.ds(pl.multiple_of(i * rows + k * part, part), part)]

        def whole(i):
            return x_ref.at[pl.ds(pl.multiple_of(i * rows, rows), rows)]

        self.first, self.second, self.third = [], [], []
        for k, span in enumerate(self.spans):
            self.first.append(
                remote(slot(diag, k), ra.at[span], ssem.at[0, k], rsem.at[0, k], self.to_sib)
            )
            self.second.append(
                remote(slot(sib, k), rb.at[span], ssem.at[1, k], rsem.at[1, k], self.to_sib)
            )
            self.third.append(
                remote(sb.at[span], rc.at[span], ssem.at[2, k], rsem.at[2, k], self.to_far)
            )
        self.load0 = pltpu.make_async_copy(whole(far), mine.at[0], lsem.at[0])
        self.load1 = pltpu.make_async_copy(whole(me), mine.at[1], lsem.at[1])

    def start(self):
        self.load0.start()
        for copy in self.first:
            copy.start()
        self.load1.start()
        for copy in self.second:
            copy.start()

    def fold(self):
        self.load0.wait()
        for k, span in enumerate(self.spans):
            self.first[k].wait_recv()
            total = self.mine[0, span, :].astype(F32) + self.ra[span, :].astype(F32)
            self.sb[span, :] = total.astype(BF)
            self.third[k].start()

    def local(self):
        self.load1.wait()
        for k in range(CHUNKS):
            self.second[k].wait_recv()

    def land(self, addend=None):
        for k, span in enumerate(self.spans):
            self.third[k].wait_recv()
            total = self.mine[1, span, :].astype(F32) + self.rb[span, :].astype(F32)
            if addend is not None:
                total = total + addend[span, :]
            self.o_ref[span, :] = (total + self.rc[span, :].astype(F32)).astype(self.o_ref.dtype)

    def finish(self):
        for k in range(CHUNKS):
            self.first[k].wait_send()
            self.second[k].wait_send()
            self.third[k].wait_send()


def sum_scratch(rows, width):
    return [pltpu.VMEM((4, rows, width), BF)] + [pltpu.VMEM((rows, width), BF)] * 4 + [
        pltpu.SemaphoreType.DMA((3, CHUNKS)),
        pltpu.SemaphoreType.DMA((3, CHUNKS)),
    ]


class LocalSum:
    def __init__(self, o_ref, scratch):
        terms, ra, rb, rc, sb, ssem, rsem = scratch
        _, sib, far, _ = mp_peers()
        dp = lax.axis_index("dp")
        self.to_sib = {"dp": dp, "mp": sib}
        self.to_far = {"dp": dp, "mp": far}
        self.o_ref, self.terms, self.ra, self.rb, self.rc, self.sb = o_ref, terms, ra, rb, rc, sb
        rows = ra.shape[0]
        part = rows // CHUNKS
        self.spans = [pl.ds(k * part, part) for k in range(CHUNKS)]
        self.first, self.second, self.third = [], [], []
        for k, span in enumerate(self.spans):
            self.first.append(
                remote(terms.at[0, span], ra.at[span], ssem.at[0, k], rsem.at[0, k], self.to_sib)
            )
            self.second.append(
                remote(terms.at[2, span], rb.at[span], ssem.at[1, k], rsem.at[1, k], self.to_sib)
            )
            self.third.append(
                remote(sb.at[span], rc.at[span], ssem.at[2, k], rsem.at[2, k], self.to_far)
            )

    def put(self, step, value):
        half = value.shape[0]
        late = step // 4
        slot = (1 - late) * (step % 2) + late * (step // 2)
        row = (1 - late) * ((step // 2) % 2) + late * (step % 2)
        self.terms[slot, pl.ds(pl.multiple_of(row * half, half), half), :] = value

    def after_step(self, step):
        half = CHUNKS // 2
        for turn in range(2):
            chunks = range(turn * half, turn * half + half)

            @pl.when(step == 2 * turn)
            def _(chunks=chunks):
                for k in chunks:
                    self.first[k].start()

            @pl.when(step == 2 * turn + 1)
            def _(chunks=chunks):
                for k in chunks:
                    span = self.spans[k]
                    self.first[k].wait_recv()
                    total = self.terms[1, span, :].astype(F32) + self.ra[span, :].astype(F32)
                    self.sb[span, :] = total.astype(BF)
                    self.third[k].start()

        @pl.when(step == 5)
        def _():
            for copy in self.second:
                copy.start()

    def land(self):
        for k, span in enumerate(self.spans):
            self.second[k].wait_recv()
            self.third[k].wait_recv()
            total = self.terms[3, span, :].astype(F32) + self.rb[span, :].astype(F32)
            self.o_ref[span, :] = (total + self.rc[span, :].astype(F32)).astype(self.o_ref.dtype)

    def finish(self):
        for copy in self.first + self.second + self.third:
            copy.wait_send()


def order_block(step):
    me = lax.axis_index("mp")
    chip, core = me // 2, me % 2
    late = step // 4
    other = 1 - late
    cross = 1 - ((1 - late) * (step % 2) + late * ((step // 2) % 2))
    quarter = (chip + other - 2 * chip * other) * 2 + (core + cross - 2 * core * cross)
    return quarter * 2 + (1 - late) * ((step // 2) % 2) + late * (step % 2)


def arrival_quarter(turn):
    me = lax.axis_index("mp")
    chip, core = me // 2, me % 2
    other = turn // 2
    cross = turn % 2
    return (chip + other - 2 * chip * other) * 2 + (core + cross - 2 * core * cross)


class Ring:
    def __init__(self, count):
        self.count = count
        self.half = count // 2
        me = lax.axis_index("dp")
        mp = lax.axis_index("mp")
        odd = me % 2
        self.me = me
        self.spot = (1 - odd) * (me // 2) + odd * (count - 1 - me // 2)
        self.ahead = {"dp": self.at(1), "mp": mp}
        self.behind = {"dp": self.at(-1), "mp": mp}

    def at(self, distance):
        spot = (self.spot + distance + self.count) % self.count
        late = spot // self.half
        return (1 - late) * 2 * spot + late * (2 * (self.count - 1 - spot) + 1)


def ring_scratch(rows, width, half):
    return [pltpu.VMEM((rows, width), BF), pltpu.SemaphoreType.DMA((2,))] + [
        pltpu.SemaphoreType.DMA((half, CUTS))
    ] * 4


class RingGather:
    def __init__(self, count, w_ref, o_ref, scratch):
        bounce, lsem, fs, fr, bs, br = scratch
        ring = Ring(count)
        self.ahead, self.behind, self.half = ring.ahead, ring.behind, ring.half
        rows = w_ref.shape[0]

        spans = column_cuts(w_ref.shape[1])

        def slot(i):
            return o_ref.at[pl.ds(pl.multiple_of(i * rows, rows), rows)]

        last = self.half - 1

        def copies(block, hop, send, recv, device, only):
            result = {}
            for c, columns in enumerate(spans):
                if hop < last or c == only:
                    place = o_ref.at[pl.ds(pl.multiple_of(block * rows, rows), rows), columns]
                    source = w_ref.at[:, columns] if hop == 0 else place
                    result[c] = remote(source, place, send.at[hop, c], recv.at[hop, c], device)
            return result

        self.forward = []
        self.backward = []
        for hop in range(self.half):
            self.forward.append(copies(ring.at(-hop), hop, fs, fr, ring.ahead, 0))
            self.backward.append(copies(ring.at(hop), hop, bs, br, ring.behind, 1))
        self.load = pltpu.make_async_copy(w_ref, bounce, lsem.at[0])
        self.store = pltpu.make_async_copy(bounce, slot(ring.me), lsem.at[1])

    def start(self):
        for c in range(CUTS):
            self.forward[0][c].start()
            self.backward[0][c].start()
        self.load.start()

    def place(self):
        self.load.wait()
        self.store.start()

    def hop(self, hop):
        for c in range(CUTS):
            for way in (self.forward, self.backward):
                way[hop - 1][c].wait_recv()
                if c in way[hop]:
                    way[hop][c].start()

    def finish(self):
        self.forward[-1][0].wait_recv()
        self.backward[-1][1].wait_recv()
        self.store.wait()
        for copies in self.forward + self.backward:
            for copy in copies.values():
                copy.wait_send()


def ring_sum_scratch(rows, wide, half, sources):
    slots = pltpu.VMEM((half, rows, wide), BF)
    hops = pltpu.SemaphoreType.DMA((half, CUTS))
    return (
        [slots] * 4
        + [pltpu.VMEM((rows, wide), BF), pltpu.SemaphoreType.DMA((2 * half + 1, sources))]
        + [hops] * 4
    )


class RingSum:
    def __init__(self, count, sources, scratch):
        self.lf, self.lb, self.rf, self.rb, self.own, lsem, fs, fr, bs, br = scratch
        ring = Ring(count)
        self.ahead, self.behind, self.half = ring.ahead, ring.behind, ring.half
        rows = self.own.shape[0]
        self.spans = column_cuts(self.own.shape[1])

        def sends(source, target, hop, send, recv, device, only):
            return {
                c: remote(
                    source.at[hop, :, span],
                    target.at[hop, :, span],
                    send.at[hop, c],
                    recv.at[hop, c],
                    device,
                )
                for c, span in enumerate(self.spans)
                if hop > 0 or c == only
            }

        def loads(block, target, at):
            span = pl.ds(pl.multiple_of(block * rows, rows), rows)
            base, copies = 0, []
            for i, source in enumerate(sources):
                wide = source.shape[1]
                copies.append(
                    pltpu.make_async_copy(
                        source.at[span], target.at[:, pl.ds(base, wide)], lsem.at[at, i]
                    )
                )
                base += wide
            return copies

        self.forward, self.backward, self.local = [], [], []
        for hop in range(self.half):
            self.local.append(
                loads(ring.at(self.half - hop), self.lf.at[hop], 2 * hop)
                + loads(ring.at(hop - self.half), self.lb.at[hop], 2 * hop + 1)
            )
            self.forward.append(sends(self.lf, self.rf, hop, fs, fr, ring.ahead, 0))
            self.backward.append(sends(self.lb, self.rb, hop, bs, br, ring.behind, 1))
        self.local.append(loads(ring.me, self.own, 2 * self.half))

    def start(self):
        for copies in self.local:
            for copy in copies:
                copy.start()
        for copy in self.local[0]:
            copy.wait()
        self.forward[0][0].start()
        self.backward[0][1].start()
        for copy in self.local[1]:
            copy.wait()
        self.forward[1][1].start()
        self.backward[1][0].start()

    def hop(self, hop):
        if hop > 1:
            for copy in self.local[hop]:
                copy.wait()
        for c, span in enumerate(self.spans):
            for way, mine, came in (
                (self.forward, self.lf, self.rf),
                (self.backward, self.lb, self.rb),
            ):
                if c in way[hop - 1]:
                    way[hop - 1][c].wait_recv()
                    total = mine[hop, :, span].astype(F32) + came[hop - 1, :, span].astype(F32)
                    mine[hop, :, span] = total.astype(BF)
                    way[hop][c].start()

    def finish(self, outs):
        last = self.half - 1
        for copy in self.local[self.half]:
            copy.wait()
        for c in range(CUTS):
            self.forward[last][c].wait_recv()
            self.backward[last][c].wait_recv()
        base = 0
        for out in outs:
            span = slice(base, base + out.shape[1])
            base += out.shape[1]
            out[...] = (
                self.own[:, span].astype(F32)
                + self.rf[last, :, span].astype(F32)
                + self.rb[last, :, span].astype(F32)
            )
        for copies in self.forward + self.backward:
            for copy in copies.values():
                copy.wait_send()


def head_kernel(count, f_ref, g_ref, w_ref, fo_ref, go_ref, wo_ref, *scratch):
    job = Gather(f_ref, fo_ref, scratch[0:4])
    late = Gather(g_ref, go_ref, scratch[4:8])
    ring = RingGather(count, w_ref, wo_ref, scratch[8:])
    greet([job.to_sib, job.to_far, ring.ahead, ring.behind])
    ring.start()
    job.start()
    ring.place()
    ring.hop(1)
    for k in range(CHUNKS):
        job.forward(k)
    late.start()
    for hop in range(2, ring.half):
        ring.hop(hop)
    for k in range(CHUNKS):
        late.forward(k)
    job.finish()
    late.finish()
    ring.finish()


def head_gather(frames, grads, packed, count):
    rows, width = frames.shape
    wide = shape_of((4 * rows, width), BF)
    return pl.pallas_call(
        functools.partial(head_kernel, count),
        out_shape=(wide, wide, shape_of((count * packed.shape[0], packed.shape[1]), BF)),
        in_specs=[ANY] * 3,
        out_specs=(ANY,) * 3,
        scratch_shapes=gather_scratch(rows, width) * 2 + ring_scratch(*packed.shape, count // 2),
        compiler_params=local_params(collective_id=0, has_side_effects=True),
        cost_estimate=BUSY,
        name="head_gather",
    )(frames, grads, packed)


SMALL = 16


def tail_kernel(
    count, buckets, q_ref, k_ref, v_ref, wq_ref, wk_ref, wv_ref,
    a_ref, f_ref, c_ref, g_ref, dg_ref, mark_ref, r_ref, k0_ref, v0_ref, o_ref, s_ref, *scratch,
):
    outs = scratch[:3]
    scratch = scratch[3:]
    total, held = scratch[0:2]
    job = LocalSum(total, scratch[2:9])
    ring = RingSum(count, [a_ref], scratch[9:19])
    sent, got, ss, rs = scratch[19:]
    step = pl.program_id(0)
    me = lax.axis_index("dp")
    mp = lax.axis_index("mp")
    partners = [job.to_sib, job.to_far]
    bit = 1
    while bit < count:
        partners.append({"dp": me + bit * (1 - 2 * ((me // bit) % 2)), "mp": mp})
        bit *= 2

    @pl.when(step == 0)
    def _():
        greet(partners + [ring.ahead, ring.behind])
        ring.start()

    @pl.when(step < 8)
    def _():
        term = (
            dot(q_ref[...], wq_ref[...], NT)
            + dot(k_ref[...], wk_ref[...], NT)
            + dot(v_ref[...], wv_ref[...], NT)
        )
        job.put(step, term.astype(BF))

    job.after_step(step)

    @pl.when(step == 8)
    def _():
        for hop in range(1, ring.half - 1):
            ring.hop(hop)
        job.land()
        unit, spread = norm_rows(f_ref[...].astype(F32))
        back, part = norm_back(total[...], unit, spread, g_ref[0:1, :])
        o_ref[...] = c_ref[...] + back
        edge = dot(k0_ref[...].astype(BF), wk_ref[...], NT) + dot(
            v0_ref[...].astype(BF), wv_ref[...], NT
        )
        unit, spread = norm_rows(r_ref[...])
        edge_back, edge_part = norm_back(edge[0:1, :], unit[0:1, :], spread[0:1, :], g_ref[0:1, :])
        row = lax.broadcasted_iota(jnp.int32, held.shape, 0)
        held[...] = (
            mark_ref[:, 0:1] * edge_back
            + jnp.where(row == buckets, part + edge_part, 0.0)
            + jnp.where(row == buckets + 1, dg_ref[1:2, :], 0.0)
            + jnp.where(row == buckets + 2, dg_ref[2:3, :], 0.0)
        )
        ring.hop(ring.half - 1)
        for i, partner in enumerate(partners):
            sent[i] = held[...]
            copy = remote(sent.at[i], got.at[i], ss.at[i], rs.at[i], partner)
            copy.start()
            copy.wait_recv()
            held[...] += got[i]
            copy.wait_send()
        s_ref[...] = held[...]
        ring.finish(outs)
        job.finish()


def tail_sums(
    count, buckets, grads_qkv, weights, grads, frames, carried, gains, grad_gains, mark, cond_row,
    dk0, dv0,
):
    share, model = frames.shape
    width = grads_qkv[0].shape[1]
    block = 2 * share // 4
    rows = grads.shape[0] // count
    wide = grads.shape[1]
    half = count // 2
    steps = 2 + (count - 1).bit_length()
    once = pl.Buffered(1)

    def full(array):
        return pl.BlockSpec(array.shape, lambda i: (0,) * array.ndim, pipeline_mode=once)

    small = pltpu.VMEM((steps, SMALL, model), F32)
    out_shape = (shape_of((share, model), F32), shape_of((SMALL, model), F32)) + (
        shape_of((rows, wide // 3), F32),
    ) * 3
    whole = [frames, carried, gains, grad_gains, mark, cond_row, dk0, dv0]
    return pl.pallas_call(
        functools.partial(tail_kernel, count, buckets),
        grid=(9,),
        out_shape=out_shape,
        in_specs=[
            pl.BlockSpec((block, width), lambda i: (order_block(jnp.minimum(i, 7)), 0))
            for _ in range(3)
        ]
        + [
            pl.BlockSpec(
                (model, width), functools.partial(lambda at, i: (0, at), at), pipeline_mode=once
            )
            for at in range(3)
        ]
        + [ANY]
        + [full(array) for array in whole],
        out_specs=tuple(pl.BlockSpec(out.shape, lambda i: (0, 0)) for out in out_shape),
        scratch_shapes=[pltpu.VMEM((share, model), F32), pltpu.VMEM((SMALL, model), F32)]
        + sum_scratch(share, model)
        + ring_sum_scratch(rows, wide, half, 1)
        + [small, small, pltpu.SemaphoreType.DMA((steps,)), pltpu.SemaphoreType.DMA((steps,))],
        compiler_params=local_params(collective_id=6, has_side_effects=True),
        cost_estimate=BUSY,
        name="tail_sums",
    )(*grads_qkv, weights, weights, weights, grads, *whole)


def out_kernel(
    count, m_ref, w_ref, p_ref, wp_ref, share_ref, o_ref, kvo_ref, full_ref, mine, *scratch
):
    side = Gather(mine, kvo_ref, scratch[:4], here=True)
    job = LocalSum(o_ref, scratch[4:11])
    ring = RingGather(count, share_ref, full_ref, scratch[11:])
    step = pl.program_id(0)

    @pl.when(step == 0)
    def _():
        greet([job.to_sib, job.to_far, ring.ahead, ring.behind])
        ring.start()

    job.put(step, dot(m_ref[...], w_ref[...], NT).astype(BF))
    job.after_step(step)

    @pl.when(step == 1)
    def _():
        mine[...] = dot(p_ref[...], wp_ref[...], NN).astype(BF)
        side.start()
        ring.place()

    @pl.when(step == 7)
    def _():
        for hop in range(1, ring.half):
            ring.hop(hop)
        for k in range(CHUNKS):
            side.forward(k)
        job.land()
        side.finish()
        job.finish()
        ring.finish()


def out_project(mixed, weights, column, prompts, prompt_weights, weight_share, count):
    length, width = mixed.shape
    model = weights.shape[0]
    rows = length // 8
    share = length // 4
    short = prompts.shape[0]
    once = pl.Buffered(1)
    return pl.pallas_call(
        functools.partial(out_kernel, count),
        grid=(8,),
        out_shape=(
            shape_of((share, model), F32),
            shape_of((4 * short, width), BF),
            shape_of((count * weight_share.shape[0], weight_share.shape[1]), BF),
        ),
        in_specs=[
            pl.BlockSpec((rows, width), lambda i: (order_block(i), 0)),
            pl.BlockSpec((model, width), lambda i: (0, column), pipeline_mode=once),
            pl.BlockSpec(prompts.shape, lambda i: (0, 0), pipeline_mode=once),
            pl.BlockSpec((model, width), lambda i: (0, 0), pipeline_mode=once),
            ANY,
        ],
        out_specs=(pl.BlockSpec((share, model), lambda i: (0, 0)), ANY, ANY),
        scratch_shapes=[pltpu.VMEM((short, width), BF)]
        + gather_scratch(16, 128)
        + sum_scratch(share, model)
        + ring_scratch(*weight_share.shape, count // 2),
        compiler_params=local_params(collective_id=1, has_side_effects=True),
        cost_estimate=BUSY,
        name="out_project",
    )(mixed, weights, prompts, prompt_weights, weight_share)


def glu_back_kernel(parts, count, d0_ref, d1_ref, h0_ref, h1_ref, *refs):
    weights = refs[:count]
    o_ref, t0_ref, t1_ref = refs[count : count + 3]
    job = LocalSum(o_ref, refs[count + 3 :])
    step = pl.program_id(0)

    def gate_up():
        term = None
        for left, group in zip((d0_ref, d1_ref), parts):
            base = 0
            for index, low, size in group:
                w_ref = weights[index]
                width = w_ref.shape[1] // 3
                if size == width:
                    part = dot(left[:, base : base + 2 * size], w_ref[:, : 2 * size], NT)
                else:
                    high = low + size
                    part = dot(left[:, base : base + size], w_ref[:, low:high], NT) + dot(
                        left[:, base + size : base + 2 * size],
                        w_ref[:, width + low : width + high],
                        NT,
                    )
                term = part if term is None else term + part
                base += 2 * size
        return term.astype(BF)

    def down():
        term = None
        for left, group in zip((h0_ref, h1_ref), parts):
            base = 0
            for index, low, size in group:
                w_ref = weights[index]
                start = 2 * w_ref.shape[1] // 3 + low
                part = dot(left[:, base : base + size], w_ref[:, start : start + size], NT)
                term = part if term is None else term + part
                base += size
        return term.astype(BF)

    @pl.when(step == 0)
    def _():
        greet([job.to_sib, job.to_far])

    @pl.when(step < 8)
    def _():
        job.put(step, gate_up())

    job.after_step(step)

    @pl.when(step >= 8)
    def _():
        term = down()
        half = t0_ref.shape[1]
        t0_ref[...] = term[:, :half]
        t1_ref[...] = term[:, half:]

    @pl.when(step == 15)
    def _():
        job.land()
        job.finish()


def glu_back(dgus, hiddens, weights, parts):
    length = dgus[0].shape[0]
    model = weights[0].shape[0]
    rows = length // 8
    share = length // 4
    once = pl.Buffered(1)
    early = lambda i: (order_block(jnp.minimum(i, 7)), 0)
    late = lambda i: (jnp.maximum(i - 8, 0), 0)
    in_specs = [pl.BlockSpec((rows, d.shape[1]), early) for d in dgus]
    in_specs += [pl.BlockSpec((rows, h.shape[1]), late) for h in hiddens]
    for weight in weights:
        in_specs.append(pl.BlockSpec(weight.shape, lambda i: (0, 0), pipeline_mode=once))
    half = pl.BlockSpec((rows, model // 2), late)
    return pl.pallas_call(
        functools.partial(glu_back_kernel, parts, len(weights)),
        grid=(16,),
        out_shape=(
            shape_of((share, model), F32),
            shape_of((length, model // 2), BF),
            shape_of((length, model // 2), BF),
        ),
        in_specs=in_specs,
        out_specs=(
            pl.BlockSpec((share, model), lambda i: (0, 0)),
            half,
            half,
        ),
        scratch_shapes=sum_scratch(share, model),
        compiler_params=local_params(collective_id=3, has_side_effects=True),
        cost_estimate=BUSY,
        name="glu_back",
    )(*dgus, *hiddens, *weights)


def mid_kernel(
    count, c_ref, t_ref, n_ref, cb_ref, q_ref, cm_ref, w_ref, m_ref, p_ref, y_ref,
    x_ref, g_ref, dw_ref, yo_ref, s_ref, slots, total, ssem, rsem, *scratch,
):
    small = Scatter(t_ref, s_ref, scratch[:8])
    ring = RingSum(count, [y_ref], scratch[8:])
    me, sib, far, diag = mp_peers()
    dp = lax.axis_index("dp")
    to_sib = {"dp": dp, "mp": sib}
    to_far = {"dp": dp, "mp": far}
    step = pl.program_id(0)
    rows = c_ref.shape[0]
    part = rows // CHUNKS
    spans = [pl.ds(k * part, part) for k in range(CHUNKS)]
    beside = remote(c_ref, slots.at[0], ssem.at[0], rsem.at[0], to_sib)
    across = [
        remote(c_ref.at[span], slots.at[1, span], ssem.at[1 + k], rsem.at[1 + k], to_far)
        for k, span in enumerate(spans)
    ]
    onward = [
        remote(
            slots.at[1, span],
            slots.at[2, span],
            ssem.at[1 + CHUNKS + k],
            rsem.at[1 + CHUNKS + k],
            to_sib,
        )
        for k, span in enumerate(spans)
    ]

    @pl.when(step == 0)
    def _():
        greet([to_sib, to_far, ring.ahead, ring.behind])
        for copy in across:
            copy.start()
        small.start()
        beside.start()
        ring.start()

    @pl.when(step == 6)
    def _():
        for hop in range(1, ring.half // 2):
            ring.hop(hop)

    @pl.when(step == 1)
    def _():
        small.fold()
        small.local()

    @pl.when(step < 8)
    def _():
        width = q_ref.shape[1]
        x_ref[:, :width] = dot(n_ref[...], q_ref[...], TN).astype(BF)
        x_ref[:, width:] = dot(cb_ref[...], cm_ref[...], TN).astype(BF)

    def use(grads):
        g_ref[...] = dot(grads, w_ref[...], NN).astype(BF)
        return dot(grads, m_ref[...], TN)

    @pl.when(step == 8)
    def _():
        total[...] = use(c_ref[...])

    @pl.when(step == 9)
    def _():
        beside.wait_recv()
        total[...] += use(slots[0])

    @pl.when(step == 10)
    def _():
        ring.hop(ring.half // 2)
        small.land()
        for k in range(CHUNKS):
            across[k].wait_recv()
            onward[k].start()
        for hop in range(ring.half // 2 + 1, ring.half):
            ring.hop(hop)
        total[...] += use(slots[1])

    @pl.when(step == 11)
    def _():
        for copy in onward:
            copy.wait_recv()
        width = m_ref.shape[1]
        dw_ref[:, :width] = (total[...] + use(slots[2])).astype(BF)
        dw_ref[:, width:] = dot(p_ref[...], s_ref[...].astype(BF), TN).astype(BF)
        small.finish()
        ring.finish([yo_ref])
        beside.wait_send()
        for copy in across + onward:
            copy.wait_send()


def mid_gather(
    carried, term, normed, cross_back, grad_cq, cross_mixed, weights, column, mixed, prompts,
    more, groups, count,
):
    share, model = carried.shape
    own = more.shape[0] // count
    length, width = mixed.shape
    short, narrow = term.shape[0] // 4, term.shape[1]
    tile = 2 * model // 4
    once = pl.Buffered(1)
    fixed = pl.BlockSpec((share, model), lambda i: (0, 0), pipeline_mode=once)
    left = pl.BlockSpec((share, tile), lambda i: (0, jnp.minimum(i, 7) % 2))
    right = pl.BlockSpec((share, width), lambda i: (0, jnp.minimum(i, 7) // 2))

    def turn(i):
        return (arrival_quarter(jnp.maximum(i - 8, 0)), 0)

    return pl.pallas_call(
        functools.partial(mid_kernel, count),
        grid=(12,),
        in_specs=[
            fixed,
            ANY,
            left,
            left,
            right,
            right,
            pl.BlockSpec((model, width), lambda i: (0, column), pipeline_mode=once),
            pl.BlockSpec((share, width), turn),
            pl.BlockSpec(prompts.shape, lambda i: (0, 0), pipeline_mode=once),
            ANY,
        ],
        out_specs=(
            pl.BlockSpec((tile, 2 * width), lambda i: (jnp.minimum(i, 7), 0)),
            pl.BlockSpec((share, width), turn),
            pl.BlockSpec((model, 2 * width), lambda i: (0, 0)),
            pl.BlockSpec((own, more.shape[1]), lambda i: (0, 0)),
        ),
        out_shape=(
            shape_of((groups * model, 2 * width), BF),
            shape_of((length, width), BF),
            shape_of((model, 2 * width), BF),
            shape_of((own, more.shape[1]), F32),
        ),
        scratch_shapes=[
            pltpu.VMEM((short, narrow), F32),
            pltpu.VMEM((3, share, model), BF),
            pltpu.VMEM((model, width), F32),
            pltpu.SemaphoreType.DMA((1 + 2 * CHUNKS,)),
            pltpu.SemaphoreType.DMA((1 + 2 * CHUNKS,)),
        ]
        + scatter_scratch(short, narrow)
        + ring_sum_scratch(own, more.shape[1], count // 2, 1),
        compiler_params=local_params(collective_id=4, has_side_effects=True),
        cost_estimate=BUSY,
        name="mid_gather",
    )(carried, term, normed, cross_back, grad_cq, cross_mixed, weights, mixed, prompts, more)


def qkv_kernel(
    scale, x_ref, s_ref, r_ref, hot_ref, w_ref, c_ref, u_ref, l_ref,
    n_ref, q_ref, k_ref, v_ref, g_ref, sw_ref, nc_ref, k0_ref, v0_ref,
):
    width = q_ref.shape[1]

    @pl.when(pl.program_id(0) == 0)
    def _():
        side = s_ref[...]
        dims = (8, side.shape[1])
        pick = lax.broadcasted_iota(jnp.int32, dims, 0) == lanes(dims)
        g_ref[...] = dot(jnp.where(pick, 1.0, 0.0).astype(BF), side, NT)
        totals = dot(jnp.ones((8, side.shape[0]), BF), side, NN)
        sw_ref[...] = jnp.broadcast_to(
            scale / jnp.sum(totals * hot_ref[...], axis=1, keepdims=True), sw_ref.shape
        )
        unit, _ = norm_rows(r_ref[...])
        normed = (unit * g_ref[0:1, :]).astype(BF)
        nc_ref[...] = normed
        out = dot(normed, w_ref[:, width:], NN).astype(BF)
        k0_ref[...] = out[:, :width]
        v0_ref[...] = out[:, width:]

    unit, _ = norm_rows(x_ref[...].astype(F32))
    normed = (unit * g_ref[0:1, :]).astype(BF)
    n_ref[...] = normed
    out = dot(normed, w_ref[...], NN)
    cosine, upper, lower = c_ref[...], u_ref[...], l_ref[...]
    for pair in range(width // 128):
        span = slice(128 * pair, 128 * pair + 128)
        q_ref[:, span] = (rope(out[:, span], cosine, upper, lower) * (LOG2E / 8.0)).astype(BF)
        keys = out[:, width + 128 * pair : width + 128 * pair + 128]
        k_ref[:, span] = rope(keys, cosine, upper, lower).astype(BF)
    v_ref[...] = out[:, 2 * width : 3 * width].astype(BF)


def qkv_project(frames, cond_row, hot, weights, tables, width, scale):
    length, model = frames.shape
    rows = 256
    block = pl.BlockSpec((rows, model), lambda i: (i, 0))
    table = pl.BlockSpec((rows, 128), lambda i: (i, 0))
    head = pl.BlockSpec((rows, width), lambda i: (i, 0))
    fixed = lambda i: (0, 0)
    extra = [
        shape_of((8, model), F32),
        shape_of((8, 128), F32),
        shape_of((16, model), BF),
        shape_of((16, width), BF),
        shape_of((16, width), BF),
    ]
    return pl.pallas_call(
        functools.partial(qkv_kernel, scale),
        grid=(length // rows,),
        in_specs=[
            block,
            pl.BlockSpec((model, 128), lambda i: (0, 3 * width // 128)),
            pl.BlockSpec(cond_row.shape, fixed),
            pl.BlockSpec(hot.shape, fixed),
            pl.BlockSpec((model, 3 * width), fixed),
            table,
            table,
            table,
        ],
        out_specs=[block, head, head, head] + [pl.BlockSpec(e.shape, fixed) for e in extra],
        out_shape=[shape_of((length, model), BF)] + [shape_of((length, width), BF)] * 3 + extra,
        compiler_params=local_params(),
        cost_estimate=cost(6 * length * model * width, 8 * length * model),
        name="qkv_project",
    )(frames, weights, cond_row, hot, weights, *tables)


def attend_kernel(
    bk, first, count, q_ref, k_ref, v_ref, k0_ref, v0_ref, x_ref, w_ref, y_ref,
    o_ref, aug_ref, xo_ref, wo_ref, yo_ref, vaug, *scratch,
):
    length = k_ref.shape[0]
    bq = q_ref.shape[0]
    step = pl.program_id(0) * pl.num_programs(1) + pl.program_id(1)
    wide = xo_ref.shape[1]
    job = Gather(x_ref, xo_ref, scratch[:4], pl.ds(first, wide))
    ring = RingGather(count, w_ref, wo_ref, scratch[4:10])
    wide_ring = RingGather(count, y_ref, yo_ref, scratch[10:])
    last = pl.num_programs(0) * pl.num_programs(1) - 1

    @pl.when(step == 0)
    def _():
        greet([job.to_sib, job.to_far, ring.ahead, ring.behind])
        ring.start()
        wide_ring.start()
        job.start()
        ring.place()
        wide_ring.place()

    for hop in range(1, ring.half):

        @pl.when(step == min(3 * hop, 11))
        def _(hop=hop):
            ring.hop(hop)

        @pl.when(step == min(1 + 3 * hop, 11))
        def _(hop=hop):
            wide_ring.hop(hop)

    @pl.when(pl.program_id(1) == 0)
    def _():
        vaug[:, :128] = v_ref[...]
        vaug[:, 128:] = jnp.ones((length, 128), BF)

    queries = q_ref[...]
    key0 = k0_ref[0:1, :].astype(F32)
    value0 = v0_ref[0:1, :].astype(F32)
    outs = []
    logs = []
    for head in range(2):
        masked = half_mask(queries, head)
        peak = jnp.sum(masked.astype(F32) * key0, axis=1, keepdims=True)
        total = jnp.concatenate(
            [jnp.broadcast_to(value0, (bq, 128)), jnp.ones((bq, 128), F32)], 1
        )
        for block in range(length // bk):
            span = slice(block * bk, (block + 1) * bk)
            scores = dot(masked, k_ref[span, :], NT)
            higher = jnp.maximum(peak, jnp.max(scores, axis=1, keepdims=True))
            exponent = jnp.exp2(scores - higher).astype(BF)
            total = total * jnp.exp2(peak - higher) + dot(exponent, vaug[span, :], NN)
            peak = higher
        weight = total[:, 128:129]
        outs.append(total[:, :128] * (1.0 / weight))
        logs.append(-(peak + jnp.log2(weight)))
    lane = lanes((bq, 128))
    o_ref[...] = jnp.where(lane < HD, outs[0], outs[1]).astype(BF)
    aug_ref[...] = (pieces(logs[0], (bq, 128), 0) + pieces(logs[1], (bq, 128), HD)).astype(BF)

    @pl.when(step == last)
    def _():
        for k in range(CHUNKS):
            job.forward(k)
        job.finish()
        ring.finish()
        wide_ring.finish()


def attend(
    queries, keys, values, key0, value0, packed, first, share, more, count, bq=512, bk=1024
):
    length, width = queries.shape
    row = pl.BlockSpec((bq, 128), lambda p, i: (i, p))
    full = pl.BlockSpec((length, 128), lambda p, i: (0, p))
    zero = pl.BlockSpec((16, 128), lambda p, i: (0, p))
    return pl.pallas_call(
        functools.partial(attend_kernel, bk, first, count),
        grid=(width // 128, length // bq),
        in_specs=[row, full, full, zero, zero, ANY, ANY, ANY],
        out_specs=[row, row, ANY, ANY, ANY],
        out_shape=[shape_of((length, width), BF)] * 2
        + [
            shape_of((4 * packed.shape[0], 2 * width), BF),
            shape_of((count * share.shape[0], share.shape[1]), BF),
            shape_of((count * more.shape[0], more.shape[1]), BF),
        ],
        scratch_shapes=[pltpu.VMEM((length, 256), BF)]
        + gather_scratch(packed.shape[0], 2 * width)
        + ring_scratch(*share.shape, count // 2)
        + ring_scratch(*more.shape, count // 2),
        compiler_params=local_params(collective_id=7, has_side_effects=True),
        cost_estimate=cost(16 * length * length * width, 10 * length * width),
        name="attend",
    )(queries, keys, values, key0, value0, packed, share, more)


def attend_back_kernel(
    bk, count, q_ref, aug_ref, o_ref, do_ref, k_ref, v_ref, k0_ref, v0_ref,
    cq_ref, uq_ref, lq_ref, ck_ref, uk_ref, lk_ref,
    x_ref, y_ref, t_ref, ac_ref, dq_ref, dk_ref, dv_ref, dk0_ref, dv0_ref, xh_ref,
    yo_ref, zo_ref,
    to_ref, xo0_ref, xo1_ref, kaug, vaug, kt, dka, dva, xs, xsem, *scratch,
):
    length = k_ref.shape[0]
    bq = q_ref.shape[0]
    step = pl.program_id(1)
    turn = pl.program_id(0) * pl.num_programs(1) + step
    job = Scatter(x_ref, xs, scratch[:8])
    late = Scatter(t_ref, to_ref, scratch[8:16])
    ring = RingSum(count, [y_ref], scratch[16:26])
    next_ring = RingSum(count, [xh_ref], scratch[26:])
    keep = pltpu.make_async_copy(xs, xh_ref, xsem)

    @pl.when(turn == 0)
    def _():
        greet([job.to_sib, job.to_far, ring.ahead, ring.behind])
        job.start()
        ring.start()

    @pl.when(turn == 1)
    def _():
        job.fold()
        job.local()
        late.start()

    for hop in range(1, ring.half):

        @pl.when(turn == min(1 + 2 * hop, 7))
        def _(hop=hop):
            ring.hop(hop)

        @pl.when(turn == min(8 + hop, 11))
        def _(hop=hop):
            next_ring.hop(hop)

    @pl.when(turn == 8)
    def _():
        job.land()
        keep.start()
        late.fold()
        late.local()
        keep.wait()
        next_ring.start()
        job.finish()
        ring.finish([yo_ref, zo_ref])

    @pl.when(step == 0)
    def _():
        lane = lanes((length, 128))
        ones = jnp.where((lane % HD) < 3, 1.0, 0.0).astype(BF)
        kaug[:, :128] = k_ref[...]
        kaug[:, 128:] = ones
        vaug[:, :128] = v_ref[...]
        vaug[:, 128:] = ones
        kt[...] = k_ref[...].astype(F32).T.astype(BF)
        dka[...] = jnp.zeros_like(dka)
        dva[...] = jnp.zeros_like(dva)
        dk0_ref[...] = jnp.zeros_like(dk0_ref)
        dv0_ref[...] = jnp.zeros_like(dv0_ref)

    queries = q_ref[...]
    grads = do_ref[...]
    aug = aug_ref[...]
    product = grads.astype(F32) * o_ref[...].astype(F32)
    lane = lanes((bq, 128))
    ones0 = jnp.where((lanes((16, 128)) % HD) < 3, 1.0, 0.0).astype(BF)
    key0 = jnp.concatenate([k0_ref[...], ones0], 1)
    value0 = jnp.concatenate([v0_ref[...], ones0], 1)
    row0 = lax.broadcasted_iota(jnp.int32, (16, bq), 0) == 0
    qa, da, qm, dm, dq = [], [], [], [], []
    for head in range(2):
        qm.append(half_mask(queries, head))
        dm.append(half_mask(grads, head))
        mine = (lane < HD) if head == 0 else (lane >= HD)
        inner = jnp.sum(jnp.where(mine, product, 0.0), axis=1, keepdims=True)
        qa.append(jnp.concatenate([qm[head], half_mask(aug, head)], 1))
        da.append(
            jnp.concatenate([dm[head], pieces(-inner, (bq, 128), HD * head).astype(BF)], 1)
        )
        prob0 = jnp.where(row0, jnp.exp2(dot(key0, qa[head], NT)), 0.0)
        ds0 = (prob0 * dot(value0, da[head], NT)).astype(BF)
        dv0_ref[...] += dot(prob0.astype(BF), dm[head], NN)
        dk0_ref[...] += dot(ds0, qm[head], NN)
        dq.append(dot(k0_ref[:, HD * head : HD * head + HD], ds0, TN))
    for block in range(length // bk):
        span = slice(block * bk, (block + 1) * bk)
        for head in range(2):
            probs = jnp.exp2(dot(kaug[span, :], qa[head], NT))
            ds = (probs * dot(vaug[span, :], da[head], NT)).astype(BF)
            dva[span, :] += dot(probs.astype(BF), dm[head], NN)
            dka[span, :] += dot(ds, qm[head], NN)
            dq[head] = dq[head] + dot(kt[HD * head : HD * head + HD, span], ds, NN)
    grad_q = jnp.concatenate(dq, 0).T * 0.125
    dq_ref[...] = rope(grad_q, cq_ref[...], -uq_ref[...], -lq_ref[...]).astype(BF)

    @pl.when(turn == pl.num_programs(0) * pl.num_programs(1) - 1)
    def _():
        late.land(ac_ref)
        late.finish()
        next_ring.finish([xo0_ref, xo1_ref])

    @pl.when(step == pl.num_programs(1) - 1)
    def _():
        grad_k = dka[...] * (1.0 / LOG2E)
        dk_ref[...] = rope(grad_k, ck_ref[...], -uk_ref[...], -lk_ref[...]).astype(BF)
        dv_ref[...] = dva[...].astype(BF)
        dk0_ref[...] = dk0_ref[...] * (1.0 / LOG2E)


def attend_back(
    queries, aug, mixed, grads, keys, values, key0, value0, tables, extra, more, term, after_cross, count,
    bq=512, bk=512,
):
    length, width = queries.shape
    row = pl.BlockSpec((bq, 128), lambda p, i: (i, p))
    full = pl.BlockSpec((length, 128), lambda p, i: (0, p))
    zero = pl.BlockSpec((16, 128), lambda p, i: (0, p))
    tq = pl.BlockSpec((bq, 128), lambda p, i: (i, 0))
    tk = pl.BlockSpec((length, 128), lambda p, i: (0, 0), pipeline_mode=pl.Buffered(1))
    own = more.shape[0] // count
    owned = pl.BlockSpec((own, more.shape[1] // 2), lambda p, i: (0, 0))
    wide, narrow = extra.shape[0] // 4, extra.shape[1]
    half_shape = (after_cross.shape[0], term.shape[1])
    share_spec = pl.BlockSpec(half_shape, lambda p, i: (0, 0))
    part = pl.BlockSpec((own, narrow // 2), lambda p, i: (0, 0))
    big = shape_of((length, width), BF)
    small = shape_of((16, width), F32)
    return pl.pallas_call(
        functools.partial(attend_back_kernel, bk, count),
        grid=(width // 128, length // bq),
        in_specs=[row, row, row, row, full, full, zero, zero, tq, tq, tq, tk, tk, tk, ANY, ANY, ANY,
            pl.BlockSpec(half_shape, lambda p, i: (0, 1), pipeline_mode=pl.Buffered(1)),
        ],
        out_specs=[row, full, full, zero, zero, ANY, owned, owned, share_spec, part, part],
        out_shape=[big, big, big, small, small]
        + [
            shape_of((wide, narrow), BF),
            shape_of((own, more.shape[1] // 2), F32),
            shape_of((own, more.shape[1] // 2), F32),
            shape_of(half_shape, BF),
            shape_of((own, narrow // 2), F32),
            shape_of((own, narrow // 2), F32),
        ],
        scratch_shapes=[pltpu.VMEM((length, 256), BF)] * 2
        + [pltpu.VMEM((128, length), BF)]
        + [pltpu.VMEM((length, 128), F32)] * 2
        + [
            pltpu.VMEM((wide, narrow), BF),
            pltpu.SemaphoreType.DMA(()),
        ]
        + scatter_scratch(wide, narrow)
        + scatter_scratch(*half_shape)
        + ring_sum_scratch(own, more.shape[1], count // 2, 1)
        + ring_sum_scratch(own, narrow, count // 2, 1),
        compiler_params=local_params(collective_id=8, has_side_effects=True),
        cost_estimate=cost(40 * length * length * width, 20 * length * width),
        name="attend_back",
    )(queries, aug, mixed, grads, keys, values, key0, value0, *tables, *tables, extra, more, term, after_cross)


def softmax_keys(scores, length):
    key = lax.broadcasted_iota(jnp.int32, scores.shape, 0)
    masked = jnp.where(key < length, scores, -1e9)
    exponent = jnp.exp2(masked - jnp.max(masked, axis=0, keepdims=True))
    return exponent * (1.0 / jnp.sum(exponent, axis=0, keepdims=True))


def two_heads(values):
    return jnp.concatenate([half_mask(values, 0), half_mask(values, 1)], 0)


def one_row(values):
    rows = values.shape[0] // 2
    lane = lanes((rows, 128))
    return jnp.where(lane < HD, values[:rows], values[rows:])


def cross_kernel(
    count, len_ref, f_ref, s_ref, g_ref, wq_ref, wo_ref, kv_ref, share_ref,
    as_ref, n2_ref, q_ref, m_ref, ac_ref, n3_ref, full_ref, mine, *scratch,
):
    job = Gather(mine, n3_ref, scratch[:4], here=True)
    ring = RingGather(count, share_ref, full_ref, scratch[4:])
    step = pl.program_id(0)
    groups, model, width = wq_ref.shape
    keys = kv_ref.shape[1] // 2

    @pl.when(step == 0)
    def _():
        greet([job.to_sib, job.to_far, ring.ahead, ring.behind])
        ring.start()

    after_self = f_ref[...].astype(F32) + s_ref[...]
    as_ref[...] = after_self
    unit, _ = norm_rows(after_self)
    normed = (unit * g_ref[1:2, :]).astype(BF)
    n2_ref[...] = normed
    rows = normed.shape[0]
    total = after_self
    for group in range(groups):
        queries = (dot(normed, wq_ref[group], NN) * (LOG2E / 8.0)).astype(BF)
        base = group * width
        q_ref[:, base : base + width] = queries
        for pair in range(width // 128):
            span = slice(128 * pair, 128 * pair + 128)
            scores = dot(kv_ref[group, :keys, span], two_heads(queries[:, span]), NT)
            probs = softmax_keys(scores, len_ref[0])
            m_ref[:, base + 128 * pair : base + 128 * pair + 128] = one_row(
                dot(probs.astype(BF), kv_ref[group, keys:, span], TN)
            ).astype(BF)
        total = total + dot(m_ref[:, base : base + width], wo_ref[group], NT)
    ac_ref[...] = total
    unit, _ = norm_rows(total)
    mine[pl.ds(pl.multiple_of(step * rows, rows), rows), :] = (unit * g_ref[2:3, :]).astype(BF)

    for turn in range(2):

        @pl.when(step == turn)
        def _(turn=turn):
            half = CHUNKS // 2
            for k in range(turn * half, turn * half + half):
                job.across[k].start()
                job.beside[k].start()
            if turn == 0:
                ring.place()
                ring.hop(1)

    @pl.when(step == 1)
    def _():
        job.store.start()
        for hop in range(2, ring.half):
            ring.hop(hop)
        for k in range(CHUNKS):
            job.forward(k)
        job.finish()
        ring.finish()


def cross_forward(plen, frames, summed, gains, weights, prompt_kv, share, count):
    own, model = frames.shape
    groups, _, both = weights.shape
    width = both // 2
    rows = own // 2
    block = pl.BlockSpec((rows, model), lambda i: (i, 0))
    gain = pl.BlockSpec(gains.shape, lambda i: (0, 0))
    once = pl.Buffered(1)
    return pl.pallas_call(
        functools.partial(cross_kernel, count),
        grid=(2,),
        in_specs=[
            pl.BlockSpec(memory_space=pltpu.SMEM),
            block,
            block,
            gain,
            pl.BlockSpec((groups, model, width), lambda i: (0, 0, 0), pipeline_mode=once),
            pl.BlockSpec((groups, model, width), lambda i: (0, 0, 1), pipeline_mode=once),
            pl.BlockSpec(prompt_kv.shape, lambda i: (0, 0, 0)),
            ANY,
        ],
        out_specs=[block] * 5 + [ANY, ANY],
        out_shape=[
            shape_of((own, model), F32),
            shape_of((own, model), BF),
            shape_of((own, model), BF),
            shape_of((own, model), BF),
            shape_of((own, model), F32),
            shape_of((4 * own, model), BF),
            shape_of((count * share.shape[0], share.shape[1]), BF),
        ],
        scratch_shapes=[pltpu.VMEM((own, model), BF)]
        + gather_scratch(16, 128)
        + ring_scratch(*share.shape, count // 2),
        compiler_params=local_params(collective_id=2, has_side_effects=True),
        cost_estimate=BUSY,
        name="cross_forward",
    )(plen, frames, summed, gains, weights, weights, prompt_kv, share)


def cross_back_kernel(
    len_ref, w_ref, go_ref, e_ref, ac_ref, as_ref, g_ref, q_ref, wq_ref, wo_ref, kv_ref, t_ref,
    cb_ref, dq_ref, c3_ref, c3b_ref, dkv_ref, dg_ref, bo_ref, dkv, hold, *scratch,
):
    groups, model, width = wq_ref.shape
    keys = kv_ref.shape[1] // 2
    job = Scatter(t_ref, bo_ref, scratch)
    step = pl.program_id(0)

    @pl.when(step == 0)
    def _():
        greet([job.to_sib, job.to_far])
        job.start()

    @pl.when(pl.program_id(0) == 0)
    def _():
        dkv[...] = jnp.zeros_like(dkv)
        dg_ref[...] = jnp.zeros_like(dg_ref)

    unit, spread = norm_rows(ac_ref[...])
    back, part = norm_back(e_ref[...], unit, spread, g_ref[2:3, :])
    dg_ref[2:3, :] += part
    carried = go_ref[...].astype(F32) * w_ref[0:1, 0:1] + back
    cross_back = carried.astype(BF)
    cb_ref[...] = cross_back
    rows = cross_back.shape[0]
    total = jnp.zeros((rows, model), F32)
    spot = pl.ds(pl.multiple_of(pl.program_id(0) * rows, rows), rows)
    hold[spot, :] = ac_ref[:, : hold.shape[1]]

    @pl.when(step == 0)
    def _():
        job.fold()
        job.local()

    for group in range(groups):
        grads = dot(cross_back, wo_ref[group], NN).astype(BF)
        base = group * width
        for pair in range(width // 128):
            span = slice(128 * pair, 128 * pair + 128)
            wide = slice(base + 128 * pair, base + 128 * pair + 128)
            queries = two_heads(q_ref[:, wide])
            masked = two_heads(grads[:, span])
            probs = softmax_keys(dot(kv_ref[group, :keys, span], queries, NT), len_ref[0])
            dprobs = dot(kv_ref[group, keys:, span], masked, NT)
            inner = jnp.sum(dprobs * probs, axis=0, keepdims=True)
            ds = (probs * (dprobs - inner)).astype(BF)
            dkv[group, :keys, span] += dot(ds, queries, NN) * (1.0 / LOG2E)
            dkv[group, keys:, span] += dot(probs.astype(BF), masked, NN)
            grad_q = one_row(dot(ds, kv_ref[group, :keys, span], TN))
            dq_ref[:, wide] = (grad_q * 0.125).astype(BF)
        total = total + dot(dq_ref[:, base : base + width], wq_ref[group], NT)
    unit, spread = norm_rows(as_ref[...])
    back, part = norm_back(total, unit, spread, g_ref[1:2, :])
    dg_ref[1:2, :] += part
    carried = carried + back
    c3_ref[...] = carried
    c3b_ref[...] = carried.astype(BF)

    @pl.when(pl.program_id(0) == pl.num_programs(0) - 1)
    def _():
        dkv_ref[...] = dkv[...].astype(BF)
        job.land(hold)
        job.finish()


def cross_backward(plen, weight, grad_out, summed, after_cross, after_self, gains, queries,
                   weights, prompt_kv, term):
    share, model = grad_out.shape
    groups, _, both = weights.shape
    width = both // 2
    rows = 256
    block = pl.BlockSpec((rows, model), lambda i: (i, 0))
    gain = pl.BlockSpec(gains.shape, lambda i: (0, 0))
    once = pl.Buffered(1)
    return pl.pallas_call(
        cross_back_kernel,
        grid=(share // rows,),
        in_specs=[
            pl.BlockSpec(memory_space=pltpu.SMEM),
            pl.BlockSpec(weight.shape, lambda i: (0, 0)),
            block,
            block,
            block,
            block,
            gain,
            block,
            pl.BlockSpec((groups, model, width), lambda i: (0, 0, 0), pipeline_mode=once),
            pl.BlockSpec((groups, model, width), lambda i: (0, 0, 1), pipeline_mode=once),
            pl.BlockSpec(prompt_kv.shape, lambda i: (0, 0, 0)),
            ANY,
        ],
        out_specs=[block] * 4
        + [pl.BlockSpec(prompt_kv.shape, lambda i: (0, 0, 0)), gain]
        + [pl.BlockSpec((share, term.shape[1]), lambda i: (0, 0))],
        out_shape=[
            shape_of((share, model), BF),
            shape_of((share, model), BF),
            shape_of((share, model), F32),
            shape_of((share, model), BF),
            shape_of(prompt_kv.shape, BF),
            shape_of(gains.shape, F32),
            shape_of((share, term.shape[1]), BF),
        ],
        scratch_shapes=[
            pltpu.VMEM(prompt_kv.shape, F32),
            pltpu.VMEM((share, term.shape[1]), F32),
        ]
        + scatter_scratch(share, term.shape[1]),
        compiler_params=local_params(collective_id=9, has_side_effects=True),
        cost_estimate=cost(4 * share * model * model, 4 * model * model + 24 * share * model),
        name="cross_backward",
    )(plen, weight, grad_out, summed, after_cross, after_self, gains, queries, weights, weights,
      prompt_kv, term)


def glu_kernel(scaled, parts, count, *refs):
    refs = list(refs)
    s_ref = None if scaled else refs.pop(0)
    n_ref, c_ref = refs[:2]
    weights, outs = refs[2 : 2 + count], refs[2 + count :]
    cot = c_ref[...]
    if not scaled:
        cot = (cot.astype(F32) * s_ref[0:1, 0:1]).astype(BF)
        outs[2][...] = cot
    h_ref, d_ref = outs[:2]
    normed = n_ref[...]
    piece = 256
    at = 0
    for index, low, size in parts:
        w_ref = weights[index]
        width = w_ref.shape[1] // 3
        for base in range(0, size, piece):
            spot = low + base
            gate = dot(normed, w_ref[:, spot : spot + piece], NN)
            up = dot(normed, w_ref[:, width + spot : width + spot + piece], NN)
            grads = dot(cot, w_ref[:, 2 * width + spot : 2 * width + spot + piece], NN)
            sig = 1.0 / (1.0 + jnp.exp(-gate))
            silu = gate * sig
            h_ref[:, at + base : at + base + piece] = (silu * up).astype(BF)
            grad_gate = grads * up * sig * (1.0 + gate * (1.0 - sig))
            spot = 2 * at + base
            d_ref[:, spot : spot + piece] = grad_gate.astype(BF)
            d_ref[:, size + spot : size + spot + piece] = (grads * silu).astype(BF)
        at += size


def glu_block(normed, cot, weights, parts, scale=None):
    length, model = normed.shape
    width = sum(size for _, _, size in parts)
    rows = 512
    block = pl.BlockSpec((rows, model), lambda i: (i, 0))
    first = scale is not None
    return pl.pallas_call(
        functools.partial(glu_kernel, not first, parts, len(weights)),
        grid=(length // rows,),
        in_specs=[pl.BlockSpec((8, 128), lambda i: (0, 0))] * first
        + [block, block]
        + [
            pl.BlockSpec(weight.shape, lambda i: (0, 0), pipeline_mode=pl.Buffered(1))
            for weight in weights
        ],
        out_specs=[
            pl.BlockSpec((rows, width), lambda i: (i, 0)),
            pl.BlockSpec((rows, 2 * width), lambda i: (i, 0)),
        ]
        + [block] * first,
        out_shape=[shape_of((length, width), BF), shape_of((length, 2 * width), BF)]
        + [shape_of((length, model), BF)] * first,
        compiler_params=local_params(),
        cost_estimate=cost(6 * length * model * width, 6 * length * model),
        name="glu_block_%d" % width,
    )(*([scale] if first else []), normed, cot, *weights)


def grads_kernel(plan, n_ref, c_ref, d_ref, h_ref, *outs):
    for out, spans in zip(outs, plan):
        base = 0
        for side, low, high in spans:
            left, right = (n_ref, d_ref) if side == 0 else (c_ref, h_ref)
            value = dot(left[...], right[:, low:high], TN)
            out[:, base : base + high - low] = value.astype(BF)
            base += high - low


def weight_grads(normed, cot, dgu, hidden, plan, tile=256):
    length, model = normed.shape
    widths = [sum(high - low for _, low, high in spans) for spans in plan]
    once = pl.Buffered(1)
    left = pl.BlockSpec((length, tile), lambda i: (0, i))
    return pl.pallas_call(
        functools.partial(grads_kernel, plan),
        grid=(model // tile,),
        in_specs=[left, left]
        + [pl.BlockSpec(right.shape, lambda i: (0, 0), pipeline_mode=once) for right in (dgu, hidden)],
        out_specs=[pl.BlockSpec((tile, wide), lambda i: (i, 0)) for wide in widths],
        out_shape=[shape_of((model, wide), BF) for wide in widths],
        compiler_params=local_params(),
        cost_estimate=cost(2 * length * model * sum(widths), 2 * length * (2 * model + sum(widths))),
        name="weight_grads_%d" % sum(widths),
    )(normed, cot, dgu, hidden)


def last_grads_kernel(plan, copies, count, n_ref, q_ref, k_ref, v_ref, nc_ref, k0_ref, v0_ref, *refs):
    sources, rest = refs[:count], refs[count:]
    passed, (o_ref, gate_ref, up_ref, down_ref), targets = (
        rest[: -4 - len(copies)],
        rest[-4 - len(copies) : len(rest) - len(copies)],
        rest[len(rest) - len(copies) :],
    )
    width = q_ref.shape[1]
    normed = n_ref[...]
    edge = nc_ref[...]
    o_ref[:, :width] = dot(normed, q_ref[...], TN).astype(BF)
    grad_k = dot(normed, k_ref[...], TN) + dot(edge, k0_ref[...].astype(BF), TN)
    o_ref[:, width : 2 * width] = grad_k.astype(BF)
    grad_v = dot(normed, v_ref[...], TN) + dot(edge, v0_ref[...].astype(BF), TN)
    o_ref[:, 2 * width :] = grad_v.astype(BF)

    @pl.when(pl.program_id(0) == 0)
    def _():
        for source, base, kind, low, size in plan:
            target = (gate_ref, up_ref, down_ref)[kind]
            target[:, low : low + size] = sources[source][:, base : base + size].astype(F32)

    @pl.when(pl.program_id(0) == 1)
    def _():
        for target, (dims, places) in zip(targets, copies):
            for index, from_row, rows, row, column in places:
                ref = passed[index]
                value = ref[from_row : from_row + rows, :]
                target[row : row + rows, column : column + ref.shape[1]] = value


def last_grads(normed, grads, edge, dk0, dv0, sources, plan, hidden, passed, copies, tile=256):
    length, model = normed.shape
    width = grads[0].shape[1]
    own = sources[0].shape[0]
    once = pl.Buffered(1)
    fixed = lambda i: (0, 0)

    def full(array):
        return pl.BlockSpec(array.shape, fixed, pipeline_mode=once)

    extra = [shape_of(dims, passed[places[0][0]].dtype) for dims, places in copies]
    return pl.pallas_call(
        functools.partial(last_grads_kernel, plan, copies, len(sources)),
        grid=(model // tile,),
        in_specs=[pl.BlockSpec((length, tile), lambda i: (0, i))]
        + [full(grad) for grad in grads]
        + [pl.BlockSpec((edge.shape[0], tile), lambda i: (0, i)), full(dk0), full(dv0)]
        + [full(source) for source in sources]
        + [full(array) for array in passed],
        out_specs=[pl.BlockSpec((tile, 3 * width), lambda i: (i, 0))]
        + [pl.BlockSpec((own, hidden), fixed)] * 3
        + [pl.BlockSpec(array.shape, fixed) for array in extra],
        out_shape=[shape_of((model, 3 * width), BF)]
        + [shape_of((own, hidden), F32)] * 3
        + extra,
        compiler_params=local_params(),
        cost_estimate=cost(6 * length * model * width, 2 * length * (model + 3 * width)),
        name="last_grads",
    )(normed, *grads, edge, dk0, dv0, *sources, *passed)


def owner_sum(term):
    return lax.psum_scatter(term, "dp", scatter_dimension=0, tiled=True)


def after(value, *others):
    return lax.optimization_barrier((value,) + others)[0]


GLU_PARTS = 3


def per_device(
    frames, cond_table, bucket_ids, prompt, prompt_len,
    attn_query, attn_key, attn_value, attn_out,
    cross_query, cross_key, cross_value, cross_out,
    glu_gate, glu_up, glu_down, first_gain, second_gain, third_gain, grad_out,
):
    groups = lax.axis_size("mp")
    count = lax.axis_size("dp")
    sequences = bucket_ids.shape[0]
    assert sequences == 1 and groups == 4
    share, model = frames.shape
    length = share * groups
    buckets = cond_table.shape[0]
    own_rows, width = attn_query.shape
    unit = glu_gate.shape[1] // GLU_PARTS
    context = prompt.shape[2]

    onehot = (bucket_ids[:, None] == jnp.arange(buckets)[None, :]).astype(F32)
    extra = jnp.concatenate(
        [
            first_gain[:, None],
            second_gain[:, None],
            third_gain[:, None],
            jnp.broadcast_to(onehot.astype(BF), (own_rows, buckets)),
            jnp.zeros((own_rows, 128 - 3 - buckets), BF),
        ],
        1,
    )
    packed = jnp.concatenate(
        [attn_query, attn_key, attn_value, extra, cross_query, cross_out, attn_out], 1
    )
    prompt_blocks = prompt.reshape(-1, count, context // count)
    blank = jnp.zeros_like(prompt_blocks)
    prompts = jnp.concatenate(
        [
            jnp.concatenate([prompt_blocks, blank], 2).reshape(-1, model),
            jnp.concatenate([blank, prompt_blocks], 2).reshape(-1, model),
        ],
        0,
    )
    prompt_share = jnp.concatenate([cross_key, cross_value], 0)
    glu_share = []
    for part in range(GLU_PARTS):
        span = slice(part * unit, (part + 1) * unit)
        glu_share.append(
            jnp.concatenate([glu_gate[:, span], glu_up[:, span], glu_down[:, span]], 1)
        )
    cond_row = jnp.pad(dot(onehot.astype(BF), cond_table, NN), ((0, 15), (0, 0)))
    hot = jnp.pad(onehot, ((0, 0), (3, 128 - 3 - buckets)))
    mark = jnp.pad(jnp.broadcast_to(onehot.T, (buckets, 128)), ((0, SMALL - buckets), (0, 0)))
    frames_all, grad_all, first = head_gather(frames, grad_out, packed, count)

    tables = rope_tables(length, 1.0)
    scale = sequences * count * own_rows / buckets
    (
        normed_one, queries, keys, values, gains, seq_weight, normed_cond, key0, value0,
    ) = qkv_project(frames_all, cond_row, hot, first, tables, width, scale)
    mixed, aug, cross_full, second, glu_first = attend(
        queries, keys, values, key0, value0, first, 3 * width + 128, prompt_share,
        glu_share[0], count,
    )
    cross_full = cross_full.reshape(groups, model, 2 * width)
    column = 5 * width + 128
    out_full = first[:, column : column + width]
    self_out, prompt_kv, glu_second = out_project(
        mixed, out_full, 0, prompts, second, glu_share[1], count
    )
    prompt_kv = prompt_kv.reshape(groups, prompts.shape[0], width)

    (
        after_self, normed_two, cross_q, cross_mixed, after_cross, normed_three, glu_third,
    ) = cross_forward(
        prompt_len, frames, self_out, gains, cross_full, prompt_kv, glu_share[2], count
    )
    glu_full = [glu_first, glu_second, glu_third]
    half = unit // 2
    parts = (((0, 0, half),), ((0, half, half), (1, 0, unit), (2, 0, unit)))
    h0, d0, cot_all = glu_block(normed_three, grad_all, glu_full[:1], parts[0], seq_weight)
    (pack0,) = weight_grads(normed_three, cot_all, d0, h0, (((0, 0, unit), (1, 0, half)),))
    h1, d1 = glu_block(after(normed_three, pack0), cot_all, glu_full, parts[1])
    wide = unit + 2 * unit
    pack1, pack2 = weight_grads(
        normed_three, cot_all, d1, h1,
        (
            (
                (0, 0, unit), (1, 0, half),
                (0, unit, wide), (1, half, half + unit),
                (0, wide, wide + half), (0, wide + unit, wide + unit + half),
                (1, half + unit, 2 * unit),
            ),
            (
                (0, wide + half, wide + unit), (0, wide + unit + half, wide + 2 * unit),
                (1, 2 * unit, 2 * unit + half),
            ),
        ),
    )
    glu_sum0 = owner_sum(pack0)
    pack1 = after(pack1, glu_sum0)
    glu_sum1 = owner_sum(pack1)
    back_term, out_term0, out_term1 = glu_back(
        [after(d0, pack1), d1], [h0, h1], glu_full, parts
    )

    cross_back, grad_cq, carried, carried_low, grad_kv, grad_gains, block0 = cross_backward(
        prompt_len, seq_weight, grad_out, back_term, after_cross, after_self, gains, cross_q,
        cross_full, prompt_kv, out_term0,
    )
    cross_term, grad_mixed, second_pack, glu_sum2 = mid_gather(
        carried_low, grad_kv.reshape(-1, width), normed_two, cross_back, grad_cq, cross_mixed,
        out_full, 0, mixed, prompts, pack2, groups, count,
    )
    (
        dq, dk, dv, dk0, dv0, _, grad_out_own, grad_prompt, block1, grad_cross_q, grad_cross_o,
    ) = attend_back(
        queries, aug, mixed, grad_mixed, keys, values, key0, value0, tables, cross_term,
        second_pack, out_term1, after_cross, count,
    )
    plan = []
    pieces_of = (
        (0, 0, 0, half), (1, 0, half, half), (1, 3 * half, unit, unit),
        (1, 9 * half, 2 * unit, half), (2, 0, 2 * unit + half, half),
    )
    for source, base, low, size in pieces_of:
        for kind in range(3):
            plan.append((source, base + kind * size, kind, low, size))
    short = context // count
    copies = (
        ((share, model), ((0, 0, share, 0, 0), (1, 0, share, 0, model // 2))),
        ((own_rows, width), ((2, 0, own_rows, 0, 0),)),
        ((own_rows, width), ((3, 0, own_rows, 0, 0),)),
        ((short, width), ((4, 0, short, 0, 0),)),
        ((short, width), ((4, short, short, 0, 0),)),
        ((own_rows, width), ((5, 0, own_rows, 0, 0),)),
    )
    (
        first_pack, *glu_out, block_out, grad_out_own, grad_cross_q, grad_cross_k, grad_cross_v,
        grad_cross_o,
    ) = last_grads(
        normed_one, [dq, dk, dv], normed_cond, dk0, dv0, [glu_sum0, glu_sum1, glu_sum2], plan,
        glu_gate.shape[1],
        [block0, block1, grad_out_own, grad_cross_q, grad_prompt, grad_cross_o], copies,
    )
    frames_grad, sums, *first_grads = tail_sums(
        count, buckets, [dq, dk, dv], first, first_pack, frames, carried, gains, grad_gains, mark,
        cond_row, dk0, dv0,
    )
    return (
        block_out,
        frames_grad,
        sums[:buckets],
        *first_grads,
        grad_out_own,
        grad_cross_q,
        grad_cross_k,
        grad_cross_v,
        grad_cross_o,
        *glu_out,
        sums[buckets],
        sums[buckets + 1],
        sums[buckets + 2],
    )


def solution(mesh):
    both = P(("dp", "mp"), None)
    weight = P("dp", "mp")
    return jax.shard_map(
        per_device,
        mesh=mesh,
        in_specs=(both, P(), P("dp"), P("dp", None, None), P("dp"))
        + (weight,) * 11
        + (P("dp"),) * 3
        + (both,),
        out_specs=(both, both, P()) + (weight,) * 11 + (P(),) * 3,
        check_vma=False,
    )
```

```python
import functools

import jax
import jax.numpy as jnp
import numpy as np
from jax import lax
from jax.experimental import pallas as pl
from jax.experimental.pallas import tpu as pltpu
from jax.sharding import PartitionSpec as P

HD = 64
ROT = 32
LOG2E = 1.4426950408889634
EPS = 1e-05
MESH = pl.DeviceIdType.MESH
NT = (((1,), (1,)), ((), ()))
TN = (((0,), (0,)), ((), ()))
NN = (((1,), (0,)), ((), ()))
BF = jnp.bfloat16
F32 = jnp.float32
ANY = pl.BlockSpec(memory_space=pl.ANY)
VM = 58 << 20


def shape_of(dims, dtype):
    return jax.ShapeDtypeStruct(dims, dtype)


def dot(left, right, dims):
    return lax.dot_general(left, right, dims, preferred_element_type=F32)


def local_params(**extra):
    return pltpu.CompilerParams(vmem_limit_bytes=VM, **extra)


def cost(flops, nbytes, trans=0):
    return pl.CostEstimate(flops=int(flops), bytes_accessed=int(nbytes), transcendentals=int(trans))


def norm_rows(values):
    center = values - jnp.mean(values, -1, keepdims=True)
    spread = lax.rsqrt(jnp.mean(center * center, -1, keepdims=True) + EPS)
    return center * spread, spread


def norm_back(grad_rows, unit_rows, spread, gain_row):
    scaled = grad_rows * gain_row
    result = spread * (
        scaled
        - jnp.mean(scaled, -1, keepdims=True)
        - unit_rows * jnp.mean(scaled * unit_rows, -1, keepdims=True)
    )
    return result, jnp.sum(grad_rows * unit_rows, 0, keepdims=True)


def rope_tables(length, offset):
    lane = np.arange(2 * HD) % HD
    half = ROT // 2
    frequency = np.power(10000.0, -2.0 * (lane % half) / ROT)
    angles = (offset + np.arange(length))[:, None] * frequency[None, :]
    cosine = np.where(lane[None] < ROT, np.cos(angles), 1.0)
    sine = np.sin(angles)
    upper = np.where((lane[None] >= half) & (lane[None] < ROT), sine, 0.0)
    lower = np.where(lane[None] < half, -sine, 0.0)
    return [jnp.asarray(table.astype(np.float32)) for table in (cosine, upper, lower)]


def rope(values, cosine, upper, lower):
    half = ROT // 2
    return (
        values * cosine
        + pltpu.roll(values, half, 1) * upper
        + pltpu.roll(values, 2 * HD - half, 1) * lower
    )


def bucket_column(hot, rows):
    dims = (rows, 128)
    pick = lax.broadcasted_iota(jnp.int32, dims, 0) + 3 == lanes(dims)
    marks = jnp.broadcast_to(hot, (8, 128)).astype(BF)
    return dot(jnp.where(pick, 1.0, 0.0).astype(BF), marks, NT)[:, 0:1]


def bucket_row(hot, table):
    rows = table.shape[0]
    return jnp.sum(table.astype(F32) * bucket_column(hot, rows), axis=0, keepdims=True)


def lanes(dims):
    return lax.broadcasted_iota(jnp.int32, dims, 1)


def half_mask(values, head):
    lane = lanes(values.shape)
    keep = (lane < HD) if head == 0 else (lane >= HD)
    return jnp.where(keep, values, jnp.zeros_like(values))


def pieces(column, dims, base):
    high = column.astype(BF).astype(F32)
    rest = column - high
    middle = rest.astype(BF).astype(F32)
    low = rest - middle
    lane = lanes(dims)
    return jnp.where(
        lane == base,
        high,
        jnp.where(lane == base + 1, middle, jnp.where(lane == base + 2, low, 0.0)),
    )


def mp_peers():
    me = lax.axis_index("mp")
    chip, core = me // 2, me % 2
    return me, chip * 2 + (1 - core), (1 - chip) * 2 + core, (1 - chip) * 2 + (1 - core)


def greet(devices):
    barrier = pltpu.get_barrier_semaphore()
    for device in devices:
        pl.semaphore_signal(barrier, inc=1, device_id=device, device_id_type=MESH)
    pl.semaphore_wait(barrier, len(devices))


def remote(source, target, send, recv, device):
    return pltpu.make_async_remote_copy(
        source, target, send, recv, device_id=device, device_id_type=MESH
    )


CHUNKS = 4
CUTS = 2


def column_cuts(width):
    first = 128 * ((width // 128 + 1) // 2)
    return [pl.ds(0, first), pl.ds(first, width - first)]


BUSY = cost(1, 140 << 20)


def gather_scratch(rows, width):
    return [
        pltpu.VMEM((rows, width), BF),
        pltpu.SemaphoreType.DMA((2,)),
        pltpu.SemaphoreType.DMA((3, CHUNKS)),
        pltpu.SemaphoreType.DMA((3, CHUNKS)),
    ]


class Gather:
    def __init__(self, x_ref, o_ref, sems, columns=None, here=False):
        bounce, lsem, ssem, rsem = sems
        if here:
            bounce = x_ref
        self.me, self.sib, self.far, _ = mp_peers()
        dp = lax.axis_index("dp")
        self.to_sib = {"dp": dp, "mp": self.sib}
        self.to_far = {"dp": dp, "mp": self.far}
        rows = x_ref.shape[0]
        part = rows // CHUNKS

        def slot(i, k):
            return o_ref.at[pl.ds(pl.multiple_of(i * rows + k * part, part), part)]

        def source(first, size):
            if columns is None:
                return x_ref.at[pl.ds(first, size)]
            return x_ref.at[pl.ds(first, size), columns]

        self.load = None if here else pltpu.make_async_copy(source(0, rows), bounce, lsem.at[0])
        self.store = pltpu.make_async_copy(
            bounce, o_ref.at[pl.ds(pl.multiple_of(self.me * rows, rows), rows)], lsem.at[1]
        )
        self.across = []
        self.beside = []
        self.onward = []
        for k in range(CHUNKS):
            mine = source(k * part, part)
            self.across.append(
                remote(mine, slot(self.me, k), ssem.at[0, k], rsem.at[0, k], self.to_far)
            )
            self.beside.append(
                remote(mine, slot(self.me, k), ssem.at[1, k], rsem.at[1, k], self.to_sib)
            )
            self.onward.append(
                remote(
                    slot(self.far, k), slot(self.far, k), ssem.at[2, k], rsem.at[2, k], self.to_sib
                )
            )

    def start(self):
        for copy in self.across:
            copy.start()
        if self.load is not None:
            self.load.start()
        for copy in self.beside:
            copy.start()
        if self.load is not None:
            self.load.wait()
        self.store.start()

    def forward(self, k):
        self.across[k].wait_recv()
        self.onward[k].start()

    def finish(self):
        for k in range(CHUNKS):
            self.beside[k].wait_recv()
            self.onward[k].wait_recv()
        for k in range(CHUNKS):
            self.across[k].wait_send()
            self.beside[k].wait_send()
            self.onward[k].wait_send()
        self.store.wait()


def scatter_scratch(rows, width):
    return [pltpu.VMEM((2, rows, width), BF)] + [pltpu.VMEM((rows, width), BF)] * 4 + [
        pltpu.SemaphoreType.DMA((2,)),
        pltpu.SemaphoreType.DMA((3, CHUNKS)),
        pltpu.SemaphoreType.DMA((3, CHUNKS)),
    ]


class Scatter:
    def __init__(self, x_ref, o_ref, scratch):
        mine, ra, rb, rc, sb, lsem, ssem, rsem = scratch
        me, sib, far, diag = mp_peers()
        dp = lax.axis_index("dp")
        self.to_sib = {"dp": dp, "mp": sib}
        self.to_far = {"dp": dp, "mp": far}
        self.o_ref, self.mine, self.ra, self.rb, self.rc, self.sb = o_ref, mine, ra, rb, rc, sb
        rows = ra.shape[0]
        part = rows // CHUNKS
        self.spans = [pl.ds(k * part, part) for k in range(CHUNKS)]

        def slot(i, k):
            return x_ref.at[pl.ds(pl.multiple_of(i * rows + k * part, part), part)]

        def whole(i):
            return x_ref.at[pl.ds(pl.multiple_of(i * rows, rows), rows)]

        self.first, self.second, self.third = [], [], []
        for k, span in enumerate(self.spans):
            self.first.append(
                remote(slot(diag, k), ra.at[span], ssem.at[0, k], rsem.at[0, k], self.to_sib)
            )
            self.second.append(
                remote(slot(sib, k), rb.at[span], ssem.at[1, k], rsem.at[1, k], self.to_sib)
            )
            self.third.append(
                remote(sb.at[span], rc.at[span], ssem.at[2, k], rsem.at[2, k], self.to_far)
            )
        self.load0 = pltpu.make_async_copy(whole(far), mine.at[0], lsem.at[0])
        self.load1 = pltpu.make_async_copy(whole(me), mine.at[1], lsem.at[1])

    def start(self):
        self.load0.start()
        for copy in self.first:
            copy.start()
        self.load1.start()
        for copy in self.second:
            copy.start()

    def fold(self):
        self.load0.wait()
        for k, span in enumerate(self.spans):
            self.first[k].wait_recv()
            total = self.mine[0, span, :].astype(F32) + self.ra[span, :].astype(F32)
            self.sb[span, :] = total.astype(BF)
            self.third[k].start()

    def local(self):
        self.load1.wait()
        for k in range(CHUNKS):
            self.second[k].wait_recv()

    def land(self, addend=None):
        for k, span in enumerate(self.spans):
            self.third[k].wait_recv()
            total = self.mine[1, span, :].astype(F32) + self.rb[span, :].astype(F32)
            if addend is not None:
                total = total + addend[span, :]
            self.o_ref[span, :] = (total + self.rc[span, :].astype(F32)).astype(self.o_ref.dtype)

    def finish(self):
        for k in range(CHUNKS):
            self.first[k].wait_send()
            self.second[k].wait_send()
            self.third[k].wait_send()


def sum_scratch(rows, width):
    return [pltpu.VMEM((4, rows, width), BF)] + [pltpu.VMEM((rows, width), BF)] * 4 + [
        pltpu.SemaphoreType.DMA((3, CHUNKS)),
        pltpu.SemaphoreType.DMA((3, CHUNKS)),
    ]


class LocalSum:
    def __init__(self, o_ref, scratch):
        terms, ra, rb, rc, sb, ssem, rsem = scratch
        _, sib, far, _ = mp_peers()
        dp = lax.axis_index("dp")
        self.to_sib = {"dp": dp, "mp": sib}
        self.to_far = {"dp": dp, "mp": far}
        self.o_ref, self.terms, self.ra, self.rb, self.rc, self.sb = o_ref, terms, ra, rb, rc, sb
        rows = ra.shape[0]
        part = rows // CHUNKS
        self.spans = [pl.ds(k * part, part) for k in range(CHUNKS)]
        self.first, self.second, self.third = [], [], []
        for k, span in enumerate(self.spans):
            self.first.append(
                remote(terms.at[0, span], ra.at[span], ssem.at[0, k], rsem.at[0, k], self.to_sib)
            )
            self.second.append(
                remote(terms.at[2, span], rb.at[span], ssem.at[1, k], rsem.at[1, k], self.to_sib)
            )
            self.third.append(
                remote(sb.at[span], rc.at[span], ssem.at[2, k], rsem.at[2, k], self.to_far)
            )

    def put(self, step, value):
        half = value.shape[0]
        late = step // 4
        slot = (1 - late) * (step % 2) + late * (step // 2)
        row = (1 - late) * ((step // 2) % 2) + late * (step % 2)
        self.terms[slot, pl.ds(pl.multiple_of(row * half, half), half), :] = value

    def after_step(self, step):
        half = CHUNKS // 2
        for turn in range(2):
            chunks = range(turn * half, turn * half + half)

            @pl.when(step == 2 * turn)
            def _(chunks=chunks):
                for k in chunks:
                    self.first[k].start()

            @pl.when(step == 2 * turn + 1)
            def _(chunks=chunks):
                for k in chunks:
                    span = self.spans[k]
                    self.first[k].wait_recv()
                    total = self.terms[1, span, :].astype(F32) + self.ra[span, :].astype(F32)
                    self.sb[span, :] = total.astype(BF)
                    self.third[k].start()

        @pl.when(step == 5)
        def _():
            for copy in self.second:
                copy.start()

    def land(self):
        for k, span in enumerate(self.spans):
            self.second[k].wait_recv()
            self.third[k].wait_recv()
            total = self.terms[3, span, :].astype(F32) + self.rb[span, :].astype(F32)
            self.o_ref[span, :] = (total + self.rc[span, :].astype(F32)).astype(self.o_ref.dtype)

    def finish(self):
        for copy in self.first + self.second + self.third:
            copy.wait_send()


def order_block(step):
    me = lax.axis_index("mp")
    chip, core = me // 2, me % 2
    late = step // 4
    other = 1 - late
    cross = 1 - ((1 - late) * (step % 2) + late * ((step // 2) % 2))
    quarter = (chip + other - 2 * chip * other) * 2 + (core + cross - 2 * core * cross)
    return quarter * 2 + (1 - late) * ((step // 2) % 2) + late * (step % 2)


def arrival_quarter(turn):
    me = lax.axis_index("mp")
    chip, core = me // 2, me % 2
    other = turn // 2
    cross = turn % 2
    return (chip + other - 2 * chip * other) * 2 + (core + cross - 2 * core * cross)


class Ring:
    def __init__(self, count):
        self.count = count
        self.half = count // 2
        me = lax.axis_index("dp")
        mp = lax.axis_index("mp")
        odd = me % 2
        self.me = me
        self.spot = (1 - odd) * (me // 2) + odd * (count - 1 - me // 2)
        self.ahead = {"dp": self.at(1), "mp": mp}
        self.behind = {"dp": self.at(-1), "mp": mp}

    def at(self, distance):
        spot = (self.spot + distance + self.count) % self.count
        late = spot // self.half
        return (1 - late) * 2 * spot + late * (2 * (self.count - 1 - spot) + 1)


def ring_scratch(rows, width, half):
    return [pltpu.VMEM((rows, width), BF), pltpu.SemaphoreType.DMA((2,))] + [
        pltpu.SemaphoreType.DMA((half, CUTS))
    ] * 4


class RingGather:
    def __init__(self, count, w_ref, o_ref, scratch, here=False):
        bounce, lsem, fs, fr, bs, br = scratch
        if here:
            bounce = w_ref
        ring = Ring(count)
        self.ahead, self.behind, self.half = ring.ahead, ring.behind, ring.half
        rows = w_ref.shape[0]

        spans = column_cuts(w_ref.shape[1])

        def slot(i):
            return o_ref.at[pl.ds(pl.multiple_of(i * rows, rows), rows)]

        last = self.half - 1

        def copies(block, hop, send, recv, device, only):
            result = {}
            for c, columns in enumerate(spans):
                if hop < last or c == only:
                    place = o_ref.at[pl.ds(pl.multiple_of(block * rows, rows), rows), columns]
                    source = w_ref.at[:, columns] if hop == 0 else place
                    result[c] = remote(source, place, send.at[hop, c], recv.at[hop, c], device)
            return result

        self.forward = []
        self.backward = []
        for hop in range(self.half):
            self.forward.append(copies(ring.at(-hop), hop, fs, fr, ring.ahead, 0))
            self.backward.append(copies(ring.at(hop), hop, bs, br, ring.behind, 1))
        self.load = None if here else pltpu.make_async_copy(w_ref, bounce, lsem.at[0])
        self.store = pltpu.make_async_copy(bounce, slot(ring.me), lsem.at[1])

    def start(self):
        for c in range(CUTS):
            self.forward[0][c].start()
            self.backward[0][c].start()
        if self.load is not None:
            self.load.start()

    def place(self):
        if self.load is not None:
            self.load.wait()
        self.store.start()

    def hop(self, hop):
        for c in range(CUTS):
            for way in (self.forward, self.backward):
                way[hop - 1][c].wait_recv()
                if c in way[hop]:
                    way[hop][c].start()

    def finish(self):
        self.forward[-1][0].wait_recv()
        self.backward[-1][1].wait_recv()
        self.store.wait()
        for copies in self.forward + self.backward:
            for copy in copies.values():
                copy.wait_send()


def ring_sum_scratch(rows, wide, half, sources):
    slots = pltpu.VMEM((half, rows, wide), BF)
    hops = pltpu.SemaphoreType.DMA((half, CUTS))
    return (
        [slots] * 4
        + [pltpu.VMEM((rows, wide), BF), pltpu.SemaphoreType.DMA((2 * half + 1, sources))]
        + [hops] * 4
    )


class RingSum:
    def __init__(self, count, sources, scratch):
        self.lf, self.lb, self.rf, self.rb, self.own, lsem, fs, fr, bs, br = scratch
        ring = Ring(count)
        self.ahead, self.behind, self.half = ring.ahead, ring.behind, ring.half
        rows = self.own.shape[0]
        self.spans = column_cuts(self.own.shape[1])

        def sends(source, target, hop, send, recv, device, only):
            return {
                c: remote(
                    source.at[hop, :, span],
                    target.at[hop, :, span],
                    send.at[hop, c],
                    recv.at[hop, c],
                    device,
                )
                for c, span in enumerate(self.spans)
                if hop > 0 or c == only
            }

        def loads(block, target, at):
            span = pl.ds(pl.multiple_of(block * rows, rows), rows)
            base, copies = 0, []
            for i, source in enumerate(sources):
                wide = source.shape[1]
                copies.append(
                    pltpu.make_async_copy(
                        source.at[span], target.at[:, pl.ds(base, wide)], lsem.at[at, i]
                    )
                )
                base += wide
            return copies

        self.forward, self.backward, self.local = [], [], []
        for hop in range(self.half):
            self.local.append(
                loads(ring.at(self.half - hop), self.lf.at[hop], 2 * hop)
                + loads(ring.at(hop - self.half), self.lb.at[hop], 2 * hop + 1)
            )
            self.forward.append(sends(self.lf, self.rf, hop, fs, fr, ring.ahead, 0))
            self.backward.append(sends(self.lb, self.rb, hop, bs, br, ring.behind, 1))
        self.local.append(loads(ring.me, self.own, 2 * self.half))

    def start(self):
        for copies in self.local:
            for copy in copies:
                copy.start()
        for copy in self.local[0]:
            copy.wait()
        self.forward[0][0].start()
        self.backward[0][1].start()
        for copy in self.local[1]:
            copy.wait()
        self.forward[1][1].start()
        self.backward[1][0].start()

    def hop(self, hop):
        if hop > 1:
            for copy in self.local[hop]:
                copy.wait()
        for c, span in enumerate(self.spans):
            for way, mine, came in (
                (self.forward, self.lf, self.rf),
                (self.backward, self.lb, self.rb),
            ):
                if c in way[hop - 1]:
                    way[hop - 1][c].wait_recv()
                    total = mine[hop, :, span].astype(F32) + came[hop - 1, :, span].astype(F32)
                    mine[hop, :, span] = total.astype(BF)
                    way[hop][c].start()

    def finish(self, outs):
        last = self.half - 1
        for copy in self.local[self.half]:
            copy.wait()
        for c in range(CUTS):
            self.forward[last][c].wait_recv()
            self.backward[last][c].wait_recv()
        base = 0
        for out in outs:
            span = slice(base, base + out.shape[1])
            base += out.shape[1]
            out[...] = (
                self.own[:, span].astype(F32)
                + self.rf[last, :, span].astype(F32)
                + self.rb[last, :, span].astype(F32)
            )
        for copies in self.forward + self.backward:
            for copy in copies.values():
                copy.wait_send()


HEAD = 6


def head_kernel(count, f_ref, g_ref, gains_ref, hot_ref, *refs):
    mats, glu = refs[:HEAD], refs[HEAD : HEAD + 3]
    fo_ref, go_ref, wo_ref = refs[HEAD + 3 : HEAD + 6]
    shares = refs[HEAD + 6 : HEAD + 9]
    scratch = refs[HEAD + 9 :]
    pack, held, psem, hsem, osem = scratch[:5]
    job = Gather(f_ref, fo_ref, scratch[5:9])
    late = Gather(g_ref, go_ref, scratch[9:13])
    ring = RingGather(count, pack, wo_ref, scratch[13:], here=True)
    width = mats[0].shape[1]
    side = 4 * width
    loads = []
    for i, mat in enumerate(mats):
        base = i * width if i < 4 else i * width + 128
        loads.append(pltpu.make_async_copy(mat, pack.at[:, pl.ds(base, width)], psem.at[i]))
    fetch = [pltpu.make_async_copy(mat, held.at[i], hsem.at[i]) for i, mat in enumerate(glu)]
    unit = held.shape[2] // len(shares)
    stores = []
    for at, share in enumerate(shares):
        for i in range(3):
            stores.append(
                pltpu.make_async_copy(
                    held.at[i, :, pl.ds(at * unit, unit)],
                    share.at[:, pl.ds(i * unit, unit)],
                    osem.at[at, i],
                )
            )
    for copy in loads + fetch:
        copy.start()
    greet([job.to_sib, job.to_far, ring.ahead, ring.behind])
    job.start()
    dims = (8, 128)
    pick = lax.broadcasted_iota(jnp.int32, dims, 0) == lanes(dims)
    columns = dot(gains_ref[...], jnp.where(pick, 1.0, 0.0).astype(BF), TN)
    pack[:, side : side + 128] = (columns + hot_ref[...]).astype(BF)
    for copy in loads:
        copy.wait()
    ring.start()
    ring.place()
    for copy in fetch:
        copy.wait()
    for copy in stores:
        copy.start()
    ring.hop(1)
    for k in range(CHUNKS):
        job.forward(k)
    late.start()
    for hop in range(2, ring.half):
        ring.hop(hop)
    for k in range(CHUNKS):
        late.forward(k)
    job.finish()
    late.finish()
    ring.finish()
    for copy in stores:
        copy.wait()


def head_gather(frames, grads, gains, hot, mats, glu, parts, count):
    rows, width = frames.shape
    own = mats[0].shape[0]
    columns = len(mats) * mats[0].shape[1] + 128
    hidden = glu[0].shape[1]
    wide = shape_of((4 * rows, width), BF)
    vmem = pl.BlockSpec(memory_space=pltpu.VMEM)
    return pl.pallas_call(
        functools.partial(head_kernel, count),
        out_shape=(wide, wide, shape_of((count * own, columns), BF))
        + (shape_of((own, 3 * hidden // parts), BF),) * parts,
        in_specs=[ANY, ANY, vmem, vmem] + [ANY] * (len(mats) + 3),
        out_specs=(ANY,) * (3 + parts),
        scratch_shapes=[
            pltpu.VMEM((own, columns), BF),
            pltpu.VMEM((3, own, hidden), BF),
            pltpu.SemaphoreType.DMA((len(mats),)),
            pltpu.SemaphoreType.DMA((3,)),
            pltpu.SemaphoreType.DMA((parts, 3)),
        ]
        + gather_scratch(rows, width) * 2
        + ring_scratch(16, 128, count // 2),
        compiler_params=local_params(collective_id=0, has_side_effects=True),
        cost_estimate=BUSY,
        name="head_gather",
    )(frames, grads, gains, hot, *mats, *glu)


SMALL = 16


def tail_kernel(
    count, buckets, q_ref, k_ref, v_ref, wq_ref, wk_ref, wv_ref,
    a_ref, f_ref, c_ref, g_ref, dg_ref, hot_ref, r_ref, k0_ref, v0_ref,
    o_ref, s_ref, w_ref, *scratch,
):
    total, held = scratch[0:2]
    job = LocalSum(total, scratch[2:9])
    ring = RingSum(count, [a_ref], scratch[9:19])
    sent, got, ss, rs = scratch[19:]
    step = pl.program_id(0)
    me = lax.axis_index("dp")
    mp = lax.axis_index("mp")
    partners = [job.to_sib, job.to_far]
    bit = 1
    while bit < count:
        partners.append({"dp": me + bit * (1 - 2 * ((me // bit) % 2)), "mp": mp})
        bit *= 2
    @pl.when(step == 0)
    def _():
        greet(partners + [ring.ahead, ring.behind])
        ring.start()

    @pl.when(step < 8)
    def _():
        term = (
            dot(q_ref[...], wq_ref[...], NT)
            + dot(k_ref[...], wk_ref[...], NT)
            + dot(v_ref[...], wv_ref[...], NT)
        )
        job.put(step, term.astype(BF))

    job.after_step(step)

    @pl.when(step == 8)
    def _():
        edge = dot(k0_ref[...].astype(BF), wk_ref[...], NT) + dot(
            v0_ref[...].astype(BF), wv_ref[...], NT
        )
        unit, spread = norm_rows(bucket_row(hot_ref[...], r_ref[...]))
        edge_back, edge_part = norm_back(edge[0:1, :], unit, spread, g_ref[0:1, :])
        place = lax.broadcasted_iota(jnp.int32, held.shape, 0)
        held[...] = (
            bucket_column(hot_ref[...], SMALL) * edge_back
            + jnp.where(place == buckets, edge_part, 0.0)
            + jnp.where(place == buckets + 1, dg_ref[1:2, :], 0.0)
            + jnp.where(place == buckets + 2, dg_ref[2:3, :], 0.0)
        )
        for hop in range(1, ring.half - 1):
            ring.hop(hop)
        job.land()
        unit, spread = norm_rows(f_ref[...].astype(F32))
        back, part = norm_back(total[...], unit, spread, g_ref[0:1, :])
        held[buckets : buckets + 1, :] += part
        copies = [
            remote(sent.at[i], got.at[i], ss.at[i], rs.at[i], partner)
            for i, partner in enumerate(partners)
        ]
        sent[0] = held[...]
        copies[0].start()
        ring.hop(ring.half - 1)
        o_ref[...] = c_ref[...] + back
        for i, copy in enumerate(copies):
            copy.wait_recv()
            held[...] += got[i]
            if i + 1 < len(copies):
                sent[i + 1] = held[...]
                copies[i + 1].start()
        for copy in copies:
            copy.wait_send()
        s_ref[...] = held[...]
        ring.finish([w_ref])
        job.finish()


def tail_sums(
    count, buckets, grads_qkv, weights, grads, frames, carried, gains, grad_gains, hot,
    table_rows, dk0, dv0,
):
    share, model = frames.shape
    width = grads_qkv[0].shape[1]
    block = 2 * share // 4
    rows = grads.shape[0] // count
    wide = grads.shape[1]
    half = count // 2
    steps = 2 + (count - 1).bit_length()
    once = pl.Buffered(1)

    def full(array):
        return pl.BlockSpec(array.shape, lambda i: (0,) * array.ndim, pipeline_mode=once)

    small = pltpu.VMEM((steps, SMALL, model), F32)
    out_shape = (
        shape_of((share, model), F32),
        shape_of((SMALL, model), F32),
        shape_of((rows, wide), F32),
    )
    whole = [frames, carried, gains, grad_gains, hot, table_rows, dk0, dv0]
    return pl.pallas_call(
        functools.partial(tail_kernel, count, buckets),
        grid=(9,),
        out_shape=out_shape,
        in_specs=[
            pl.BlockSpec((block, width), lambda i: (order_block(jnp.minimum(i, 7)), 0))
            for _ in range(3)
        ]
        + [
            pl.BlockSpec(
                (model, width), functools.partial(lambda at, i: (0, at), at), pipeline_mode=once
            )
            for at in range(3)
        ]
        + [ANY]
        + [full(array) for array in whole],
        out_specs=tuple(pl.BlockSpec(out.shape, lambda i: (0, 0)) for out in out_shape),
        scratch_shapes=[pltpu.VMEM((share, model), F32), pltpu.VMEM((SMALL, model), F32)]
        + sum_scratch(share, model)
        + ring_sum_scratch(rows, wide, half, 1)
        + [small, small, pltpu.SemaphoreType.DMA((steps,)), pltpu.SemaphoreType.DMA((steps,))],
        compiler_params=local_params(collective_id=6, has_side_effects=True),
        cost_estimate=BUSY,
        name="tail_sums",
    )(*grads_qkv, weights, weights, weights, grads, *whole)


def out_kernel(
    count, m_ref, w_ref, p_ref, wp_ref, share_ref, o_ref, kvo_ref, full_ref, mine, *scratch
):
    side = Gather(mine, kvo_ref, scratch[:4], here=True)
    job = LocalSum(o_ref, scratch[4:11])
    ring = RingGather(count, share_ref, full_ref, scratch[11:])
    step = pl.program_id(0)

    @pl.when(step == 0)
    def _():
        greet([job.to_sib, job.to_far, ring.ahead, ring.behind])
        ring.start()

    job.put(step, dot(m_ref[...], w_ref[...], NT).astype(BF))
    job.after_step(step)

    @pl.when(step == 1)
    def _():
        mine[...] = dot(p_ref[...], wp_ref[...], NN).astype(BF)
        side.start()
        ring.place()

    @pl.when(step == 7)
    def _():
        for hop in range(1, ring.half):
            ring.hop(hop)
        for k in range(CHUNKS):
            side.forward(k)
        job.land()
        side.finish()
        job.finish()
        ring.finish()


def out_project(mixed, weights, column, prompts, prompt_weights, weight_share, count):
    length, width = mixed.shape
    model = weights.shape[0]
    rows = length // 8
    share = length // 4
    short = prompts.shape[0]
    once = pl.Buffered(1)
    return pl.pallas_call(
        functools.partial(out_kernel, count),
        grid=(8,),
        out_shape=(
            shape_of((share, model), F32),
            shape_of((4 * short, width), BF),
            shape_of((count * weight_share.shape[0], weight_share.shape[1]), BF),
        ),
        in_specs=[
            pl.BlockSpec((rows, width), lambda i: (order_block(i), 0)),
            pl.BlockSpec((model, width), lambda i: (0, column), pipeline_mode=once),
            pl.BlockSpec(prompts.shape, lambda i: (0, 0), pipeline_mode=once),
            pl.BlockSpec((model, width), lambda i: (0, 0), pipeline_mode=once),
            ANY,
        ],
        out_specs=(pl.BlockSpec((share, model), lambda i: (0, 0)), ANY, ANY),
        scratch_shapes=[pltpu.VMEM((short, width), BF)]
        + gather_scratch(16, 128)
        + sum_scratch(share, model)
        + ring_scratch(*weight_share.shape, count // 2),
        compiler_params=local_params(collective_id=1, has_side_effects=True),
        cost_estimate=BUSY,
        name="out_project",
    )(mixed, weights, prompts, prompt_weights, weight_share)


def glu_back_kernel(parts, count, d0_ref, d1_ref, h0_ref, h1_ref, *refs):
    weights = refs[:count]
    o_ref, t0_ref, t1_ref = refs[count : count + 3]
    job = LocalSum(o_ref, refs[count + 3 :])
    step = pl.program_id(0)

    def gate_up():
        term = None
        for left, group in zip((d0_ref, d1_ref), parts):
            base = 0
            for index, low, size in group:
                w_ref = weights[index]
                width = w_ref.shape[1] // 3
                if size == width:
                    part = dot(left[:, base : base + 2 * size], w_ref[:, : 2 * size], NT)
                else:
                    high = low + size
                    part = dot(left[:, base : base + size], w_ref[:, low:high], NT) + dot(
                        left[:, base + size : base + 2 * size],
                        w_ref[:, width + low : width + high],
                        NT,
                    )
                term = part if term is None else term + part
                base += 2 * size
        return term.astype(BF)

    def down():
        term = None
        for left, group in zip((h0_ref, h1_ref), parts):
            base = 0
            for index, low, size in group:
                w_ref = weights[index]
                start = 2 * w_ref.shape[1] // 3 + low
                part = dot(left[:, base : base + size], w_ref[:, start : start + size], NT)
                term = part if term is None else term + part
                base += size
        return term.astype(BF)

    @pl.when(step == 0)
    def _():
        greet([job.to_sib, job.to_far])

    @pl.when(step < 8)
    def _():
        job.put(step, gate_up())

    job.after_step(step)

    @pl.when(step >= 8)
    def _():
        term = down()
        half = t0_ref.shape[1]
        t0_ref[...] = term[:, :half]
        t1_ref[...] = term[:, half:]

    @pl.when(step == 15)
    def _():
        job.land()
        job.finish()


def glu_back(dgus, hiddens, weights, parts):
    length = dgus[0].shape[0]
    model = weights[0].shape[0]
    rows = length // 8
    share = length // 4
    once = pl.Buffered(1)
    early = lambda i: (order_block(jnp.minimum(i, 7)), 0)
    late = lambda i: (jnp.maximum(i - 8, 0), 0)
    in_specs = [pl.BlockSpec((rows, d.shape[1]), early) for d in dgus]
    in_specs += [pl.BlockSpec((rows, h.shape[1]), late) for h in hiddens]
    for weight in weights:
        in_specs.append(pl.BlockSpec(weight.shape, lambda i: (0, 0), pipeline_mode=once))
    half = pl.BlockSpec((rows, model // 2), late)
    return pl.pallas_call(
        functools.partial(glu_back_kernel, parts, len(weights)),
        grid=(16,),
        out_shape=(
            shape_of((share, model), F32),
            shape_of((length, model // 2), BF),
            shape_of((length, model // 2), BF),
        ),
        in_specs=in_specs,
        out_specs=(
            pl.BlockSpec((share, model), lambda i: (0, 0)),
            half,
            half,
        ),
        scratch_shapes=sum_scratch(share, model),
        compiler_params=local_params(collective_id=3, has_side_effects=True),
        cost_estimate=BUSY,
        name="glu_back",
    )(*dgus, *hiddens, *weights)


def mid_kernel(
    count, c_ref, t_ref, n_ref, cb_ref, q_ref, cm_ref, w_ref, m_ref, p_ref, y_ref,
    x_ref, g_ref, dw_ref, yo_ref, s_ref, slots, total, ssem, rsem, *scratch,
):
    small = Scatter(t_ref, s_ref, scratch[:8])
    ring = RingSum(count, [y_ref], scratch[8:])
    me, sib, far, diag = mp_peers()
    dp = lax.axis_index("dp")
    to_sib = {"dp": dp, "mp": sib}
    to_far = {"dp": dp, "mp": far}
    step = pl.program_id(0)
    rows = c_ref.shape[0]
    part = rows // CHUNKS
    spans = [pl.ds(k * part, part) for k in range(CHUNKS)]
    beside = remote(c_ref, slots.at[0], ssem.at[0], rsem.at[0], to_sib)
    across = [
        remote(c_ref.at[span], slots.at[1, span], ssem.at[1 + k], rsem.at[1 + k], to_far)
        for k, span in enumerate(spans)
    ]
    onward = [
        remote(
            slots.at[1, span],
            slots.at[2, span],
            ssem.at[1 + CHUNKS + k],
            rsem.at[1 + CHUNKS + k],
            to_sib,
        )
        for k, span in enumerate(spans)
    ]

    @pl.when(step == 0)
    def _():
        greet([to_sib, to_far, ring.ahead, ring.behind])
        for copy in across:
            copy.start()
        small.start()
        beside.start()
        ring.start()

    @pl.when(step == 6)
    def _():
        for hop in range(1, ring.half // 2):
            ring.hop(hop)

    @pl.when(step == 1)
    def _():
        small.fold()
        small.local()

    @pl.when(step < 8)
    def _():
        width = q_ref.shape[1]
        x_ref[:, :width] = dot(n_ref[...], q_ref[...], TN).astype(BF)
        x_ref[:, width:] = dot(cb_ref[...], cm_ref[...], TN).astype(BF)

    def use(grads):
        g_ref[...] = dot(grads, w_ref[...], NN).astype(BF)
        return dot(grads, m_ref[...], TN)

    @pl.when(step == 8)
    def _():
        total[...] = use(c_ref[...])

    @pl.when(step == 9)
    def _():
        beside.wait_recv()
        total[...] += use(slots[0])

    @pl.when(step == 10)
    def _():
        ring.hop(ring.half // 2)
        small.land()
        for k in range(CHUNKS):
            across[k].wait_recv()
            onward[k].start()
        for hop in range(ring.half // 2 + 1, ring.half):
            ring.hop(hop)
        total[...] += use(slots[1])

    @pl.when(step == 11)
    def _():
        for copy in onward:
            copy.wait_recv()
        width = m_ref.shape[1]
        dw_ref[:, :width] = (total[...] + use(slots[2])).astype(BF)
        dw_ref[:, width:] = dot(p_ref[...], s_ref[...].astype(BF), TN).astype(BF)
        small.finish()
        ring.finish([yo_ref])
        beside.wait_send()
        for copy in across + onward:
            copy.wait_send()


def mid_gather(
    carried, term, normed, cross_back, grad_cq, cross_mixed, weights, column, mixed, prompts,
    more, groups, count,
):
    share, model = carried.shape
    own = more.shape[0] // count
    length, width = mixed.shape
    short, narrow = term.shape[0] // 4, term.shape[1]
    tile = 2 * model // 4
    once = pl.Buffered(1)
    fixed = pl.BlockSpec((share, model), lambda i: (0, 0), pipeline_mode=once)
    left = pl.BlockSpec((share, tile), lambda i: (0, jnp.minimum(i, 7) % 2))
    right = pl.BlockSpec((share, width), lambda i: (0, jnp.minimum(i, 7) // 2))

    def turn(i):
        return (arrival_quarter(jnp.maximum(i - 8, 0)), 0)

    return pl.pallas_call(
        functools.partial(mid_kernel, count),
        grid=(12,),
        in_specs=[
            fixed,
            ANY,
            left,
            left,
            right,
            right,
            pl.BlockSpec((model, width), lambda i: (0, column), pipeline_mode=once),
            pl.BlockSpec((share, width), turn),
            pl.BlockSpec(prompts.shape, lambda i: (0, 0), pipeline_mode=once),
            ANY,
        ],
        out_specs=(
            pl.BlockSpec((tile, 2 * width), lambda i: (jnp.minimum(i, 7), 0)),
            pl.BlockSpec((share, width), turn),
            pl.BlockSpec((model, 2 * width), lambda i: (0, 0)),
            pl.BlockSpec((own, more.shape[1]), lambda i: (0, 0)),
        ),
        out_shape=(
            shape_of((groups * model, 2 * width), BF),
            shape_of((length, width), BF),
            shape_of((model, 2 * width), BF),
            shape_of((own, more.shape[1]), F32),
        ),
        scratch_shapes=[
            pltpu.VMEM((short, narrow), F32),
            pltpu.VMEM((3, share, model), BF),
            pltpu.VMEM((model, width), F32),
            pltpu.SemaphoreType.DMA((1 + 2 * CHUNKS,)),
            pltpu.SemaphoreType.DMA((1 + 2 * CHUNKS,)),
        ]
        + scatter_scratch(short, narrow)
        + ring_sum_scratch(own, more.shape[1], count // 2, 1),
        compiler_params=local_params(collective_id=4, has_side_effects=True),
        cost_estimate=BUSY,
        name="mid_gather",
    )(carried, term, normed, cross_back, grad_cq, cross_mixed, weights, mixed, prompts, more)


def qkv_kernel(
    scale, x_ref, s_ref, r_ref, hot_ref, w_ref, c_ref, u_ref, l_ref,
    n_ref, q_ref, k_ref, v_ref, g_ref, sw_ref, nc_ref, k0_ref, v0_ref,
):
    width = q_ref.shape[1]

    @pl.when(pl.program_id(0) == 0)
    def _():
        side = s_ref[...]
        dims = (8, side.shape[1])
        pick = lax.broadcasted_iota(jnp.int32, dims, 0) == lanes(dims)
        g_ref[...] = dot(jnp.where(pick, 1.0, 0.0).astype(BF), side, NT)
        totals = dot(jnp.ones((8, side.shape[0]), BF), side, NN)
        sw_ref[...] = jnp.broadcast_to(
            scale / jnp.sum(totals * hot_ref[...], axis=1, keepdims=True), sw_ref.shape
        )
        unit, _ = norm_rows(bucket_row(hot_ref[...], r_ref[...]))
        normed = jnp.broadcast_to(unit * g_ref[0:1, :], nc_ref.shape).astype(BF)
        nc_ref[...] = normed
        out = dot(normed, w_ref[:, width:], NN).astype(BF)
        k0_ref[...] = out[:, :width]
        v0_ref[...] = out[:, width:]

    unit, _ = norm_rows(x_ref[...].astype(F32))
    normed = (unit * g_ref[0:1, :]).astype(BF)
    n_ref[...] = normed
    out = dot(normed, w_ref[...], NN)
    cosine, upper, lower = c_ref[...], u_ref[...], l_ref[...]
    for pair in range(width // 128):
        span = slice(128 * pair, 128 * pair + 128)
        q_ref[:, span] = (rope(out[:, span], cosine, upper, lower) * (LOG2E / 8.0)).astype(BF)
        keys = out[:, width + 128 * pair : width + 128 * pair + 128]
        k_ref[:, span] = rope(keys, cosine, upper, lower).astype(BF)
    v_ref[...] = out[:, 2 * width : 3 * width].astype(BF)


def qkv_project(frames, table_rows, hot, weights, tables, width, scale):
    length, model = frames.shape
    rows = 256
    block = pl.BlockSpec((rows, model), lambda i: (i, 0))
    table = pl.BlockSpec((rows, 128), lambda i: (i, 0))
    head = pl.BlockSpec((rows, width), lambda i: (i, 0))
    fixed = lambda i: (0, 0)
    extra = [
        shape_of((8, model), F32),
        shape_of((8, 128), F32),
        shape_of((16, model), BF),
        shape_of((16, width), BF),
        shape_of((16, width), BF),
    ]
    return pl.pallas_call(
        functools.partial(qkv_kernel, scale),
        grid=(length // rows,),
        in_specs=[
            block,
            pl.BlockSpec((model, 128), lambda i: (0, 4 * width // 128)),
            pl.BlockSpec(table_rows.shape, fixed),
            pl.BlockSpec(hot.shape, fixed),
            pl.BlockSpec((model, 3 * width), fixed),
            table,
            table,
            table,
        ],
        out_specs=[block, head, head, head] + [pl.BlockSpec(e.shape, fixed) for e in extra],
        out_shape=[shape_of((length, model), BF)] + [shape_of((length, width), BF)] * 3 + extra,
        compiler_params=local_params(),
        cost_estimate=cost(6 * length * model * width, 8 * length * model),
        name="qkv_project",
    )(frames, weights, table_rows, hot, weights, *tables)


def attend_kernel(
    bk, first, count, q_ref, k_ref, v_ref, k0_ref, v0_ref, x_ref, w_ref, y_ref,
    o_ref, aug_ref, xo_ref, wo_ref, yo_ref, vaug, *scratch,
):
    length = k_ref.shape[0]
    bq = q_ref.shape[0]
    step = pl.program_id(0) * pl.num_programs(1) + pl.program_id(1)
    wide = xo_ref.shape[1]
    job = Gather(x_ref, xo_ref, scratch[:4], pl.ds(first, wide))
    ring = RingGather(count, w_ref, wo_ref, scratch[4:10])
    wide_ring = RingGather(count, y_ref, yo_ref, scratch[10:])
    last = pl.num_programs(0) * pl.num_programs(1) - 1

    @pl.when(step == 0)
    def _():
        greet([job.to_sib, job.to_far, ring.ahead, ring.behind])
        ring.start()
        wide_ring.start()
        job.start()
        ring.place()
        wide_ring.place()

    for hop in range(1, ring.half):

        @pl.when(step == min(3 * hop, 11))
        def _(hop=hop):
            ring.hop(hop)

        @pl.when(step == min(1 + 3 * hop, 11))
        def _(hop=hop):
            wide_ring.hop(hop)

    @pl.when(pl.program_id(1) == 0)
    def _():
        vaug[:, :128] = v_ref[...]
        vaug[:, 128:] = jnp.ones((length, 128), BF)

    queries = q_ref[...]
    key0 = k0_ref[0:1, :].astype(F32)
    value0 = v0_ref[0:1, :].astype(F32)
    outs = []
    logs = []
    for head in range(2):
        masked = half_mask(queries, head)
        peak = jnp.sum(masked.astype(F32) * key0, axis=1, keepdims=True)
        total = jnp.concatenate(
            [jnp.broadcast_to(value0, (bq, 128)), jnp.ones((bq, 128), F32)], 1
        )
        for block in range(length // bk):
            span = slice(block * bk, (block + 1) * bk)
            scores = dot(masked, k_ref[span, :], NT)
            higher = jnp.maximum(peak, jnp.max(scores, axis=1, keepdims=True))
            exponent = jnp.exp2(scores - higher).astype(BF)
            total = total * jnp.exp2(peak - higher) + dot(exponent, vaug[span, :], NN)
            peak = higher
        weight = total[:, 128:129]
        outs.append(total[:, :128] * (1.0 / weight))
        logs.append(-(peak + jnp.log2(weight)))
    lane = lanes((bq, 128))
    o_ref[...] = jnp.where(lane < HD, outs[0], outs[1]).astype(BF)
    aug_ref[...] = (pieces(logs[0], (bq, 128), 0) + pieces(logs[1], (bq, 128), HD)).astype(BF)

    @pl.when(step == last)
    def _():
        for k in range(CHUNKS):
            job.forward(k)
        job.finish()
        ring.finish()
        wide_ring.finish()


def attend(
    queries, keys, values, key0, value0, packed, first, share, more, count, bq=512, bk=1024
):
    length, width = queries.shape
    row = pl.BlockSpec((bq, 128), lambda p, i: (i, p))
    full = pl.BlockSpec((length, 128), lambda p, i: (0, p))
    zero = pl.BlockSpec((16, 128), lambda p, i: (0, p))
    return pl.pallas_call(
        functools.partial(attend_kernel, bk, first, count),
        grid=(width // 128, length // bq),
        in_specs=[row, full, full, zero, zero, ANY, ANY, ANY],
        out_specs=[row, row, ANY, ANY, ANY],
        out_shape=[shape_of((length, width), BF)] * 2
        + [
            shape_of((4 * packed.shape[0], 2 * width), BF),
            shape_of((count * share.shape[0], share.shape[1]), BF),
            shape_of((count * more.shape[0], more.shape[1]), BF),
        ],
        scratch_shapes=[pltpu.VMEM((length, 256), BF)]
        + gather_scratch(packed.shape[0], 2 * width)
        + ring_scratch(*share.shape, count // 2)
        + ring_scratch(*more.shape, count // 2),
        compiler_params=local_params(collective_id=7, has_side_effects=True),
        cost_estimate=cost(16 * length * length * width, 10 * length * width),
        name="attend",
    )(queries, keys, values, key0, value0, packed, share, more)


def attend_back_kernel(
    bk, count, q_ref, aug_ref, o_ref, do_ref, k_ref, v_ref, k0_ref, v0_ref,
    cq_ref, uq_ref, lq_ref, ck_ref, uk_ref, lk_ref,
    x_ref, y_ref, t_ref, ac_ref, dq_ref, dk_ref, dv_ref, dk0_ref, dv0_ref, xh_ref,
    yo_ref, zo_ref,
    to_ref, xo0_ref, xo1_ref, kaug, vaug, kt, dka, dva, xs, xsem, *scratch,
):
    length = k_ref.shape[0]
    bq = q_ref.shape[0]
    step = pl.program_id(1)
    turn = pl.program_id(0) * pl.num_programs(1) + step
    job = Scatter(x_ref, xs, scratch[:8])
    late = Scatter(t_ref, to_ref, scratch[8:16])
    ring = RingSum(count, [y_ref], scratch[16:26])
    next_ring = RingSum(count, [xh_ref], scratch[26:])
    keep = pltpu.make_async_copy(xs, xh_ref, xsem)

    @pl.when(turn == 0)
    def _():
        greet([job.to_sib, job.to_far, ring.ahead, ring.behind])
        job.start()
        ring.start()

    @pl.when(turn == 1)
    def _():
        job.fold()
        job.local()
        late.start()

    for hop in range(1, ring.half):

        @pl.when(turn == min(1 + 2 * hop, 7))
        def _(hop=hop):
            ring.hop(hop)

        @pl.when(turn == min(8 + hop, 11))
        def _(hop=hop):
            next_ring.hop(hop)

    @pl.when(turn == 8)
    def _():
        job.land()
        keep.start()
        late.fold()
        late.local()
        keep.wait()
        next_ring.start()
        job.finish()
        ring.finish([yo_ref, zo_ref])

    @pl.when(step == 0)
    def _():
        lane = lanes((length, 128))
        ones = jnp.where((lane % HD) < 3, 1.0, 0.0).astype(BF)
        kaug[:, :128] = k_ref[...]
        kaug[:, 128:] = ones
        vaug[:, :128] = v_ref[...]
        vaug[:, 128:] = ones
        kt[...] = k_ref[...].astype(F32).T.astype(BF)
        dka[...] = jnp.zeros_like(dka)
        dva[...] = jnp.zeros_like(dva)
        dk0_ref[...] = jnp.zeros_like(dk0_ref)
        dv0_ref[...] = jnp.zeros_like(dv0_ref)

    queries = q_ref[...]
    grads = do_ref[...]
    aug = aug_ref[...]
    product = grads.astype(F32) * o_ref[...].astype(F32)
    lane = lanes((bq, 128))
    ones0 = jnp.where((lanes((16, 128)) % HD) < 3, 1.0, 0.0).astype(BF)
    key0 = jnp.concatenate([k0_ref[...], ones0], 1)
    value0 = jnp.concatenate([v0_ref[...], ones0], 1)
    row0 = lax.broadcasted_iota(jnp.int32, (16, bq), 0) == 0
    qa, da, qm, dm, dq = [], [], [], [], []
    for head in range(2):
        qm.append(half_mask(queries, head))
        dm.append(half_mask(grads, head))
        mine = (lane < HD) if head == 0 else (lane >= HD)
        inner = jnp.sum(jnp.where(mine, product, 0.0), axis=1, keepdims=True)
        qa.append(jnp.concatenate([qm[head], half_mask(aug, head)], 1))
        da.append(
            jnp.concatenate([dm[head], pieces(-inner, (bq, 128), HD * head).astype(BF)], 1)
        )
        prob0 = jnp.where(row0, jnp.exp2(dot(key0, qa[head], NT)), 0.0)
        ds0 = (prob0 * dot(value0, da[head], NT)).astype(BF)
        dv0_ref[...] += dot(prob0.astype(BF), dm[head], NN)
        dk0_ref[...] += dot(ds0, qm[head], NN)
        dq.append(dot(k0_ref[:, HD * head : HD * head + HD], ds0, TN))
    for block in range(length // bk):
        span = slice(block * bk, (block + 1) * bk)
        for head in range(2):
            probs = jnp.exp2(dot(kaug[span, :], qa[head], NT))
            ds = (probs * dot(vaug[span, :], da[head], NT)).astype(BF)
            dva[span, :] += dot(probs.astype(BF), dm[head], NN)
            dka[span, :] += dot(ds, qm[head], NN)
            dq[head] = dq[head] + dot(kt[HD * head : HD * head + HD, span], ds, NN)
    grad_q = jnp.concatenate(dq, 0).T * 0.125
    dq_ref[...] = rope(grad_q, cq_ref[...], -uq_ref[...], -lq_ref[...]).astype(BF)

    @pl.when(turn == pl.num_programs(0) * pl.num_programs(1) - 1)
    def _():
        late.land(ac_ref)
        late.finish()
        next_ring.finish([xo0_ref, xo1_ref])

    @pl.when(step == pl.num_programs(1) - 1)
    def _():
        grad_k = dka[...] * (1.0 / LOG2E)
        dk_ref[...] = rope(grad_k, ck_ref[...], -uk_ref[...], -lk_ref[...]).astype(BF)
        dv_ref[...] = dva[...].astype(BF)
        dk0_ref[...] = dk0_ref[...] * (1.0 / LOG2E)


def attend_back(
    queries, aug, mixed, grads, keys, values, key0, value0, tables, extra, more, term, after_cross, count,
    bq=512, bk=512,
):
    length, width = queries.shape
    row = pl.BlockSpec((bq, 128), lambda p, i: (i, p))
    full = pl.BlockSpec((length, 128), lambda p, i: (0, p))
    zero = pl.BlockSpec((16, 128), lambda p, i: (0, p))
    tq = pl.BlockSpec((bq, 128), lambda p, i: (i, 0))
    tk = pl.BlockSpec((length, 128), lambda p, i: (0, 0), pipeline_mode=pl.Buffered(1))
    own = more.shape[0] // count
    owned = pl.BlockSpec((own, more.shape[1] // 2), lambda p, i: (0, 0))
    wide, narrow = extra.shape[0] // 4, extra.shape[1]
    half_shape = (after_cross.shape[0], term.shape[1])
    share_spec = pl.BlockSpec(half_shape, lambda p, i: (0, 0))
    part = pl.BlockSpec((own, narrow // 2), lambda p, i: (0, 0))
    big = shape_of((length, width), BF)
    small = shape_of((16, width), F32)
    return pl.pallas_call(
        functools.partial(attend_back_kernel, bk, count),
        grid=(width // 128, length // bq),
        in_specs=[row, row, row, row, full, full, zero, zero, tq, tq, tq, tk, tk, tk, ANY, ANY, ANY,
            pl.BlockSpec(half_shape, lambda p, i: (0, 1), pipeline_mode=pl.Buffered(1)),
        ],
        out_specs=[row, full, full, zero, zero, ANY, owned, owned, share_spec, part, part],
        out_shape=[big, big, big, small, small]
        + [
            shape_of((wide, narrow), BF),
            shape_of((own, more.shape[1] // 2), F32),
            shape_of((own, more.shape[1] // 2), F32),
            shape_of(half_shape, BF),
            shape_of((own, narrow // 2), F32),
            shape_of((own, narrow // 2), F32),
        ],
        scratch_shapes=[pltpu.VMEM((length, 256), BF)] * 2
        + [pltpu.VMEM((128, length), BF)]
        + [pltpu.VMEM((length, 128), F32)] * 2
        + [
            pltpu.VMEM((wide, narrow), BF),
            pltpu.SemaphoreType.DMA(()),
        ]
        + scatter_scratch(wide, narrow)
        + scatter_scratch(*half_shape)
        + ring_sum_scratch(own, more.shape[1], count // 2, 1)
        + ring_sum_scratch(own, narrow, count // 2, 1),
        compiler_params=local_params(collective_id=8, has_side_effects=True),
        cost_estimate=cost(40 * length * length * width, 20 * length * width),
        name="attend_back",
    )(queries, aug, mixed, grads, keys, values, key0, value0, *tables, *tables, extra, more, term, after_cross)


def softmax_keys(scores, length):
    key = lax.broadcasted_iota(jnp.int32, scores.shape, 0)
    masked = jnp.where(key < length, scores, -1e9)
    exponent = jnp.exp2(masked - jnp.max(masked, axis=0, keepdims=True))
    return exponent * (1.0 / jnp.sum(exponent, axis=0, keepdims=True))


def two_heads(values):
    return jnp.concatenate([half_mask(values, 0), half_mask(values, 1)], 0)


def one_row(values):
    rows = values.shape[0] // 2
    lane = lanes((rows, 128))
    return jnp.where(lane < HD, values[:rows], values[rows:])


def cross_kernel(
    count, len_ref, f_ref, s_ref, g_ref, wq_ref, wo_ref, kv_ref, share_ref,
    as_ref, n2_ref, q_ref, m_ref, ac_ref, n3_ref, full_ref, mine, *scratch,
):
    job = Gather(mine, n3_ref, scratch[:4], here=True)
    ring = RingGather(count, share_ref, full_ref, scratch[4:])
    step = pl.program_id(0)
    groups, model, width = wq_ref.shape
    keys = kv_ref.shape[1] // 2

    @pl.when(step == 0)
    def _():
        greet([job.to_sib, job.to_far, ring.ahead, ring.behind])
        ring.start()

    after_self = f_ref[...].astype(F32) + s_ref[...]
    as_ref[...] = after_self
    unit, _ = norm_rows(after_self)
    normed = (unit * g_ref[1:2, :]).astype(BF)
    n2_ref[...] = normed
    rows = normed.shape[0]
    total = after_self
    for group in range(groups):
        queries = (dot(normed, wq_ref[group], NN) * (LOG2E / 8.0)).astype(BF)
        base = group * width
        q_ref[:, base : base + width] = queries
        for pair in range(width // 128):
            span = slice(128 * pair, 128 * pair + 128)
            scores = dot(kv_ref[group, :keys, span], two_heads(queries[:, span]), NT)
            probs = softmax_keys(scores, len_ref[0])
            m_ref[:, base + 128 * pair : base + 128 * pair + 128] = one_row(
                dot(probs.astype(BF), kv_ref[group, keys:, span], TN)
            ).astype(BF)
        total = total + dot(m_ref[:, base : base + width], wo_ref[group], NT)
    ac_ref[...] = total
    unit, _ = norm_rows(total)
    mine[pl.ds(pl.multiple_of(step * rows, rows), rows), :] = (unit * g_ref[2:3, :]).astype(BF)

    for turn in range(2):

        @pl.when(step == turn)
        def _(turn=turn):
            half = CHUNKS // 2
            for k in range(turn * half, turn * half + half):
                job.across[k].start()
                job.beside[k].start()
            if turn == 0:
                ring.place()
                ring.hop(1)

    @pl.when(step == 1)
    def _():
        job.store.start()
        for hop in range(2, ring.half):
            ring.hop(hop)
        for k in range(CHUNKS):
            job.forward(k)
        job.finish()
        ring.finish()


def cross_forward(plen, frames, summed, gains, weights, prompt_kv, share, count):
    own, model = frames.shape
    groups, _, both = weights.shape
    width = both // 2
    rows = own // 2
    block = pl.BlockSpec((rows, model), lambda i: (i, 0))
    gain = pl.BlockSpec(gains.shape, lambda i: (0, 0))
    once = pl.Buffered(1)
    return pl.pallas_call(
        functools.partial(cross_kernel, count),
        grid=(2,),
        in_specs=[
            pl.BlockSpec(memory_space=pltpu.SMEM),
            block,
            block,
            gain,
            pl.BlockSpec((groups, model, width), lambda i: (0, 0, 0), pipeline_mode=once),
            pl.BlockSpec((groups, model, width), lambda i: (0, 0, 1), pipeline_mode=once),
            pl.BlockSpec(prompt_kv.shape, lambda i: (0, 0, 0)),
            ANY,
        ],
        out_specs=[block] * 5 + [ANY, ANY],
        out_shape=[
            shape_of((own, model), F32),
            shape_of((own, model), BF),
            shape_of((own, model), BF),
            shape_of((own, model), BF),
            shape_of((own, model), F32),
            shape_of((4 * own, model), BF),
            shape_of((count * share.shape[0], share.shape[1]), BF),
        ],
        scratch_shapes=[pltpu.VMEM((own, model), BF)]
        + gather_scratch(16, 128)
        + ring_scratch(*share.shape, count // 2),
        compiler_params=local_params(collective_id=2, has_side_effects=True),
        cost_estimate=BUSY,
        name="cross_forward",
    )(plen, frames, summed, gains, weights, weights, prompt_kv, share)


def cross_back_kernel(
    len_ref, w_ref, go_ref, e_ref, ac_ref, as_ref, g_ref, q_ref, wq_ref, wo_ref, kv_ref, t_ref,
    cb_ref, dq_ref, c3_ref, c3b_ref, dkv_ref, dg_ref, bo_ref, dkv, hold, *scratch,
):
    groups, model, width = wq_ref.shape
    keys = kv_ref.shape[1] // 2
    job = Scatter(t_ref, bo_ref, scratch)
    step = pl.program_id(0)

    @pl.when(step == 0)
    def _():
        greet([job.to_sib, job.to_far])
        job.start()

    @pl.when(pl.program_id(0) == 0)
    def _():
        dkv[...] = jnp.zeros_like(dkv)
        dg_ref[...] = jnp.zeros_like(dg_ref)

    unit, spread = norm_rows(ac_ref[...])
    back, part = norm_back(e_ref[...], unit, spread, g_ref[2:3, :])
    dg_ref[2:3, :] += part
    carried = go_ref[...].astype(F32) * w_ref[0:1, 0:1] + back
    cross_back = carried.astype(BF)
    cb_ref[...] = cross_back
    rows = cross_back.shape[0]
    total = jnp.zeros((rows, model), F32)
    spot = pl.ds(pl.multiple_of(pl.program_id(0) * rows, rows), rows)
    hold[spot, :] = ac_ref[:, : hold.shape[1]]

    @pl.when(step == 0)
    def _():
        job.fold()
        job.local()

    for group in range(groups):
        grads = dot(cross_back, wo_ref[group], NN).astype(BF)
        base = group * width
        for pair in range(width // 128):
            span = slice(128 * pair, 128 * pair + 128)
            wide = slice(base + 128 * pair, base + 128 * pair + 128)
            queries = two_heads(q_ref[:, wide])
            masked = two_heads(grads[:, span])
            probs = softmax_keys(dot(kv_ref[group, :keys, span], queries, NT), len_ref[0])
            dprobs = dot(kv_ref[group, keys:, span], masked, NT)
            inner = jnp.sum(dprobs * probs, axis=0, keepdims=True)
            ds = (probs * (dprobs - inner)).astype(BF)
            dkv[group, :keys, span] += dot(ds, queries, NN) * (1.0 / LOG2E)
            dkv[group, keys:, span] += dot(probs.astype(BF), masked, NN)
            grad_q = one_row(dot(ds, kv_ref[group, :keys, span], TN))
            dq_ref[:, wide] = (grad_q * 0.125).astype(BF)
        total = total + dot(dq_ref[:, base : base + width], wq_ref[group], NT)
    unit, spread = norm_rows(as_ref[...])
    back, part = norm_back(total, unit, spread, g_ref[1:2, :])
    dg_ref[1:2, :] += part
    carried = carried + back
    c3_ref[...] = carried
    c3b_ref[...] = carried.astype(BF)

    @pl.when(pl.program_id(0) == pl.num_programs(0) - 1)
    def _():
        dkv_ref[...] = dkv[...].astype(BF)
        job.land(hold)
        job.finish()


def cross_backward(plen, weight, grad_out, summed, after_cross, after_self, gains, queries,
                   weights, prompt_kv, term):
    share, model = grad_out.shape
    groups, _, both = weights.shape
    width = both // 2
    rows = 256
    block = pl.BlockSpec((rows, model), lambda i: (i, 0))
    gain = pl.BlockSpec(gains.shape, lambda i: (0, 0))
    once = pl.Buffered(1)
    return pl.pallas_call(
        cross_back_kernel,
        grid=(share // rows,),
        in_specs=[
            pl.BlockSpec(memory_space=pltpu.SMEM),
            pl.BlockSpec(weight.shape, lambda i: (0, 0)),
            block,
            block,
            block,
            block,
            gain,
            block,
            pl.BlockSpec((groups, model, width), lambda i: (0, 0, 0), pipeline_mode=once),
            pl.BlockSpec((groups, model, width), lambda i: (0, 0, 1), pipeline_mode=once),
            pl.BlockSpec(prompt_kv.shape, lambda i: (0, 0, 0)),
            ANY,
        ],
        out_specs=[block] * 4
        + [pl.BlockSpec(prompt_kv.shape, lambda i: (0, 0, 0)), gain]
        + [pl.BlockSpec((share, term.shape[1]), lambda i: (0, 0))],
        out_shape=[
            shape_of((share, model), BF),
            shape_of((share, model), BF),
            shape_of((share, model), F32),
            shape_of((share, model), BF),
            shape_of(prompt_kv.shape, BF),
            shape_of(gains.shape, F32),
            shape_of((share, term.shape[1]), BF),
        ],
        scratch_shapes=[
            pltpu.VMEM(prompt_kv.shape, F32),
            pltpu.VMEM((share, term.shape[1]), F32),
        ]
        + scatter_scratch(share, term.shape[1]),
        compiler_params=local_params(collective_id=9, has_side_effects=True),
        cost_estimate=cost(4 * share * model * model, 4 * model * model + 24 * share * model),
        name="cross_backward",
    )(plen, weight, grad_out, summed, after_cross, after_self, gains, queries, weights, weights,
      prompt_kv, term)


def glu_kernel(scaled, parts, count, *refs):
    refs = list(refs)
    s_ref = None if scaled else refs.pop(0)
    n_ref, c_ref = refs[:2]
    weights, outs = refs[2 : 2 + count], refs[2 + count :]
    cot = c_ref[...]
    if not scaled:
        cot = (cot.astype(F32) * s_ref[0:1, 0:1]).astype(BF)
        outs[2][...] = cot
    h_ref, d_ref = outs[:2]
    normed = n_ref[...]
    piece = 256
    at = 0
    for index, low, size in parts:
        w_ref = weights[index]
        width = w_ref.shape[1] // 3
        for base in range(0, size, piece):
            spot = low + base
            gate = dot(normed, w_ref[:, spot : spot + piece], NN)
            up = dot(normed, w_ref[:, width + spot : width + spot + piece], NN)
            grads = dot(cot, w_ref[:, 2 * width + spot : 2 * width + spot + piece], NN)
            sig = 1.0 / (1.0 + jnp.exp(-gate))
            silu = gate * sig
            h_ref[:, at + base : at + base + piece] = (silu * up).astype(BF)
            grad_gate = grads * up * sig * (1.0 + gate * (1.0 - sig))
            spot = 2 * at + base
            d_ref[:, spot : spot + piece] = grad_gate.astype(BF)
            d_ref[:, size + spot : size + spot + piece] = (grads * silu).astype(BF)
        at += size


def glu_block(normed, cot, weights, parts, scale=None):
    length, model = normed.shape
    width = sum(size for _, _, size in parts)
    rows = 512
    block = pl.BlockSpec((rows, model), lambda i: (i, 0))
    first = scale is not None
    return pl.pallas_call(
        functools.partial(glu_kernel, not first, parts, len(weights)),
        grid=(length // rows,),
        in_specs=[pl.BlockSpec((8, 128), lambda i: (0, 0))] * first
        + [block, block]
        + [
            pl.BlockSpec(weight.shape, lambda i: (0, 0), pipeline_mode=pl.Buffered(1))
            for weight in weights
        ],
        out_specs=[
            pl.BlockSpec((rows, width), lambda i: (i, 0)),
            pl.BlockSpec((rows, 2 * width), lambda i: (i, 0)),
        ]
        + [block] * first,
        out_shape=[shape_of((length, width), BF), shape_of((length, 2 * width), BF)]
        + [shape_of((length, model), BF)] * first,
        compiler_params=local_params(),
        cost_estimate=cost(6 * length * model * width, 6 * length * model),
        name="glu_block_%d" % width,
    )(*([scale] if first else []), normed, cot, *weights)


def grads_kernel(plan, n_ref, c_ref, d_ref, h_ref, *outs):
    for out, spans in zip(outs, plan):
        base = 0
        for side, low, high in spans:
            left, right = (n_ref, d_ref) if side == 0 else (c_ref, h_ref)
            value = dot(left[...], right[:, low:high], TN)
            out[:, base : base + high - low] = value.astype(BF)
            base += high - low


def weight_grads(normed, cot, dgu, hidden, plan, tile=256):
    length, model = normed.shape
    widths = [sum(high - low for _, low, high in spans) for spans in plan]
    once = pl.Buffered(1)
    left = pl.BlockSpec((length, tile), lambda i: (0, i))
    return pl.pallas_call(
        functools.partial(grads_kernel, plan),
        grid=(model // tile,),
        in_specs=[left, left]
        + [pl.BlockSpec(right.shape, lambda i: (0, 0), pipeline_mode=once) for right in (dgu, hidden)],
        out_specs=[pl.BlockSpec((tile, wide), lambda i: (i, 0)) for wide in widths],
        out_shape=[shape_of((model, wide), BF) for wide in widths],
        compiler_params=local_params(),
        cost_estimate=cost(2 * length * model * sum(widths), 2 * length * (2 * model + sum(widths))),
        name="weight_grads_%d" % sum(widths),
    )(normed, cot, dgu, hidden)


def last_grads_kernel(plan, copies, count, n_ref, q_ref, k_ref, v_ref, nc_ref, k0_ref, v0_ref, *refs):
    sources, rest = refs[:count], refs[count:]
    passed, (o_ref, gate_ref, up_ref, down_ref), targets = (
        rest[: -4 - len(copies)],
        rest[-4 - len(copies) : len(rest) - len(copies)],
        rest[len(rest) - len(copies) :],
    )
    width = q_ref.shape[1]
    normed = n_ref[...]
    edge = nc_ref[...]
    o_ref[:, :width] = dot(normed, q_ref[...], TN).astype(BF)
    grad_k = dot(normed, k_ref[...], TN) + dot(edge, k0_ref[...].astype(BF), TN)
    o_ref[:, width : 2 * width] = grad_k.astype(BF)
    grad_v = dot(normed, v_ref[...], TN) + dot(edge, v0_ref[...].astype(BF), TN)
    o_ref[:, 2 * width :] = grad_v.astype(BF)

    @pl.when(pl.program_id(0) == 0)
    def _():
        for source, base, kind, low, size in plan:
            target = (gate_ref, up_ref, down_ref)[kind]
            target[:, low : low + size] = sources[source][:, base : base + size].astype(F32)

    @pl.when(pl.program_id(0) == 1)
    def _():
        for target, (dims, places) in zip(targets, copies):
            for index, from_row, rows, row, column in places:
                ref = passed[index]
                value = ref[from_row : from_row + rows, :]
                target[row : row + rows, column : column + ref.shape[1]] = value


def last_grads(normed, grads, edge, dk0, dv0, sources, plan, hidden, passed, copies, tile=256):
    length, model = normed.shape
    width = grads[0].shape[1]
    own = sources[0].shape[0]
    once = pl.Buffered(1)
    fixed = lambda i: (0, 0)

    def full(array):
        return pl.BlockSpec(array.shape, fixed, pipeline_mode=once)

    extra = [shape_of(dims, passed[places[0][0]].dtype) for dims, places in copies]
    return pl.pallas_call(
        functools.partial(last_grads_kernel, plan, copies, len(sources)),
        grid=(model // tile,),
        in_specs=[pl.BlockSpec((length, tile), lambda i: (0, i))]
        + [full(grad) for grad in grads]
        + [pl.BlockSpec((edge.shape[0], tile), lambda i: (0, i)), full(dk0), full(dv0)]
        + [full(source) for source in sources]
        + [full(array) for array in passed],
        out_specs=[pl.BlockSpec((tile, 3 * width), lambda i: (i, 0))]
        + [pl.BlockSpec((own, hidden), fixed)] * 3
        + [pl.BlockSpec(array.shape, fixed) for array in extra],
        out_shape=[shape_of((model, 3 * width), BF)]
        + [shape_of((own, hidden), F32)] * 3
        + extra,
        compiler_params=local_params(),
        cost_estimate=cost(6 * length * model * width, 2 * length * (model + 3 * width)),
        name="last_grads",
    )(normed, *grads, edge, dk0, dv0, *sources, *passed)


def owner_sum(term):
    return lax.psum_scatter(term, "dp", scatter_dimension=0, tiled=True)


def after(value, *others):
    return lax.optimization_barrier((value,) + others)[0]


GLU_PARTS = 3


def per_device(
    frames, cond_table, bucket_ids, prompt, prompt_len,
    attn_query, attn_key, attn_value, attn_out,
    cross_query, cross_key, cross_value, cross_out,
    glu_gate, glu_up, glu_down, first_gain, second_gain, third_gain, grad_out,
):
    groups = lax.axis_size("mp")
    count = lax.axis_size("dp")
    sequences = bucket_ids.shape[0]
    assert sequences == 1 and groups == 4
    share, model = frames.shape
    length = share * groups
    buckets = cond_table.shape[0]
    own_rows, width = attn_query.shape
    unit = glu_gate.shape[1] // GLU_PARTS
    context = prompt.shape[2]

    onehot = (bucket_ids[:, None] == jnp.arange(buckets)[None, :]).astype(F32)
    gain_rows = jnp.pad(jnp.stack([first_gain, second_gain, third_gain]), ((0, 5), (0, 0)))
    hot = jnp.pad(onehot, ((0, 0), (3, 128 - 3 - buckets)))
    prompt_blocks = prompt.reshape(-1, count, context // count)
    blank = jnp.zeros_like(prompt_blocks)
    prompts = jnp.concatenate(
        [
            jnp.concatenate([prompt_blocks, blank], 2).reshape(-1, model),
            jnp.concatenate([blank, prompt_blocks], 2).reshape(-1, model),
        ],
        0,
    )
    prompt_share = jnp.concatenate([cross_key, cross_value], 0)
    frames_all, grad_all, first, *glu_share = head_gather(
        frames, grad_out, gain_rows, hot,
        [attn_query, attn_key, attn_value, attn_out, cross_query, cross_out],
        [glu_gate, glu_up, glu_down], GLU_PARTS, count,
    )

    tables = rope_tables(length, 1.0)
    scale = sequences * count * own_rows / buckets
    (
        normed_one, queries, keys, values, gains, seq_weight, normed_cond, key0, value0,
    ) = qkv_project(frames_all, cond_table, hot, first, tables, width, scale)
    mixed, aug, cross_full, second, glu_first = attend(
        queries, keys, values, key0, value0, first, 4 * width + 128, prompt_share,
        glu_share[0], count,
    )
    cross_full = cross_full.reshape(groups, model, 2 * width)
    self_out, prompt_kv, glu_second = out_project(
        mixed, first, 3, prompts, second, glu_share[1], count
    )
    prompt_kv = prompt_kv.reshape(groups, prompts.shape[0], width)

    (
        after_self, normed_two, cross_q, cross_mixed, after_cross, normed_three, glu_third,
    ) = cross_forward(
        prompt_len, frames, self_out, gains, cross_full, prompt_kv, glu_share[2], count
    )
    glu_full = [glu_first, glu_second, glu_third]
    half = unit // 2
    parts = (((0, 0, half),), ((0, half, half), (1, 0, unit), (2, 0, unit)))
    h0, d0, cot_all = glu_block(normed_three, grad_all, glu_full[:1], parts[0], seq_weight)
    (pack0,) = weight_grads(normed_three, cot_all, d0, h0, (((0, 0, unit), (1, 0, half)),))
    h1, d1 = glu_block(after(normed_three, pack0), cot_all, glu_full, parts[1])
    wide = unit + 2 * unit
    pack1, pack2 = weight_grads(
        normed_three, cot_all, d1, h1,
        (
            (
                (0, 0, unit), (1, 0, half),
                (0, unit, wide), (1, half, half + unit),
                (0, wide, wide + half), (0, wide + unit, wide + unit + half),
                (1, half + unit, 2 * unit),
            ),
            (
                (0, wide + half, wide + unit), (0, wide + unit + half, wide + 2 * unit),
                (1, 2 * unit, 2 * unit + half),
            ),
        ),
    )
    glu_sum0 = owner_sum(pack0)
    pack1 = after(pack1, glu_sum0)
    glu_sum1 = owner_sum(pack1)
    back_term, out_term0, out_term1 = glu_back(
        [after(d0, pack1), d1], [h0, h1], glu_full, parts
    )

    cross_back, grad_cq, carried, carried_low, grad_kv, grad_gains, block0 = cross_backward(
        prompt_len, seq_weight, grad_out, back_term, after_cross, after_self, gains, cross_q,
        cross_full, prompt_kv, out_term0,
    )
    cross_term, grad_mixed, second_pack, glu_sum2 = mid_gather(
        carried_low, grad_kv.reshape(-1, width), normed_two, cross_back, grad_cq, cross_mixed,
        first, 3, mixed, prompts, pack2, groups, count,
    )
    (
        dq, dk, dv, dk0, dv0, _, grad_out_own, grad_prompt, block1, grad_cross_q, grad_cross_o,
    ) = attend_back(
        queries, aug, mixed, grad_mixed, keys, values, key0, value0, tables, cross_term,
        second_pack, out_term1, after_cross, count,
    )
    plan = []
    pieces_of = (
        (0, 0, 0, half), (1, 0, half, half), (1, 3 * half, unit, unit),
        (1, 9 * half, 2 * unit, half), (2, 0, 2 * unit + half, half),
    )
    for source, base, low, size in pieces_of:
        for kind in range(3):
            plan.append((source, base + kind * size, kind, low, size))
    short = context // count
    copies = (
        ((share, model), ((0, 0, share, 0, 0), (1, 0, share, 0, model // 2))),
        ((own_rows, width), ((2, 0, own_rows, 0, 0),)),
        ((own_rows, width), ((3, 0, own_rows, 0, 0),)),
        ((short, width), ((4, 0, short, 0, 0),)),
        ((short, width), ((4, short, short, 0, 0),)),
        ((own_rows, width), ((5, 0, own_rows, 0, 0),)),
    )
    (
        first_pack, *glu_out, block_out, grad_out_own, grad_cross_q, grad_cross_k, grad_cross_v,
        grad_cross_o,
    ) = last_grads(
        normed_one, [dq, dk, dv], normed_cond, dk0, dv0, [glu_sum0, glu_sum1, glu_sum2], plan,
        glu_gate.shape[1],
        [block0, block1, grad_out_own, grad_cross_q, grad_prompt, grad_cross_o], copies,
    )
    frames_grad, sums, first_grad = tail_sums(
        count, buckets, [dq, dk, dv], first, first_pack, frames, carried, gains, grad_gains, hot,
        cond_table, dk0, dv0,
    )
    return (
        block_out,
        frames_grad,
        sums[:buckets],
        first_grad[:, :width],
        first_grad[:, width : 2 * width],
        first_grad[:, 2 * width :],
        grad_out_own,
        grad_cross_q,
        grad_cross_k,
        grad_cross_v,
        grad_cross_o,
        *glu_out,
        sums[buckets],
        sums[buckets + 1],
        sums[buckets + 2],
    )


def solution(mesh):
    both = P(("dp", "mp"), None)
    weight = P("dp", "mp")
    return jax.shard_map(
        per_device,
        mesh=mesh,
        in_specs=(both, P(), P("dp"), P("dp", None, None), P("dp"))
        + (weight,) * 11
        + (P("dp"),) * 3
        + (both,),
        out_specs=(both, both, P()) + (weight,) * 11 + (P(),) * 3,
        check_vma=False,
    )
```

```python
import functools

import jax
import jax.numpy as jnp
import numpy as np
from jax import lax
from jax.experimental import pallas as pl
from jax.experimental.pallas import tpu as pltpu
from jax.sharding import PartitionSpec as P

HD = 64
ROT = 32
LOG2E = 1.4426950408889634
EPS = 1e-05
MESH = pl.DeviceIdType.MESH
NT = (((1,), (1,)), ((), ()))
TN = (((0,), (0,)), ((), ()))
NN = (((1,), (0,)), ((), ()))
BF = jnp.bfloat16
F32 = jnp.float32
ANY = pl.BlockSpec(memory_space=pl.ANY)
VM = 58 << 20


def shape_of(dims, dtype):
    return jax.ShapeDtypeStruct(dims, dtype)


def dot(left, right, dims):
    return lax.dot_general(left, right, dims, preferred_element_type=F32)


def local_params(**extra):
    return pltpu.CompilerParams(vmem_limit_bytes=VM, **extra)


def cost(flops, nbytes, trans=0):
    return pl.CostEstimate(flops=int(flops), bytes_accessed=int(nbytes), transcendentals=int(trans))


def norm_rows(values):
    center = values - jnp.mean(values, -1, keepdims=True)
    spread = lax.rsqrt(jnp.mean(center * center, -1, keepdims=True) + EPS)
    return center * spread, spread


def norm_back(grad_rows, unit_rows, spread, gain_row):
    scaled = grad_rows * gain_row
    result = spread * (
        scaled
        - jnp.mean(scaled, -1, keepdims=True)
        - unit_rows * jnp.mean(scaled * unit_rows, -1, keepdims=True)
    )
    return result, jnp.sum(grad_rows * unit_rows, 0, keepdims=True)


def rope_tables(length, offset):
    lane = np.arange(2 * HD) % HD
    half = ROT // 2
    frequency = np.power(10000.0, -2.0 * (lane % half) / ROT)
    angles = (offset + np.arange(length))[:, None] * frequency[None, :]
    cosine = np.where(lane[None] < ROT, np.cos(angles), 1.0)
    sine = np.sin(angles)
    upper = np.where((lane[None] >= half) & (lane[None] < ROT), sine, 0.0)
    lower = np.where(lane[None] < half, -sine, 0.0)
    return [jnp.asarray(table.astype(np.float32)) for table in (cosine, upper, lower)]


def rope(values, cosine, upper, lower):
    half = ROT // 2
    return (
        values * cosine
        + pltpu.roll(values, half, 1) * upper
        + pltpu.roll(values, 2 * HD - half, 1) * lower
    )


def bucket_column(hot, rows):
    dims = (rows, 128)
    pick = lax.broadcasted_iota(jnp.int32, dims, 0) + 3 == lanes(dims)
    marks = jnp.broadcast_to(hot, (8, 128)).astype(BF)
    return dot(jnp.where(pick, 1.0, 0.0).astype(BF), marks, NT)[:, 0:1]


def bucket_row(hot, table):
    rows = table.shape[0]
    return jnp.sum(table.astype(F32) * bucket_column(hot, rows), axis=0, keepdims=True)


def lanes(dims):
    return lax.broadcasted_iota(jnp.int32, dims, 1)


def half_mask(values, head):
    lane = lanes(values.shape)
    keep = (lane < HD) if head == 0 else (lane >= HD)
    return jnp.where(keep, values, jnp.zeros_like(values))


def pieces(column, dims, base):
    high = column.astype(BF).astype(F32)
    rest = column - high
    middle = rest.astype(BF).astype(F32)
    low = rest - middle
    lane = lanes(dims)
    return jnp.where(
        lane == base,
        high,
        jnp.where(lane == base + 1, middle, jnp.where(lane == base + 2, low, 0.0)),
    )


def mp_peers():
    me = lax.axis_index("mp")
    chip, core = me // 2, me % 2
    return me, chip * 2 + (1 - core), (1 - chip) * 2 + core, (1 - chip) * 2 + (1 - core)


def greet(devices):
    barrier = pltpu.get_barrier_semaphore()
    for device in devices:
        pl.semaphore_signal(barrier, inc=1, device_id=device, device_id_type=MESH)
    pl.semaphore_wait(barrier, len(devices))


def remote(source, target, send, recv, device):
    return pltpu.make_async_remote_copy(
        source, target, send, recv, device_id=device, device_id_type=MESH
    )


CHUNKS = 4
CUTS = 2


def column_cuts(width):
    first = 128 * ((width // 128 + 1) // 2)
    return [pl.ds(0, first), pl.ds(first, width - first)]


BUSY = cost(1, 140 << 20)


def gather_scratch(rows, width):
    return [
        pltpu.VMEM((rows, width), BF),
        pltpu.SemaphoreType.DMA((2,)),
        pltpu.SemaphoreType.DMA((3, CHUNKS)),
        pltpu.SemaphoreType.DMA((3, CHUNKS)),
    ]


class Gather:
    def __init__(self, x_ref, o_ref, sems, columns=None, here=False):
        bounce, lsem, ssem, rsem = sems
        if here:
            bounce = x_ref
        self.me, self.sib, self.far, _ = mp_peers()
        dp = lax.axis_index("dp")
        self.to_sib = {"dp": dp, "mp": self.sib}
        self.to_far = {"dp": dp, "mp": self.far}
        rows = x_ref.shape[0]
        part = rows // CHUNKS

        def slot(i, k):
            return o_ref.at[pl.ds(pl.multiple_of(i * rows + k * part, part), part)]

        def source(first, size):
            if columns is None:
                return x_ref.at[pl.ds(first, size)]
            return x_ref.at[pl.ds(first, size), columns]

        self.load = None if here else pltpu.make_async_copy(source(0, rows), bounce, lsem.at[0])
        self.store = pltpu.make_async_copy(
            bounce, o_ref.at[pl.ds(pl.multiple_of(self.me * rows, rows), rows)], lsem.at[1]
        )
        self.across = []
        self.beside = []
        self.onward = []
        for k in range(CHUNKS):
            mine = source(k * part, part)
            self.across.append(
                remote(mine, slot(self.me, k), ssem.at[0, k], rsem.at[0, k], self.to_far)
            )
            self.beside.append(
                remote(mine, slot(self.me, k), ssem.at[1, k], rsem.at[1, k], self.to_sib)
            )
            self.onward.append(
                remote(
                    slot(self.far, k), slot(self.far, k), ssem.at[2, k], rsem.at[2, k], self.to_sib
                )
            )

    def start(self):
        for copy in self.across:
            copy.start()
        if self.load is not None:
            self.load.start()
        for copy in self.beside:
            copy.start()
        if self.load is not None:
            self.load.wait()
        self.store.start()

    def forward(self, k):
        self.across[k].wait_recv()
        self.onward[k].start()

    def finish(self):
        for k in range(CHUNKS):
            self.beside[k].wait_recv()
            self.onward[k].wait_recv()
        for k in range(CHUNKS):
            self.across[k].wait_send()
            self.beside[k].wait_send()
            self.onward[k].wait_send()
        self.store.wait()


def scatter_scratch(rows, width):
    return [pltpu.VMEM((2, rows, width), BF)] + [pltpu.VMEM((rows, width), BF)] * 4 + [
        pltpu.SemaphoreType.DMA((2,)),
        pltpu.SemaphoreType.DMA((3, CHUNKS)),
        pltpu.SemaphoreType.DMA((3, CHUNKS)),
    ]


class Scatter:
    def __init__(self, x_ref, o_ref, scratch):
        mine, ra, rb, rc, sb, lsem, ssem, rsem = scratch
        me, sib, far, diag = mp_peers()
        dp = lax.axis_index("dp")
        self.to_sib = {"dp": dp, "mp": sib}
        self.to_far = {"dp": dp, "mp": far}
        self.o_ref, self.mine, self.ra, self.rb, self.rc, self.sb = o_ref, mine, ra, rb, rc, sb
        rows = ra.shape[0]
        part = rows // CHUNKS
        self.spans = [pl.ds(k * part, part) for k in range(CHUNKS)]

        def slot(i, k):
            return x_ref.at[pl.ds(pl.multiple_of(i * rows + k * part, part), part)]

        def whole(i):
            return x_ref.at[pl.ds(pl.multiple_of(i * rows, rows), rows)]

        self.first, self.second, self.third = [], [], []
        for k, span in enumerate(self.spans):
            self.first.append(
                remote(slot(diag, k), ra.at[span], ssem.at[0, k], rsem.at[0, k], self.to_sib)
            )
            self.second.append(
                remote(slot(sib, k), rb.at[span], ssem.at[1, k], rsem.at[1, k], self.to_sib)
            )
            self.third.append(
                remote(sb.at[span], rc.at[span], ssem.at[2, k], rsem.at[2, k], self.to_far)
            )
        self.load0 = pltpu.make_async_copy(whole(far), mine.at[0], lsem.at[0])
        self.load1 = pltpu.make_async_copy(whole(me), mine.at[1], lsem.at[1])

    def start(self):
        self.load0.start()
        for copy in self.first:
            copy.start()
        self.load1.start()
        for copy in self.second:
            copy.start()

    def fold(self):
        self.load0.wait()
        for k, span in enumerate(self.spans):
            self.first[k].wait_recv()
            total = self.mine[0, span, :].astype(F32) + self.ra[span, :].astype(F32)
            self.sb[span, :] = total.astype(BF)
            self.third[k].start()

    def local(self):
        self.load1.wait()
        for k in range(CHUNKS):
            self.second[k].wait_recv()

    def land(self, addend=None):
        for k, span in enumerate(self.spans):
            self.third[k].wait_recv()
            total = self.mine[1, span, :].astype(F32) + self.rb[span, :].astype(F32)
            if addend is not None:
                total = total + addend[span, :]
            self.o_ref[span, :] = (total + self.rc[span, :].astype(F32)).astype(self.o_ref.dtype)

    def finish(self):
        for k in range(CHUNKS):
            self.first[k].wait_send()
            self.second[k].wait_send()
            self.third[k].wait_send()


def sum_scratch(rows, width):
    return [pltpu.VMEM((4, rows, width), BF)] + [pltpu.VMEM((rows, width), BF)] * 4 + [
        pltpu.SemaphoreType.DMA((3, CHUNKS)),
        pltpu.SemaphoreType.DMA((3, CHUNKS)),
    ]


class LocalSum:
    def __init__(self, o_ref, scratch):
        terms, ra, rb, rc, sb, ssem, rsem = scratch
        _, sib, far, _ = mp_peers()
        dp = lax.axis_index("dp")
        self.to_sib = {"dp": dp, "mp": sib}
        self.to_far = {"dp": dp, "mp": far}
        self.o_ref, self.terms, self.ra, self.rb, self.rc, self.sb = o_ref, terms, ra, rb, rc, sb
        rows = ra.shape[0]
        part = rows // CHUNKS
        self.spans = [pl.ds(k * part, part) for k in range(CHUNKS)]
        self.first, self.second, self.third = [], [], []
        for k, span in enumerate(self.spans):
            self.first.append(
                remote(terms.at[0, span], ra.at[span], ssem.at[0, k], rsem.at[0, k], self.to_sib)
            )
            self.second.append(
                remote(terms.at[2, span], rb.at[span], ssem.at[1, k], rsem.at[1, k], self.to_sib)
            )
            self.third.append(
                remote(sb.at[span], rc.at[span], ssem.at[2, k], rsem.at[2, k], self.to_far)
            )

    def put(self, step, value):
        half = value.shape[0]
        late = step // 4
        slot = (1 - late) * (step % 2) + late * (step // 2)
        row = (1 - late) * ((step // 2) % 2) + late * (step % 2)
        self.terms[slot, pl.ds(pl.multiple_of(row * half, half), half), :] = value

    def after_step(self, step):
        half = CHUNKS // 2
        for turn in range(2):
            chunks = range(turn * half, turn * half + half)

            @pl.when(step == 2 * turn)
            def _(chunks=chunks):
                for k in chunks:
                    self.first[k].start()

            @pl.when(step == 2 * turn + 1)
            def _(chunks=chunks):
                for k in chunks:
                    span = self.spans[k]
                    self.first[k].wait_recv()
                    total = self.terms[1, span, :].astype(F32) + self.ra[span, :].astype(F32)
                    self.sb[span, :] = total.astype(BF)
                    self.third[k].start()

        @pl.when(step == 5)
        def _():
            for copy in self.second:
                copy.start()

    def land(self):
        for k, span in enumerate(self.spans):
            self.second[k].wait_recv()
            self.third[k].wait_recv()
            total = self.terms[3, span, :].astype(F32) + self.rb[span, :].astype(F32)
            self.o_ref[span, :] = (total + self.rc[span, :].astype(F32)).astype(self.o_ref.dtype)

    def finish(self):
        for copy in self.first + self.second + self.third:
            copy.wait_send()


def order_block(step):
    me = lax.axis_index("mp")
    chip, core = me // 2, me % 2
    late = step // 4
    other = 1 - late
    cross = 1 - ((1 - late) * (step % 2) + late * ((step // 2) % 2))
    quarter = (chip + other - 2 * chip * other) * 2 + (core + cross - 2 * core * cross)
    return quarter * 2 + (1 - late) * ((step // 2) % 2) + late * (step % 2)


def term_quarter(slot):
    me = lax.axis_index("mp")
    chip, core = me // 2, me % 2
    other = 1 - slot // 2
    cross = 1 - slot % 2
    return (chip + other - 2 * chip * other) * 2 + (core + cross - 2 * core * cross)


def arrival_quarter(turn):
    me = lax.axis_index("mp")
    chip, core = me // 2, me % 2
    other = turn // 2
    cross = turn % 2
    return (chip + other - 2 * chip * other) * 2 + (core + cross - 2 * core * cross)


class Ring:
    def __init__(self, count):
        self.count = count
        self.half = count // 2
        me = lax.axis_index("dp")
        mp = lax.axis_index("mp")
        odd = me % 2
        self.me = me
        self.spot = (1 - odd) * (me // 2) + odd * (count - 1 - me // 2)
        self.ahead = {"dp": self.at(1), "mp": mp}
        self.behind = {"dp": self.at(-1), "mp": mp}

    def at(self, distance):
        spot = (self.spot + distance + self.count) % self.count
        late = spot // self.half
        return (1 - late) * 2 * spot + late * (2 * (self.count - 1 - spot) + 1)


def ring_scratch(rows, width, half):
    return [pltpu.VMEM((rows, width), BF), pltpu.SemaphoreType.DMA((2,))] + [
        pltpu.SemaphoreType.DMA((half, CUTS))
    ] * 4


class RingGather:
    def __init__(self, count, w_ref, o_ref, scratch, here=False):
        bounce, lsem, fs, fr, bs, br = scratch
        if here:
            bounce = w_ref
        ring = Ring(count)
        self.ahead, self.behind, self.half = ring.ahead, ring.behind, ring.half
        rows = w_ref.shape[0]

        spans = column_cuts(w_ref.shape[1])

        def slot(i):
            return o_ref.at[pl.ds(pl.multiple_of(i * rows, rows), rows)]

        last = self.half - 1

        def copies(block, hop, send, recv, device, only):
            result = {}
            for c, columns in enumerate(spans):
                if hop < last or c == only:
                    place = o_ref.at[pl.ds(pl.multiple_of(block * rows, rows), rows), columns]
                    source = w_ref.at[:, columns] if hop == 0 else place
                    result[c] = remote(source, place, send.at[hop, c], recv.at[hop, c], device)
            return result

        self.forward = []
        self.backward = []
        for hop in range(self.half):
            self.forward.append(copies(ring.at(-hop), hop, fs, fr, ring.ahead, 0))
            self.backward.append(copies(ring.at(hop), hop, bs, br, ring.behind, 1))
        self.load = None if here else pltpu.make_async_copy(w_ref, bounce, lsem.at[0])
        self.store = pltpu.make_async_copy(bounce, slot(ring.me), lsem.at[1])

    def start(self):
        for c in range(CUTS):
            self.forward[0][c].start()
            self.backward[0][c].start()
        if self.load is not None:
            self.load.start()

    def place(self):
        if self.load is not None:
            self.load.wait()
        self.store.start()

    def hop(self, hop):
        for c in range(CUTS):
            for way in (self.forward, self.backward):
                way[hop - 1][c].wait_recv()
                if c in way[hop]:
                    way[hop][c].start()

    def finish(self):
        self.forward[-1][0].wait_recv()
        self.backward[-1][1].wait_recv()
        self.store.wait()
        for copies in self.forward + self.backward:
            for copy in copies.values():
                copy.wait_send()


def ring_sum_scratch(rows, wide, half, sources):
    slots = pltpu.VMEM((half, rows, wide), BF)
    hops = pltpu.SemaphoreType.DMA((half, CUTS))
    return (
        [slots] * 4
        + [pltpu.VMEM((rows, wide), BF), pltpu.SemaphoreType.DMA((2 * half + 1, sources))]
        + [hops] * 4
    )


class RingSum:
    def __init__(self, count, sources, scratch):
        self.lf, self.lb, self.rf, self.rb, self.own, lsem, fs, fr, bs, br = scratch
        ring = Ring(count)
        self.ahead, self.behind, self.half = ring.ahead, ring.behind, ring.half
        rows = self.own.shape[0]
        self.spans = column_cuts(self.own.shape[1])

        def sends(source, target, hop, send, recv, device, only):
            return {
                c: remote(
                    source.at[hop, :, span],
                    target.at[hop, :, span],
                    send.at[hop, c],
                    recv.at[hop, c],
                    device,
                )
                for c, span in enumerate(self.spans)
                if hop > 0 or c == only
            }

        def loads(block, target, at):
            span = pl.ds(pl.multiple_of(block * rows, rows), rows)
            base, copies = 0, []
            for i, source in enumerate(sources):
                wide = source.shape[1]
                copies.append(
                    pltpu.make_async_copy(
                        source.at[span], target.at[:, pl.ds(base, wide)], lsem.at[at, i]
                    )
                )
                base += wide
            return copies

        self.forward, self.backward, self.local = [], [], []
        for hop in range(self.half):
            self.local.append(
                loads(ring.at(self.half - hop), self.lf.at[hop], 2 * hop)
                + loads(ring.at(hop - self.half), self.lb.at[hop], 2 * hop + 1)
            )
            self.forward.append(sends(self.lf, self.rf, hop, fs, fr, ring.ahead, 0))
            self.backward.append(sends(self.lb, self.rb, hop, bs, br, ring.behind, 1))
        self.local.append(loads(ring.me, self.own, 2 * self.half))

    def start(self):
        for copies in self.local:
            for copy in copies:
                copy.start()
        for copy in self.local[0]:
            copy.wait()
        self.forward[0][0].start()
        self.backward[0][1].start()
        for copy in self.local[1]:
            copy.wait()
        self.forward[1][1].start()
        self.backward[1][0].start()

    def hop(self, hop):
        if hop > 1:
            for copy in self.local[hop]:
                copy.wait()
        for c, span in enumerate(self.spans):
            for way, mine, came in (
                (self.forward, self.lf, self.rf),
                (self.backward, self.lb, self.rb),
            ):
                if c in way[hop - 1]:
                    way[hop - 1][c].wait_recv()
                    total = mine[hop, :, span].astype(F32) + came[hop - 1, :, span].astype(F32)
                    mine[hop, :, span] = total.astype(BF)
                    way[hop][c].start()

    def finish(self, outs):
        last = self.half - 1
        for copy in self.local[self.half]:
            copy.wait()
        for c in range(CUTS):
            self.forward[last][c].wait_recv()
            self.backward[last][c].wait_recv()
        base = 0
        for out in outs:
            span = slice(base, base + out.shape[1])
            base += out.shape[1]
            out[...] = (
                self.own[:, span].astype(F32)
                + self.rf[last, :, span].astype(F32)
                + self.rb[last, :, span].astype(F32)
            )
        for copies in self.forward + self.backward:
            for copy in copies.values():
                copy.wait_send()


HEAD = 6


def head_kernel(count, f_ref, g_ref, gains_ref, hot_ref, *refs):
    mats, glu = refs[:HEAD], refs[HEAD : HEAD + 3]
    fo_ref, go_ref, wo_ref = refs[HEAD + 3 : HEAD + 6]
    shares = refs[HEAD + 6 : HEAD + 9]
    scratch = refs[HEAD + 9 :]
    pack, held, psem, hsem, osem = scratch[:5]
    job = Gather(f_ref, fo_ref, scratch[5:9])
    late = Gather(g_ref, go_ref, scratch[9:13])
    ring = RingGather(count, pack, wo_ref, scratch[13:], here=True)
    width = mats[0].shape[1]
    side = 4 * width
    loads = []
    for i, mat in enumerate(mats):
        base = i * width if i < 4 else i * width + 128
        loads.append(pltpu.make_async_copy(mat, pack.at[:, pl.ds(base, width)], psem.at[i]))
    fetch = [pltpu.make_async_copy(mat, held.at[i], hsem.at[i]) for i, mat in enumerate(glu)]
    unit = held.shape[2] // len(shares)
    stores = []
    for at, share in enumerate(shares):
        for i in range(3):
            stores.append(
                pltpu.make_async_copy(
                    held.at[i, :, pl.ds(at * unit, unit)],
                    share.at[:, pl.ds(i * unit, unit)],
                    osem.at[at, i],
                )
            )
    for copy in loads + fetch:
        copy.start()
    greet([job.to_sib, job.to_far, ring.ahead, ring.behind])
    job.start()
    dims = (8, 128)
    pick = lax.broadcasted_iota(jnp.int32, dims, 0) == lanes(dims)
    columns = dot(gains_ref[...], jnp.where(pick, 1.0, 0.0).astype(BF), TN)
    pack[:, side : side + 128] = (columns + hot_ref[...]).astype(BF)
    for copy in loads:
        copy.wait()
    ring.start()
    ring.place()
    for copy in fetch:
        copy.wait()
    for copy in stores:
        copy.start()
    ring.hop(1)
    for k in range(CHUNKS):
        job.forward(k)
    late.start()
    for hop in range(2, ring.half):
        ring.hop(hop)
    for k in range(CHUNKS):
        late.forward(k)
    job.finish()
    late.finish()
    ring.finish()
    for copy in stores:
        copy.wait()


def head_gather(frames, grads, gains, hot, mats, glu, parts, count):
    rows, width = frames.shape
    own = mats[0].shape[0]
    columns = len(mats) * mats[0].shape[1] + 128
    hidden = glu[0].shape[1]
    wide = shape_of((4 * rows, width), BF)
    vmem = pl.BlockSpec(memory_space=pltpu.VMEM)
    return pl.pallas_call(
        functools.partial(head_kernel, count),
        out_shape=(wide, wide, shape_of((count * own, columns), BF))
        + (shape_of((own, 3 * hidden // parts), BF),) * parts,
        in_specs=[ANY, ANY, vmem, vmem] + [ANY] * (len(mats) + 3),
        out_specs=(ANY,) * (3 + parts),
        scratch_shapes=[
            pltpu.VMEM((own, columns), BF),
            pltpu.VMEM((3, own, hidden), BF),
            pltpu.SemaphoreType.DMA((len(mats),)),
            pltpu.SemaphoreType.DMA((3,)),
            pltpu.SemaphoreType.DMA((parts, 3)),
        ]
        + gather_scratch(rows, width) * 2
        + ring_scratch(16, 128, count // 2),
        compiler_params=local_params(collective_id=0, has_side_effects=True),
        cost_estimate=BUSY,
        name="head_gather",
    )(frames, grads, gains, hot, *mats, *glu)


SMALL = 16


def tail_kernel(
    count, buckets, q_ref, k_ref, v_ref, fa_ref, wq_ref, wk_ref, wv_ref,
    a_ref, f_ref, c_ref, g_ref, dg_ref, hot_ref, r_ref, k0_ref, v0_ref,
    o_ref, s_ref, w_ref, *scratch,
):
    total, held = scratch[0:2]
    job = LocalSum(total, scratch[2:9])
    ring = RingSum(count, [a_ref], scratch[9:19])
    sent, got, ss, rs = scratch[19:]
    step = pl.program_id(0)
    me = lax.axis_index("dp")
    mp = lax.axis_index("mp")
    partners = [job.to_sib, job.to_far]
    bit = 1
    while bit < count:
        partners.append({"dp": me + bit * (1 - 2 * ((me // bit) % 2)), "mp": mp})
        bit *= 2
    @pl.when(step == 0)
    def _():
        greet(partners + [ring.ahead, ring.behind])
        ring.start()
        held[...] = jnp.zeros_like(held)

    @pl.when(step < 8)
    def _():
        term = (
            dot(q_ref[...], wq_ref[...], NT)
            + dot(k_ref[...], wk_ref[...], NT)
            + dot(v_ref[...], wv_ref[...], NT)
        )
        job.put(step, term.astype(BF))

    job.after_step(step)

    @pl.when((step >= 8) & (step < 12))
    def _():
        unit, _ = norm_rows(fa_ref[...].astype(F32))
        part = jnp.sum(unit * job.terms[step - 8].astype(F32), axis=0, keepdims=True)
        held[buckets : buckets + 1, :] += part

    @pl.when(step == 8)
    def _():
        edge = dot(k0_ref[...].astype(BF), wk_ref[...], NT) + dot(
            v0_ref[...].astype(BF), wv_ref[...], NT
        )
        unit, spread = norm_rows(bucket_row(hot_ref[...], r_ref[...]))
        edge_back, edge_part = norm_back(edge[0:1, :], unit, spread, g_ref[0:1, :])
        place = lax.broadcasted_iota(jnp.int32, held.shape, 0)
        held[...] += (
            bucket_column(hot_ref[...], SMALL) * edge_back
            + jnp.where(place == buckets, edge_part, 0.0)
            + jnp.where(place == buckets + 1, dg_ref[1:2, :], 0.0)
            + jnp.where(place == buckets + 2, dg_ref[2:3, :], 0.0)
        )
        for hop in range(2, ring.half - 1):
            ring.hop(hop)

    @pl.when(step == 4)
    def _():
        ring.hop(1)

    @pl.when(step == 11)
    def _():
        ring.hop(ring.half - 1)

    @pl.when(step == 12)
    def _():
        copies = [
            remote(sent.at[i], got.at[i], ss.at[i], rs.at[i], partner)
            for i, partner in enumerate(partners)
        ]
        sent[0] = held[...]
        copies[0].start()
        for i, copy in enumerate(copies):
            copy.wait_recv()
            held[...] += got[i]
            if i + 1 < len(copies):
                sent[i + 1] = held[...]
                copies[i + 1].start()
        job.land()
        unit, spread = norm_rows(f_ref[...].astype(F32))
        back, _ = norm_back(total[...], unit, spread, g_ref[0:1, :])
        o_ref[...] = c_ref[...] + back
        for copy in copies:
            copy.wait_send()
        s_ref[...] = held[...]
        ring.finish([w_ref])
        job.finish()


def tail_sums(
    count, buckets, grads_qkv, frames_all, weights, grads, frames, carried, gains, grad_gains, hot,
    table_rows, dk0, dv0,
):
    share, model = frames.shape
    width = grads_qkv[0].shape[1]
    block = 2 * share // 4
    rows = grads.shape[0] // count
    wide = grads.shape[1]
    half = count // 2
    steps = 2 + (count - 1).bit_length()
    once = pl.Buffered(1)

    def full(array):
        return pl.BlockSpec(array.shape, lambda i: (0,) * array.ndim, pipeline_mode=once)

    small = pltpu.VMEM((steps, SMALL, model), F32)
    out_shape = (
        shape_of((share, model), F32),
        shape_of((SMALL, model), F32),
        shape_of((rows, wide), F32),
    )
    whole = [frames, carried, gains, grad_gains, hot, table_rows, dk0, dv0]
    return pl.pallas_call(
        functools.partial(tail_kernel, count, buckets),
        grid=(13,),
        out_shape=out_shape,
        in_specs=[
            pl.BlockSpec((block, width), lambda i: (order_block(jnp.minimum(i, 7)), 0))
            for _ in range(3)
        ]
        + [pl.BlockSpec((share, model), lambda i: (term_quarter(jnp.clip(i - 8, 0, 3)), 0))]
        + [
            pl.BlockSpec(
                (model, width), functools.partial(lambda at, i: (0, at), at), pipeline_mode=once
            )
            for at in range(3)
        ]
        + [ANY]
        + [full(array) for array in whole],
        out_specs=tuple(pl.BlockSpec(out.shape, lambda i: (0, 0)) for out in out_shape),
        scratch_shapes=[pltpu.VMEM((share, model), F32), pltpu.VMEM((SMALL, model), F32)]
        + sum_scratch(share, model)
        + ring_sum_scratch(rows, wide, half, 1)
        + [small, small, pltpu.SemaphoreType.DMA((steps,)), pltpu.SemaphoreType.DMA((steps,))],
        compiler_params=local_params(collective_id=6, has_side_effects=True),
        cost_estimate=BUSY,
        name="tail_sums",
    )(*grads_qkv, frames_all, weights, weights, weights, grads, *whole)


def out_kernel(
    count, m_ref, w_ref, p_ref, wp_ref, share_ref, o_ref, kvo_ref, full_ref, mine, *scratch
):
    side = Gather(mine, kvo_ref, scratch[:4], here=True)
    job = LocalSum(o_ref, scratch[4:11])
    ring = RingGather(count, share_ref, full_ref, scratch[11:])
    step = pl.program_id(0)

    @pl.when(step == 0)
    def _():
        greet([job.to_sib, job.to_far, ring.ahead, ring.behind])
        ring.start()

    job.put(step, dot(m_ref[...], w_ref[...], NT).astype(BF))
    job.after_step(step)

    @pl.when(step == 1)
    def _():
        mine[...] = dot(p_ref[...], wp_ref[...], NN).astype(BF)
        side.start()
        ring.place()

    @pl.when(step == 7)
    def _():
        for hop in range(1, ring.half):
            ring.hop(hop)
        for k in range(CHUNKS):
            side.forward(k)
        job.land()
        side.finish()
        job.finish()
        ring.finish()


def out_project(mixed, weights, column, prompts, prompt_weights, weight_share, count):
    length, width = mixed.shape
    model = weights.shape[0]
    rows = length // 8
    share = length // 4
    short = prompts.shape[0]
    once = pl.Buffered(1)
    return pl.pallas_call(
        functools.partial(out_kernel, count),
        grid=(8,),
        out_shape=(
            shape_of((share, model), F32),
            shape_of((4 * short, width), BF),
            shape_of((count * weight_share.shape[0], weight_share.shape[1]), BF),
        ),
        in_specs=[
            pl.BlockSpec((rows, width), lambda i: (order_block(i), 0)),
            pl.BlockSpec((model, width), lambda i: (0, column), pipeline_mode=once),
            pl.BlockSpec(prompts.shape, lambda i: (0, 0), pipeline_mode=once),
            pl.BlockSpec((model, width), lambda i: (0, 0), pipeline_mode=once),
            ANY,
        ],
        out_specs=(pl.BlockSpec((share, model), lambda i: (0, 0)), ANY, ANY),
        scratch_shapes=[pltpu.VMEM((short, width), BF)]
        + gather_scratch(16, 128)
        + sum_scratch(share, model)
        + ring_scratch(*weight_share.shape, count // 2),
        compiler_params=local_params(collective_id=1, has_side_effects=True),
        cost_estimate=BUSY,
        name="out_project",
    )(mixed, weights, prompts, prompt_weights, weight_share)


def glu_back_kernel(parts, count, d0_ref, d1_ref, h0_ref, h1_ref, *refs):
    weights = refs[:count]
    o_ref, t0_ref, t1_ref = refs[count : count + 3]
    job = LocalSum(o_ref, refs[count + 3 :])
    step = pl.program_id(0)

    def gate_up():
        term = None
        for left, group in zip((d0_ref, d1_ref), parts):
            base = 0
            for index, low, size in group:
                w_ref = weights[index]
                width = w_ref.shape[1] // 3
                if size == width:
                    part = dot(left[:, base : base + 2 * size], w_ref[:, : 2 * size], NT)
                else:
                    high = low + size
                    part = dot(left[:, base : base + size], w_ref[:, low:high], NT) + dot(
                        left[:, base + size : base + 2 * size],
                        w_ref[:, width + low : width + high],
                        NT,
                    )
                term = part if term is None else term + part
                base += 2 * size
        return term.astype(BF)

    def down():
        term = None
        for left, group in zip((h0_ref, h1_ref), parts):
            base = 0
            for index, low, size in group:
                w_ref = weights[index]
                start = 2 * w_ref.shape[1] // 3 + low
                part = dot(left[:, base : base + size], w_ref[:, start : start + size], NT)
                term = part if term is None else term + part
                base += size
        return term.astype(BF)

    @pl.when(step == 0)
    def _():
        greet([job.to_sib, job.to_far])

    @pl.when(step < 8)
    def _():
        job.put(step, gate_up())

    job.after_step(step)

    @pl.when(step >= 8)
    def _():
        term = down()
        half = t0_ref.shape[1]
        t0_ref[...] = term[:, :half]
        t1_ref[...] = term[:, half:]

    @pl.when(step == 15)
    def _():
        job.land()
        job.finish()


def glu_back(dgus, hiddens, weights, parts):
    length = dgus[0].shape[0]
    model = weights[0].shape[0]
    rows = length // 8
    share = length // 4
    once = pl.Buffered(1)
    early = lambda i: (order_block(jnp.minimum(i, 7)), 0)
    late = lambda i: (jnp.maximum(i - 8, 0), 0)
    in_specs = [pl.BlockSpec((rows, d.shape[1]), early) for d in dgus]
    in_specs += [pl.BlockSpec((rows, h.shape[1]), late) for h in hiddens]
    for weight in weights:
        in_specs.append(pl.BlockSpec(weight.shape, lambda i: (0, 0), pipeline_mode=once))
    half = pl.BlockSpec((rows, model // 2), late)
    return pl.pallas_call(
        functools.partial(glu_back_kernel, parts, len(weights)),
        grid=(16,),
        out_shape=(
            shape_of((share, model), F32),
            shape_of((length, model // 2), BF),
            shape_of((length, model // 2), BF),
        ),
        in_specs=in_specs,
        out_specs=(
            pl.BlockSpec((share, model), lambda i: (0, 0)),
            half,
            half,
        ),
        scratch_shapes=sum_scratch(share, model),
        compiler_params=local_params(collective_id=3, has_side_effects=True),
        cost_estimate=BUSY,
        name="glu_back",
    )(*dgus, *hiddens, *weights)


def mid_kernel(
    count, c_ref, t_ref, n_ref, cb_ref, q_ref, cm_ref, w_ref, m_ref, p_ref, y_ref,
    x_ref, g_ref, dw_ref, yo_ref, s_ref, slots, total, ssem, rsem, *scratch,
):
    small = Scatter(t_ref, s_ref, scratch[:8])
    ring = RingSum(count, [y_ref], scratch[8:])
    me, sib, far, diag = mp_peers()
    dp = lax.axis_index("dp")
    to_sib = {"dp": dp, "mp": sib}
    to_far = {"dp": dp, "mp": far}
    step = pl.program_id(0)
    rows = c_ref.shape[0]
    part = rows // CHUNKS
    spans = [pl.ds(k * part, part) for k in range(CHUNKS)]
    beside = remote(c_ref, slots.at[0], ssem.at[0], rsem.at[0], to_sib)
    across = [
        remote(c_ref.at[span], slots.at[1, span], ssem.at[1 + k], rsem.at[1 + k], to_far)
        for k, span in enumerate(spans)
    ]
    onward = [
        remote(
            slots.at[1, span],
            slots.at[2, span],
            ssem.at[1 + CHUNKS + k],
            rsem.at[1 + CHUNKS + k],
            to_sib,
        )
        for k, span in enumerate(spans)
    ]

    @pl.when(step == 0)
    def _():
        greet([to_sib, to_far, ring.ahead, ring.behind])
        for copy in across:
            copy.start()
        small.start()
        beside.start()
        ring.start()

    @pl.when(step == 6)
    def _():
        for hop in range(1, ring.half // 2):
            ring.hop(hop)

    @pl.when(step == 1)
    def _():
        small.fold()
        small.local()

    @pl.when(step < 8)
    def _():
        width = q_ref.shape[1]
        x_ref[:, :width] = dot(n_ref[...], q_ref[...], TN).astype(BF)
        x_ref[:, width:] = dot(cb_ref[...], cm_ref[...], TN).astype(BF)

    def use(grads):
        g_ref[...] = dot(grads, w_ref[...], NN).astype(BF)
        return dot(grads, m_ref[...], TN)

    @pl.when(step == 8)
    def _():
        total[...] = use(c_ref[...])

    @pl.when(step == 9)
    def _():
        beside.wait_recv()
        total[...] += use(slots[0])

    @pl.when(step == 10)
    def _():
        ring.hop(ring.half // 2)
        small.land()
        for k in range(CHUNKS):
            across[k].wait_recv()
            onward[k].start()
        for hop in range(ring.half // 2 + 1, ring.half):
            ring.hop(hop)
        total[...] += use(slots[1])

    @pl.when(step == 11)
    def _():
        for copy in onward:
            copy.wait_recv()
        width = m_ref.shape[1]
        dw_ref[:, :width] = (total[...] + use(slots[2])).astype(BF)
        dw_ref[:, width:] = dot(p_ref[...], s_ref[...].astype(BF), TN).astype(BF)
        small.finish()
        ring.finish([yo_ref])
        beside.wait_send()
        for copy in across + onward:
            copy.wait_send()


def mid_gather(
    carried, term, normed, cross_back, grad_cq, cross_mixed, weights, column, mixed, prompts,
    more, groups, count,
):
    share, model = carried.shape
    own = more.shape[0] // count
    length, width = mixed.shape
    short, narrow = term.shape[0] // 4, term.shape[1]
    tile = 2 * model // 4
    once = pl.Buffered(1)
    fixed = pl.BlockSpec((share, model), lambda i: (0, 0), pipeline_mode=once)
    left = pl.BlockSpec((share, tile), lambda i: (0, jnp.minimum(i, 7) % 2))
    right = pl.BlockSpec((share, width), lambda i: (0, jnp.minimum(i, 7) // 2))

    def turn(i):
        return (arrival_quarter(jnp.maximum(i - 8, 0)), 0)

    return pl.pallas_call(
        functools.partial(mid_kernel, count),
        grid=(12,),
        in_specs=[
            fixed,
            ANY,
            left,
            left,
            right,
            right,
            pl.BlockSpec((model, width), lambda i: (0, column), pipeline_mode=once),
            pl.BlockSpec((share, width), turn),
            pl.BlockSpec(prompts.shape, lambda i: (0, 0), pipeline_mode=once),
            ANY,
        ],
        out_specs=(
            pl.BlockSpec((tile, 2 * width), lambda i: (jnp.minimum(i, 7), 0)),
            pl.BlockSpec((share, width), turn),
            pl.BlockSpec((model, 2 * width), lambda i: (0, 0)),
            pl.BlockSpec((own, more.shape[1]), lambda i: (0, 0)),
        ),
        out_shape=(
            shape_of((groups * model, 2 * width), BF),
            shape_of((length, width), BF),
            shape_of((model, 2 * width), BF),
            shape_of((own, more.shape[1]), F32),
        ),
        scratch_shapes=[
            pltpu.VMEM((short, narrow), F32),
            pltpu.VMEM((3, share, model), BF),
            pltpu.VMEM((model, width), F32),
            pltpu.SemaphoreType.DMA((1 + 2 * CHUNKS,)),
            pltpu.SemaphoreType.DMA((1 + 2 * CHUNKS,)),
        ]
        + scatter_scratch(short, narrow)
        + ring_sum_scratch(own, more.shape[1], count // 2, 1),
        compiler_params=local_params(collective_id=4, has_side_effects=True),
        cost_estimate=BUSY,
        name="mid_gather",
    )(carried, term, normed, cross_back, grad_cq, cross_mixed, weights, mixed, prompts, more)


def qkv_kernel(
    scale, x_ref, s_ref, r_ref, hot_ref, w_ref, c_ref, u_ref, l_ref,
    n_ref, q_ref, k_ref, v_ref, g_ref, sw_ref, nc_ref, k0_ref, v0_ref,
):
    width = q_ref.shape[1]

    @pl.when(pl.program_id(0) == 0)
    def _():
        side = s_ref[...]
        dims = (8, side.shape[1])
        pick = lax.broadcasted_iota(jnp.int32, dims, 0) == lanes(dims)
        g_ref[...] = dot(jnp.where(pick, 1.0, 0.0).astype(BF), side, NT)
        totals = dot(jnp.ones((8, side.shape[0]), BF), side, NN)
        sw_ref[...] = jnp.broadcast_to(
            scale / jnp.sum(totals * hot_ref[...], axis=1, keepdims=True), sw_ref.shape
        )
        unit, _ = norm_rows(bucket_row(hot_ref[...], r_ref[...]))
        normed = jnp.broadcast_to(unit * g_ref[0:1, :], nc_ref.shape).astype(BF)
        nc_ref[...] = normed
        out = dot(normed, w_ref[:, width:], NN).astype(BF)
        k0_ref[...] = out[:, :width]
        v0_ref[...] = out[:, width:]

    unit, _ = norm_rows(x_ref[...].astype(F32))
    normed = (unit * g_ref[0:1, :]).astype(BF)
    n_ref[...] = normed
    out = dot(normed, w_ref[...], NN)
    cosine, upper, lower = c_ref[...], u_ref[...], l_ref[...]
    for pair in range(width // 128):
        span = slice(128 * pair, 128 * pair + 128)
        q_ref[:, span] = (rope(out[:, span], cosine, upper, lower) * (LOG2E / 8.0)).astype(BF)
        keys = out[:, width + 128 * pair : width + 128 * pair + 128]
        k_ref[:, span] = rope(keys, cosine, upper, lower).astype(BF)
    v_ref[...] = out[:, 2 * width : 3 * width].astype(BF)


def qkv_project(frames, table_rows, hot, weights, tables, width, scale):
    length, model = frames.shape
    rows = 256
    block = pl.BlockSpec((rows, model), lambda i: (i, 0))
    table = pl.BlockSpec((rows, 128), lambda i: (i, 0))
    head = pl.BlockSpec((rows, width), lambda i: (i, 0))
    fixed = lambda i: (0, 0)
    extra = [
        shape_of((8, model), F32),
        shape_of((8, 128), F32),
        shape_of((16, model), BF),
        shape_of((16, width), BF),
        shape_of((16, width), BF),
    ]
    return pl.pallas_call(
        functools.partial(qkv_kernel, scale),
        grid=(length // rows,),
        in_specs=[
            block,
            pl.BlockSpec((model, 128), lambda i: (0, 4 * width // 128)),
            pl.BlockSpec(table_rows.shape, fixed),
            pl.BlockSpec(hot.shape, fixed),
            pl.BlockSpec((model, 3 * width), fixed),
            table,
            table,
            table,
        ],
        out_specs=[block, head, head, head] + [pl.BlockSpec(e.shape, fixed) for e in extra],
        out_shape=[shape_of((length, model), BF)] + [shape_of((length, width), BF)] * 3 + extra,
        compiler_params=local_params(),
        cost_estimate=cost(6 * length * model * width, 8 * length * model),
        name="qkv_project",
    )(frames, weights, table_rows, hot, weights, *tables)


def attend_kernel(
    bk, first, count, q_ref, k_ref, v_ref, k0_ref, v0_ref, x_ref, w_ref, y_ref,
    o_ref, aug_ref, xo_ref, wo_ref, yo_ref, vaug, *scratch,
):
    length = k_ref.shape[0]
    bq = q_ref.shape[0]
    step = pl.program_id(0) * pl.num_programs(1) + pl.program_id(1)
    wide = xo_ref.shape[1]
    job = Gather(x_ref, xo_ref, scratch[:4], pl.ds(first, wide))
    ring = RingGather(count, w_ref, wo_ref, scratch[4:10])
    wide_ring = RingGather(count, y_ref, yo_ref, scratch[10:])
    last = pl.num_programs(0) * pl.num_programs(1) - 1

    @pl.when(step == 0)
    def _():
        greet([job.to_sib, job.to_far, ring.ahead, ring.behind])
        ring.start()
        wide_ring.start()
        job.start()
        ring.place()
        wide_ring.place()

    for hop in range(1, ring.half):

        @pl.when(step == min(3 * hop, 11))
        def _(hop=hop):
            ring.hop(hop)

        @pl.when(step == min(1 + 3 * hop, 11))
        def _(hop=hop):
            wide_ring.hop(hop)

    @pl.when(pl.program_id(1) == 0)
    def _():
        vaug[:, :128] = v_ref[...]
        vaug[:, 128:] = jnp.ones((length, 128), BF)

    queries = q_ref[...]
    key0 = k0_ref[0:1, :].astype(F32)
    value0 = v0_ref[0:1, :].astype(F32)
    outs = []
    logs = []
    for head in range(2):
        masked = half_mask(queries, head)
        peak = jnp.sum(masked.astype(F32) * key0, axis=1, keepdims=True)
        total = jnp.concatenate(
            [jnp.broadcast_to(value0, (bq, 128)), jnp.ones((bq, 128), F32)], 1
        )
        for block in range(length // bk):
            span = slice(block * bk, (block + 1) * bk)
            scores = dot(masked, k_ref[span, :], NT)
            higher = jnp.maximum(peak, jnp.max(scores, axis=1, keepdims=True))
            exponent = jnp.exp2(scores - higher).astype(BF)
            total = total * jnp.exp2(peak - higher) + dot(exponent, vaug[span, :], NN)
            peak = higher
        weight = total[:, 128:129]
        outs.append(total[:, :128] * (1.0 / weight))
        logs.append(-(peak + jnp.log2(weight)))
    lane = lanes((bq, 128))
    o_ref[...] = jnp.where(lane < HD, outs[0], outs[1]).astype(BF)
    aug_ref[...] = (pieces(logs[0], (bq, 128), 0) + pieces(logs[1], (bq, 128), HD)).astype(BF)

    @pl.when(step == last)
    def _():
        for k in range(CHUNKS):
            job.forward(k)
        job.finish()
        ring.finish()
        wide_ring.finish()


def attend(
    queries, keys, values, key0, value0, packed, first, share, more, count, bq=512, bk=1024
):
    length, width = queries.shape
    row = pl.BlockSpec((bq, 128), lambda p, i: (i, p))
    full = pl.BlockSpec((length, 128), lambda p, i: (0, p))
    zero = pl.BlockSpec((16, 128), lambda p, i: (0, p))
    return pl.pallas_call(
        functools.partial(attend_kernel, bk, first, count),
        grid=(width // 128, length // bq),
        in_specs=[row, full, full, zero, zero, ANY, ANY, ANY],
        out_specs=[row, row, ANY, ANY, ANY],
        out_shape=[shape_of((length, width), BF)] * 2
        + [
            shape_of((4 * packed.shape[0], 2 * width), BF),
            shape_of((count * share.shape[0], share.shape[1]), BF),
            shape_of((count * more.shape[0], more.shape[1]), BF),
        ],
        scratch_shapes=[pltpu.VMEM((length, 256), BF)]
        + gather_scratch(packed.shape[0], 2 * width)
        + ring_scratch(*share.shape, count // 2)
        + ring_scratch(*more.shape, count // 2),
        compiler_params=local_params(collective_id=7, has_side_effects=True),
        cost_estimate=cost(16 * length * length * width, 10 * length * width),
        name="attend",
    )(queries, keys, values, key0, value0, packed, share, more)


def attend_back_kernel(
    bk, count, q_ref, aug_ref, o_ref, do_ref, k_ref, v_ref, k0_ref, v0_ref,
    cq_ref, uq_ref, lq_ref, ck_ref, uk_ref, lk_ref,
    x_ref, y_ref, t_ref, ac_ref, dq_ref, dk_ref, dv_ref, dk0_ref, dv0_ref, xh_ref,
    yo_ref, zo_ref,
    to_ref, xo0_ref, xo1_ref, kaug, vaug, kt, dka, dva, xs, xsem, *scratch,
):
    length = k_ref.shape[0]
    bq = q_ref.shape[0]
    step = pl.program_id(1)
    turn = pl.program_id(0) * pl.num_programs(1) + step
    job = Scatter(x_ref, xs, scratch[:8])
    late = Scatter(t_ref, to_ref, scratch[8:16])
    ring = RingSum(count, [y_ref], scratch[16:26])
    next_ring = RingSum(count, [xh_ref], scratch[26:])
    keep = pltpu.make_async_copy(xs, xh_ref, xsem)

    @pl.when(turn == 0)
    def _():
        greet([job.to_sib, job.to_far, ring.ahead, ring.behind])
        job.start()
        ring.start()

    @pl.when(turn == 1)
    def _():
        job.fold()
        job.local()
        late.start()

    for hop in range(1, ring.half):

        @pl.when(turn == min(1 + 2 * hop, 7))
        def _(hop=hop):
            ring.hop(hop)

        @pl.when(turn == min(8 + hop, 11))
        def _(hop=hop):
            next_ring.hop(hop)

    @pl.when(turn == 8)
    def _():
        job.land()
        keep.start()
        late.fold()
        late.local()
        keep.wait()
        next_ring.start()
        job.finish()
        ring.finish([yo_ref, zo_ref])

    @pl.when(step == 0)
    def _():
        lane = lanes((length, 128))
        ones = jnp.where((lane % HD) < 3, 1.0, 0.0).astype(BF)
        kaug[:, :128] = k_ref[...]
        kaug[:, 128:] = ones
        vaug[:, :128] = v_ref[...]
        vaug[:, 128:] = ones
        kt[...] = k_ref[...].astype(F32).T.astype(BF)
        dka[...] = jnp.zeros_like(dka)
        dva[...] = jnp.zeros_like(dva)
        dk0_ref[...] = jnp.zeros_like(dk0_ref)
        dv0_ref[...] = jnp.zeros_like(dv0_ref)

    queries = q_ref[...]
    grads = do_ref[...]
    aug = aug_ref[...]
    product = grads.astype(F32) * o_ref[...].astype(F32)
    lane = lanes((bq, 128))
    ones0 = jnp.where((lanes((16, 128)) % HD) < 3, 1.0, 0.0).astype(BF)
    key0 = jnp.concatenate([k0_ref[...], ones0], 1)
    value0 = jnp.concatenate([v0_ref[...], ones0], 1)
    row0 = lax.broadcasted_iota(jnp.int32, (16, bq), 0) == 0
    qa, da, qm, dm, dq = [], [], [], [], []
    for head in range(2):
        qm.append(half_mask(queries, head))
        dm.append(half_mask(grads, head))
        mine = (lane < HD) if head == 0 else (lane >= HD)
        inner = jnp.sum(jnp.where(mine, product, 0.0), axis=1, keepdims=True)
        qa.append(jnp.concatenate([qm[head], half_mask(aug, head)], 1))
        da.append(
            jnp.concatenate([dm[head], pieces(-inner, (bq, 128), HD * head).astype(BF)], 1)
        )
        prob0 = jnp.where(row0, jnp.exp2(dot(key0, qa[head], NT)), 0.0)
        ds0 = (prob0 * dot(value0, da[head], NT)).astype(BF)
        dv0_ref[...] += dot(prob0.astype(BF), dm[head], NN)
        dk0_ref[...] += dot(ds0, qm[head], NN)
        dq.append(dot(k0_ref[:, HD * head : HD * head + HD], ds0, TN))
    for block in range(length // bk):
        span = slice(block * bk, (block + 1) * bk)
        for head in range(2):
            probs = jnp.exp2(dot(kaug[span, :], qa[head], NT))
            ds = (probs * dot(vaug[span, :], da[head], NT)).astype(BF)
            dva[span, :] += dot(probs.astype(BF), dm[head], NN)
            dka[span, :] += dot(ds, qm[head], NN)
            dq[head] = dq[head] + dot(kt[HD * head : HD * head + HD, span], ds, NN)
    grad_q = jnp.concatenate(dq, 0).T * 0.125
    dq_ref[...] = rope(grad_q, cq_ref[...], -uq_ref[...], -lq_ref[...]).astype(BF)

    @pl.when(turn == pl.num_programs(0) * pl.num_programs(1) - 1)
    def _():
        late.land(ac_ref)
        late.finish()
        next_ring.finish([xo0_ref, xo1_ref])

    @pl.when(step == pl.num_programs(1) - 1)
    def _():
        grad_k = dka[...] * (1.0 / LOG2E)
        dk_ref[...] = rope(grad_k, ck_ref[...], -uk_ref[...], -lk_ref[...]).astype(BF)
        dv_ref[...] = dva[...].astype(BF)
        dk0_ref[...] = dk0_ref[...] * (1.0 / LOG2E)


def attend_back(
    queries, aug, mixed, grads, keys, values, key0, value0, tables, extra, more, term, after_cross, count,
    bq=512, bk=512,
):
    length, width = queries.shape
    row = pl.BlockSpec((bq, 128), lambda p, i: (i, p))
    full = pl.BlockSpec((length, 128), lambda p, i: (0, p))
    zero = pl.BlockSpec((16, 128), lambda p, i: (0, p))
    tq = pl.BlockSpec((bq, 128), lambda p, i: (i, 0))
    tk = pl.BlockSpec((length, 128), lambda p, i: (0, 0), pipeline_mode=pl.Buffered(1))
    own = more.shape[0] // count
    owned = pl.BlockSpec((own, more.shape[1] // 2), lambda p, i: (0, 0))
    wide, narrow = extra.shape[0] // 4, extra.shape[1]
    half_shape = (after_cross.shape[0], term.shape[1])
    share_spec = pl.BlockSpec(half_shape, lambda p, i: (0, 0))
    part = pl.BlockSpec((own, narrow // 2), lambda p, i: (0, 0))
    big = shape_of((length, width), BF)
    small = shape_of((16, width), F32)
    return pl.pallas_call(
        functools.partial(attend_back_kernel, bk, count),
        grid=(width // 128, length // bq),
        in_specs=[row, row, row, row, full, full, zero, zero, tq, tq, tq, tk, tk, tk, ANY, ANY, ANY,
            pl.BlockSpec(half_shape, lambda p, i: (0, 1), pipeline_mode=pl.Buffered(1)),
        ],
        out_specs=[row, full, full, zero, zero, ANY, owned, owned, share_spec, part, part],
        out_shape=[big, big, big, small, small]
        + [
            shape_of((wide, narrow), BF),
            shape_of((own, more.shape[1] // 2), F32),
            shape_of((own, more.shape[1] // 2), F32),
            shape_of(half_shape, BF),
            shape_of((own, narrow // 2), F32),
            shape_of((own, narrow // 2), F32),
        ],
        scratch_shapes=[pltpu.VMEM((length, 256), BF)] * 2
        + [pltpu.VMEM((128, length), BF)]
        + [pltpu.VMEM((length, 128), F32)] * 2
        + [
            pltpu.VMEM((wide, narrow), BF),
            pltpu.SemaphoreType.DMA(()),
        ]
        + scatter_scratch(wide, narrow)
        + scatter_scratch(*half_shape)
        + ring_sum_scratch(own, more.shape[1], count // 2, 1)
        + ring_sum_scratch(own, narrow, count // 2, 1),
        compiler_params=local_params(collective_id=8, has_side_effects=True),
        cost_estimate=cost(40 * length * length * width, 20 * length * width),
        name="attend_back",
    )(queries, aug, mixed, grads, keys, values, key0, value0, *tables, *tables, extra, more, term, after_cross)


def softmax_keys(scores, length):
    key = lax.broadcasted_iota(jnp.int32, scores.shape, 0)
    masked = jnp.where(key < length, scores, -1e9)
    exponent = jnp.exp2(masked - jnp.max(masked, axis=0, keepdims=True))
    return exponent * (1.0 / jnp.sum(exponent, axis=0, keepdims=True))


def two_heads(values):
    return jnp.concatenate([half_mask(values, 0), half_mask(values, 1)], 0)


def one_row(values):
    rows = values.shape[0] // 2
    lane = lanes((rows, 128))
    return jnp.where(lane < HD, values[:rows], values[rows:])


def cross_kernel(
    count, len_ref, f_ref, s_ref, g_ref, wq_ref, wo_ref, kv_ref, share_ref,
    as_ref, n2_ref, q_ref, m_ref, ac_ref, n3_ref, full_ref, mine, *scratch,
):
    job = Gather(mine, n3_ref, scratch[:4], here=True)
    ring = RingGather(count, share_ref, full_ref, scratch[4:])
    step = pl.program_id(0)
    groups, model, width = wq_ref.shape
    keys = kv_ref.shape[1] // 2

    @pl.when(step == 0)
    def _():
        greet([job.to_sib, job.to_far, ring.ahead, ring.behind])
        ring.start()

    after_self = f_ref[...].astype(F32) + s_ref[...]
    as_ref[...] = after_self
    unit, _ = norm_rows(after_self)
    normed = (unit * g_ref[1:2, :]).astype(BF)
    n2_ref[...] = normed
    rows = normed.shape[0]
    total = after_self
    for group in range(groups):
        queries = (dot(normed, wq_ref[group], NN) * (LOG2E / 8.0)).astype(BF)
        base = group * width
        q_ref[:, base : base + width] = queries
        for pair in range(width // 128):
            span = slice(128 * pair, 128 * pair + 128)
            scores = dot(kv_ref[group, :keys, span], two_heads(queries[:, span]), NT)
            probs = softmax_keys(scores, len_ref[0])
            m_ref[:, base + 128 * pair : base + 128 * pair + 128] = one_row(
                dot(probs.astype(BF), kv_ref[group, keys:, span], TN)
            ).astype(BF)
        total = total + dot(m_ref[:, base : base + width], wo_ref[group], NT)
    ac_ref[...] = total
    unit, _ = norm_rows(total)
    mine[pl.ds(pl.multiple_of(step * rows, rows), rows), :] = (unit * g_ref[2:3, :]).astype(BF)

    for turn in range(2):

        @pl.when(step == turn)
        def _(turn=turn):
            half = CHUNKS // 2
            for k in range(turn * half, turn * half + half):
                job.across[k].start()
                job.beside[k].start()
            if turn == 0:
                ring.place()
                ring.hop(1)

    @pl.when(step == 1)
    def _():
        job.store.start()
        for hop in range(2, ring.half):
            ring.hop(hop)
        for k in range(CHUNKS):
            job.forward(k)
        job.finish()
        ring.finish()


def cross_forward(plen, frames, summed, gains, weights, prompt_kv, share, count):
    own, model = frames.shape
    groups, _, both = weights.shape
    width = both // 2
    rows = own // 2
    block = pl.BlockSpec((rows, model), lambda i: (i, 0))
    gain = pl.BlockSpec(gains.shape, lambda i: (0, 0))
    once = pl.Buffered(1)
    return pl.pallas_call(
        functools.partial(cross_kernel, count),
        grid=(2,),
        in_specs=[
            pl.BlockSpec(memory_space=pltpu.SMEM),
            block,
            block,
            gain,
            pl.BlockSpec((groups, model, width), lambda i: (0, 0, 0), pipeline_mode=once),
            pl.BlockSpec((groups, model, width), lambda i: (0, 0, 1), pipeline_mode=once),
            pl.BlockSpec(prompt_kv.shape, lambda i: (0, 0, 0)),
            ANY,
        ],
        out_specs=[block] * 5 + [ANY, ANY],
        out_shape=[
            shape_of((own, model), F32),
            shape_of((own, model), BF),
            shape_of((own, model), BF),
            shape_of((own, model), BF),
            shape_of((own, model), F32),
            shape_of((4 * own, model), BF),
            shape_of((count * share.shape[0], share.shape[1]), BF),
        ],
        scratch_shapes=[pltpu.VMEM((own, model), BF)]
        + gather_scratch(16, 128)
        + ring_scratch(*share.shape, count // 2),
        compiler_params=local_params(collective_id=2, has_side_effects=True),
        cost_estimate=BUSY,
        name="cross_forward",
    )(plen, frames, summed, gains, weights, weights, prompt_kv, share)


def cross_back_kernel(
    len_ref, w_ref, go_ref, e_ref, ac_ref, as_ref, g_ref, q_ref, wq_ref, wo_ref, kv_ref, t_ref,
    cb_ref, dq_ref, c3_ref, c3b_ref, dkv_ref, dg_ref, bo_ref, dkv, hold, *scratch,
):
    groups, model, width = wq_ref.shape
    keys = kv_ref.shape[1] // 2
    job = Scatter(t_ref, bo_ref, scratch)
    step = pl.program_id(0)

    @pl.when(step == 0)
    def _():
        greet([job.to_sib, job.to_far])
        job.start()

    @pl.when(pl.program_id(0) == 0)
    def _():
        dkv[...] = jnp.zeros_like(dkv)
        dg_ref[...] = jnp.zeros_like(dg_ref)

    unit, spread = norm_rows(ac_ref[...])
    back, part = norm_back(e_ref[...], unit, spread, g_ref[2:3, :])
    dg_ref[2:3, :] += part
    carried = go_ref[...].astype(F32) * w_ref[0:1, 0:1] + back
    cross_back = carried.astype(BF)
    cb_ref[...] = cross_back
    rows = cross_back.shape[0]
    total = jnp.zeros((rows, model), F32)
    spot = pl.ds(pl.multiple_of(pl.program_id(0) * rows, rows), rows)
    hold[spot, :] = ac_ref[:, : hold.shape[1]]

    @pl.when(step == 0)
    def _():
        job.fold()
        job.local()

    for group in range(groups):
        grads = dot(cross_back, wo_ref[group], NN).astype(BF)
        base = group * width
        for pair in range(width // 128):
            span = slice(128 * pair, 128 * pair + 128)
            wide = slice(base + 128 * pair, base + 128 * pair + 128)
            queries = two_heads(q_ref[:, wide])
            masked = two_heads(grads[:, span])
            probs = softmax_keys(dot(kv_ref[group, :keys, span], queries, NT), len_ref[0])
            dprobs = dot(kv_ref[group, keys:, span], masked, NT)
            inner = jnp.sum(dprobs * probs, axis=0, keepdims=True)
            ds = (probs * (dprobs - inner)).astype(BF)
            dkv[group, :keys, span] += dot(ds, queries, NN) * (1.0 / LOG2E)
            dkv[group, keys:, span] += dot(probs.astype(BF), masked, NN)
            grad_q = one_row(dot(ds, kv_ref[group, :keys, span], TN))
            dq_ref[:, wide] = (grad_q * 0.125).astype(BF)
        total = total + dot(dq_ref[:, base : base + width], wq_ref[group], NT)
    unit, spread = norm_rows(as_ref[...])
    back, part = norm_back(total, unit, spread, g_ref[1:2, :])
    dg_ref[1:2, :] += part
    carried = carried + back
    c3_ref[...] = carried
    c3b_ref[...] = carried.astype(BF)

    @pl.when(pl.program_id(0) == pl.num_programs(0) - 1)
    def _():
        dkv_ref[...] = dkv[...].astype(BF)
        job.land(hold)
        job.finish()


def cross_backward(plen, weight, grad_out, summed, after_cross, after_self, gains, queries,
                   weights, prompt_kv, term):
    share, model = grad_out.shape
    groups, _, both = weights.shape
    width = both // 2
    rows = 256
    block = pl.BlockSpec((rows, model), lambda i: (i, 0))
    gain = pl.BlockSpec(gains.shape, lambda i: (0, 0))
    once = pl.Buffered(1)
    return pl.pallas_call(
        cross_back_kernel,
        grid=(share // rows,),
        in_specs=[
            pl.BlockSpec(memory_space=pltpu.SMEM),
            pl.BlockSpec(weight.shape, lambda i: (0, 0)),
            block,
            block,
            block,
            block,
            gain,
            block,
            pl.BlockSpec((groups, model, width), lambda i: (0, 0, 0), pipeline_mode=once),
            pl.BlockSpec((groups, model, width), lambda i: (0, 0, 1), pipeline_mode=once),
            pl.BlockSpec(prompt_kv.shape, lambda i: (0, 0, 0)),
            ANY,
        ],
        out_specs=[block] * 4
        + [pl.BlockSpec(prompt_kv.shape, lambda i: (0, 0, 0)), gain]
        + [pl.BlockSpec((share, term.shape[1]), lambda i: (0, 0))],
        out_shape=[
            shape_of((share, model), BF),
            shape_of((share, model), BF),
            shape_of((share, model), F32),
            shape_of((share, model), BF),
            shape_of(prompt_kv.shape, BF),
            shape_of(gains.shape, F32),
            shape_of((share, term.shape[1]), BF),
        ],
        scratch_shapes=[
            pltpu.VMEM(prompt_kv.shape, F32),
            pltpu.VMEM((share, term.shape[1]), F32),
        ]
        + scatter_scratch(share, term.shape[1]),
        compiler_params=local_params(collective_id=9, has_side_effects=True),
        cost_estimate=cost(4 * share * model * model, 4 * model * model + 24 * share * model),
        name="cross_backward",
    )(plen, weight, grad_out, summed, after_cross, after_self, gains, queries, weights, weights,
      prompt_kv, term)


def glu_kernel(scaled, parts, count, *refs):
    refs = list(refs)
    s_ref = None if scaled else refs.pop(0)
    n_ref, c_ref = refs[:2]
    weights, outs = refs[2 : 2 + count], refs[2 + count :]
    cot = c_ref[...]
    if not scaled:
        cot = (cot.astype(F32) * s_ref[0:1, 0:1]).astype(BF)
        outs[2][...] = cot
    h_ref, d_ref = outs[:2]
    normed = n_ref[...]
    piece = 256
    at = 0
    for index, low, size in parts:
        w_ref = weights[index]
        width = w_ref.shape[1] // 3
        for base in range(0, size, piece):
            spot = low + base
            gate = dot(normed, w_ref[:, spot : spot + piece], NN)
            up = dot(normed, w_ref[:, width + spot : width + spot + piece], NN)
            grads = dot(cot, w_ref[:, 2 * width + spot : 2 * width + spot + piece], NN)
            sig = 1.0 / (1.0 + jnp.exp(-gate))
            silu = gate * sig
            h_ref[:, at + base : at + base + piece] = (silu * up).astype(BF)
            grad_gate = grads * up * sig * (1.0 + gate * (1.0 - sig))
            spot = 2 * at + base
            d_ref[:, spot : spot + piece] = grad_gate.astype(BF)
            d_ref[:, size + spot : size + spot + piece] = (grads * silu).astype(BF)
        at += size


def glu_block(normed, cot, weights, parts, scale=None):
    length, model = normed.shape
    width = sum(size for _, _, size in parts)
    rows = 512
    block = pl.BlockSpec((rows, model), lambda i: (i, 0))
    first = scale is not None
    return pl.pallas_call(
        functools.partial(glu_kernel, not first, parts, len(weights)),
        grid=(length // rows,),
        in_specs=[pl.BlockSpec((8, 128), lambda i: (0, 0))] * first
        + [block, block]
        + [
            pl.BlockSpec(weight.shape, lambda i: (0, 0), pipeline_mode=pl.Buffered(1))
            for weight in weights
        ],
        out_specs=[
            pl.BlockSpec((rows, width), lambda i: (i, 0)),
            pl.BlockSpec((rows, 2 * width), lambda i: (i, 0)),
        ]
        + [block] * first,
        out_shape=[shape_of((length, width), BF), shape_of((length, 2 * width), BF)]
        + [shape_of((length, model), BF)] * first,
        compiler_params=local_params(),
        cost_estimate=cost(6 * length * model * width, 6 * length * model),
        name="glu_block_%d" % width,
    )(*([scale] if first else []), normed, cot, *weights)


def grads_kernel(plan, n_ref, c_ref, d_ref, h_ref, *outs):
    for out, spans in zip(outs, plan):
        base = 0
        for side, low, high in spans:
            left, right = (n_ref, d_ref) if side == 0 else (c_ref, h_ref)
            value = dot(left[...], right[:, low:high], TN)
            out[:, base : base + high - low] = value.astype(BF)
            base += high - low


def weight_grads(normed, cot, dgu, hidden, plan, tile=256):
    length, model = normed.shape
    widths = [sum(high - low for _, low, high in spans) for spans in plan]
    once = pl.Buffered(1)
    left = pl.BlockSpec((length, tile), lambda i: (0, i))
    return pl.pallas_call(
        functools.partial(grads_kernel, plan),
        grid=(model // tile,),
        in_specs=[left, left]
        + [pl.BlockSpec(right.shape, lambda i: (0, 0), pipeline_mode=once) for right in (dgu, hidden)],
        out_specs=[pl.BlockSpec((tile, wide), lambda i: (i, 0)) for wide in widths],
        out_shape=[shape_of((model, wide), BF) for wide in widths],
        compiler_params=local_params(),
        cost_estimate=cost(2 * length * model * sum(widths), 2 * length * (2 * model + sum(widths))),
        name="weight_grads_%d" % sum(widths),
    )(normed, cot, dgu, hidden)


def last_grads_kernel(plan, copies, count, n_ref, q_ref, k_ref, v_ref, nc_ref, k0_ref, v0_ref, *refs):
    sources, rest = refs[:count], refs[count:]
    passed, (o_ref, gate_ref, up_ref, down_ref), targets = (
        rest[: -4 - len(copies)],
        rest[-4 - len(copies) : len(rest) - len(copies)],
        rest[len(rest) - len(copies) :],
    )
    width = q_ref.shape[1]
    normed = n_ref[...]
    edge = nc_ref[...]
    o_ref[:, :width] = dot(normed, q_ref[...], TN).astype(BF)
    grad_k = dot(normed, k_ref[...], TN) + dot(edge, k0_ref[...].astype(BF), TN)
    o_ref[:, width : 2 * width] = grad_k.astype(BF)
    grad_v = dot(normed, v_ref[...], TN) + dot(edge, v0_ref[...].astype(BF), TN)
    o_ref[:, 2 * width :] = grad_v.astype(BF)

    @pl.when(pl.program_id(0) == 0)
    def _():
        for source, base, kind, low, size in plan:
            target = (gate_ref, up_ref, down_ref)[kind]
            target[:, low : low + size] = sources[source][:, base : base + size].astype(F32)

    @pl.when(pl.program_id(0) == 1)
    def _():
        for target, (dims, places) in zip(targets, copies):
            for index, from_row, rows, row, column in places:
                ref = passed[index]
                value = ref[from_row : from_row + rows, :]
                target[row : row + rows, column : column + ref.shape[1]] = value


def last_grads(normed, grads, edge, dk0, dv0, sources, plan, hidden, passed, copies, tile=256):
    length, model = normed.shape
    width = grads[0].shape[1]
    own = sources[0].shape[0]
    once = pl.Buffered(1)
    fixed = lambda i: (0, 0)

    def full(array):
        return pl.BlockSpec(array.shape, fixed, pipeline_mode=once)

    extra = [shape_of(dims, passed[places[0][0]].dtype) for dims, places in copies]
    return pl.pallas_call(
        functools.partial(last_grads_kernel, plan, copies, len(sources)),
        grid=(model // tile,),
        in_specs=[pl.BlockSpec((length, tile), lambda i: (0, i))]
        + [full(grad) for grad in grads]
        + [pl.BlockSpec((edge.shape[0], tile), lambda i: (0, i)), full(dk0), full(dv0)]
        + [full(source) for source in sources]
        + [full(array) for array in passed],
        out_specs=[pl.BlockSpec((tile, 3 * width), lambda i: (i, 0))]
        + [pl.BlockSpec((own, hidden), fixed)] * 3
        + [pl.BlockSpec(array.shape, fixed) for array in extra],
        out_shape=[shape_of((model, 3 * width), BF)]
        + [shape_of((own, hidden), F32)] * 3
        + extra,
        compiler_params=local_params(),
        cost_estimate=cost(6 * length * model * width, 2 * length * (model + 3 * width)),
        name="last_grads",
    )(normed, *grads, edge, dk0, dv0, *sources, *passed)


def owner_sum(term):
    return lax.psum_scatter(term, "dp", scatter_dimension=0, tiled=True)


def after(value, *others):
    return lax.optimization_barrier((value,) + others)[0]


GLU_PARTS = 3


def per_device(
    frames, cond_table, bucket_ids, prompt, prompt_len,
    attn_query, attn_key, attn_value, attn_out,
    cross_query, cross_key, cross_value, cross_out,
    glu_gate, glu_up, glu_down, first_gain, second_gain, third_gain, grad_out,
):
    groups = lax.axis_size("mp")
    count = lax.axis_size("dp")
    sequences = bucket_ids.shape[0]
    assert sequences == 1 and groups == 4
    share, model = frames.shape
    length = share * groups
    buckets = cond_table.shape[0]
    own_rows, width = attn_query.shape
    unit = glu_gate.shape[1] // GLU_PARTS
    context = prompt.shape[2]

    onehot = (bucket_ids[:, None] == jnp.arange(buckets)[None, :]).astype(F32)
    gain_rows = jnp.pad(jnp.stack([first_gain, second_gain, third_gain]), ((0, 5), (0, 0)))
    hot = jnp.pad(onehot, ((0, 0), (3, 128 - 3 - buckets)))
    prompt_blocks = prompt.reshape(-1, count, context // count)
    blank = jnp.zeros_like(prompt_blocks)
    prompts = jnp.concatenate(
        [
            jnp.concatenate([prompt_blocks, blank], 2).reshape(-1, model),
            jnp.concatenate([blank, prompt_blocks], 2).reshape(-1, model),
        ],
        0,
    )
    prompt_share = jnp.concatenate([cross_key, cross_value], 0)
    frames_all, grad_all, first, *glu_share = head_gather(
        frames, grad_out, gain_rows, hot,
        [attn_query, attn_key, attn_value, attn_out, cross_query, cross_out],
        [glu_gate, glu_up, glu_down], GLU_PARTS, count,
    )

    tables = rope_tables(length, 1.0)
    scale = sequences * count * own_rows / buckets
    (
        normed_one, queries, keys, values, gains, seq_weight, normed_cond, key0, value0,
    ) = qkv_project(frames_all, cond_table, hot, first, tables, width, scale)
    mixed, aug, cross_full, second, glu_first = attend(
        queries, keys, values, key0, value0, first, 4 * width + 128, prompt_share,
        glu_share[0], count,
    )
    cross_full = cross_full.reshape(groups, model, 2 * width)
    self_out, prompt_kv, glu_second = out_project(
        mixed, first, 3, prompts, second, glu_share[1], count
    )
    prompt_kv = prompt_kv.reshape(groups, prompts.shape[0], width)

    (
        after_self, normed_two, cross_q, cross_mixed, after_cross, normed_three, glu_third,
    ) = cross_forward(
        prompt_len, frames, self_out, gains, cross_full, prompt_kv, glu_share[2], count
    )
    glu_full = [glu_first, glu_second, glu_third]
    half = unit // 2
    parts = (((0, 0, half),), ((0, half, half), (1, 0, unit), (2, 0, unit)))
    h0, d0, cot_all = glu_block(normed_three, grad_all, glu_full[:1], parts[0], seq_weight)
    (pack0,) = weight_grads(normed_three, cot_all, d0, h0, (((0, 0, unit), (1, 0, half)),))
    h1, d1 = glu_block(after(normed_three, pack0), cot_all, glu_full, parts[1])
    wide = unit + 2 * unit
    pack1, pack2 = weight_grads(
        normed_three, cot_all, d1, h1,
        (
            (
                (0, 0, unit), (1, 0, half),
                (0, unit, wide), (1, half, half + unit),
                (0, wide, wide + half), (0, wide + unit, wide + unit + half),
                (1, half + unit, 2 * unit),
            ),
            (
                (0, wide + half, wide + unit), (0, wide + unit + half, wide + 2 * unit),
                (1, 2 * unit, 2 * unit + half),
            ),
        ),
    )
    glu_sum0 = owner_sum(pack0)
    pack1 = after(pack1, glu_sum0)
    glu_sum1 = owner_sum(pack1)
    back_term, out_term0, out_term1 = glu_back(
        [after(d0, pack1), d1], [h0, h1], glu_full, parts
    )

    cross_back, grad_cq, carried, carried_low, grad_kv, grad_gains, block0 = cross_backward(
        prompt_len, seq_weight, grad_out, back_term, after_cross, after_self, gains, cross_q,
        cross_full, prompt_kv, out_term0,
    )
    cross_term, grad_mixed, second_pack, glu_sum2 = mid_gather(
        carried_low, grad_kv.reshape(-1, width), normed_two, cross_back, grad_cq, cross_mixed,
        first, 3, mixed, prompts, pack2, groups, count,
    )
    (
        dq, dk, dv, dk0, dv0, _, grad_out_own, grad_prompt, block1, grad_cross_q, grad_cross_o,
    ) = attend_back(
        queries, aug, mixed, grad_mixed, keys, values, key0, value0, tables, cross_term,
        second_pack, out_term1, after_cross, count,
    )
    plan = []
    pieces_of = (
        (0, 0, 0, half), (1, 0, half, half), (1, 3 * half, unit, unit),
        (1, 9 * half, 2 * unit, half), (2, 0, 2 * unit + half, half),
    )
    for source, base, low, size in pieces_of:
        for kind in range(3):
            plan.append((source, base + kind * size, kind, low, size))
    short = context // count
    copies = (
        ((share, model), ((0, 0, share, 0, 0), (1, 0, share, 0, model // 2))),
        ((own_rows, width), ((2, 0, own_rows, 0, 0),)),
        ((own_rows, width), ((3, 0, own_rows, 0, 0),)),
        ((short, width), ((4, 0, short, 0, 0),)),
        ((short, width), ((4, short, short, 0, 0),)),
        ((own_rows, width), ((5, 0, own_rows, 0, 0),)),
    )
    (
        first_pack, *glu_out, block_out, grad_out_own, grad_cross_q, grad_cross_k, grad_cross_v,
        grad_cross_o,
    ) = last_grads(
        normed_one, [dq, dk, dv], normed_cond, dk0, dv0, [glu_sum0, glu_sum1, glu_sum2], plan,
        glu_gate.shape[1],
        [block0, block1, grad_out_own, grad_cross_q, grad_prompt, grad_cross_o], copies,
    )
    frames_grad, sums, first_grad = tail_sums(
        count, buckets, [dq, dk, dv], frames_all, first, first_pack, frames, carried, gains, grad_gains, hot,
        cond_table, dk0, dv0,
    )
    return (
        block_out,
        frames_grad,
        sums[:buckets],
        first_grad[:, :width],
        first_grad[:, width : 2 * width],
        first_grad[:, 2 * width :],
        grad_out_own,
        grad_cross_q,
        grad_cross_k,
        grad_cross_v,
        grad_cross_o,
        *glu_out,
        sums[buckets],
        sums[buckets + 1],
        sums[buckets + 2],
    )


def solution(mesh):
    both = P(("dp", "mp"), None)
    weight = P("dp", "mp")
    return jax.shard_map(
        per_device,
        mesh=mesh,
        in_specs=(both, P(), P("dp"), P("dp", None, None), P("dp"))
        + (weight,) * 11
        + (P("dp"),) * 3
        + (both,),
        out_specs=(both, both, P()) + (weight,) * 11 + (P(),) * 3,
        check_vma=False,
    )
```

```python
import functools

import jax
import jax.numpy as jnp
import numpy as np
from jax import lax
from jax.experimental import pallas as pl
from jax.experimental.pallas import tpu as pltpu
from jax.sharding import PartitionSpec as P

HD = 64
ROT = 32
LOG2E = 1.4426950408889634
EPS = 1e-05
MESH = pl.DeviceIdType.MESH
NT = (((1,), (1,)), ((), ()))
TN = (((0,), (0,)), ((), ()))
NN = (((1,), (0,)), ((), ()))
BF = jnp.bfloat16
F32 = jnp.float32
ANY = pl.BlockSpec(memory_space=pl.ANY)
VM = 58 << 20


def shape_of(dims, dtype):
    return jax.ShapeDtypeStruct(dims, dtype)


def dot(left, right, dims):
    return lax.dot_general(left, right, dims, preferred_element_type=F32)


def local_params(**extra):
    return pltpu.CompilerParams(vmem_limit_bytes=VM, **extra)


def cost(flops, nbytes, trans=0):
    return pl.CostEstimate(flops=int(flops), bytes_accessed=int(nbytes), transcendentals=int(trans))


def norm_rows(values):
    center = values - jnp.mean(values, -1, keepdims=True)
    spread = lax.rsqrt(jnp.mean(center * center, -1, keepdims=True) + EPS)
    return center * spread, spread


def norm_back(grad_rows, unit_rows, spread, gain_row):
    scaled = grad_rows * gain_row
    result = spread * (
        scaled
        - jnp.mean(scaled, -1, keepdims=True)
        - unit_rows * jnp.mean(scaled * unit_rows, -1, keepdims=True)
    )
    return result, jnp.sum(grad_rows * unit_rows, 0, keepdims=True)


def rope_tables(length, offset):
    lane = np.arange(2 * HD) % HD
    half = ROT // 2
    frequency = np.power(10000.0, -2.0 * (lane % half) / ROT)
    angles = (offset + np.arange(length))[:, None] * frequency[None, :]
    cosine = np.where(lane[None] < ROT, np.cos(angles), 1.0)
    sine = np.sin(angles)
    upper = np.where((lane[None] >= half) & (lane[None] < ROT), sine, 0.0)
    lower = np.where(lane[None] < half, -sine, 0.0)
    return [jnp.asarray(table.astype(np.float32)) for table in (cosine, upper, lower)]


def rope(values, cosine, upper, lower):
    half = ROT // 2
    return (
        values * cosine
        + pltpu.roll(values, half, 1) * upper
        + pltpu.roll(values, 2 * HD - half, 1) * lower
    )


def bucket_column(hot, rows):
    dims = (rows, 128)
    pick = lax.broadcasted_iota(jnp.int32, dims, 0) + 3 == lanes(dims)
    marks = jnp.broadcast_to(hot, (8, 128)).astype(BF)
    return dot(jnp.where(pick, 1.0, 0.0).astype(BF), marks, NT)[:, 0:1]


def bucket_row(hot, table):
    rows = table.shape[0]
    return jnp.sum(table.astype(F32) * bucket_column(hot, rows), axis=0, keepdims=True)


def lanes(dims):
    return lax.broadcasted_iota(jnp.int32, dims, 1)


def half_mask(values, head):
    lane = lanes(values.shape)
    keep = (lane < HD) if head == 0 else (lane >= HD)
    return jnp.where(keep, values, jnp.zeros_like(values))


def pieces(column, dims, base):
    high = column.astype(BF).astype(F32)
    rest = column - high
    middle = rest.astype(BF).astype(F32)
    low = rest - middle
    lane = lanes(dims)
    return jnp.where(
        lane == base,
        high,
        jnp.where(lane == base + 1, middle, jnp.where(lane == base + 2, low, 0.0)),
    )


def mp_peers():
    me = lax.axis_index("mp")
    chip, core = me // 2, me % 2
    return me, chip * 2 + (1 - core), (1 - chip) * 2 + core, (1 - chip) * 2 + (1 - core)


def greet(devices):
    barrier = pltpu.get_barrier_semaphore()
    for device in devices:
        pl.semaphore_signal(barrier, inc=1, device_id=device, device_id_type=MESH)
    pl.semaphore_wait(barrier, len(devices))


def remote(source, target, send, recv, device):
    return pltpu.make_async_remote_copy(
        source, target, send, recv, device_id=device, device_id_type=MESH
    )


CHUNKS = 4
CUTS = 2


def column_cuts(width):
    first = 128 * ((width // 128 + 1) // 2)
    return [pl.ds(0, first), pl.ds(first, width - first)]


BUSY = cost(1, 140 << 20)


def gather_scratch(rows, width):
    return [
        pltpu.VMEM((rows, width), BF),
        pltpu.SemaphoreType.DMA((2,)),
        pltpu.SemaphoreType.DMA((3, CHUNKS)),
        pltpu.SemaphoreType.DMA((3, CHUNKS)),
    ]


class Gather:
    def __init__(self, x_ref, o_ref, sems, columns=None, here=False):
        bounce, lsem, ssem, rsem = sems
        if here:
            bounce = x_ref
        self.me, self.sib, self.far, _ = mp_peers()
        dp = lax.axis_index("dp")
        self.to_sib = {"dp": dp, "mp": self.sib}
        self.to_far = {"dp": dp, "mp": self.far}
        rows = x_ref.shape[0]
        part = rows // CHUNKS

        def slot(i, k):
            return o_ref.at[pl.ds(pl.multiple_of(i * rows + k * part, part), part)]

        def source(first, size):
            if columns is None:
                return x_ref.at[pl.ds(first, size)]
            return x_ref.at[pl.ds(first, size), columns]

        self.load = None if here else pltpu.make_async_copy(source(0, rows), bounce, lsem.at[0])
        self.store = pltpu.make_async_copy(
            bounce, o_ref.at[pl.ds(pl.multiple_of(self.me * rows, rows), rows)], lsem.at[1]
        )
        self.across = []
        self.beside = []
        self.onward = []
        for k in range(CHUNKS):
            mine = source(k * part, part)
            self.across.append(
                remote(mine, slot(self.me, k), ssem.at[0, k], rsem.at[0, k], self.to_far)
            )
            self.beside.append(
                remote(mine, slot(self.me, k), ssem.at[1, k], rsem.at[1, k], self.to_sib)
            )
            self.onward.append(
                remote(
                    slot(self.far, k), slot(self.far, k), ssem.at[2, k], rsem.at[2, k], self.to_sib
                )
            )

    def start(self):
        for copy in self.across:
            copy.start()
        if self.load is not None:
            self.load.start()
        for copy in self.beside:
            copy.start()
        if self.load is not None:
            self.load.wait()
        self.store.start()

    def forward(self, k):
        self.across[k].wait_recv()
        self.onward[k].start()

    def finish(self):
        for k in range(CHUNKS):
            self.beside[k].wait_recv()
            self.onward[k].wait_recv()
        for k in range(CHUNKS):
            self.across[k].wait_send()
            self.beside[k].wait_send()
            self.onward[k].wait_send()
        self.store.wait()


def scatter_scratch(rows, width):
    return [pltpu.VMEM((2, rows, width), BF)] + [pltpu.VMEM((rows, width), BF)] * 4 + [
        pltpu.SemaphoreType.DMA((2,)),
        pltpu.SemaphoreType.DMA((3, CHUNKS)),
        pltpu.SemaphoreType.DMA((3, CHUNKS)),
    ]


class Scatter:
    def __init__(self, x_ref, o_ref, scratch):
        mine, ra, rb, rc, sb, lsem, ssem, rsem = scratch
        me, sib, far, diag = mp_peers()
        dp = lax.axis_index("dp")
        self.to_sib = {"dp": dp, "mp": sib}
        self.to_far = {"dp": dp, "mp": far}
        self.o_ref, self.mine, self.ra, self.rb, self.rc, self.sb = o_ref, mine, ra, rb, rc, sb
        rows = ra.shape[0]
        part = rows // CHUNKS
        self.spans = [pl.ds(k * part, part) for k in range(CHUNKS)]

        def slot(i, k):
            return x_ref.at[pl.ds(pl.multiple_of(i * rows + k * part, part), part)]

        def whole(i):
            return x_ref.at[pl.ds(pl.multiple_of(i * rows, rows), rows)]

        self.first, self.second, self.third = [], [], []
        for k, span in enumerate(self.spans):
            self.first.append(
                remote(slot(diag, k), ra.at[span], ssem.at[0, k], rsem.at[0, k], self.to_sib)
            )
            self.second.append(
                remote(slot(sib, k), rb.at[span], ssem.at[1, k], rsem.at[1, k], self.to_sib)
            )
            self.third.append(
                remote(sb.at[span], rc.at[span], ssem.at[2, k], rsem.at[2, k], self.to_far)
            )
        self.load0 = pltpu.make_async_copy(whole(far), mine.at[0], lsem.at[0])
        self.load1 = pltpu.make_async_copy(whole(me), mine.at[1], lsem.at[1])

    def start(self):
        self.load0.start()
        for copy in self.first:
            copy.start()
        self.load1.start()
        for copy in self.second:
            copy.start()

    def fold(self):
        self.load0.wait()
        for k, span in enumerate(self.spans):
            self.first[k].wait_recv()
            total = self.mine[0, span, :].astype(F32) + self.ra[span, :].astype(F32)
            self.sb[span, :] = total.astype(BF)
            self.third[k].start()

    def local(self):
        self.load1.wait()
        for k in range(CHUNKS):
            self.second[k].wait_recv()

    def land(self, addend=None):
        for k, span in enumerate(self.spans):
            self.third[k].wait_recv()
            total = self.mine[1, span, :].astype(F32) + self.rb[span, :].astype(F32)
            if addend is not None:
                total = total + addend[span, :]
            self.o_ref[span, :] = (total + self.rc[span, :].astype(F32)).astype(self.o_ref.dtype)

    def finish(self):
        for k in range(CHUNKS):
            self.first[k].wait_send()
            self.second[k].wait_send()
            self.third[k].wait_send()


def sum_scratch(rows, width):
    return [pltpu.VMEM((4, rows, width), BF)] + [pltpu.VMEM((rows, width), BF)] * 4 + [
        pltpu.SemaphoreType.DMA((3, CHUNKS)),
        pltpu.SemaphoreType.DMA((3, CHUNKS)),
    ]


class LocalSum:
    def __init__(self, o_ref, scratch):
        terms, ra, rb, rc, sb, ssem, rsem = scratch
        _, sib, far, _ = mp_peers()
        dp = lax.axis_index("dp")
        self.to_sib = {"dp": dp, "mp": sib}
        self.to_far = {"dp": dp, "mp": far}
        self.o_ref, self.terms, self.ra, self.rb, self.rc, self.sb = o_ref, terms, ra, rb, rc, sb
        rows = ra.shape[0]
        part = rows // CHUNKS
        self.spans = [pl.ds(k * part, part) for k in range(CHUNKS)]
        self.first, self.second, self.third = [], [], []
        for k, span in enumerate(self.spans):
            self.first.append(
                remote(terms.at[0, span], ra.at[span], ssem.at[0, k], rsem.at[0, k], self.to_sib)
            )
            self.second.append(
                remote(terms.at[2, span], rb.at[span], ssem.at[1, k], rsem.at[1, k], self.to_sib)
            )
            self.third.append(
                remote(sb.at[span], rc.at[span], ssem.at[2, k], rsem.at[2, k], self.to_far)
            )

    def put(self, step, value):
        half = value.shape[0]
        late = step // 4
        slot = (1 - late) * (step % 2) + late * (step // 2)
        row = (1 - late) * ((step // 2) % 2) + late * (step % 2)
        self.terms[slot, pl.ds(pl.multiple_of(row * half, half), half), :] = value

    def after_step(self, step):
        half = CHUNKS // 2
        for turn in range(2):
            chunks = range(turn * half, turn * half + half)

            @pl.when(step == 2 * turn)
            def _(chunks=chunks):
                for k in chunks:
                    self.first[k].start()

            @pl.when(step == 2 * turn + 1)
            def _(chunks=chunks):
                for k in chunks:
                    span = self.spans[k]
                    self.first[k].wait_recv()
                    total = self.terms[1, span, :].astype(F32) + self.ra[span, :].astype(F32)
                    self.sb[span, :] = total.astype(BF)
                    self.third[k].start()

        @pl.when(step == 5)
        def _():
            for copy in self.second:
                copy.start()

    def land(self):
        for k, span in enumerate(self.spans):
            self.second[k].wait_recv()
            self.third[k].wait_recv()
            total = self.terms[3, span, :].astype(F32) + self.rb[span, :].astype(F32)
            self.o_ref[span, :] = (total + self.rc[span, :].astype(F32)).astype(self.o_ref.dtype)

    def finish(self):
        for copy in self.first + self.second + self.third:
            copy.wait_send()


def order_block(step):
    me = lax.axis_index("mp")
    chip, core = me // 2, me % 2
    late = step // 4
    other = 1 - late
    cross = 1 - ((1 - late) * (step % 2) + late * ((step // 2) % 2))
    quarter = (chip + other - 2 * chip * other) * 2 + (core + cross - 2 * core * cross)
    return quarter * 2 + (1 - late) * ((step // 2) % 2) + late * (step % 2)


def term_quarter(slot):
    me = lax.axis_index("mp")
    chip, core = me // 2, me % 2
    other = 1 - slot // 2
    cross = 1 - slot % 2
    return (chip + other - 2 * chip * other) * 2 + (core + cross - 2 * core * cross)


def arrival_quarter(turn):
    me = lax.axis_index("mp")
    chip, core = me // 2, me % 2
    other = turn // 2
    cross = turn % 2
    return (chip + other - 2 * chip * other) * 2 + (core + cross - 2 * core * cross)


class Ring:
    def __init__(self, count):
        self.count = count
        self.half = count // 2
        me = lax.axis_index("dp")
        mp = lax.axis_index("mp")
        odd = me % 2
        self.me = me
        self.spot = (1 - odd) * (me // 2) + odd * (count - 1 - me // 2)
        self.ahead = {"dp": self.at(1), "mp": mp}
        self.behind = {"dp": self.at(-1), "mp": mp}

    def at(self, distance):
        spot = (self.spot + distance + self.count) % self.count
        late = spot // self.half
        return (1 - late) * 2 * spot + late * (2 * (self.count - 1 - spot) + 1)


def ring_scratch(rows, width, half):
    return [pltpu.VMEM((rows, width), BF), pltpu.SemaphoreType.DMA((2,))] + [
        pltpu.SemaphoreType.DMA((half, CUTS))
    ] * 4


class RingGather:
    def __init__(self, count, w_ref, o_ref, scratch, here=False):
        bounce, lsem, fs, fr, bs, br = scratch
        if here:
            bounce = w_ref
        ring = Ring(count)
        self.ahead, self.behind, self.half = ring.ahead, ring.behind, ring.half
        rows = w_ref.shape[0]

        spans = column_cuts(w_ref.shape[1])

        def slot(i):
            return o_ref.at[pl.ds(pl.multiple_of(i * rows, rows), rows)]

        last = self.half - 1

        def copies(block, hop, send, recv, device, only):
            result = {}
            for c, columns in enumerate(spans):
                if hop < last or c == only:
                    place = o_ref.at[pl.ds(pl.multiple_of(block * rows, rows), rows), columns]
                    source = w_ref.at[:, columns] if hop == 0 else place
                    result[c] = remote(source, place, send.at[hop, c], recv.at[hop, c], device)
            return result

        self.forward = []
        self.backward = []
        for hop in range(self.half):
            self.forward.append(copies(ring.at(-hop), hop, fs, fr, ring.ahead, 0))
            self.backward.append(copies(ring.at(hop), hop, bs, br, ring.behind, 1))
        self.load = None if here else pltpu.make_async_copy(w_ref, bounce, lsem.at[0])
        self.store = pltpu.make_async_copy(bounce, slot(ring.me), lsem.at[1])

    def start(self):
        for c in range(CUTS):
            self.forward[0][c].start()
            self.backward[0][c].start()
        if self.load is not None:
            self.load.start()

    def place(self):
        if self.load is not None:
            self.load.wait()
        self.store.start()

    def hop(self, hop):
        for c in range(CUTS):
            for way in (self.forward, self.backward):
                way[hop - 1][c].wait_recv()
                if c in way[hop]:
                    way[hop][c].start()

    def finish(self):
        self.forward[-1][0].wait_recv()
        self.backward[-1][1].wait_recv()
        self.store.wait()
        for copies in self.forward + self.backward:
            for copy in copies.values():
                copy.wait_send()


def ring_sum_scratch(rows, wide, half, sources):
    slots = pltpu.VMEM((half, rows, wide), BF)
    hops = pltpu.SemaphoreType.DMA((half, CUTS))
    return (
        [slots] * 4
        + [pltpu.VMEM((rows, wide), BF), pltpu.SemaphoreType.DMA((2 * half + 1, sources))]
        + [hops] * 4
    )


class RingSum:
    def __init__(self, count, sources, scratch):
        self.lf, self.lb, self.rf, self.rb, self.own, lsem, fs, fr, bs, br = scratch
        ring = Ring(count)
        self.ahead, self.behind, self.half = ring.ahead, ring.behind, ring.half
        rows = self.own.shape[0]
        self.spans = column_cuts(self.own.shape[1])

        def sends(source, target, hop, send, recv, device, only):
            return {
                c: remote(
                    source.at[hop, :, span],
                    target.at[hop, :, span],
                    send.at[hop, c],
                    recv.at[hop, c],
                    device,
                )
                for c, span in enumerate(self.spans)
                if hop > 0 or c == only
            }

        def loads(block, target, at):
            span = pl.ds(pl.multiple_of(block * rows, rows), rows)
            base, copies = 0, []
            for i, source in enumerate(sources):
                wide = source.shape[1]
                copies.append(
                    pltpu.make_async_copy(
                        source.at[span], target.at[:, pl.ds(base, wide)], lsem.at[at, i]
                    )
                )
                base += wide
            return copies

        self.forward, self.backward, self.local = [], [], []
        for hop in range(self.half):
            self.local.append(
                loads(ring.at(self.half - hop), self.lf.at[hop], 2 * hop)
                + loads(ring.at(hop - self.half), self.lb.at[hop], 2 * hop + 1)
            )
            self.forward.append(sends(self.lf, self.rf, hop, fs, fr, ring.ahead, 0))
            self.backward.append(sends(self.lb, self.rb, hop, bs, br, ring.behind, 1))
        self.local.append(loads(ring.me, self.own, 2 * self.half))

    def start(self):
        for copies in self.local:
            for copy in copies:
                copy.start()
        for copy in self.local[0]:
            copy.wait()
        self.forward[0][0].start()
        self.backward[0][1].start()
        for copy in self.local[1]:
            copy.wait()
        self.forward[1][1].start()
        self.backward[1][0].start()

    def hop(self, hop):
        if hop > 1:
            for copy in self.local[hop]:
                copy.wait()
        for c, span in enumerate(self.spans):
            for way, mine, came in (
                (self.forward, self.lf, self.rf),
                (self.backward, self.lb, self.rb),
            ):
                if c in way[hop - 1]:
                    way[hop - 1][c].wait_recv()
                    total = mine[hop, :, span].astype(F32) + came[hop - 1, :, span].astype(F32)
                    mine[hop, :, span] = total.astype(BF)
                    way[hop][c].start()

    def finish(self, outs):
        last = self.half - 1
        for copy in self.local[self.half]:
            copy.wait()
        for c in range(CUTS):
            self.forward[last][c].wait_recv()
            self.backward[last][c].wait_recv()
        base = 0
        for out in outs:
            span = slice(base, base + out.shape[1])
            base += out.shape[1]
            out[...] = (
                self.own[:, span].astype(F32)
                + self.rf[last, :, span].astype(F32)
                + self.rb[last, :, span].astype(F32)
            )
        for copies in self.forward + self.backward:
            for copy in copies.values():
                copy.wait_send()


HEAD = 6


def head_kernel(count, f_ref, g_ref, gains_ref, hot_ref, *refs):
    mats, glu = refs[:HEAD], refs[HEAD : HEAD + 3]
    fo_ref, go_ref, wo_ref = refs[HEAD + 3 : HEAD + 6]
    shares = refs[HEAD + 6 : HEAD + 9]
    scratch = refs[HEAD + 9 :]
    pack, held, psem, hsem, osem = scratch[:5]
    job = Gather(f_ref, fo_ref, scratch[5:9])
    late = Gather(g_ref, go_ref, scratch[9:13])
    ring = RingGather(count, pack, wo_ref, scratch[13:], here=True)
    width = mats[0].shape[1]
    side = 4 * width
    loads = []
    for i, mat in enumerate(mats):
        base = i * width if i < 4 else i * width + 128
        loads.append(pltpu.make_async_copy(mat, pack.at[:, pl.ds(base, width)], psem.at[i]))
    fetch = [pltpu.make_async_copy(mat, held.at[i], hsem.at[i]) for i, mat in enumerate(glu)]
    unit = held.shape[2] // len(shares)
    stores = []
    for at, share in enumerate(shares):
        for i in range(3):
            stores.append(
                pltpu.make_async_copy(
                    held.at[i, :, pl.ds(at * unit, unit)],
                    share.at[:, pl.ds(i * unit, unit)],
                    osem.at[at, i],
                )
            )
    for copy in loads + fetch:
        copy.start()
    greet([job.to_sib, job.to_far, ring.ahead, ring.behind])
    job.start()
    dims = (8, 128)
    pick = lax.broadcasted_iota(jnp.int32, dims, 0) == lanes(dims)
    columns = dot(gains_ref[...], jnp.where(pick, 1.0, 0.0).astype(BF), TN)
    pack[:, side : side + 128] = (columns + hot_ref[...]).astype(BF)
    for copy in loads:
        copy.wait()
    ring.start()
    ring.place()
    for copy in fetch:
        copy.wait()
    for copy in stores:
        copy.start()
    ring.hop(1)
    for k in range(CHUNKS):
        job.forward(k)
    late.start()
    for hop in range(2, ring.half):
        ring.hop(hop)
    for k in range(CHUNKS):
        late.forward(k)
    job.finish()
    late.finish()
    ring.finish()
    for copy in stores:
        copy.wait()


def head_gather(frames, grads, gains, hot, mats, glu, parts, count):
    rows, width = frames.shape
    own = mats[0].shape[0]
    columns = len(mats) * mats[0].shape[1] + 128
    hidden = glu[0].shape[1]
    wide = shape_of((4 * rows, width), BF)
    vmem = pl.BlockSpec(memory_space=pltpu.VMEM)
    return pl.pallas_call(
        functools.partial(head_kernel, count),
        out_shape=(wide, wide, shape_of((count * own, columns), BF))
        + (shape_of((own, 3 * hidden // parts), BF),) * parts,
        in_specs=[ANY, ANY, vmem, vmem] + [ANY] * (len(mats) + 3),
        out_specs=(ANY,) * (3 + parts),
        scratch_shapes=[
            pltpu.VMEM((own, columns), BF),
            pltpu.VMEM((3, own, hidden), BF),
            pltpu.SemaphoreType.DMA((len(mats),)),
            pltpu.SemaphoreType.DMA((3,)),
            pltpu.SemaphoreType.DMA((parts, 3)),
        ]
        + gather_scratch(rows, width) * 2
        + ring_scratch(16, 128, count // 2),
        compiler_params=local_params(collective_id=0, has_side_effects=True),
        cost_estimate=BUSY,
        name="head_gather",
    )(frames, grads, gains, hot, *mats, *glu)


SMALL = 16


def tail_kernel(
    count, buckets, q_ref, k_ref, v_ref, fa_ref, wq_ref, wk_ref, wv_ref,
    a_ref, f_ref, c_ref, g_ref, dg_ref, hot_ref, r_ref, k0_ref, v0_ref,
    o_ref, s_ref, w_ref, *scratch,
):
    total, held = scratch[0:2]
    job = LocalSum(total, scratch[2:9])
    ring = RingSum(count, [a_ref], scratch[9:19])
    sent, got, ss, rs = scratch[19:]
    step = pl.program_id(0)
    me = lax.axis_index("dp")
    mp = lax.axis_index("mp")
    partners = [job.to_sib, job.to_far]
    bit = 1
    while bit < count:
        partners.append({"dp": me + bit * (1 - 2 * ((me // bit) % 2)), "mp": mp})
        bit *= 2
    @pl.when(step == 0)
    def _():
        greet(partners + [ring.ahead, ring.behind])
        ring.start()
        held[...] = jnp.zeros_like(held)

    @pl.when(step < 8)
    def _():
        term = (
            dot(q_ref[...], wq_ref[...], NT)
            + dot(k_ref[...], wk_ref[...], NT)
            + dot(v_ref[...], wv_ref[...], NT)
        )
        job.put(step, term.astype(BF))

    job.after_step(step)

    @pl.when((step >= 8) & (step < 12))
    def _():
        unit, _ = norm_rows(fa_ref[...].astype(F32))
        part = jnp.sum(unit * job.terms[step - 8].astype(F32), axis=0, keepdims=True)
        held[buckets : buckets + 1, :] += part

    @pl.when(step == 8)
    def _():
        edge = dot(k0_ref[...].astype(BF), wk_ref[...], NT) + dot(
            v0_ref[...].astype(BF), wv_ref[...], NT
        )
        unit, spread = norm_rows(bucket_row(hot_ref[...], r_ref[...]))
        edge_back, edge_part = norm_back(edge[0:1, :], unit, spread, g_ref[0:1, :])
        place = lax.broadcasted_iota(jnp.int32, held.shape, 0)
        held[...] += (
            bucket_column(hot_ref[...], SMALL) * edge_back
            + jnp.where(place == buckets, edge_part, 0.0)
            + jnp.where(place == buckets + 1, dg_ref[1:2, :], 0.0)
            + jnp.where(place == buckets + 2, dg_ref[2:3, :], 0.0)
        )
        for hop in range(2, ring.half - 1):
            ring.hop(hop)

    @pl.when(step == 4)
    def _():
        ring.hop(1)

    @pl.when(step == 11)
    def _():
        ring.hop(ring.half - 1)

    @pl.when(step == 12)
    def _():
        copies = [
            remote(sent.at[i], got.at[i], ss.at[i], rs.at[i], partner)
            for i, partner in enumerate(partners)
        ]
        sent[0] = held[...]
        copies[0].start()
        for i, copy in enumerate(copies):
            copy.wait_recv()
            held[...] += got[i]
            if i + 1 < len(copies):
                sent[i + 1] = held[...]
                copies[i + 1].start()
        job.land()
        unit, spread = norm_rows(f_ref[...].astype(F32))
        back, _ = norm_back(total[...], unit, spread, g_ref[0:1, :])
        o_ref[...] = c_ref[...] + back
        for copy in copies:
            copy.wait_send()
        s_ref[...] = held[...]
        ring.finish([w_ref])
        job.finish()


def tail_sums(
    count, buckets, grads_qkv, frames_all, weights, grads, frames, carried, gains, grad_gains, hot,
    table_rows, dk0, dv0,
):
    share, model = frames.shape
    width = grads_qkv[0].shape[1]
    block = 2 * share // 4
    rows = grads.shape[0] // count
    wide = grads.shape[1]
    half = count // 2
    steps = 2 + (count - 1).bit_length()
    once = pl.Buffered(1)

    def full(array):
        return pl.BlockSpec(array.shape, lambda i: (0,) * array.ndim, pipeline_mode=once)

    small = pltpu.VMEM((steps, SMALL, model), F32)
    out_shape = (
        shape_of((share, model), F32),
        shape_of((SMALL, model), F32),
        shape_of((rows, wide), F32),
    )
    whole = [frames, carried, gains, grad_gains, hot, table_rows, dk0, dv0]
    return pl.pallas_call(
        functools.partial(tail_kernel, count, buckets),
        grid=(13,),
        out_shape=out_shape,
        in_specs=[
            pl.BlockSpec((block, width), lambda i: (order_block(jnp.minimum(i, 7)), 0))
            for _ in range(3)
        ]
        + [pl.BlockSpec((share, model), lambda i: (term_quarter(jnp.clip(i - 8, 0, 3)), 0))]
        + [
            pl.BlockSpec(
                (model, width), functools.partial(lambda at, i: (0, at), at), pipeline_mode=once
            )
            for at in range(3)
        ]
        + [ANY]
        + [full(array) for array in whole],
        out_specs=tuple(pl.BlockSpec(out.shape, lambda i: (0, 0)) for out in out_shape),
        scratch_shapes=[pltpu.VMEM((share, model), F32), pltpu.VMEM((SMALL, model), F32)]
        + sum_scratch(share, model)
        + ring_sum_scratch(rows, wide, half, 1)
        + [small, small, pltpu.SemaphoreType.DMA((steps,)), pltpu.SemaphoreType.DMA((steps,))],
        compiler_params=local_params(collective_id=6, has_side_effects=True),
        cost_estimate=BUSY,
        name="tail_sums",
    )(*grads_qkv, frames_all, weights, weights, weights, grads, *whole)


def out_kernel(
    count, m_ref, w_ref, p_ref, wp_ref, share_ref, o_ref, kvo_ref, full_ref, mine, *scratch
):
    side = Gather(mine, kvo_ref, scratch[:4], here=True)
    job = LocalSum(o_ref, scratch[4:11])
    ring = RingGather(count, share_ref, full_ref, scratch[11:])
    step = pl.program_id(0)

    @pl.when(step == 0)
    def _():
        greet([job.to_sib, job.to_far, ring.ahead, ring.behind])
        ring.start()

    job.put(step, dot(m_ref[...], w_ref[...], NT).astype(BF))
    job.after_step(step)

    @pl.when(step == 1)
    def _():
        mine[...] = dot(p_ref[...], wp_ref[...], NN).astype(BF)
        side.start()
        ring.place()

    @pl.when(step == 7)
    def _():
        for hop in range(1, ring.half):
            ring.hop(hop)
        for k in range(CHUNKS):
            side.forward(k)
        job.land()
        side.finish()
        job.finish()
        ring.finish()


def out_project(mixed, weights, column, prompts, prompt_weights, weight_share, count):
    length, width = mixed.shape
    model = weights.shape[0]
    rows = length // 8
    share = length // 4
    short = prompts.shape[0]
    once = pl.Buffered(1)
    return pl.pallas_call(
        functools.partial(out_kernel, count),
        grid=(8,),
        out_shape=(
            shape_of((share, model), F32),
            shape_of((4 * short, width), BF),
            shape_of((count * weight_share.shape[0], weight_share.shape[1]), BF),
        ),
        in_specs=[
            pl.BlockSpec((rows, width), lambda i: (order_block(i), 0)),
            pl.BlockSpec((model, width), lambda i: (0, column), pipeline_mode=once),
            pl.BlockSpec(prompts.shape, lambda i: (0, 0), pipeline_mode=once),
            pl.BlockSpec((model, width), lambda i: (0, 0), pipeline_mode=once),
            ANY,
        ],
        out_specs=(pl.BlockSpec((share, model), lambda i: (0, 0)), ANY, ANY),
        scratch_shapes=[pltpu.VMEM((short, width), BF)]
        + gather_scratch(16, 128)
        + sum_scratch(share, model)
        + ring_scratch(*weight_share.shape, count // 2),
        compiler_params=local_params(collective_id=1, has_side_effects=True),
        cost_estimate=BUSY,
        name="out_project",
    )(mixed, weights, prompts, prompt_weights, weight_share)


def glu_back_kernel(parts, count, d0_ref, d1_ref, h0_ref, h1_ref, *refs):
    weights = refs[:count]
    o_ref, t0_ref, t1_ref = refs[count : count + 3]
    job = LocalSum(o_ref, refs[count + 3 :])
    step = pl.program_id(0)

    def gate_up():
        term = None
        for left, group in zip((d0_ref, d1_ref), parts):
            base = 0
            for index, low, size in group:
                w_ref = weights[index]
                width = w_ref.shape[1] // 3
                if size == width:
                    part = dot(left[:, base : base + 2 * size], w_ref[:, : 2 * size], NT)
                else:
                    high = low + size
                    part = dot(left[:, base : base + size], w_ref[:, low:high], NT) + dot(
                        left[:, base + size : base + 2 * size],
                        w_ref[:, width + low : width + high],
                        NT,
                    )
                term = part if term is None else term + part
                base += 2 * size
        return term.astype(BF)

    def down():
        term = None
        for left, group in zip((h0_ref, h1_ref), parts):
            base = 0
            for index, low, size in group:
                w_ref = weights[index]
                start = 2 * w_ref.shape[1] // 3 + low
                part = dot(left[:, base : base + size], w_ref[:, start : start + size], NT)
                term = part if term is None else term + part
                base += size
        return term.astype(BF)

    @pl.when(step == 0)
    def _():
        greet([job.to_sib, job.to_far])

    @pl.when(step < 8)
    def _():
        job.put(step, gate_up())

    job.after_step(step)

    @pl.when(step >= 8)
    def _():
        term = down()
        half = t0_ref.shape[1]
        t0_ref[...] = term[:, :half]
        t1_ref[...] = term[:, half:]

    @pl.when(step == 15)
    def _():
        job.land()
        job.finish()


def glu_back(dgus, hiddens, weights, parts):
    length = dgus[0].shape[0]
    model = weights[0].shape[0]
    rows = length // 8
    share = length // 4
    once = pl.Buffered(1)
    early = lambda i: (order_block(jnp.minimum(i, 7)), 0)
    late = lambda i: (jnp.maximum(i - 8, 0), 0)
    in_specs = [pl.BlockSpec((rows, d.shape[1]), early) for d in dgus]
    in_specs += [pl.BlockSpec((rows, h.shape[1]), late) for h in hiddens]
    for weight in weights:
        in_specs.append(pl.BlockSpec(weight.shape, lambda i: (0, 0), pipeline_mode=once))
    half = pl.BlockSpec((rows, model // 2), late)
    return pl.pallas_call(
        functools.partial(glu_back_kernel, parts, len(weights)),
        grid=(16,),
        out_shape=(
            shape_of((share, model), F32),
            shape_of((length, model // 2), BF),
            shape_of((length, model // 2), BF),
        ),
        in_specs=in_specs,
        out_specs=(
            pl.BlockSpec((share, model), lambda i: (0, 0)),
            half,
            half,
        ),
        scratch_shapes=sum_scratch(share, model),
        compiler_params=local_params(collective_id=3, has_side_effects=True),
        cost_estimate=BUSY,
        name="glu_back",
    )(*dgus, *hiddens, *weights)


def mid_kernel(
    count, c_ref, t_ref, n_ref, cb_ref, q_ref, cm_ref, w_ref, m_ref, p_ref, y_ref,
    x_ref, g_ref, dw_ref, yo_ref, s_ref, slots, total, ssem, rsem, *scratch,
):
    small = Scatter(t_ref, s_ref, scratch[:8])
    ring = RingSum(count, [y_ref], scratch[8:])
    me, sib, far, diag = mp_peers()
    dp = lax.axis_index("dp")
    to_sib = {"dp": dp, "mp": sib}
    to_far = {"dp": dp, "mp": far}
    step = pl.program_id(0)
    rows = c_ref.shape[0]
    part = rows // CHUNKS
    spans = [pl.ds(k * part, part) for k in range(CHUNKS)]
    beside = remote(c_ref, slots.at[0], ssem.at[0], rsem.at[0], to_sib)
    across = [
        remote(c_ref.at[span], slots.at[1, span], ssem.at[1 + k], rsem.at[1 + k], to_far)
        for k, span in enumerate(spans)
    ]
    onward = [
        remote(
            slots.at[1, span],
            slots.at[2, span],
            ssem.at[1 + CHUNKS + k],
            rsem.at[1 + CHUNKS + k],
            to_sib,
        )
        for k, span in enumerate(spans)
    ]

    @pl.when(step == 0)
    def _():
        greet([to_sib, to_far, ring.ahead, ring.behind])
        for copy in across:
            copy.start()
        small.start()
        beside.start()
        ring.start()

    @pl.when(step == 4)
    def _():
        for hop in range(1, ring.half // 2):
            ring.hop(hop)

    @pl.when(step == 8)
    def _():
        ring.hop(ring.half // 2)

    @pl.when(step == 1)
    def _():
        small.fold()
        small.local()

    @pl.when(step < 8)
    def _():
        width = q_ref.shape[1]
        x_ref[:, :width] = dot(n_ref[...], q_ref[...], TN).astype(BF)
        x_ref[:, width:] = dot(cb_ref[...], cm_ref[...], TN).astype(BF)

    def use(grads):
        g_ref[...] = dot(grads, w_ref[...], NN).astype(BF)
        return dot(grads, m_ref[...], TN)

    @pl.when(step == 8)
    def _():
        total[...] = use(c_ref[...])

    @pl.when(step == 9)
    def _():
        beside.wait_recv()
        total[...] += use(slots[0])

    @pl.when(step == 10)
    def _():
        for hop in range(ring.half // 2 + 1, ring.half):
            ring.hop(hop)
        small.land()
        for k in range(CHUNKS):
            across[k].wait_recv()
            onward[k].start()
        total[...] += use(slots[1])

    @pl.when(step == 11)
    def _():
        for copy in onward:
            copy.wait_recv()
        width = m_ref.shape[1]
        dw_ref[:, :width] = (total[...] + use(slots[2])).astype(BF)
        dw_ref[:, width:] = dot(p_ref[...], s_ref[...].astype(BF), TN).astype(BF)
        small.finish()
        ring.finish([yo_ref])
        beside.wait_send()
        for copy in across + onward:
            copy.wait_send()


def mid_gather(
    carried, term, normed, cross_back, grad_cq, cross_mixed, weights, column, mixed, prompts,
    more, groups, count,
):
    share, model = carried.shape
    own = more.shape[0] // count
    length, width = mixed.shape
    short, narrow = term.shape[0] // 4, term.shape[1]
    tile = 2 * model // 4
    once = pl.Buffered(1)
    fixed = pl.BlockSpec((share, model), lambda i: (0, 0), pipeline_mode=once)
    left = pl.BlockSpec((share, tile), lambda i: (0, jnp.minimum(i, 7) % 2))
    right = pl.BlockSpec((share, width), lambda i: (0, jnp.minimum(i, 7) // 2))

    def turn(i):
        return (arrival_quarter(jnp.maximum(i - 8, 0)), 0)

    return pl.pallas_call(
        functools.partial(mid_kernel, count),
        grid=(12,),
        in_specs=[
            fixed,
            ANY,
            left,
            left,
            right,
            right,
            pl.BlockSpec((model, width), lambda i: (0, column), pipeline_mode=once),
            pl.BlockSpec((share, width), turn),
            pl.BlockSpec(prompts.shape, lambda i: (0, 0), pipeline_mode=once),
            ANY,
        ],
        out_specs=(
            pl.BlockSpec((tile, 2 * width), lambda i: (jnp.minimum(i, 7), 0)),
            pl.BlockSpec((share, width), turn),
            pl.BlockSpec((model, 2 * width), lambda i: (0, 0)),
            pl.BlockSpec((own, more.shape[1]), lambda i: (0, 0)),
        ),
        out_shape=(
            shape_of((groups * model, 2 * width), BF),
            shape_of((length, width), BF),
            shape_of((model, 2 * width), BF),
            shape_of((own, more.shape[1]), F32),
        ),
        scratch_shapes=[
            pltpu.VMEM((short, narrow), F32),
            pltpu.VMEM((3, share, model), BF),
            pltpu.VMEM((model, width), F32),
            pltpu.SemaphoreType.DMA((1 + 2 * CHUNKS,)),
            pltpu.SemaphoreType.DMA((1 + 2 * CHUNKS,)),
        ]
        + scatter_scratch(short, narrow)
        + ring_sum_scratch(own, more.shape[1], count // 2, 1),
        compiler_params=local_params(collective_id=4, has_side_effects=True),
        cost_estimate=BUSY,
        name="mid_gather",
    )(carried, term, normed, cross_back, grad_cq, cross_mixed, weights, mixed, prompts, more)


def qkv_kernel(
    scale, x_ref, s_ref, r_ref, hot_ref, w_ref, c_ref, u_ref, l_ref,
    n_ref, q_ref, k_ref, v_ref, g_ref, sw_ref, nc_ref, k0_ref, v0_ref,
):
    width = q_ref.shape[1]

    @pl.when(pl.program_id(0) == 0)
    def _():
        side = s_ref[...]
        dims = (8, side.shape[1])
        pick = lax.broadcasted_iota(jnp.int32, dims, 0) == lanes(dims)
        g_ref[...] = dot(jnp.where(pick, 1.0, 0.0).astype(BF), side, NT)
        totals = dot(jnp.ones((8, side.shape[0]), BF), side, NN)
        sw_ref[...] = jnp.broadcast_to(
            scale / jnp.sum(totals * hot_ref[...], axis=1, keepdims=True), sw_ref.shape
        )
        unit, _ = norm_rows(bucket_row(hot_ref[...], r_ref[...]))
        normed = jnp.broadcast_to(unit * g_ref[0:1, :], nc_ref.shape).astype(BF)
        nc_ref[...] = normed
        out = dot(normed, w_ref[:, width:], NN).astype(BF)
        k0_ref[...] = out[:, :width]
        v0_ref[...] = out[:, width:]

    unit, _ = norm_rows(x_ref[...].astype(F32))
    normed = (unit * g_ref[0:1, :]).astype(BF)
    n_ref[...] = normed
    out = dot(normed, w_ref[...], NN)
    cosine, upper, lower = c_ref[...], u_ref[...], l_ref[...]
    for pair in range(width // 128):
        span = slice(128 * pair, 128 * pair + 128)
        q_ref[:, span] = (rope(out[:, span], cosine, upper, lower) * (LOG2E / 8.0)).astype(BF)
        keys = out[:, width + 128 * pair : width + 128 * pair + 128]
        k_ref[:, span] = rope(keys, cosine, upper, lower).astype(BF)
    v_ref[...] = out[:, 2 * width : 3 * width].astype(BF)


def qkv_project(frames, table_rows, hot, weights, tables, width, scale):
    length, model = frames.shape
    rows = 256
    block = pl.BlockSpec((rows, model), lambda i: (i, 0))
    table = pl.BlockSpec((rows, 128), lambda i: (i, 0))
    head = pl.BlockSpec((rows, width), lambda i: (i, 0))
    fixed = lambda i: (0, 0)
    extra = [
        shape_of((8, model), F32),
        shape_of((8, 128), F32),
        shape_of((16, model), BF),
        shape_of((16, width), BF),
        shape_of((16, width), BF),
    ]
    return pl.pallas_call(
        functools.partial(qkv_kernel, scale),
        grid=(length // rows,),
        in_specs=[
            block,
            pl.BlockSpec((model, 128), lambda i: (0, 4 * width // 128)),
            pl.BlockSpec(table_rows.shape, fixed),
            pl.BlockSpec(hot.shape, fixed),
            pl.BlockSpec((model, 3 * width), fixed),
            table,
            table,
            table,
        ],
        out_specs=[block, head, head, head] + [pl.BlockSpec(e.shape, fixed) for e in extra],
        out_shape=[shape_of((length, model), BF)] + [shape_of((length, width), BF)] * 3 + extra,
        compiler_params=local_params(),
        cost_estimate=cost(6 * length * model * width, 8 * length * model),
        name="qkv_project",
    )(frames, weights, table_rows, hot, weights, *tables)


def attend_kernel(
    bk, first, count, q_ref, k_ref, v_ref, k0_ref, v0_ref, x_ref, w_ref, y_ref,
    o_ref, aug_ref, xo_ref, wo_ref, yo_ref, vaug, *scratch,
):
    length = k_ref.shape[0]
    bq = q_ref.shape[0]
    step = pl.program_id(0) * pl.num_programs(1) + pl.program_id(1)
    wide = xo_ref.shape[1]
    job = Gather(x_ref, xo_ref, scratch[:4], pl.ds(first, wide))
    ring = RingGather(count, w_ref, wo_ref, scratch[4:10])
    wide_ring = RingGather(count, y_ref, yo_ref, scratch[10:])
    last = pl.num_programs(0) * pl.num_programs(1) - 1

    @pl.when(step == 0)
    def _():
        greet([job.to_sib, job.to_far, ring.ahead, ring.behind])
        ring.start()
        wide_ring.start()
        job.start()
        ring.place()
        wide_ring.place()

    for hop in range(1, ring.half):

        @pl.when(step == min(3 * hop, 11))
        def _(hop=hop):
            ring.hop(hop)

        @pl.when(step == min(1 + 3 * hop, 11))
        def _(hop=hop):
            wide_ring.hop(hop)

    @pl.when(pl.program_id(1) == 0)
    def _():
        vaug[:, :128] = v_ref[...]
        vaug[:, 128:] = jnp.ones((length, 128), BF)

    queries = q_ref[...]
    key0 = k0_ref[0:1, :].astype(F32)
    value0 = v0_ref[0:1, :].astype(F32)
    outs = []
    logs = []
    for head in range(2):
        masked = half_mask(queries, head)
        peak = jnp.sum(masked.astype(F32) * key0, axis=1, keepdims=True)
        total = jnp.concatenate(
            [jnp.broadcast_to(value0, (bq, 128)), jnp.ones((bq, 128), F32)], 1
        )
        for block in range(length // bk):
            span = slice(block * bk, (block + 1) * bk)
            scores = dot(masked, k_ref[span, :], NT)
            higher = jnp.maximum(peak, jnp.max(scores, axis=1, keepdims=True))
            exponent = jnp.exp2(scores - higher).astype(BF)
            total = total * jnp.exp2(peak - higher) + dot(exponent, vaug[span, :], NN)
            peak = higher
        weight = total[:, 128:129]
        outs.append(total[:, :128] * (1.0 / weight))
        logs.append(-(peak + jnp.log2(weight)))
    lane = lanes((bq, 128))
    o_ref[...] = jnp.where(lane < HD, outs[0], outs[1]).astype(BF)
    aug_ref[...] = (pieces(logs[0], (bq, 128), 0) + pieces(logs[1], (bq, 128), HD)).astype(BF)

    @pl.when(step == last)
    def _():
        for k in range(CHUNKS):
            job.forward(k)
        job.finish()
        ring.finish()
        wide_ring.finish()


def attend(
    queries, keys, values, key0, value0, packed, first, share, more, count, bq=512, bk=1024
):
    length, width = queries.shape
    row = pl.BlockSpec((bq, 128), lambda p, i: (i, p))
    full = pl.BlockSpec((length, 128), lambda p, i: (0, p))
    zero = pl.BlockSpec((16, 128), lambda p, i: (0, p))
    return pl.pallas_call(
        functools.partial(attend_kernel, bk, first, count),
        grid=(width // 128, length // bq),
        in_specs=[row, full, full, zero, zero, ANY, ANY, ANY],
        out_specs=[row, row, ANY, ANY, ANY],
        out_shape=[shape_of((length, width), BF)] * 2
        + [
            shape_of((4 * packed.shape[0], 2 * width), BF),
            shape_of((count * share.shape[0], share.shape[1]), BF),
            shape_of((count * more.shape[0], more.shape[1]), BF),
        ],
        scratch_shapes=[pltpu.VMEM((length, 256), BF)]
        + gather_scratch(packed.shape[0], 2 * width)
        + ring_scratch(*share.shape, count // 2)
        + ring_scratch(*more.shape, count // 2),
        compiler_params=local_params(collective_id=7, has_side_effects=True),
        cost_estimate=cost(16 * length * length * width, 10 * length * width),
        name="attend",
    )(queries, keys, values, key0, value0, packed, share, more)


def attend_back_kernel(
    bk, count, q_ref, aug_ref, o_ref, do_ref, k_ref, v_ref, k0_ref, v0_ref,
    cq_ref, uq_ref, lq_ref, ck_ref, uk_ref, lk_ref,
    x_ref, y_ref, t_ref, ac_ref, dq_ref, dk_ref, dv_ref, dk0_ref, dv0_ref, xh_ref,
    yo_ref, zo_ref,
    to_ref, xo0_ref, xo1_ref, kaug, vaug, kt, dka, dva, xs, xsem, *scratch,
):
    length = k_ref.shape[0]
    bq = q_ref.shape[0]
    step = pl.program_id(1)
    turn = pl.program_id(0) * pl.num_programs(1) + step
    job = Scatter(x_ref, xs, scratch[:8])
    late = Scatter(t_ref, to_ref, scratch[8:16])
    ring = RingSum(count, [y_ref], scratch[16:26])
    next_ring = RingSum(count, [xh_ref], scratch[26:])
    keep = pltpu.make_async_copy(xs, xh_ref, xsem)

    @pl.when(turn == 0)
    def _():
        greet([job.to_sib, job.to_far, ring.ahead, ring.behind])
        job.start()
        ring.start()

    @pl.when(turn == 1)
    def _():
        job.fold()
        job.local()
        late.start()

    for hop in range(1, ring.half):

        @pl.when(turn == min(1 + 2 * hop, 7))
        def _(hop=hop):
            ring.hop(hop)

        @pl.when(turn == min(8 + hop, 11))
        def _(hop=hop):
            next_ring.hop(hop)

    @pl.when(turn == 8)
    def _():
        job.land()
        keep.start()
        late.fold()
        late.local()
        keep.wait()
        next_ring.start()
        job.finish()
        ring.finish([yo_ref, zo_ref])

    @pl.when(step == 0)
    def _():
        lane = lanes((length, 128))
        ones = jnp.where((lane % HD) < 3, 1.0, 0.0).astype(BF)
        kaug[:, :128] = k_ref[...]
        kaug[:, 128:] = ones
        vaug[:, :128] = v_ref[...]
        vaug[:, 128:] = ones
        kt[...] = k_ref[...].astype(F32).T.astype(BF)
        dka[...] = jnp.zeros_like(dka)
        dva[...] = jnp.zeros_like(dva)
        dk0_ref[...] = jnp.zeros_like(dk0_ref)
        dv0_ref[...] = jnp.zeros_like(dv0_ref)

    queries = q_ref[...]
    grads = do_ref[...]
    aug = aug_ref[...]
    product = grads.astype(F32) * o_ref[...].astype(F32)
    lane = lanes((bq, 128))
    ones0 = jnp.where((lanes((16, 128)) % HD) < 3, 1.0, 0.0).astype(BF)
    key0 = jnp.concatenate([k0_ref[...], ones0], 1)
    value0 = jnp.concatenate([v0_ref[...], ones0], 1)
    row0 = lax.broadcasted_iota(jnp.int32, (16, bq), 0) == 0
    qa, da, qm, dm, dq = [], [], [], [], []
    for head in range(2):
        qm.append(half_mask(queries, head))
        dm.append(half_mask(grads, head))
        mine = (lane < HD) if head == 0 else (lane >= HD)
        inner = jnp.sum(jnp.where(mine, product, 0.0), axis=1, keepdims=True)
        qa.append(jnp.concatenate([qm[head], half_mask(aug, head)], 1))
        da.append(
            jnp.concatenate([dm[head], pieces(-inner, (bq, 128), HD * head).astype(BF)], 1)
        )
        prob0 = jnp.where(row0, jnp.exp2(dot(key0, qa[head], NT)), 0.0)
        ds0 = (prob0 * dot(value0, da[head], NT)).astype(BF)
        dv0_ref[...] += dot(prob0.astype(BF), dm[head], NN)
        dk0_ref[...] += dot(ds0, qm[head], NN)
        dq.append(dot(k0_ref[:, HD * head : HD * head + HD], ds0, TN))
    for block in range(length // bk):
        span = slice(block * bk, (block + 1) * bk)
        for head in range(2):
            probs = jnp.exp2(dot(kaug[span, :], qa[head], NT))
            ds = (probs * dot(vaug[span, :], da[head], NT)).astype(BF)
            dva[span, :] += dot(probs.astype(BF), dm[head], NN)
            dka[span, :] += dot(ds, qm[head], NN)
            dq[head] = dq[head] + dot(kt[HD * head : HD * head + HD, span], ds, NN)
    grad_q = jnp.concatenate(dq, 0).T * 0.125
    dq_ref[...] = rope(grad_q, cq_ref[...], -uq_ref[...], -lq_ref[...]).astype(BF)

    @pl.when(turn == pl.num_programs(0) * pl.num_programs(1) - 1)
    def _():
        late.land(ac_ref)
        late.finish()
        next_ring.finish([xo0_ref, xo1_ref])

    @pl.when(step == pl.num_programs(1) - 1)
    def _():
        grad_k = dka[...] * (1.0 / LOG2E)
        dk_ref[...] = rope(grad_k, ck_ref[...], -uk_ref[...], -lk_ref[...]).astype(BF)
        dv_ref[...] = dva[...].astype(BF)
        dk0_ref[...] = dk0_ref[...] * (1.0 / LOG2E)


def attend_back(
    queries, aug, mixed, grads, keys, values, key0, value0, tables, extra, more, term, after_cross, count,
    bq=512, bk=512,
):
    length, width = queries.shape
    row = pl.BlockSpec((bq, 128), lambda p, i: (i, p))
    full = pl.BlockSpec((length, 128), lambda p, i: (0, p))
    zero = pl.BlockSpec((16, 128), lambda p, i: (0, p))
    tq = pl.BlockSpec((bq, 128), lambda p, i: (i, 0))
    tk = pl.BlockSpec((length, 128), lambda p, i: (0, 0), pipeline_mode=pl.Buffered(1))
    own = more.shape[0] // count
    owned = pl.BlockSpec((own, more.shape[1] // 2), lambda p, i: (0, 0))
    wide, narrow = extra.shape[0] // 4, extra.shape[1]
    half_shape = (after_cross.shape[0], term.shape[1])
    share_spec = pl.BlockSpec(half_shape, lambda p, i: (0, 0))
    part = pl.BlockSpec((own, narrow // 2), lambda p, i: (0, 0))
    big = shape_of((length, width), BF)
    small = shape_of((16, width), F32)
    return pl.pallas_call(
        functools.partial(attend_back_kernel, bk, count),
        grid=(width // 128, length // bq),
        in_specs=[row, row, row, row, full, full, zero, zero, tq, tq, tq, tk, tk, tk, ANY, ANY, ANY,
            pl.BlockSpec(half_shape, lambda p, i: (0, 1), pipeline_mode=pl.Buffered(1)),
        ],
        out_specs=[row, full, full, zero, zero, ANY, owned, owned, share_spec, part, part],
        out_shape=[big, big, big, small, small]
        + [
            shape_of((wide, narrow), BF),
            shape_of((own, more.shape[1] // 2), F32),
            shape_of((own, more.shape[1] // 2), F32),
            shape_of(half_shape, BF),
            shape_of((own, narrow // 2), F32),
            shape_of((own, narrow // 2), F32),
        ],
        scratch_shapes=[pltpu.VMEM((length, 256), BF)] * 2
        + [pltpu.VMEM((128, length), BF)]
        + [pltpu.VMEM((length, 128), F32)] * 2
        + [
            pltpu.VMEM((wide, narrow), BF),
            pltpu.SemaphoreType.DMA(()),
        ]
        + scatter_scratch(wide, narrow)
        + scatter_scratch(*half_shape)
        + ring_sum_scratch(own, more.shape[1], count // 2, 1)
        + ring_sum_scratch(own, narrow, count // 2, 1),
        compiler_params=local_params(collective_id=8, has_side_effects=True),
        cost_estimate=cost(40 * length * length * width, 20 * length * width),
        name="attend_back",
    )(queries, aug, mixed, grads, keys, values, key0, value0, *tables, *tables, extra, more, term, after_cross)


def softmax_keys(scores, length):
    key = lax.broadcasted_iota(jnp.int32, scores.shape, 0)
    masked = jnp.where(key < length, scores, -1e9)
    exponent = jnp.exp2(masked - jnp.max(masked, axis=0, keepdims=True))
    return exponent * (1.0 / jnp.sum(exponent, axis=0, keepdims=True))


def two_heads(values):
    return jnp.concatenate([half_mask(values, 0), half_mask(values, 1)], 0)


def one_row(values):
    rows = values.shape[0] // 2
    lane = lanes((rows, 128))
    return jnp.where(lane < HD, values[:rows], values[rows:])


def cross_kernel(
    count, len_ref, f_ref, s_ref, g_ref, wq_ref, wo_ref, kv_ref, share_ref,
    as_ref, n2_ref, q_ref, m_ref, ac_ref, n3_ref, full_ref, mine, *scratch,
):
    job = Gather(mine, n3_ref, scratch[:4], here=True)
    ring = RingGather(count, share_ref, full_ref, scratch[4:])
    step = pl.program_id(0)
    groups, model, width = wq_ref.shape
    keys = kv_ref.shape[1] // 2

    @pl.when(step == 0)
    def _():
        greet([job.to_sib, job.to_far, ring.ahead, ring.behind])
        ring.start()

    after_self = f_ref[...].astype(F32) + s_ref[...]
    as_ref[...] = after_self
    unit, _ = norm_rows(after_self)
    normed = (unit * g_ref[1:2, :]).astype(BF)
    n2_ref[...] = normed
    rows = normed.shape[0]
    total = after_self
    for group in range(groups):
        queries = (dot(normed, wq_ref[group], NN) * (LOG2E / 8.0)).astype(BF)
        base = group * width
        q_ref[:, base : base + width] = queries
        for pair in range(width // 128):
            span = slice(128 * pair, 128 * pair + 128)
            scores = dot(kv_ref[group, :keys, span], two_heads(queries[:, span]), NT)
            probs = softmax_keys(scores, len_ref[0])
            m_ref[:, base + 128 * pair : base + 128 * pair + 128] = one_row(
                dot(probs.astype(BF), kv_ref[group, keys:, span], TN)
            ).astype(BF)
        total = total + dot(m_ref[:, base : base + width], wo_ref[group], NT)
    ac_ref[...] = total
    unit, _ = norm_rows(total)
    mine[pl.ds(pl.multiple_of(step * rows, rows), rows), :] = (unit * g_ref[2:3, :]).astype(BF)

    for turn in range(2):

        @pl.when(step == turn)
        def _(turn=turn):
            half = CHUNKS // 2
            for k in range(turn * half, turn * half + half):
                job.across[k].start()
                job.beside[k].start()
            if turn == 0:
                ring.place()
                ring.hop(1)

    @pl.when(step == 1)
    def _():
        job.store.start()
        for hop in range(2, ring.half):
            ring.hop(hop)
        for k in range(CHUNKS):
            job.forward(k)
        job.finish()
        ring.finish()


def cross_forward(plen, frames, summed, gains, weights, prompt_kv, share, count):
    own, model = frames.shape
    groups, _, both = weights.shape
    width = both // 2
    rows = own // 2
    block = pl.BlockSpec((rows, model), lambda i: (i, 0))
    gain = pl.BlockSpec(gains.shape, lambda i: (0, 0))
    once = pl.Buffered(1)
    return pl.pallas_call(
        functools.partial(cross_kernel, count),
        grid=(2,),
        in_specs=[
            pl.BlockSpec(memory_space=pltpu.SMEM),
            block,
            block,
            gain,
            pl.BlockSpec((groups, model, width), lambda i: (0, 0, 0), pipeline_mode=once),
            pl.BlockSpec((groups, model, width), lambda i: (0, 0, 1), pipeline_mode=once),
            pl.BlockSpec(prompt_kv.shape, lambda i: (0, 0, 0)),
            ANY,
        ],
        out_specs=[block] * 5 + [ANY, ANY],
        out_shape=[
            shape_of((own, model), F32),
            shape_of((own, model), BF),
            shape_of((own, model), BF),
            shape_of((own, model), BF),
            shape_of((own, model), F32),
            shape_of((4 * own, model), BF),
            shape_of((count * share.shape[0], share.shape[1]), BF),
        ],
        scratch_shapes=[pltpu.VMEM((own, model), BF)]
        + gather_scratch(16, 128)
        + ring_scratch(*share.shape, count // 2),
        compiler_params=local_params(collective_id=2, has_side_effects=True),
        cost_estimate=BUSY,
        name="cross_forward",
    )(plen, frames, summed, gains, weights, weights, prompt_kv, share)


def cross_back_kernel(
    len_ref, w_ref, go_ref, e_ref, ac_ref, as_ref, g_ref, q_ref, wq_ref, wo_ref, kv_ref, t_ref,
    cb_ref, dq_ref, c3_ref, c3b_ref, dkv_ref, dg_ref, bo_ref, dkv, hold, *scratch,
):
    groups, model, width = wq_ref.shape
    keys = kv_ref.shape[1] // 2
    job = Scatter(t_ref, bo_ref, scratch)
    step = pl.program_id(0)

    @pl.when(step == 0)
    def _():
        greet([job.to_sib, job.to_far])
        job.start()

    @pl.when(pl.program_id(0) == 0)
    def _():
        dkv[...] = jnp.zeros_like(dkv)
        dg_ref[...] = jnp.zeros_like(dg_ref)

    unit, spread = norm_rows(ac_ref[...])
    back, part = norm_back(e_ref[...], unit, spread, g_ref[2:3, :])
    dg_ref[2:3, :] += part
    carried = go_ref[...].astype(F32) * w_ref[0:1, 0:1] + back
    cross_back = carried.astype(BF)
    cb_ref[...] = cross_back
    rows = cross_back.shape[0]
    total = jnp.zeros((rows, model), F32)
    spot = pl.ds(pl.multiple_of(pl.program_id(0) * rows, rows), rows)
    hold[spot, :] = ac_ref[:, : hold.shape[1]]

    @pl.when(step == 0)
    def _():
        job.fold()
        job.local()

    for group in range(groups):
        grads = dot(cross_back, wo_ref[group], NN).astype(BF)
        base = group * width
        for pair in range(width // 128):
            span = slice(128 * pair, 128 * pair + 128)
            wide = slice(base + 128 * pair, base + 128 * pair + 128)
            queries = two_heads(q_ref[:, wide])
            masked = two_heads(grads[:, span])
            probs = softmax_keys(dot(kv_ref[group, :keys, span], queries, NT), len_ref[0])
            dprobs = dot(kv_ref[group, keys:, span], masked, NT)
            inner = jnp.sum(dprobs * probs, axis=0, keepdims=True)
            ds = (probs * (dprobs - inner)).astype(BF)
            dkv[group, :keys, span] += dot(ds, queries, NN) * (1.0 / LOG2E)
            dkv[group, keys:, span] += dot(probs.astype(BF), masked, NN)
            grad_q = one_row(dot(ds, kv_ref[group, :keys, span], TN))
            dq_ref[:, wide] = (grad_q * 0.125).astype(BF)
        total = total + dot(dq_ref[:, base : base + width], wq_ref[group], NT)
    unit, spread = norm_rows(as_ref[...])
    back, part = norm_back(total, unit, spread, g_ref[1:2, :])
    dg_ref[1:2, :] += part
    carried = carried + back
    c3_ref[...] = carried
    c3b_ref[...] = carried.astype(BF)

    @pl.when(pl.program_id(0) == pl.num_programs(0) - 1)
    def _():
        dkv_ref[...] = dkv[...].astype(BF)
        job.land(hold)
        job.finish()


def cross_backward(plen, weight, grad_out, summed, after_cross, after_self, gains, queries,
                   weights, prompt_kv, term):
    share, model = grad_out.shape
    groups, _, both = weights.shape
    width = both // 2
    rows = 256
    block = pl.BlockSpec((rows, model), lambda i: (i, 0))
    gain = pl.BlockSpec(gains.shape, lambda i: (0, 0))
    once = pl.Buffered(1)
    return pl.pallas_call(
        cross_back_kernel,
        grid=(share // rows,),
        in_specs=[
            pl.BlockSpec(memory_space=pltpu.SMEM),
            pl.BlockSpec(weight.shape, lambda i: (0, 0)),
            block,
            block,
            block,
            block,
            gain,
            block,
            pl.BlockSpec((groups, model, width), lambda i: (0, 0, 0), pipeline_mode=once),
            pl.BlockSpec((groups, model, width), lambda i: (0, 0, 1), pipeline_mode=once),
            pl.BlockSpec(prompt_kv.shape, lambda i: (0, 0, 0)),
            ANY,
        ],
        out_specs=[block] * 4
        + [pl.BlockSpec(prompt_kv.shape, lambda i: (0, 0, 0)), gain]
        + [pl.BlockSpec((share, term.shape[1]), lambda i: (0, 0))],
        out_shape=[
            shape_of((share, model), BF),
            shape_of((share, model), BF),
            shape_of((share, model), F32),
            shape_of((share, model), BF),
            shape_of(prompt_kv.shape, BF),
            shape_of(gains.shape, F32),
            shape_of((share, term.shape[1]), BF),
        ],
        scratch_shapes=[
            pltpu.VMEM(prompt_kv.shape, F32),
            pltpu.VMEM((share, term.shape[1]), F32),
        ]
        + scatter_scratch(share, term.shape[1]),
        compiler_params=local_params(collective_id=9, has_side_effects=True),
        cost_estimate=cost(4 * share * model * model, 4 * model * model + 24 * share * model),
        name="cross_backward",
    )(plen, weight, grad_out, summed, after_cross, after_self, gains, queries, weights, weights,
      prompt_kv, term)


def glu_kernel(scaled, parts, count, *refs):
    refs = list(refs)
    s_ref = None if scaled else refs.pop(0)
    n_ref, c_ref = refs[:2]
    weights, outs = refs[2 : 2 + count], refs[2 + count :]
    cot = c_ref[...]
    if not scaled:
        cot = (cot.astype(F32) * s_ref[0:1, 0:1]).astype(BF)
        outs[2][...] = cot
    h_ref, d_ref = outs[:2]
    normed = n_ref[...]
    piece = 256
    at = 0
    for index, low, size in parts:
        w_ref = weights[index]
        width = w_ref.shape[1] // 3
        for base in range(0, size, piece):
            spot = low + base
            gate = dot(normed, w_ref[:, spot : spot + piece], NN)
            up = dot(normed, w_ref[:, width + spot : width + spot + piece], NN)
            grads = dot(cot, w_ref[:, 2 * width + spot : 2 * width + spot + piece], NN)
            sig = 1.0 / (1.0 + jnp.exp(-gate))
            silu = gate * sig
            h_ref[:, at + base : at + base + piece] = (silu * up).astype(BF)
            grad_gate = grads * up * sig * (1.0 + gate * (1.0 - sig))
            spot = 2 * at + base
            d_ref[:, spot : spot + piece] = grad_gate.astype(BF)
            d_ref[:, size + spot : size + spot + piece] = (grads * silu).astype(BF)
        at += size


def glu_block(normed, cot, weights, parts, scale=None):
    length, model = normed.shape
    width = sum(size for _, _, size in parts)
    rows = 512
    block = pl.BlockSpec((rows, model), lambda i: (i, 0))
    first = scale is not None
    return pl.pallas_call(
        functools.partial(glu_kernel, not first, parts, len(weights)),
        grid=(length // rows,),
        in_specs=[pl.BlockSpec((8, 128), lambda i: (0, 0))] * first
        + [block, block]
        + [
            pl.BlockSpec(weight.shape, lambda i: (0, 0), pipeline_mode=pl.Buffered(1))
            for weight in weights
        ],
        out_specs=[
            pl.BlockSpec((rows, width), lambda i: (i, 0)),
            pl.BlockSpec((rows, 2 * width), lambda i: (i, 0)),
        ]
        + [block] * first,
        out_shape=[shape_of((length, width), BF), shape_of((length, 2 * width), BF)]
        + [shape_of((length, model), BF)] * first,
        compiler_params=local_params(),
        cost_estimate=cost(6 * length * model * width, 6 * length * model),
        name="glu_block_%d" % width,
    )(*([scale] if first else []), normed, cot, *weights)


def grads_kernel(plan, n_ref, c_ref, d_ref, h_ref, *outs):
    for out, spans in zip(outs, plan):
        base = 0
        for side, low, high in spans:
            left, right = (n_ref, d_ref) if side == 0 else (c_ref, h_ref)
            value = dot(left[...], right[:, low:high], TN)
            out[:, base : base + high - low] = value.astype(BF)
            base += high - low


def weight_grads(normed, cot, dgu, hidden, plan, tile=256):
    length, model = normed.shape
    widths = [sum(high - low for _, low, high in spans) for spans in plan]
    once = pl.Buffered(1)
    left = pl.BlockSpec((length, tile), lambda i: (0, i))
    return pl.pallas_call(
        functools.partial(grads_kernel, plan),
        grid=(model // tile,),
        in_specs=[left, left]
        + [pl.BlockSpec(right.shape, lambda i: (0, 0), pipeline_mode=once) for right in (dgu, hidden)],
        out_specs=[pl.BlockSpec((tile, wide), lambda i: (i, 0)) for wide in widths],
        out_shape=[shape_of((model, wide), BF) for wide in widths],
        compiler_params=local_params(),
        cost_estimate=cost(2 * length * model * sum(widths), 2 * length * (2 * model + sum(widths))),
        name="weight_grads_%d" % sum(widths),
    )(normed, cot, dgu, hidden)


def last_grads_kernel(plan, copies, count, n_ref, q_ref, k_ref, v_ref, nc_ref, k0_ref, v0_ref, *refs):
    sources, rest = refs[:count], refs[count:]
    passed, (o_ref, gate_ref, up_ref, down_ref), targets = (
        rest[: -4 - len(copies)],
        rest[-4 - len(copies) : len(rest) - len(copies)],
        rest[len(rest) - len(copies) :],
    )
    width = q_ref.shape[1]
    normed = n_ref[...]
    edge = nc_ref[...]
    o_ref[:, :width] = dot(normed, q_ref[...], TN).astype(BF)
    grad_k = dot(normed, k_ref[...], TN) + dot(edge, k0_ref[...].astype(BF), TN)
    o_ref[:, width : 2 * width] = grad_k.astype(BF)
    grad_v = dot(normed, v_ref[...], TN) + dot(edge, v0_ref[...].astype(BF), TN)
    o_ref[:, 2 * width :] = grad_v.astype(BF)

    @pl.when(pl.program_id(0) == 0)
    def _():
        for source, base, kind, low, size in plan:
            target = (gate_ref, up_ref, down_ref)[kind]
            target[:, low : low + size] = sources[source][:, base : base + size].astype(F32)

    @pl.when(pl.program_id(0) == 1)
    def _():
        for target, (dims, places) in zip(targets, copies):
            for index, from_row, rows, row, column in places:
                ref = passed[index]
                value = ref[from_row : from_row + rows, :]
                target[row : row + rows, column : column + ref.shape[1]] = value


def last_grads(normed, grads, edge, dk0, dv0, sources, plan, hidden, passed, copies, tile=256):
    length, model = normed.shape
    width = grads[0].shape[1]
    own = sources[0].shape[0]
    once = pl.Buffered(1)
    fixed = lambda i: (0, 0)

    def full(array):
        return pl.BlockSpec(array.shape, fixed, pipeline_mode=once)

    extra = [shape_of(dims, passed[places[0][0]].dtype) for dims, places in copies]
    return pl.pallas_call(
        functools.partial(last_grads_kernel, plan, copies, len(sources)),
        grid=(model // tile,),
        in_specs=[pl.BlockSpec((length, tile), lambda i: (0, i))]
        + [full(grad) for grad in grads]
        + [pl.BlockSpec((edge.shape[0], tile), lambda i: (0, i)), full(dk0), full(dv0)]
        + [full(source) for source in sources]
        + [full(array) for array in passed],
        out_specs=[pl.BlockSpec((tile, 3 * width), lambda i: (i, 0))]
        + [pl.BlockSpec((own, hidden), fixed)] * 3
        + [pl.BlockSpec(array.shape, fixed) for array in extra],
        out_shape=[shape_of((model, 3 * width), BF)]
        + [shape_of((own, hidden), F32)] * 3
        + extra,
        compiler_params=local_params(),
        cost_estimate=cost(6 * length * model * width, 2 * length * (model + 3 * width)),
        name="last_grads",
    )(normed, *grads, edge, dk0, dv0, *sources, *passed)


def owner_sum(term):
    return lax.psum_scatter(term, "dp", scatter_dimension=0, tiled=True)


def after(value, *others):
    return lax.optimization_barrier((value,) + others)[0]


GLU_PARTS = 3


def per_device(
    frames, cond_table, bucket_ids, prompt, prompt_len,
    attn_query, attn_key, attn_value, attn_out,
    cross_query, cross_key, cross_value, cross_out,
    glu_gate, glu_up, glu_down, first_gain, second_gain, third_gain, grad_out,
):
    groups = lax.axis_size("mp")
    count = lax.axis_size("dp")
    sequences = bucket_ids.shape[0]
    assert sequences == 1 and groups == 4
    share, model = frames.shape
    length = share * groups
    buckets = cond_table.shape[0]
    own_rows, width = attn_query.shape
    unit = glu_gate.shape[1] // GLU_PARTS
    context = prompt.shape[2]

    onehot = (bucket_ids[:, None] == jnp.arange(buckets)[None, :]).astype(F32)
    gain_rows = jnp.pad(jnp.stack([first_gain, second_gain, third_gain]), ((0, 5), (0, 0)))
    hot = jnp.pad(onehot, ((0, 0), (3, 128 - 3 - buckets)))
    prompt_blocks = prompt.reshape(-1, count, context // count)
    blank = jnp.zeros_like(prompt_blocks)
    prompts = jnp.concatenate(
        [
            jnp.concatenate([prompt_blocks, blank], 2).reshape(-1, model),
            jnp.concatenate([blank, prompt_blocks], 2).reshape(-1, model),
        ],
        0,
    )
    prompt_share = jnp.concatenate([cross_key, cross_value], 0)
    frames_all, grad_all, first, *glu_share = head_gather(
        frames, grad_out, gain_rows, hot,
        [attn_query, attn_key, attn_value, attn_out, cross_query, cross_out],
        [glu_gate, glu_up, glu_down], GLU_PARTS, count,
    )

    tables = rope_tables(length, 1.0)
    scale = sequences * count * own_rows / buckets
    (
        normed_one, queries, keys, values, gains, seq_weight, normed_cond, key0, value0,
    ) = qkv_project(frames_all, cond_table, hot, first, tables, width, scale)
    mixed, aug, cross_full, second, glu_first = attend(
        queries, keys, values, key0, value0, first, 4 * width + 128, prompt_share,
        glu_share[0], count,
    )
    cross_full = cross_full.reshape(groups, model, 2 * width)
    self_out, prompt_kv, glu_second = out_project(
        mixed, first, 3, prompts, second, glu_share[1], count
    )
    prompt_kv = prompt_kv.reshape(groups, prompts.shape[0], width)

    (
        after_self, normed_two, cross_q, cross_mixed, after_cross, normed_three, glu_third,
    ) = cross_forward(
        prompt_len, frames, self_out, gains, cross_full, prompt_kv, glu_share[2], count
    )
    glu_full = [glu_first, glu_second, glu_third]
    half = unit // 2
    parts = (((0, 0, half),), ((0, half, half), (1, 0, unit), (2, 0, unit)))
    h0, d0, cot_all = glu_block(normed_three, grad_all, glu_full[:1], parts[0], seq_weight)
    (pack0,) = weight_grads(normed_three, cot_all, d0, h0, (((0, 0, unit), (1, 0, half)),))
    h1, d1 = glu_block(after(normed_three, pack0), cot_all, glu_full, parts[1])
    wide = unit + 2 * unit
    pack1, pack2 = weight_grads(
        normed_three, cot_all, d1, h1,
        (
            (
                (0, 0, unit), (1, 0, half),
                (0, unit, wide), (1, half, half + unit),
                (0, wide, wide + half), (0, wide + unit, wide + unit + half),
                (1, half + unit, 2 * unit),
            ),
            (
                (0, wide + half, wide + unit), (0, wide + unit + half, wide + 2 * unit),
                (1, 2 * unit, 2 * unit + half),
            ),
        ),
    )
    glu_sum0 = owner_sum(pack0)
    pack1 = after(pack1, glu_sum0)
    glu_sum1 = owner_sum(pack1)
    back_term, out_term0, out_term1 = glu_back(
        [after(d0, pack1), d1], [h0, h1], glu_full, parts
    )

    cross_back, grad_cq, carried, carried_low, grad_kv, grad_gains, block0 = cross_backward(
        prompt_len, seq_weight, grad_out, back_term, after_cross, after_self, gains, cross_q,
        cross_full, prompt_kv, out_term0,
    )
    cross_term, grad_mixed, second_pack, glu_sum2 = mid_gather(
        carried_low, grad_kv.reshape(-1, width), normed_two, cross_back, grad_cq, cross_mixed,
        first, 3, mixed, prompts, pack2, groups, count,
    )
    (
        dq, dk, dv, dk0, dv0, _, grad_out_own, grad_prompt, block1, grad_cross_q, grad_cross_o,
    ) = attend_back(
        queries, aug, mixed, grad_mixed, keys, values, key0, value0, tables, cross_term,
        second_pack, out_term1, after_cross, count,
    )
    plan = []
    pieces_of = (
        (0, 0, 0, half), (1, 0, half, half), (1, 3 * half, unit, unit),
        (1, 9 * half, 2 * unit, half), (2, 0, 2 * unit + half, half),
    )
    for source, base, low, size in pieces_of:
        for kind in range(3):
            plan.append((source, base + kind * size, kind, low, size))
    short = context // count
    copies = (
        ((share, model), ((0, 0, share, 0, 0), (1, 0, share, 0, model // 2))),
        ((own_rows, width), ((2, 0, own_rows, 0, 0),)),
        ((own_rows, width), ((3, 0, own_rows, 0, 0),)),
        ((short, width), ((4, 0, short, 0, 0),)),
        ((short, width), ((4, short, short, 0, 0),)),
        ((own_rows, width), ((5, 0, own_rows, 0, 0),)),
    )
    (
        first_pack, *glu_out, block_out, grad_out_own, grad_cross_q, grad_cross_k, grad_cross_v,
        grad_cross_o,
    ) = last_grads(
        normed_one, [dq, dk, dv], normed_cond, dk0, dv0, [glu_sum0, glu_sum1, glu_sum2], plan,
        glu_gate.shape[1],
        [block0, block1, grad_out_own, grad_cross_q, grad_prompt, grad_cross_o], copies,
    )
    frames_grad, sums, first_grad = tail_sums(
        count, buckets, [dq, dk, dv], frames_all, first, first_pack, frames, carried, gains, grad_gains, hot,
        cond_table, dk0, dv0,
    )
    return (
        block_out,
        frames_grad,
        sums[:buckets],
        first_grad[:, :width],
        first_grad[:, width : 2 * width],
        first_grad[:, 2 * width :],
        grad_out_own,
        grad_cross_q,
        grad_cross_k,
        grad_cross_v,
        grad_cross_o,
        *glu_out,
        sums[buckets],
        sums[buckets + 1],
        sums[buckets + 2],
    )


def solution(mesh):
    both = P(("dp", "mp"), None)
    weight = P("dp", "mp")
    return jax.shard_map(
        per_device,
        mesh=mesh,
        in_specs=(both, P(), P("dp"), P("dp", None, None), P("dp"))
        + (weight,) * 11
        + (P("dp"),) * 3
        + (both,),
        out_specs=(both, both, P()) + (weight,) * 11 + (P(),) * 3,
        check_vma=False,
    )
```
